32 devices in a mesh: batch: 8 (over y, x, core), wide: 4 (over z).
Axes of the slice: x: 2, y: 2, z: 4, core: 2. Of those that a mesh axis runs over, the one named last changes fastest.
Arguments:
- inputs: bfloat16 [2, 8, 2048, 1024], P(None, 'batch', 'wide'), may hold values from -6 to 6
- skips: bfloat16 [2, 8, 2048, 1024], P(None, 'batch', 'wide'), may hold values from -6 to 6
- cotangent: bfloat16 [2, 8, 2048, 1024], P(None, 'batch', 'wide'), may hold values from -6 to 6
- segment_ids: int32 [2, 8, 2048], P(None, 'batch'), may hold values from 0 to 3, never falling along the last dimension, each value on 1 to 1024 neighbouring positions
- time_steps: int32 [2, 8, 4], P(None, 'batch'), may hold values from 0 to 999
- w_skip: bfloat16 [2048, 1024], P(('batch', 'wide')), may hold values from -0.125 to 0.125
- w_qkv: bfloat16 [1024, 3072], P(('batch', 'wide')), may hold values from -0.1875 to 0.1875
- w_out: bfloat16 [1024, 1024], P(('batch', 'wide')), may hold values from -1.5 to 1.5
- w_up: bfloat16 [1024, 4096], P(('batch', 'wide')), may hold values from -0.1875 to 0.1875
- w_down: bfloat16 [4096, 1024], P(('batch', 'wide')), may hold values from -0.09375 to 0.09375
- w_mod: bfloat16 [256, 4096], P(None, ('batch', 'wide')), may hold values from -0.25 to 0.25
Outputs:
- block_out: bfloat16 [2, 8, 2048, 1024], P(None, 'batch', 'wide')
- grad_inputs: bfloat16 [2, 8, 2048, 1024], P(None, 'batch', 'wide')
- grad_skips: bfloat16 [2, 8, 2048, 1024], P(None, 'batch', 'wide')
- grad_w_skip: float32 [2048, 1024], P(('batch', 'wide'))
- grad_w_qkv: float32 [1024, 3072], P(('batch', 'wide'))
- grad_w_out: float32 [1024, 1024], P(('batch', 'wide'))
- grad_w_up: float32 [1024, 4096], P(('batch', 'wide'))
- grad_w_down: float32 [4096, 1024], P(('batch', 'wide'))
- grad_w_mod: float32 [256, 4096], P(None, ('batch', 'wide'))
The draws below stay inside these ranges and needn't reach their ends.
Inputs may be any that keep to these rules, and one draw needn't show every extreme that they name: `segment_ids`: segment ids never fall along a row; each of the 4 ids holds 1 to 1024 frames of its row, and some row of every draw has an utterance of exactly 1024 frames.
All inputs are finite; a program needn't handle non-finite values.
Results may differ from the reference program's by a relative error of at most 0.017.
Values may be sent and summed in bfloat16 or wider, within the bound.
No kernel may reach another device: no remote copies, remote signals or barrier semaphores. Data moves between devices by JAX's collectives and lax.ppermute only.
A program may use at most 320 MiB of HBM per device.

```python
import math
import jax
import jax.numpy as jnp
import numpy as np
from jax import lax

D = 1024
HEADS = 16
HEAD_DIM = 64
FF = 4096
FREQ = 256
SEQ = 2048
NSEG = 4
MB = 2
NROWS = 8


def touch_ends(drawn, key, smallest, largest):
    longest = drawn.shape.index(max(drawn.shape))
    spots = []
    for shift in (0, 1):
        where = [jax.random.randint(jax.random.fold_in(key, axis), (), 0, length) for axis, length in enumerate(drawn.shape)]
        where[longest] = (where[longest] + shift) % drawn.shape[longest]
        spots.append(tuple(where))
    return drawn.at[spots[0]].set(smallest).at[spots[1]].set(largest)


def shard_levels(stream_key, extent, cuts, least, high):
    gain, own = 1.0, jax.random.fold_in(stream_key, 6)
    for position, blocks in cuts:
        draws = jnp.exp(jax.random.uniform(jax.random.fold_in(own, position), (blocks,), jnp.float32, least / len(cuts), high / len(cuts)))
        gain = gain * jnp.repeat(draws, extent[position] // blocks).reshape([-1 if axis == position else 1 for axis in range(len(extent))])
    return gain


def profile(count, total, most, lean):
    portions = [(1 << 20) // math.isqrt(standing ** lean) + 1 for standing in range(2, count + 1)]
    spare, given = total - most - (count - 1), [1] * (count - 1)
    while spare > 0:
        candidates = [i for i in range(count - 1) if given[i] < most]
        mass, budget = sum([portions[i] for i in candidates]), spare
        for i in candidates:
            extra = min(most - given[i], max(1, budget * portions[i] // mass), spare)
            given[i] = given[i] + extra
            spare = spare - extra
    return np.array([most] + given)


def ragged_sizes(stream_key, amount, total, bound, skew):
    if amount == 2:
        one = jax.random.randint(stream_key, (), max(1, total - bound), min(bound, total - 1) + 1)
        return jnp.stack([one, total - one])
    sizes = jnp.asarray(profile(amount, total, bound, skew), jnp.int32)
    twos = (amount - 1) // 2
    giver, taker = sizes[1:1 + 2 * twos:2], sizes[2:2 + 2 * twos:2]
    margin = jnp.minimum(giver - 1, bound - taker)
    moved = jax.random.randint(jax.random.fold_in(stream_key, 1), (twos,), 0, 1 << 20) % (margin + 1)
    sizes = sizes.at[1:1 + 2 * twos:2].set(giver - moved).at[2:2 + 2 * twos:2].set(taker + moved)
    return sizes[jax.random.permutation(jax.random.fold_in(stream_key, 2), amount)]


def gaussian(key, shape, deviation, reach, shards=(), kind=jnp.bfloat16):
    values = deviation * jax.random.normal(key, shape, jnp.float32)
    if shards:
        values = values * shard_levels(key, shape, shards, -0.22, 0.18)
    return jnp.clip(values, -reach, reach).astype(kind)


def setup_inputs(seed: int = 0) -> dict:
    arg_keys = jax.random.split(jax.random.key(seed), 12)
    inputs = gaussian(arg_keys[0], (MB, NROWS, SEQ, D), 1.0, 6.0, ((1, 8), (2, 4)))
    skips = gaussian(arg_keys[1], (MB, NROWS, SEQ, D), 1.0, 6.0, ((1, 8), (2, 4)))
    cotangent = gaussian(arg_keys[2], (MB, NROWS, SEQ, D), 1.0, 6.0, ((1, 8), (2, 4)))
    segment_ids = jax.vmap(lambda own: jnp.searchsorted(jnp.cumsum(ragged_sizes(own, NSEG, SEQ, SEQ // 2, 1)), jnp.arange(SEQ), side="right"))(jax.random.split(arg_keys[3], MB * NROWS)).reshape((MB, NROWS, SEQ)).astype(jnp.int32)
    time_steps = touch_ends(jax.random.randint(arg_keys[4], (MB, NROWS, NSEG), 0, 1000), jax.random.fold_in(arg_keys[4], 1), 0, 999).astype(jnp.int32)
    w_skip = gaussian(arg_keys[5], (2 * D, D), (2 * D) ** -0.5, 0.125, ((0, 32),))
    w_qkv = gaussian(arg_keys[6], (D, 3 * D), D ** -0.5, 0.1875, ((0, 32),))
    w_out = gaussian(arg_keys[7], (D, D), (D // 64) ** -0.5, 1.5, ((0, 32),))
    w_up = gaussian(arg_keys[8], (D, FF), D ** -0.5, 0.1875, ((0, 32),))
    w_down = gaussian(arg_keys[9], (FF, D), FF ** -0.5, 0.09375, ((0, 32),))
    w_mod = gaussian(arg_keys[10], (FREQ, 4 * D), (2 * FREQ) ** -0.5, 0.25, ((1, 32),))
    return {"inputs": inputs, "skips": skips, "cotangent": cotangent, "segment_ids": segment_ids, "time_steps": time_steps, "w_skip": w_skip, "w_qkv": w_qkv, "w_out": w_out, "w_up": w_up, "w_down": w_down, "w_mod": w_mod}


@jax.custom_vjp
def low(v):
    return lax.optimization_barrier(v.astype(jnp.bfloat16)).astype(jnp.float32)

@jax.custom_vjp
def low_back(v):
    return v

def low_keep(v):
    return (low(v), None)

def low_pass(kept, grad):
    return (grad,)

def back_keep(v):
    return (v, None)

def back_low(kept, grad):
    return (low(grad),)
low.defvjp(low_keep, low_pass)
low_back.defvjp(back_keep, back_low)

def matmul_hi(left_op, right_op):
    return jnp.dot(left_op, right_op, preferred_element_type=jnp.float32, precision=lax.Precision.HIGHEST)

def sinus(step_row):
    half_dim = FREQ // 2
    frequency = jnp.exp(-math.log(10000.0) * jnp.arange(half_dim, dtype=jnp.float32) / half_dim)
    angles = step_row.astype(jnp.float32)[:, None] * frequency[None, :]
    return jnp.concatenate([jnp.sin(angles), jnp.cos(angles)], axis=1)

def positions(segment_row):
    labels = jnp.arange(NSEG, dtype=jnp.int32)
    member = (segment_row[:, None] == labels[None, :]).astype(jnp.int32)
    counts = lax.optimization_barrier(jnp.sum(member, axis=0)).astype(jnp.int32)
    starts = (jnp.cumsum(counts) - counts).astype(jnp.int32)
    offsets = lax.optimization_barrier(jnp.sum(member * starts[None, :], axis=1)).astype(jnp.int32)
    return (jnp.arange(segment_row.shape[0], dtype=jnp.int32) - offsets).astype(jnp.int32)

def rotate(features, where_at):
    half_dim = features.shape[-1] // 2
    frequency = jnp.exp(-math.log(10000.0) * jnp.arange(half_dim, dtype=jnp.float32) / half_dim)
    angles = where_at.astype(jnp.float32)[:, None] * frequency[None, :]
    cosine = jnp.cos(angles)[:, None, :]
    sine_part = jnp.sin(angles)[:, None, :]
    first_half = features[..., :half_dim]
    second_half = features[..., half_dim:]
    return jnp.concatenate([first_half * cosine - second_half * sine_part, second_half * cosine + first_half * sine_part], axis=-1)

def layer_norm(values):
    centred = values - lax.optimization_barrier(jnp.mean(values, axis=-1, keepdims=True))
    variance = lax.optimization_barrier(jnp.mean(centred * centred, axis=-1, keepdims=True))
    return centred * lax.rsqrt(variance + 1e-06)

def attend(queries, keys_all, values_all, segment_row):
    length = queries.shape[0]
    block_len = min(512, length)
    count_blocks = length // block_len
    score_scale = 1.0 / math.sqrt(HEAD_DIM)
    query_blocks = queries.reshape(count_blocks, block_len, HEADS, HEAD_DIM)
    segment_blocks = segment_row.reshape(count_blocks, block_len)

    def one_block(block_pair):
        query_part, segment_part = block_pair
        scores = low_back(score_scale * jnp.einsum('qhd,khd->hqk', query_part, keys_all, precision=lax.Precision.HIGHEST))
        allowed = segment_part[:, None] == segment_row[None, :]
        scores = jnp.where(allowed[None], scores, -1e+30)
        probability = jax.nn.softmax(scores, axis=-1)
        return jnp.einsum('hqk,khd->qhd', low(probability), values_all, precision=lax.Precision.HIGHEST)
    mixed_heads = lax.map(jax.checkpoint(one_block), (query_blocks, segment_blocks))
    return mixed_heads.reshape(length, HEADS * HEAD_DIM)

def layer(stacked, segment_row, embedded, w_skip, w_qkv, w_out, w_up, w_down, w_mod):
    resid_in = low_back(matmul_hi(stacked, w_skip))
    modulation = matmul_hi(embedded, w_mod)
    member = (segment_row[:, None] == jnp.arange(NSEG, dtype=jnp.int32)[None, :]).astype(jnp.float32)
    per_frame = matmul_hi(member, modulation)
    shift_one = per_frame[:, 0:D]
    scale_one = per_frame[:, D:2 * D]
    shift_two = per_frame[:, 2 * D:3 * D]
    scale_two = per_frame[:, 3 * D:4 * D]
    normed_one = low(layer_norm(resid_in) * (1.0 + scale_one) + shift_one)
    projected = low_back(low(matmul_hi(normed_one, w_qkv)))
    length = projected.shape[0]
    query_raw = projected[:, 0:D].reshape(length, HEADS, HEAD_DIM)
    key_raw = projected[:, D:2 * D].reshape(length, HEADS, HEAD_DIM)
    values_all = projected[:, 2 * D:3 * D].reshape(length, HEADS, HEAD_DIM)
    where_at = positions(segment_row)
    queries = low(rotate(query_raw, where_at))
    keys_all = low(rotate(key_raw, where_at))
    mixed = low_back(low(attend(queries, keys_all, values_all, segment_row)))
    resid_mid = resid_in + low_back(matmul_hi(mixed, w_out))
    normed_two = low(layer_norm(resid_mid) * (1.0 + scale_two) + shift_two)
    hidden_pre = low_back(matmul_hi(normed_two, w_up))
    activated = low(jax.nn.gelu(hidden_pre, approximate=True))
    return resid_mid + matmul_hi(activated, w_down)

def reference(inputs, skips, cotangent, segment_ids, time_steps, w_skip, w_qkv, w_out, w_up, w_down, w_mod):
    weights = tuple((matrix.astype(jnp.float32) for matrix in (w_skip, w_qkv, w_out, w_up, w_down, w_mod)))
    row_total = MB * NROWS
    stacked_all = jnp.concatenate([inputs, skips], axis=-1).astype(jnp.float32).reshape(row_total, SEQ, 2 * D)
    cot_all = cotangent.astype(jnp.float32).reshape(row_total, SEQ, D)
    segment_all = segment_ids.reshape(row_total, SEQ)
    steps_all = time_steps.reshape(row_total, NSEG)

    def one_row(running, row_items):
        stacked, segment_row, step_row, cot_row = row_items
        embedded = low(sinus(step_row))

        def forward(stacked_in, *weight_list):
            return layer(stacked_in, segment_row, embedded, *weight_list)
        result, pull_back = jax.vjp(forward, stacked, *weights)
        grad_terms = pull_back(cot_row)
        running = tuple((earlier + latest for earlier, latest in zip(running, grad_terms[1:])))
        return (running, (result, grad_terms[0]))
    zero_grads = tuple((jnp.zeros(matrix.shape, jnp.float32) for matrix in weights))
    totals, (results, grad_stacked) = lax.scan(one_row, zero_grads, (stacked_all, segment_all, steps_all, cot_all))
    block_out = results.reshape(MB, NROWS, SEQ, D).astype(jnp.bfloat16)
    grad_stacked = grad_stacked.reshape(MB, NROWS, SEQ, 2 * D)
    grad_inputs = grad_stacked[..., :D].astype(jnp.bfloat16)
    grad_skips = grad_stacked[..., D:].astype(jnp.bfloat16)
    return (block_out, grad_inputs, grad_skips, totals[0], totals[1], totals[2], totals[3], totals[4], totals[5])
```

```python
import functools
import math

import jax
import jax.numpy as jnp
from jax import lax
from jax.experimental import pallas as pl
from jax.experimental.pallas import tpu as pltpu
from jax.sharding import Mesh
from jax.sharding import PartitionSpec as P

HEAD_DIM = 64
PAIR = 2 * HEAD_DIM
BLOCK = 256
VMEM_BYTES = 60 * 1024 * 1024
ROW_AXES = ("core", "lo")
LINE_AXES = ("core", "hi", "lo")
ALL_AXES = ("plane", "core", "hi", "lo")
f32 = jnp.float32
bf16 = jnp.bfloat16


def dot_nn(left, right):
    return lax.dot_general(left, right, (((1,), (0,)), ((), ())), preferred_element_type=f32)


def dot_nt(left, right):
    return lax.dot_general(left, right, (((1,), (1,)), ((), ())), preferred_element_type=f32)


def dot_tn(left, right):
    return lax.dot_general(left, right, (((0,), (0,)), ((), ())), preferred_element_type=f32)


def params(*semantics):
    return pltpu.CompilerParams(dimension_semantics=semantics, vmem_limit_bytes=VMEM_BYTES)


def cost(flops, moved, special=0):
    return pl.CostEstimate(flops=int(flops), bytes_accessed=int(moved), transcendentals=int(special))


def choose(segment_column, table_ref):
    count = table_ref.shape[0]
    picked = table_ref[count - 1 : count, :]
    for label in range(count - 2, -1, -1):
        picked = jnp.where(segment_column == label, table_ref[label : label + 1, :], picked)
    return picked


def normalise(values):
    centred = values - jnp.mean(values, axis=-1, keepdims=True)
    variance = jnp.mean(centred * centred, axis=-1, keepdims=True)
    inverse = lax.rsqrt(variance + 1e-06)
    return centred * inverse, inverse


def skip_norm_kernel(x_ref, s_ref, top_ref, bottom_ref, seg_ref, shift_ref, scale_ref, resid_ref, normed_ref):
    resid = dot_nn(x_ref[...], top_ref[...]) + dot_nn(s_ref[...], bottom_ref[...])
    resid_ref[...] = resid
    unit, _ = normalise(resid)
    label = seg_ref[...]
    normed = unit * (1.0 + choose(label, scale_ref)) + choose(label, shift_ref)
    normed_ref[...] = normed.astype(bf16)


def out_norm_kernel(mixed_ref, w_ref, resid_in_ref, seg_ref, shift_ref, scale_ref, resid_ref, normed_ref):
    resid = resid_in_ref[...] + dot_nn(mixed_ref[...], w_ref[...])
    resid_ref[...] = resid
    unit, _ = normalise(resid)
    label = seg_ref[...]
    normed = unit * (1.0 + choose(label, scale_ref)) + choose(label, shift_ref)
    normed_ref[...] = normed.astype(bf16)


def segment_sums(row_labels, values, total_ref):
    members = lax.broadcasted_iota(jnp.int32, (total_ref.shape[0], row_labels.shape[1]), 0) == row_labels
    members = members.astype(f32).astype(bf16)
    high = values.astype(bf16)
    low = (values - high.astype(f32)).astype(bf16)
    total_ref[...] += dot_nn(members, high) + dot_nn(members, low)


def norm_pull(grad, resid, scale):
    unit, inverse = normalise(resid)
    inner = grad * (1.0 + scale)
    pulled = inverse * (
        inner
        - jnp.mean(inner, axis=-1, keepdims=True)
        - unit * jnp.mean(inner * unit, axis=-1, keepdims=True)
    )
    return pulled, grad * unit


def norm_two_back_kernel(
    g_ref, resid_ref, cot_ref, seg_ref, segr_ref, scale_ref, w_ref, mid_ref, low_ref, mix_ref, dshift_ref, dscale_ref
):
    @pl.when(pl.program_id(0) == 0)
    def _():
        dshift_ref[...] = jnp.zeros_like(dshift_ref)
        dscale_ref[...] = jnp.zeros_like(dscale_ref)

    grad = g_ref[...]
    pulled, by_scale = norm_pull(grad, resid_ref[...], choose(seg_ref[...], scale_ref))
    grad_mid = cot_ref[...].astype(f32) + pulled
    low = grad_mid.astype(bf16)
    mid_ref[...] = grad_mid
    low_ref[...] = low
    mix_ref[...] = dot_nt(low, w_ref[...]).astype(bf16)
    segment_sums(segr_ref[...], grad, dshift_ref)
    segment_sums(segr_ref[...], by_scale, dscale_ref)


def norm_one_back_kernel(
    own_ref, other_ref, resid_ref, mid_ref, seg_ref, segr_ref, scale_ref, grad_ref, dshift_ref, dscale_ref
):
    @pl.when(pl.program_id(0) == 0)
    def _():
        dshift_ref[...] = jnp.zeros_like(dshift_ref)
        dscale_ref[...] = jnp.zeros_like(dscale_ref)

    grad = own_ref[...] + other_ref[...].astype(f32)
    pulled, by_scale = norm_pull(grad, resid_ref[...], choose(seg_ref[...], scale_ref))
    grad_ref[...] = (mid_ref[...] + pulled).astype(bf16)
    segment_sums(segr_ref[...], grad, dshift_ref)
    segment_sums(segr_ref[...], by_scale, dscale_ref)


def rowwise(kernel, frames, blocked, whole, outs, sums=0, flops=0):
    tile = min(BLOCK, frames)
    in_specs, args, moved = [], [], 0
    for kind, value in blocked:
        if kind == "row":
            in_specs.append(pl.BlockSpec((1, tile), lambda i: (0, i)))
        elif kind == "whole":
            in_specs.append(pl.BlockSpec(value.shape, lambda i: (0, 0)))
        else:
            in_specs.append(pl.BlockSpec((tile, value.shape[1]), lambda i: (i, 0)))
        args.append(value)
        moved += value.size * value.dtype.itemsize
    out_specs, shapes = [], []
    for width, kind in outs:
        out_specs.append(pl.BlockSpec((tile, width), lambda i: (i, 0)))
        shapes.append(jax.ShapeDtypeStruct((frames, width), kind))
        moved += frames * width * jnp.dtype(kind).itemsize
    for _ in range(sums):
        out_specs.append(pl.BlockSpec((8, outs[0][0]), lambda i: (0, 0)))
        shapes.append(jax.ShapeDtypeStruct((8, outs[0][0]), f32))
    return pl.pallas_call(
        kernel,
        grid=(frames // tile,),
        in_specs=in_specs,
        out_specs=out_specs,
        out_shape=shapes,
        compiler_params=params("arbitrary"),
        cost_estimate=cost(flops, moved),
    )(*args)


def swap_halves(values, lanes):
    half = HEAD_DIM // 2
    ahead = pltpu.roll(values, PAIR - half, 1)
    behind = pltpu.roll(values, half, 1)
    return jnp.where(lanes % HEAD_DIM < half, ahead, behind)


def attend_forward_kernel(
    range_ref, q_ref, k_ref, v_ref, cos_ref, sin_ref, segc_ref, segr_ref,
    out_ref, qrot_ref, krot_ref, lse_ref, scores, seg_wide,
):
    length = q_ref.shape[0]
    blocks = length // BLOCK
    lanes = lax.broadcasted_iota(jnp.int32, (BLOCK, PAIR), 1)
    first = lanes < HEAD_DIM

    def turn(i, carry):
        rows = pl.ds(pl.multiple_of(i * BLOCK, BLOCK), BLOCK)
        cosine, sine = cos_ref[rows, :], sin_ref[rows, :]
        for source, target, factor in ((q_ref, qrot_ref, HEAD_DIM**-0.5), (k_ref, krot_ref, None)):
            values = source[rows, :].astype(f32)
            turned = (values * cosine + swap_halves(values, lanes) * sine).astype(bf16)
            if factor is not None:
                turned = turned * jnp.asarray(factor, bf16)
            target[rows, :] = turned
        seg_wide[rows, :] = jnp.broadcast_to(segc_ref[rows, :], (BLOCK, PAIR))
        return carry

    lax.fori_loop(0, blocks, turn, 0)

    def one_query(i, carry):
        rows = pl.ds(pl.multiple_of(i * BLOCK, BLOCK), BLOCK)
        low, high = range_ref[0, i], range_ref[1, i]
        query = qrot_ref[rows, :]
        zero = jnp.zeros_like(query)
        both = jnp.concatenate([jnp.where(first, query, zero), jnp.where(first, zero, query)], axis=0)
        label = seg_wide[rows, :]
        label = jnp.concatenate([label] * (BLOCK // PAIR), axis=1)

        def score(j, highest):
            keys = krot_ref[pl.ds(pl.multiple_of(j * BLOCK, BLOCK), BLOCK), :]
            found = dot_nt(both, keys)
            allowed = label == segr_ref[:, pl.ds(pl.multiple_of(j * BLOCK, BLOCK), BLOCK)]
            allowed = jnp.concatenate([allowed, allowed], axis=0)
            found = jnp.where(allowed, found, -1e30)
            scores[j] = found
            for part in range(BLOCK // PAIR):
                highest = jnp.maximum(highest, found[:, part * PAIR : (part + 1) * PAIR])
            return highest

        highest = lax.fori_loop(low, high, score, jnp.full((2 * BLOCK, PAIR), -1e30, f32))
        highest = jnp.max(highest, axis=1, keepdims=True)

        def gather(j, running):
            totals, mixed = running
            powers = jnp.exp(scores[j] - highest)
            for part in range(BLOCK // PAIR):
                totals = totals + powers[:, part * PAIR : (part + 1) * PAIR]
            values = v_ref[pl.ds(pl.multiple_of(j * BLOCK, BLOCK), BLOCK), :]
            return totals, mixed + dot_nn(powers.astype(bf16), values)

        blank = jnp.zeros((2 * BLOCK, PAIR), f32)
        totals, mixed = lax.fori_loop(low, high, gather, (blank, blank))
        totals = jnp.sum(totals, axis=1, keepdims=True)
        mixed = mixed * (1.0 / totals)
        logsum = jnp.broadcast_to(highest + jnp.log(totals), (2 * BLOCK, PAIR))
        out_ref[rows, :] = jnp.where(first, mixed[:BLOCK], mixed[BLOCK:]).astype(bf16)
        turned = jnp.where(first, logsum[:BLOCK], logsum[BLOCK:]).T
        lse_ref[0, 0:1, rows] = turned[0:1]
        lse_ref[0, 1:2, rows] = turned[HEAD_DIM : HEAD_DIM + 1]
        return carry

    lax.fori_loop(0, blocks, one_query, 0)


def attend_forward(ranges, projected, cosine, sine, seg_column, seg_row):
    length, width = projected.shape
    width //= 3
    pairs = width // PAIR
    panel = lambda shift: pl.BlockSpec((length, PAIR), lambda p, r: (0, shift * pairs + p))
    whole = lambda shape: pl.BlockSpec(shape, lambda p, r: (0,) * len(shape))
    return pl.pallas_call(
        attend_forward_kernel,
        grid_spec=pltpu.PrefetchScalarGridSpec(
            num_scalar_prefetch=1,
            grid=(pairs,),
            in_specs=[panel(0), panel(1), panel(2), whole(cosine.shape), whole(sine.shape),
                      whole(seg_column.shape), whole(seg_row.shape)],
            out_specs=[panel(0), panel(0), panel(0), pl.BlockSpec((1, 2, length), lambda p, r: (p, 0, 0))],
            scratch_shapes=[
                pltpu.VMEM((length // BLOCK, 2 * BLOCK, BLOCK), f32),
                pltpu.VMEM((length, PAIR), jnp.int32),
            ],
        ),
        out_shape=[jax.ShapeDtypeStruct((length, width), bf16)] * 3
        + [jax.ShapeDtypeStruct((pairs, 2, length), f32)],
        compiler_params=params("arbitrary"),
        cost_estimate=cost(4 * length * length * width, 14 * length * width, length * length * 2 * pairs),
    )(ranges, projected, projected, projected, cosine, sine, seg_column, seg_row)


def attend_backward_kernel(
    range_ref, q_ref, k_ref, v_ref, out_ref, do_ref, lse_ref, cos_ref, sin_ref, segc_ref, segr_ref,
    grad_ref, dq, dk_low, dv_low, delta, seg_wide,
):
    length = q_ref.shape[0]
    blocks = length // BLOCK
    step = pl.program_id(1)

    def span(i):
        return pl.ds(pl.multiple_of(i * BLOCK, BLOCK), BLOCK)

    @pl.when(step == 0)
    def _():
        lanes = lax.broadcasted_iota(jnp.int32, (BLOCK, PAIR), 1)
        first = lanes < HEAD_DIM
        picker = (
            lax.broadcasted_iota(jnp.int32, (8, PAIR), 0)
            == lax.broadcasted_iota(jnp.int32, (8, PAIR), 1) // HEAD_DIM
        ).astype(f32)

        def prepare(i, carry):
            rows = span(i)
            product = do_ref[rows, :].astype(f32) * out_ref[rows, :].astype(f32)
            delta[:, rows] = lax.dot_general(
                picker, product, (((1,), (1,)), ((), ())),
                precision=lax.Precision.HIGHEST, preferred_element_type=f32,
            )
            dq[rows, :] = jnp.zeros((BLOCK, PAIR), f32)
            seg_wide[rows, :] = jnp.broadcast_to(segc_ref[rows, :], (BLOCK, PAIR))
            return carry

        lax.fori_loop(0, blocks, prepare, 0)

        def unturn(values, rows):
            return values * cos_ref[rows, :] - swap_halves(values, lanes) * sin_ref[rows, :]

        def one_key(j, carry):
            rows = span(j)
            keys, values = k_ref[rows, :], v_ref[rows, :]
            zero = jnp.zeros_like(keys)
            keys = jnp.concatenate([jnp.where(first, keys, zero), jnp.where(first, zero, keys)], axis=0)
            values = jnp.concatenate([jnp.where(first, values, zero), jnp.where(first, zero, values)], axis=0)
            label = seg_wide[rows, :]
            label = jnp.concatenate([label] * (BLOCK // PAIR), axis=1)

            def one_query(i, running):
                grad_k, grad_v = running
                there = span(i)
                query, grad_out = q_ref[there, :], do_ref[there, :]
                allowed = label == segr_ref[:, there]
                scores = dot_nt(keys, query)
                grad_prob = dot_nt(values, grad_out)
                parts, lows = [], []
                for head in range(2):
                    half = slice(head * BLOCK, (head + 1) * BLOCK)
                    found = scores[half] - lse_ref[0, head : head + 1, there]
                    part = jnp.exp(jnp.where(allowed, found, -1e30))
                    parts.append(part.astype(bf16))
                    lows.append((part * (grad_prob[half] - delta[head : head + 1, there])).astype(bf16))
                probability = jnp.concatenate(parts, axis=0)
                grad_scores = jnp.concatenate(lows, axis=0)
                dq[there, :] += dot_tn(grad_scores, keys)
                return grad_k + dot_nn(grad_scores, query), grad_v + dot_nn(probability, grad_out)

            blank = jnp.zeros((2 * BLOCK, PAIR), f32)
            grad_k, grad_v = lax.fori_loop(range_ref[0, j], range_ref[1, j], one_query, (blank, blank))
            grad_k = jnp.where(first, grad_k[:BLOCK], grad_k[BLOCK:])
            grad_v = jnp.where(first, grad_v[:BLOCK], grad_v[BLOCK:])
            dk_low[rows, :] = unturn(grad_k, rows).astype(bf16)
            dv_low[rows, :] = grad_v.astype(bf16)
            return carry

        lax.fori_loop(0, blocks, one_key, 0)

        def finish(i, carry):
            rows = span(i)
            grad_ref[rows, :] = unturn(dq[rows, :] * HEAD_DIM**-0.5, rows).astype(bf16)
            return carry

        lax.fori_loop(0, blocks, finish, 0)

    @pl.when(step == 1)
    def _():
        grad_ref[...] = dk_low[...]

    @pl.when(step == 2)
    def _():
        grad_ref[...] = dv_low[...]


def attend_backward(ranges, queries, keys, projected, mixed, grad_mixed, logsum, cosine, sine, seg_column, seg_row):
    length, width = queries.shape
    pairs = width // PAIR
    panel = lambda shift: pl.BlockSpec((length, PAIR), lambda p, t, r: (0, shift * pairs + p))
    whole = lambda shape: pl.BlockSpec(shape, lambda p, t, r: (0,) * len(shape))
    return pl.pallas_call(
        attend_backward_kernel,
        grid_spec=pltpu.PrefetchScalarGridSpec(
            num_scalar_prefetch=1,
            grid=(pairs, 3),
            in_specs=[panel(0), panel(0), panel(2), panel(0), panel(0),
                      pl.BlockSpec((1, 2, length), lambda p, t, r: (p, 0, 0)),
                      whole(cosine.shape), whole(sine.shape), whole(seg_column.shape), whole(seg_row.shape)],
            out_specs=pl.BlockSpec((length, PAIR), lambda p, t, r: (0, t * pairs + p)),
            scratch_shapes=[
                pltpu.VMEM((length, PAIR), f32),
                pltpu.VMEM((length, PAIR), bf16),
                pltpu.VMEM((length, PAIR), bf16),
                pltpu.VMEM((8, length), f32),
                pltpu.VMEM((length, PAIR), jnp.int32),
            ],
        ),
        out_shape=jax.ShapeDtypeStruct((length, 3 * width), bf16),
        compiler_params=params("arbitrary", "arbitrary"),
        cost_estimate=cost(10 * length * length * width, 16 * length * width, length * length * 2 * pairs),
    )(ranges, queries, keys, projected, mixed, grad_mixed, logsum, cosine, sine, seg_column, seg_row)


def gelu_and_slope(x):
    root = math.sqrt(2.0 / math.pi)
    square = x * x
    bend = jnp.tanh(x * (root + root * 0.044715 * square))
    half = 0.5 * x
    half_up = 0.5 + 0.5 * bend
    slope = half_up + half * (1.0 - bend * bend) * (root + 3.0 * root * 0.044715 * square)
    return half + half * bend, slope


def feed_kernel(
    n_ref, cot_ref, resid_ref, up_ref, down_ref, out_ref, back_ref, gup_ref, gdown_ref,
    total, n_turned, cot_turned, act, pre,
):
    step, last = pl.program_id(0), pl.num_programs(0) - 1
    frames, width = n_ref.shape
    tile = min(BLOCK, frames)
    planes = gup_ref.shape[1]
    part = width // planes

    def rows_of(i):
        return pl.ds(pl.multiple_of(i * tile, tile), tile)

    @pl.when(step == 0)
    def _():
        def turn(i, carry):
            rows = rows_of(i)
            n_turned[:, rows] = n_ref[rows, :].T
            cot_turned[:, rows] = cot_ref[rows, :].T
            total[rows, :] = resid_ref[rows, :]
            back_ref[rows, :] = jnp.zeros((tile, width), f32)
            return carry

        lax.fori_loop(0, frames // tile, turn, 0)

    def chunk(i, carry):
        rows = rows_of(i)
        hidden = dot_nn(n_ref[rows, :], up_ref[...])
        grad_act = dot_nt(cot_ref[rows, :], down_ref[...])
        activated, slope = gelu_and_slope(hidden)
        activated = activated.astype(bf16)
        grad_pre = (grad_act * slope).astype(bf16)
        act[rows, :] = activated
        pre[rows, :] = grad_pre
        total[rows, :] += dot_nn(activated, down_ref[...])
        back_ref[rows, :] += dot_nt(grad_pre, up_ref[...])
        return carry

    lax.fori_loop(0, frames // tile, chunk, 0)

    def weights(i, carry):
        rows = pl.ds(pl.multiple_of(i * part, part), part)
        grad_up = dot_nn(n_turned[rows, :], pre[...]).astype(bf16)
        gup_ref[0, i] = grad_up[: part // 2]
        gup_ref[1, i] = grad_up[part // 2 :]
        gdown_ref[0, 0, rows, :] = dot_nn(cot_turned[rows, :], act[...]).astype(bf16)
        return carry

    lax.fori_loop(0, planes, weights, 0)

    @pl.when(step == last)
    def _():
        out_ref[...] = total[...].astype(bf16)


def feed_forward_and_back(normed, cot, resid, w_up, w_down, planes):
    frames, width = normed.shape
    hidden = w_up.shape[1]
    piece = hidden // (2 * planes)
    once = dict(pipeline_mode=pl.Buffered(1))
    return pl.pallas_call(
        feed_kernel,
        grid=(hidden // piece,),
        in_specs=[
            pl.BlockSpec((frames, width), lambda j: (0, 0), **once),
            pl.BlockSpec((frames, width), lambda j: (0, 0), **once),
            pl.BlockSpec((frames, width), lambda j: (0, 0), **once),
            pl.BlockSpec((width, piece), lambda j: (0, j)),
            pl.BlockSpec((piece, width), lambda j: (j, 0)),
        ],
        out_specs=[
            pl.BlockSpec((frames, width), lambda j: (0, 0)),
            pl.BlockSpec((frames, width), lambda j: (0, 0)),
            pl.BlockSpec((2, planes, width // (2 * planes), piece), lambda j: (0, 0, 0, j)),
            pl.BlockSpec((1, 1, width, piece), lambda j: (j % 2, j // 2, 0, 0)),
        ],
        out_shape=[
            jax.ShapeDtypeStruct((frames, width), bf16),
            jax.ShapeDtypeStruct((frames, width), f32),
            jax.ShapeDtypeStruct((2, planes, width // (2 * planes), hidden), bf16),
            jax.ShapeDtypeStruct((2, planes, width, piece), bf16),
        ],
        scratch_shapes=[
            pltpu.VMEM((frames, width), f32),
            pltpu.VMEM((width, frames), bf16),
            pltpu.VMEM((width, frames), bf16),
            pltpu.VMEM((frames, piece), bf16),
            pltpu.VMEM((frames, piece), bf16),
        ],
        compiler_params=params("arbitrary"),
        cost_estimate=cost(12 * frames * width * hidden, 8 * width * hidden + 16 * frames * width, frames * hidden),
    )(normed, cot, resid, w_up, w_down)


def body(inputs, skips, cotangent, segment_ids, time_steps, w_skip, w_qkv, w_out, w_up, w_down, w_mod):
    micro, _, piece, width = inputs.shape
    length = segment_ids.shape[-1]
    labels = time_steps.shape[-1]
    planes, lows, highs = lax.axis_size("plane"), lax.axis_size("lo"), lax.axis_size("hi")
    line = highs * lows
    group = 2 * lows
    devices = planes * 2 * line
    core, high, low = lax.axis_index("core"), lax.axis_index("hi"), lax.axis_index("lo")
    place = high * lows + low
    member = core * lows + low
    frames = 2 * piece
    heads_wide = width // group
    first_core = core == 0
    swap = [(0, 1), (1, 0)]

    def route(parity):
        pairs = []
        for c in range(2):
            for z in range(line):
                row = c * micro + ((z % 2) ^ parity)
                to_core, to_low = divmod(z // 2, lows)
                pairs.append((c * line + z, (to_core * highs + row) * lows + to_low))
        return pairs

    there = (route(0), route(1))
    back = tuple([(b, a) for a, b in pairs] for pairs in there)
    odd_place = place % 2
    even_row = high % 2 == 0

    def to_rows(value):
        value = value[:, 0]
        near = lax.ppermute(lax.dynamic_index_in_dim(value, odd_place, 0, False), LINE_AXES, there[0])
        far = lax.ppermute(lax.dynamic_index_in_dim(value, 1 - odd_place, 0, False), LINE_AXES, there[1])
        return jnp.concatenate([jnp.where(even_row, near, far), jnp.where(even_row, far, near)], axis=0)

    def from_rows(value):
        value = value.reshape(2, piece, width)
        near = lax.ppermute(lax.dynamic_index_in_dim(value, high % 2, 0, False), LINE_AXES, back[0])
        far = lax.ppermute(lax.dynamic_index_in_dim(value, 1 - high % 2, 0, False), LINE_AXES, back[1])
        even = odd_place == 0
        return jnp.stack([jnp.where(even, near, far), jnp.where(even, far, near)])[:, None]

    def frames_to_row(value):
        if group > 2:
            return lax.all_gather(value, ROW_AXES, axis=0, tiled=True)
        other = lax.ppermute(value, "core", swap)
        return jnp.concatenate([jnp.where(first_core, value, other), jnp.where(first_core, other, value)], axis=0)

    def heads_to_frames(value):
        if group > 2:
            return lax.all_to_all(value, ROW_AXES, split_axis=0, concat_axis=1, tiled=True)
        other = lax.ppermute(lax.dynamic_slice_in_dim(value, (1 - core) * frames, frames, 0), "core", swap)
        own = lax.dynamic_slice_in_dim(value, core * frames, frames, 0)
        return jnp.concatenate([jnp.where(first_core, own, other), jnp.where(first_core, other, own)], axis=1)

    def frames_to_heads(value):
        if group > 2:
            return lax.all_to_all(value, ROW_AXES, split_axis=1, concat_axis=0, tiled=True)
        other = lax.ppermute(lax.dynamic_slice_in_dim(value, (1 - core) * heads_wide, heads_wide, 1), "core", swap)
        own = lax.dynamic_slice_in_dim(value, core * heads_wide, heads_wide, 1)
        return jnp.concatenate([jnp.where(first_core, own, other), jnp.where(first_core, other, own)], axis=0)

    up_rows, down_rows, out_rows = w_up.shape[0], w_down.shape[0], w_out.shape[0]
    skip_rows = w_skip.shape[0]
    early = jnp.concatenate([w_skip] + [w_qkv[:, i * width : (i + 1) * width] for i in range(3)], axis=0)
    early = lax.all_gather(early, ALL_AXES, axis=0, tiled=True).reshape(devices, -1, width)
    skip_full = early[:, :skip_rows].reshape(-1, width)
    qkv_parts = []
    for i in range(3):
        begin = skip_rows + i * out_rows
        whole = early[:, begin : begin + out_rows].reshape(width, width)
        qkv_parts.append(lax.dynamic_slice_in_dim(whole, member * heads_wide, heads_wide, 1))
    qkv_own = jnp.concatenate(qkv_parts, axis=1)
    columns = w_up.shape[1] // width
    late = jnp.concatenate([w_down, w_out] + [w_up[:, i * width : (i + 1) * width] for i in range(columns)], axis=0)
    late, early = lax.optimization_barrier((late, early))
    late = lax.all_gather(late, ALL_AXES, axis=0, tiled=True).reshape(devices, -1, width)
    down_full = late[:, :down_rows].reshape(-1, width)
    out_full = late[:, down_rows : down_rows + out_rows].reshape(width, width)
    up_full = jnp.concatenate(
        [
            late[:, down_rows + out_rows + i * up_rows : down_rows + out_rows + (i + 1) * up_rows].reshape(width, width)
            for i in range(columns)
        ],
        axis=1,
    )

    labels_own = segment_ids[:, 0]
    labels_other = lax.ppermute(labels_own, "core", swap)
    labels_pick = jnp.where(core == high // micro, labels_own, labels_other)
    seg = lax.dynamic_index_in_dim(labels_pick, high % micro, 0, False)
    names = jnp.arange(labels, dtype=jnp.int32)
    starts = jnp.sum((seg[:, None] < names[None, :]).astype(jnp.int32), axis=0)
    ends = jnp.sum((seg[:, None] <= names[None, :]).astype(jnp.int32), axis=0)
    offset = jnp.sum(jnp.where(seg[:, None] == names[None, :], starts[None, :], 0), axis=1)
    where_at = jnp.arange(length, dtype=jnp.int32) - offset
    by_block = seg.reshape(-1, BLOCK)
    begin = jnp.sum(jnp.where(by_block[:, :1] == names[None, :], starts[None, :], 0), axis=1)
    finish = jnp.sum(jnp.where(by_block[:, -1:] == names[None, :], ends[None, :], 0), axis=1)
    ranges = jnp.stack([begin // BLOCK, (finish + BLOCK - 1) // BLOCK]).astype(jnp.int32)
    half = HEAD_DIM // 2
    rates = jnp.exp(-math.log(10000.0) * jnp.arange(half, dtype=f32) / half)
    angles = where_at.astype(f32)[:, None] * rates
    cosine = jnp.tile(jnp.cos(angles), (1, 4))
    sine = jnp.sin(angles)
    sine = jnp.concatenate([-sine, sine, -sine, sine], axis=1)
    seg_column, seg_row = seg[:, None], seg[None, :]
    mine = lax.dynamic_slice_in_dim(seg, member * frames, frames, 0)
    mine_column, mine_row = mine[:, None], mine[None, :]

    steps = lax.all_gather(time_steps[:, 0], ("plane", "core"), axis=0, tiled=True).reshape(-1)
    quarter = w_mod.shape[0] // 2
    pace = jnp.exp(-math.log(10000.0) * jnp.arange(quarter, dtype=f32) / quarter)
    turns = steps.astype(f32)[:, None] * pace
    embedded = jnp.concatenate([jnp.sin(turns), jnp.cos(turns)], axis=1).astype(bf16)
    block_mod = jnp.dot(embedded, w_mod, preferred_element_type=f32)
    own_columns = block_mod.shape[1]
    block_mod = block_mod.reshape(planes, 1, highs, 1, labels, own_columns)
    block_mod = jnp.broadcast_to(block_mod, (planes, 2, highs, lows, labels, own_columns))
    block_mod = lax.all_to_all(
        block_mod.reshape(devices, labels, own_columns), ALL_AXES, split_axis=0, concat_axis=0, tiled=True
    )
    modulation = jnp.moveaxis(block_mod, 0, 1).reshape(labels, 4, width)
    shift_one, scale_one, shift_two, scale_two = (modulation[:, i] for i in range(4))

    x, s = to_rows(inputs), to_rows(skips)
    cot_in, x = lax.optimization_barrier((cotangent, x))
    cot = to_rows(cot_in)
    resid_in, normed_one = rowwise(
        skip_norm_kernel,
        frames,
        [("", x), ("", s), ("whole", skip_full[:width]), ("whole", skip_full[width:]), ("", mine_column),
         ("whole", shift_one), ("whole", scale_one)],
        None,
        [(width, f32), (width, bf16)],
        flops=4 * frames * width * width,
    )
    normed_row = frames_to_row(normed_one)
    projected = jnp.dot(normed_row, qkv_own, preferred_element_type=f32).astype(bf16)
    mixed_heads, queries, keys, logsum = attend_forward(ranges, projected, cosine, sine, seg_column, seg_row)
    mixed = heads_to_frames(mixed_heads)
    resid_mid, normed_two = rowwise(
        out_norm_kernel,
        frames,
        [("", mixed), ("whole", out_full), ("", resid_in), ("", mine_column), ("whole", shift_two), ("whole", scale_two)],
        None,
        [(width, f32), (width, bf16)],
        flops=2 * frames * width * width,
    )
    result, grad_normed_two, grad_up, grad_down = feed_forward_and_back(
        normed_two, cot, resid_mid, up_full, down_full, planes
    )

    def over_cores(kept):
        other = lax.ppermute(lax.dynamic_index_in_dim(kept, 1 - core, 0, False), "core", swap)
        own = lax.dynamic_index_in_dim(kept, core, 0, False)
        return (own.astype(f32) + other.astype(f32)).astype(bf16)

    def scatter(value):
        return lax.psum_scatter(value, ("plane", "hi", "lo"), scatter_dimension=0, tiled=True)

    def scatter_rows(value):
        split = jnp.moveaxis(value.reshape(planes, 2, -1, value.shape[1]), 1, 0)
        return scatter(over_cores(split).reshape(-1, value.shape[1]))

    grad_up = scatter(over_cores(grad_up).reshape(-1, grad_up.shape[-1])).astype(f32)
    grad_down = over_cores(grad_down)
    grad_down = grad_down.reshape(planes, width, line, -1)
    grad_down = jnp.moveaxis(grad_down, 2, 1).reshape(planes * line * width, -1)
    grad_down = scatter(grad_down).T.astype(f32)

    grad_mid, grad_mid_low, grad_frames, grad_shift_two, grad_scale_two = rowwise(
        norm_two_back_kernel,
        frames,
        [("", grad_normed_two), ("", resid_mid), ("", cot), ("", mine_column), ("row", mine_row),
         ("whole", scale_two), ("whole", out_full)],
        None,
        [(width, f32), (width, bf16), (width, bf16)],
        sums=2,
        flops=2 * frames * width * width,
    )
    grad_heads = frames_to_heads(grad_frames)
    grad_out = lax.dot_general(mixed, grad_mid_low, (((0,), (0,)), ((), ())), preferred_element_type=f32)
    grad_out = scatter_rows(grad_out.astype(bf16)).astype(f32)
    grad_proj = attend_backward(
        ranges, queries, keys, projected, mixed_heads, grad_heads, logsum, cosine, sine, seg_column, seg_row
    )
    if group > 2:
        partial = dot_nt(grad_proj, qkv_own).astype(bf16)
        grad_one = lax.psum_scatter(partial, ROW_AXES, scatter_dimension=0, tiled=True).astype(f32)
        grad_one_other = jnp.zeros((frames, width), bf16)
    else:
        away = lax.dynamic_slice_in_dim(grad_proj, (1 - core) * frames, frames, 0)
        home = lax.dynamic_slice_in_dim(grad_proj, core * frames, frames, 0)
        grad_one_other = lax.ppermute(dot_nt(away, qkv_own).astype(bf16), "core", swap)
        grad_one = dot_nt(home, qkv_own)
    grad_in, grad_shift_one, grad_scale_one = rowwise(
        norm_one_back_kernel,
        frames,
        [("", grad_one), ("", grad_one_other), ("", resid_in), ("", grad_mid), ("", mine_column), ("row", mine_row),
         ("whole", scale_one)],
        None,
        [(width, bf16)],
        sums=2,
    )
    grad_in_home = from_rows(grad_in)
    grad_qkv = lax.dot_general(normed_row, grad_proj, (((0,), (0,)), ((), ())), preferred_element_type=f32)
    grad_qkv = grad_qkv.astype(bf16)
    if group > 2:
        grad_qkv = grad_qkv.reshape(planes, 2, highs, lows, -1, 3, 1, heads_wide)
        grad_qkv = jnp.moveaxis(grad_qkv, (1, 3), (0, 1)).reshape(group, -1, 3, 1, heads_wide)
        grad_qkv = lax.all_to_all(grad_qkv, ROW_AXES, split_axis=0, concat_axis=3, tiled=True)
        grad_qkv = grad_qkv.reshape(-1, 3 * width)
        grad_qkv = lax.psum_scatter(grad_qkv, ("plane", "hi"), scatter_dimension=0, tiled=True)
    else:
        split = grad_qkv.reshape(planes, 2, -1, 3 * heads_wide)
        other = lax.ppermute(lax.dynamic_index_in_dim(split, 1 - core, 1, False), "core", swap)
        own = lax.dynamic_index_in_dim(split, core, 1, False)
        own, other = (v.reshape(-1, 3 * heads_wide) for v in (own, other))
        left, right = jnp.where(first_core, own, other), jnp.where(first_core, other, own)
        grad_qkv = jnp.concatenate(
            [v[:, i * heads_wide : (i + 1) * heads_wide] for i in range(3) for v in (left, right)], axis=1
        )
        grad_qkv = scatter(grad_qkv)
    grad_qkv = grad_qkv.astype(f32)

    grad_skip_w = jnp.concatenate(
        [
            lax.dot_general(v, grad_in, (((0,), (0,)), ((), ())), preferred_element_type=f32).astype(bf16)
            for v in (x, s)
        ],
        axis=0,
    )
    grad_skip_w = scatter_rows(grad_skip_w).astype(f32)

    grad_inputs = jnp.einsum("mrfd,cd->mrfc", grad_in_home, skip_full[:width], preferred_element_type=f32).astype(bf16)
    grad_skips = jnp.einsum("mrfd,cd->mrfc", grad_in_home, skip_full[width:], preferred_element_type=f32).astype(bf16)

    grad_mod = jnp.stack([v[:labels] for v in (grad_shift_one, grad_scale_one, grad_shift_two, grad_scale_two)], axis=1)
    grad_mod = jnp.moveaxis(grad_mod.reshape(labels, devices, own_columns), 1, 0)
    grad_mod = lax.all_to_all(grad_mod, ALL_AXES, split_axis=0, concat_axis=0, tiled=True)
    grad_mod = jnp.sum(grad_mod.reshape(planes, 2, highs, lows, labels, own_columns), axis=(1, 3))
    grad_mod = lax.dot_general(
        embedded.astype(f32),
        grad_mod.reshape(-1, own_columns),
        (((0,), (0,)), ((), ())),
        precision=lax.Precision.HIGHEST,
        preferred_element_type=f32,
    )
    return (
        from_rows(result),
        grad_inputs,
        grad_skips,
        grad_skip_w,
        grad_qkv,
        grad_out,
        grad_up,
        grad_down,
        grad_mod,
    )


def solution(mesh):
    batch, wide = mesh.devices.shape

    def run(inputs, *rest):
        rows = 2 * inputs.shape[0]
        assert inputs.shape[0] == 2 and inputs.shape[1] == batch and wide % rows == 0
        fine = Mesh(mesh.devices.reshape(batch // 2, 2, rows, wide // rows), ALL_AXES)
        by_batch, by_wide = ("plane", "core"), ("hi", "lo")
        frames = P(None, by_batch, by_wide, None)
        rowed = P(None, by_batch, None)
        weight, columns = P(ALL_AXES, None), P(None, ALL_AXES)
        mapped = jax.shard_map(
            body,
            mesh=fine,
            in_specs=(frames, frames, frames, rowed, rowed) + (weight,) * 5 + (columns,),
            out_specs=(frames, frames, frames) + (weight,) * 5 + (columns,),
            check_vma=False,
        )
        return mapped(inputs, *rest)

    return run
```

```python
import functools
import math

import jax
import jax.numpy as jnp
from jax import lax
from jax.experimental import pallas as pl
from jax.experimental.pallas import tpu as pltpu
from jax.sharding import Mesh
from jax.sharding import PartitionSpec as P

HEAD_DIM = 64
TILE = 128
BLOCK = 256
VMEM_BYTES = 60 * 1024 * 1024
ROW_AXES = ("core", "lo")
LINE_AXES = ("core", "hi", "lo")
ALL_AXES = ("plane", "core", "hi", "lo")
f32 = jnp.float32
bf16 = jnp.bfloat16


def dot_nn(left, right):
    return lax.dot_general(left, right, (((1,), (0,)), ((), ())), preferred_element_type=f32)


def dot_nt(left, right):
    return lax.dot_general(left, right, (((1,), (1,)), ((), ())), preferred_element_type=f32)


def dot_tn(left, right):
    return lax.dot_general(left, right, (((0,), (0,)), ((), ())), preferred_element_type=f32)


def params(*semantics):
    return pltpu.CompilerParams(dimension_semantics=semantics, vmem_limit_bytes=VMEM_BYTES)


def cost(flops, moved, special=0):
    return pl.CostEstimate(flops=int(flops), bytes_accessed=int(moved), transcendentals=int(special))


def choose(segment_column, table_ref):
    count = table_ref.shape[0]
    picked = table_ref[count - 1 : count, :]
    for label in range(count - 2, -1, -1):
        picked = jnp.where(segment_column == label, table_ref[label : label + 1, :], picked)
    return picked


def normalise(values):
    centred = values - jnp.mean(values, axis=-1, keepdims=True)
    variance = jnp.mean(centred * centred, axis=-1, keepdims=True)
    inverse = lax.rsqrt(variance + 1e-06)
    return centred * inverse, inverse


def skip_norm_kernel(x_ref, s_ref, top_ref, bottom_ref, seg_ref, shift_ref, scale_ref, resid_ref, normed_ref):
    resid = dot_nn(x_ref[...], top_ref[...]) + dot_nn(s_ref[...], bottom_ref[...])
    resid_ref[...] = resid
    unit, _ = normalise(resid)
    label = seg_ref[...]
    normed = unit * (1.0 + choose(label, scale_ref)) + choose(label, shift_ref)
    normed_ref[...] = normed.astype(bf16)


def out_norm_kernel(mixed_ref, w_ref, resid_in_ref, seg_ref, shift_ref, scale_ref, resid_ref, normed_ref):
    resid = resid_in_ref[...] + dot_nn(mixed_ref[...], w_ref[...])
    resid_ref[...] = resid
    unit, _ = normalise(resid)
    label = seg_ref[...]
    normed = unit * (1.0 + choose(label, scale_ref)) + choose(label, shift_ref)
    normed_ref[...] = normed.astype(bf16)


def segment_sums(row_labels, values, total_ref):
    members = lax.broadcasted_iota(jnp.int32, (total_ref.shape[0], row_labels.shape[1]), 0) == row_labels
    members = members.astype(f32).astype(bf16)
    high = values.astype(bf16)
    low = (values - high.astype(f32)).astype(bf16)
    total_ref[...] += dot_nn(members, high) + dot_nn(members, low)


def norm_pull(grad, resid, scale):
    unit, inverse = normalise(resid)
    inner = grad * (1.0 + scale)
    pulled = inverse * (
        inner
        - jnp.mean(inner, axis=-1, keepdims=True)
        - unit * jnp.mean(inner * unit, axis=-1, keepdims=True)
    )
    return pulled, grad * unit


def norm_two_back_kernel(
    g_ref, resid_ref, cot_ref, seg_ref, segr_ref, scale_ref, w_ref, mid_ref, low_ref, mix_ref, dshift_ref, dscale_ref
):
    @pl.when(pl.program_id(0) == 0)
    def _():
        dshift_ref[...] = jnp.zeros_like(dshift_ref)
        dscale_ref[...] = jnp.zeros_like(dscale_ref)

    grad = g_ref[...]
    pulled, by_scale = norm_pull(grad, resid_ref[...], choose(seg_ref[...], scale_ref))
    grad_mid = cot_ref[...].astype(f32) + pulled
    low = grad_mid.astype(bf16)
    mid_ref[...] = grad_mid
    low_ref[...] = low
    mix_ref[...] = dot_nt(low, w_ref[...]).astype(bf16)
    segment_sums(segr_ref[...], grad, dshift_ref)
    segment_sums(segr_ref[...], by_scale, dscale_ref)


def norm_one_back_kernel(
    own_ref, other_ref, resid_ref, mid_ref, seg_ref, segr_ref, scale_ref, grad_ref, dshift_ref, dscale_ref
):
    @pl.when(pl.program_id(0) == 0)
    def _():
        dshift_ref[...] = jnp.zeros_like(dshift_ref)
        dscale_ref[...] = jnp.zeros_like(dscale_ref)

    grad = own_ref[...] + other_ref[...].astype(f32)
    pulled, by_scale = norm_pull(grad, resid_ref[...], choose(seg_ref[...], scale_ref))
    grad_ref[...] = (mid_ref[...] + pulled).astype(bf16)
    segment_sums(segr_ref[...], grad, dshift_ref)
    segment_sums(segr_ref[...], by_scale, dscale_ref)


def rowwise(kernel, frames, blocked, whole, outs, sums=0, flops=0):
    tile = min(BLOCK, frames)
    in_specs, args, moved = [], [], 0
    for kind, value in blocked:
        if kind == "row":
            in_specs.append(pl.BlockSpec((1, tile), lambda i: (0, i)))
        elif kind == "whole":
            in_specs.append(pl.BlockSpec(value.shape, lambda i: (0, 0)))
        else:
            in_specs.append(pl.BlockSpec((tile, value.shape[1]), lambda i: (i, 0)))
        args.append(value)
        moved += value.size * value.dtype.itemsize
    out_specs, shapes = [], []
    for width, kind in outs:
        out_specs.append(pl.BlockSpec((tile, width), lambda i: (i, 0)))
        shapes.append(jax.ShapeDtypeStruct((frames, width), kind))
        moved += frames * width * jnp.dtype(kind).itemsize
    for _ in range(sums):
        out_specs.append(pl.BlockSpec((8, outs[0][0]), lambda i: (0, 0)))
        shapes.append(jax.ShapeDtypeStruct((8, outs[0][0]), f32))
    return pl.pallas_call(
        kernel,
        grid=(frames // tile,),
        in_specs=in_specs,
        out_specs=out_specs,
        out_shape=shapes,
        compiler_params=params("arbitrary"),
        cost_estimate=cost(flops, moved),
    )(*args)


def swap_halves(values, lanes):
    half = HEAD_DIM // 2
    ahead = pltpu.roll(values, values.shape[1] - half, 1)
    behind = pltpu.roll(values, half, 1)
    return jnp.where(lanes % HEAD_DIM < half, ahead, behind)


def widen(table, width):
    return jnp.concatenate([table] * (width // table.shape[1]), axis=1)


def span(i):
    return pl.ds(pl.multiple_of(i * BLOCK, BLOCK), BLOCK)


def own_lanes(parts, lanes):
    picked = parts[0]
    for h in range(1, len(parts)):
        picked = jnp.where(lanes // HEAD_DIM == h, parts[h], picked)
    return picked


def by_count(count, most, run):
    for each in range(1, most + 1):
        pl.when(count == each)(functools.partial(run, each))


def attend_forward_kernel(
    range_ref, q_ref, k_ref, v_ref, cos_ref, sin_ref, segc_ref, segr_ref,
    out_ref, qrot_ref, krot_ref, lse_ref, seg_wide,
):
    length, width = q_ref.shape
    heads = width // HEAD_DIM
    blocks = length // BLOCK
    lanes = lax.broadcasted_iota(jnp.int32, (BLOCK, width), 1)

    def turn(i, carry):
        rows = span(i)
        cosine, sine = widen(cos_ref[rows, :], width), widen(sin_ref[rows, :], width)
        for source, target, factor in ((q_ref, qrot_ref, HEAD_DIM**-0.5), (k_ref, krot_ref, None)):
            values = source[rows, :].astype(f32)
            turned = (values * cosine + swap_halves(values, lanes) * sine).astype(bf16)
            if factor is not None:
                turned = turned * jnp.asarray(factor, bf16)
            target[rows, :] = turned
        seg_wide[rows, :] = jnp.broadcast_to(segc_ref[rows, :], (BLOCK, TILE))
        return carry

    lax.fori_loop(0, blocks, turn, 0)

    def one_query(i, carry):
        rows = span(i)

        def work(count):
            keys = pl.ds(pl.multiple_of(range_ref[0, i] * BLOCK, BLOCK), count * BLOCK)
            allowed = widen(seg_wide[rows, :], count * BLOCK) == segr_ref[:, keys]
            query = qrot_ref[rows, :]
            zero = jnp.zeros_like(query)
            mixed = []
            for h in range(heads):
                scores = dot_nt(jnp.where(lanes // HEAD_DIM == h, query, zero), krot_ref[keys, :])
                scores = jnp.where(allowed, scores, -1e30)
                highest = jnp.max(scores, axis=1, keepdims=True)
                powers = jnp.exp(scores - highest)
                totals = jnp.sum(powers, axis=1, keepdims=True)
                mixed.append(dot_nn(powers.astype(bf16), v_ref[keys, :]) * (1.0 / totals))
                logsum = jnp.broadcast_to(highest + jnp.log(totals), (BLOCK, TILE))
                lse_ref[0, h : h + 1, rows] = logsum.T[0:1]
            out_ref[rows, :] = own_lanes(mixed, lanes).astype(bf16)

        by_count(range_ref[1, i] - range_ref[0, i], blocks, work)
        return carry

    lax.fori_loop(0, blocks, one_query, 0)


def attend_forward(ranges, projected, cosine, sine, seg_column, seg_row):
    length, width = projected.shape
    width //= 3
    panels, heads = width // TILE, TILE // HEAD_DIM
    panel = lambda shift: pl.BlockSpec((length, TILE), lambda p, r: (0, shift * panels + p))
    whole = lambda shape: pl.BlockSpec(shape, lambda p, r: (0,) * len(shape))
    return pl.pallas_call(
        attend_forward_kernel,
        grid_spec=pltpu.PrefetchScalarGridSpec(
            num_scalar_prefetch=1,
            grid=(panels,),
            in_specs=[panel(0), panel(1), panel(2), whole(cosine.shape), whole(sine.shape),
                      whole(seg_column.shape), whole(seg_row.shape)],
            out_specs=[panel(0), panel(0), panel(0), pl.BlockSpec((1, heads, length), lambda p, r: (p, 0, 0))],
            scratch_shapes=[pltpu.VMEM((length, TILE), jnp.int32)],
        ),
        out_shape=[jax.ShapeDtypeStruct((length, width), bf16)] * 3
        + [jax.ShapeDtypeStruct((panels, heads, length), f32)],
        compiler_params=params("arbitrary"),
        cost_estimate=cost(8 * length * length * width, 14 * length * width, length * length * width // HEAD_DIM),
    )(ranges, projected, projected, projected, cosine, sine, seg_column, seg_row)


def attend_backward_kernel(
    range_ref, q_ref, k_ref, v_ref, out_ref, do_ref, lse_ref, cos_ref, sin_ref, segc_ref, segr_ref,
    grad_ref, dq, dk_low, dv_low, delta, seg_wide,
):
    length, width = q_ref.shape
    heads = width // HEAD_DIM
    blocks = length // BLOCK
    step = pl.program_id(1)

    @pl.when(step == 0)
    def _():
        lanes = lax.broadcasted_iota(jnp.int32, (BLOCK, width), 1)
        picker = (
            lax.broadcasted_iota(jnp.int32, (8, width), 0)
            == lax.broadcasted_iota(jnp.int32, (8, width), 1) // HEAD_DIM
        ).astype(f32)

        def prepare(i, carry):
            rows = span(i)
            product = do_ref[rows, :].astype(f32) * out_ref[rows, :].astype(f32)
            delta[:, rows] = lax.dot_general(
                picker, product, (((1,), (1,)), ((), ())),
                precision=lax.Precision.HIGHEST, preferred_element_type=f32,
            )
            dq[rows, :] = jnp.zeros((BLOCK, width), f32)
            seg_wide[rows, :] = jnp.broadcast_to(segc_ref[rows, :], (BLOCK, TILE))
            return carry

        lax.fori_loop(0, blocks, prepare, 0)

        def unturn(values, rows):
            return values * widen(cos_ref[rows, :], width) - swap_halves(values, lanes) * widen(sin_ref[rows, :], width)

        def one_key(j, carry):
            rows = span(j)

            def work(count):
                there = pl.ds(pl.multiple_of(range_ref[0, j] * BLOCK, BLOCK), count * BLOCK)
                allowed = widen(seg_wide[rows, :], count * BLOCK) == segr_ref[:, there]
                zero = jnp.zeros((BLOCK, width), bf16)
                grad_k, grad_v, grad_q = [], [], None
                for h in range(heads):
                    key = jnp.where(lanes // HEAD_DIM == h, k_ref[rows, :], zero)
                    value = jnp.where(lanes // HEAD_DIM == h, v_ref[rows, :], zero)
                    scores = dot_nt(key, q_ref[there, :]) - lse_ref[0, h : h + 1, there]
                    probability = jnp.exp(jnp.where(allowed, scores, -1e30))
                    grad_prob = dot_nt(value, do_ref[there, :])
                    grad_scores = (probability * (grad_prob - delta[h : h + 1, there])).astype(bf16)
                    grad_v.append(dot_nn(probability.astype(bf16), do_ref[there, :]))
                    grad_k.append(dot_nn(grad_scores, q_ref[there, :]))
                    part = dot_tn(grad_scores, key)
                    grad_q = part if grad_q is None else grad_q + part
                dq[there, :] += grad_q
                dk_low[rows, :] = unturn(own_lanes(grad_k, lanes), rows).astype(bf16)
                dv_low[rows, :] = own_lanes(grad_v, lanes).astype(bf16)

            by_count(range_ref[1, j] - range_ref[0, j], blocks, work)
            return carry

        lax.fori_loop(0, blocks, one_key, 0)

        def finish(i, carry):
            rows = span(i)
            grad_ref[rows, :] = unturn(dq[rows, :] * HEAD_DIM**-0.5, rows).astype(bf16)
            return carry

        lax.fori_loop(0, blocks, finish, 0)

    @pl.when(step == 1)
    def _():
        grad_ref[...] = dk_low[...]

    @pl.when(step == 2)
    def _():
        grad_ref[...] = dv_low[...]


def attend_backward(ranges, queries, keys, projected, mixed, grad_mixed, logsum, cosine, sine, seg_column, seg_row):
    length, width = queries.shape
    panels, heads = width // TILE, TILE // HEAD_DIM
    panel = lambda shift: pl.BlockSpec((length, TILE), lambda p, t, r: (0, shift * panels + p))
    whole = lambda shape: pl.BlockSpec(shape, lambda p, t, r: (0,) * len(shape))
    return pl.pallas_call(
        attend_backward_kernel,
        grid_spec=pltpu.PrefetchScalarGridSpec(
            num_scalar_prefetch=1,
            grid=(panels, 3),
            in_specs=[panel(0), panel(0), panel(2), panel(0), panel(0),
                      pl.BlockSpec((1, heads, length), lambda p, t, r: (p, 0, 0)),
                      whole(cosine.shape), whole(sine.shape), whole(seg_column.shape), whole(seg_row.shape)],
            out_specs=pl.BlockSpec((length, TILE), lambda p, t, r: (0, t * panels + p)),
            scratch_shapes=[
                pltpu.VMEM((length, TILE), f32),
                pltpu.VMEM((length, TILE), bf16),
                pltpu.VMEM((length, TILE), bf16),
                pltpu.VMEM((8, length), f32),
                pltpu.VMEM((length, TILE), jnp.int32),
            ],
        ),
        out_shape=jax.ShapeDtypeStruct((length, 3 * width), bf16),
        compiler_params=params("arbitrary", "arbitrary"),
        cost_estimate=cost(20 * length * length * width, 16 * length * width, length * length * width // HEAD_DIM),
    )(ranges, queries, keys, projected, mixed, grad_mixed, logsum, cosine, sine, seg_column, seg_row)


def gelu_and_slope(x):
    root = math.sqrt(2.0 / math.pi)
    square = x * x
    bend = jnp.tanh(x * (root + root * 0.044715 * square))
    half = 0.5 * x
    half_up = 0.5 + 0.5 * bend
    slope = half_up + half * (1.0 - bend * bend) * (root + 3.0 * root * 0.044715 * square)
    return half + half * bend, slope


def feed_kernel(
    n_ref, cot_ref, resid_ref, up_ref, down_ref, out_ref, back_ref, gup_ref, gdown_ref,
    total, n_turned, act_turned, pre,
):
    step, last = pl.program_id(0), pl.num_programs(0) - 1
    frames, width = n_ref.shape
    tile = min(BLOCK, frames)
    planes = gup_ref.shape[1]
    part = width // planes

    def rows_of(i):
        return pl.ds(pl.multiple_of(i * tile, tile), tile)

    @pl.when(step == 0)
    def _():
        def turn(i, carry):
            rows = rows_of(i)
            n_turned[:, rows] = n_ref[rows, :].T
            total[rows, :] = resid_ref[rows, :]
            back_ref[rows, :] = jnp.zeros((tile, width), f32)
            return carry

        lax.fori_loop(0, frames // tile, turn, 0)

    def chunk(i, carry):
        rows = rows_of(i)
        hidden = dot_nn(n_ref[rows, :], up_ref[...])
        grad_act = dot_nt(cot_ref[rows, :], down_ref[...])
        activated, slope = gelu_and_slope(hidden)
        activated = activated.astype(bf16)
        grad_pre = (grad_act * slope).astype(bf16)
        act_turned[:, rows] = activated.T
        pre[rows, :] = grad_pre
        total[rows, :] += dot_nn(activated, down_ref[...])
        back_ref[rows, :] += dot_nt(grad_pre, up_ref[...])
        return carry

    lax.fori_loop(0, frames // tile, chunk, 0)

    def weights(i, carry):
        rows = pl.ds(pl.multiple_of(i * part, part), part)
        grad_up = dot_nn(n_turned[rows, :], pre[...]).astype(bf16)
        gup_ref[0, i] = grad_up[: part // 2]
        gup_ref[1, i] = grad_up[part // 2 :]
        return carry

    lax.fori_loop(0, planes, weights, 0)

    def down_weights(i, carry):
        rows = span(i)
        gdown_ref[0, 0, rows, :] = dot_nn(act_turned[rows, :], cot_ref[...]).astype(bf16)
        return carry

    lax.fori_loop(0, act_turned.shape[0] // BLOCK, down_weights, 0)

    @pl.when(step == last)
    def _():
        out_ref[...] = total[...].astype(bf16)


def feed_forward_and_back(normed, cot, resid, w_up, w_down, planes):
    frames, width = normed.shape
    hidden = w_up.shape[1]
    piece = hidden // (2 * planes)
    once = dict(pipeline_mode=pl.Buffered(1))
    return pl.pallas_call(
        feed_kernel,
        grid=(hidden // piece,),
        in_specs=[
            pl.BlockSpec((frames, width), lambda j: (0, 0), **once),
            pl.BlockSpec((frames, width), lambda j: (0, 0), **once),
            pl.BlockSpec((frames, width), lambda j: (0, 0), **once),
            pl.BlockSpec((width, piece), lambda j: (0, j)),
            pl.BlockSpec((piece, width), lambda j: (j, 0)),
        ],
        out_specs=[
            pl.BlockSpec((frames, width), lambda j: (0, 0)),
            pl.BlockSpec((frames, width), lambda j: (0, 0)),
            pl.BlockSpec((2, planes, width // (2 * planes), piece), lambda j: (0, 0, 0, j)),
            pl.BlockSpec((1, 1, piece, width), lambda j: (j % 2, j // 2, 0, 0)),
        ],
        out_shape=[
            jax.ShapeDtypeStruct((frames, width), bf16),
            jax.ShapeDtypeStruct((frames, width), f32),
            jax.ShapeDtypeStruct((2, planes, width // (2 * planes), hidden), bf16),
            jax.ShapeDtypeStruct((2, planes, piece, width), bf16),
        ],
        scratch_shapes=[
            pltpu.VMEM((frames, width), f32),
            pltpu.VMEM((width, frames), bf16),
            pltpu.VMEM((piece, frames), bf16),
            pltpu.VMEM((frames, piece), bf16),
        ],
        compiler_params=params("arbitrary"),
        cost_estimate=cost(12 * frames * width * hidden, 8 * width * hidden + 16 * frames * width, frames * hidden),
    )(normed, cot, resid, w_up, w_down)


def body(inputs, skips, cotangent, segment_ids, time_steps, w_skip, w_qkv, w_out, w_up, w_down, w_mod):
    micro, _, piece, width = inputs.shape
    length = segment_ids.shape[-1]
    labels = time_steps.shape[-1]
    planes, lows, highs = lax.axis_size("plane"), lax.axis_size("lo"), lax.axis_size("hi")
    line = highs * lows
    group = 2 * lows
    devices = planes * 2 * line
    core, high, low = lax.axis_index("core"), lax.axis_index("hi"), lax.axis_index("lo")
    place = high * lows + low
    member = core * lows + low
    frames = 2 * piece
    heads_wide = width // group
    first_core = core == 0
    swap = [(0, 1), (1, 0)]

    def route(parity):
        pairs = []
        for c in range(2):
            for z in range(line):
                row = c * micro + ((z % 2) ^ parity)
                to_core, to_low = divmod(z // 2, lows)
                pairs.append((c * line + z, (to_core * highs + row) * lows + to_low))
        return pairs

    there = (route(0), route(1))
    back = tuple([(b, a) for a, b in pairs] for pairs in there)
    odd_place = place % 2
    even_row = high % 2 == 0

    def to_rows(value):
        value = value[:, 0]
        near = lax.ppermute(lax.dynamic_index_in_dim(value, odd_place, 0, False), LINE_AXES, there[0])
        far = lax.ppermute(lax.dynamic_index_in_dim(value, 1 - odd_place, 0, False), LINE_AXES, there[1])
        return jnp.concatenate([jnp.where(even_row, near, far), jnp.where(even_row, far, near)], axis=0)

    def from_rows(value):
        value = value.reshape(2, piece, width)
        near = lax.ppermute(lax.dynamic_index_in_dim(value, high % 2, 0, False), LINE_AXES, back[0])
        far = lax.ppermute(lax.dynamic_index_in_dim(value, 1 - high % 2, 0, False), LINE_AXES, back[1])
        even = odd_place == 0
        return jnp.stack([jnp.where(even, near, far), jnp.where(even, far, near)])[:, None]

    def frames_to_row(value):
        if group > 2:
            return lax.all_gather(value, ROW_AXES, axis=0, tiled=True)
        other = lax.ppermute(value, "core", swap)
        return jnp.concatenate([jnp.where(first_core, value, other), jnp.where(first_core, other, value)], axis=0)

    def heads_to_frames(value):
        if group > 2:
            return lax.all_to_all(value, ROW_AXES, split_axis=0, concat_axis=1, tiled=True)
        other = lax.ppermute(lax.dynamic_slice_in_dim(value, (1 - core) * frames, frames, 0), "core", swap)
        own = lax.dynamic_slice_in_dim(value, core * frames, frames, 0)
        return jnp.concatenate([jnp.where(first_core, own, other), jnp.where(first_core, other, own)], axis=1)

    def frames_to_heads(value):
        if group > 2:
            return lax.all_to_all(value, ROW_AXES, split_axis=1, concat_axis=0, tiled=True)
        other = lax.ppermute(lax.dynamic_slice_in_dim(value, (1 - core) * heads_wide, heads_wide, 1), "core", swap)
        own = lax.dynamic_slice_in_dim(value, core * heads_wide, heads_wide, 1)
        return jnp.concatenate([jnp.where(first_core, own, other), jnp.where(first_core, other, own)], axis=0)

    up_rows, down_rows, out_rows = w_up.shape[0], w_down.shape[0], w_out.shape[0]
    skip_rows = w_skip.shape[0]
    early = jnp.concatenate([w_skip] + [w_qkv[:, i * width : (i + 1) * width] for i in range(3)], axis=0)
    early = lax.all_gather(early, ALL_AXES, axis=0, tiled=True).reshape(devices, -1, width)
    x, s = to_rows(inputs), to_rows(skips)

    labels_own = segment_ids[:, 0]
    labels_other = lax.ppermute(labels_own, "core", swap)
    labels_pick = jnp.where(core == high // micro, labels_own, labels_other)
    seg = lax.dynamic_index_in_dim(labels_pick, high % micro, 0, False)
    names = jnp.arange(labels, dtype=jnp.int32)
    starts = jnp.sum((seg[:, None] < names[None, :]).astype(jnp.int32), axis=0)
    ends = jnp.sum((seg[:, None] <= names[None, :]).astype(jnp.int32), axis=0)
    offset = jnp.sum(jnp.where(seg[:, None] == names[None, :], starts[None, :], 0), axis=1)
    where_at = jnp.arange(length, dtype=jnp.int32) - offset
    by_block = seg.reshape(-1, BLOCK)
    begin = jnp.sum(jnp.where(by_block[:, :1] == names[None, :], starts[None, :], 0), axis=1)
    finish = jnp.sum(jnp.where(by_block[:, -1:] == names[None, :], ends[None, :], 0), axis=1)
    ranges = jnp.stack([begin // BLOCK, (finish + BLOCK - 1) // BLOCK]).astype(jnp.int32)
    half = HEAD_DIM // 2
    rates = jnp.exp(-math.log(10000.0) * jnp.arange(half, dtype=f32) / half)
    angles = where_at.astype(f32)[:, None] * rates
    cosine = jnp.tile(jnp.cos(angles), (1, 4))
    sine = jnp.sin(angles)
    sine = jnp.concatenate([-sine, sine, -sine, sine], axis=1)
    seg_column, seg_row = seg[:, None], seg[None, :]
    mine = lax.dynamic_slice_in_dim(seg, member * frames, frames, 0)

    steps = lax.all_gather(time_steps[:, 0], ("plane", "core"), axis=0, tiled=True).reshape(-1)
    quarter = w_mod.shape[0] // 2
    pace = jnp.exp(-math.log(10000.0) * jnp.arange(quarter, dtype=f32) / quarter)
    turns = steps.astype(f32)[:, None] * pace
    embedded = jnp.concatenate([jnp.sin(turns), jnp.cos(turns)], axis=1).astype(bf16)
    block_mod = jnp.dot(embedded, w_mod, preferred_element_type=f32)
    own_columns = block_mod.shape[1]
    block_mod = block_mod.reshape(planes, 1, highs, 1, labels, own_columns)
    block_mod = jnp.broadcast_to(block_mod, (planes, 2, highs, lows, labels, own_columns))
    block_mod = lax.all_to_all(
        block_mod.reshape(devices, labels, own_columns), ALL_AXES, split_axis=0, concat_axis=0, tiled=True
    )
    modulation = jnp.moveaxis(block_mod, 0, 1).reshape(labels, 4, width)

    columns = w_up.shape[1] // width
    late = jnp.concatenate([w_down, w_out] + [w_up[:, i * width : (i + 1) * width] for i in range(columns)], axis=0)
    late, cotangent, x, s, modulation, cosine, sine, ranges, mine = lax.optimization_barrier(
        (late, cotangent, x, s, modulation, cosine, sine, ranges, mine)
    )
    late = lax.all_gather(late, ALL_AXES, axis=0, tiled=True).reshape(devices, -1, width)
    cot = to_rows(cotangent)
    down_full = late[:, :down_rows].reshape(-1, width)
    out_full = late[:, down_rows : down_rows + out_rows].reshape(width, width)
    up_full = jnp.concatenate(
        [
            late[:, down_rows + out_rows + i * up_rows : down_rows + out_rows + (i + 1) * up_rows].reshape(width, width)
            for i in range(columns)
        ],
        axis=1,
    )
    skip_full = early[:, :skip_rows].reshape(-1, width)
    qkv_parts = []
    for i in range(3):
        begin = skip_rows + i * out_rows
        whole = early[:, begin : begin + out_rows].reshape(width, width)
        qkv_parts.append(lax.dynamic_slice_in_dim(whole, member * heads_wide, heads_wide, 1))
    qkv_own = jnp.concatenate(qkv_parts, axis=1)
    mine_column, mine_row = mine[:, None], mine[None, :]
    shift_one, scale_one, shift_two, scale_two = (modulation[:, i] for i in range(4))

    resid_in, normed_one = rowwise(
        skip_norm_kernel,
        frames,
        [("", x), ("", s), ("whole", skip_full[:width]), ("whole", skip_full[width:]), ("", mine_column),
         ("whole", shift_one), ("whole", scale_one)],
        None,
        [(width, f32), (width, bf16)],
        flops=4 * frames * width * width,
    )
    normed_row = frames_to_row(normed_one)
    projected = jnp.dot(normed_row, qkv_own, preferred_element_type=f32).astype(bf16)
    mixed_heads, queries, keys, logsum = attend_forward(ranges, projected, cosine, sine, seg_column, seg_row)
    mixed = heads_to_frames(mixed_heads)
    resid_mid, normed_two = rowwise(
        out_norm_kernel,
        frames,
        [("", mixed), ("whole", out_full), ("", resid_in), ("", mine_column), ("whole", shift_two), ("whole", scale_two)],
        None,
        [(width, f32), (width, bf16)],
        flops=2 * frames * width * width,
    )
    result, grad_normed_two, grad_up, grad_down = feed_forward_and_back(
        normed_two, cot, resid_mid, up_full, down_full, planes
    )

    def over_cores(kept, axis):
        other = lax.ppermute(lax.dynamic_index_in_dim(kept, 1 - core, axis, False), "core", swap)
        own = lax.dynamic_index_in_dim(kept, core, axis, False)
        return (own.astype(f32) + other.astype(f32)).astype(bf16)

    plane = lax.axis_index("plane")

    def exchange(value, axes, here, count):
        total = lax.dynamic_index_in_dim(value, here, 0, False).astype(f32)
        for flip in range(1, count):
            sent = lax.dynamic_index_in_dim(value, here ^ flip, 0, False)
            total += lax.ppermute(sent, axes, [(i, i ^ flip) for i in range(count)]).astype(f32)
        return total

    def exchange_planes(value):
        return exchange(value, "plane", plane, planes).astype(bf16)

    def exchange_line(value):
        return exchange(value.reshape(line, -1, value.shape[1]), ("hi", "lo"), place, line)

    def over_planes(value):
        value = value.reshape(-1, value.shape[-1])
        return lax.psum_scatter(value, "plane", scatter_dimension=0, tiled=True)

    grad_up, grad_down = over_cores(grad_up, 0), over_cores(grad_down, 0)
    block_out = from_rows(result)

    grad_mid, grad_mid_low, grad_frames, grad_shift_two, grad_scale_two = rowwise(
        norm_two_back_kernel,
        frames,
        [("", grad_normed_two), ("", resid_mid), ("", cot), ("", mine_column), ("row", mine_row),
         ("whole", scale_two), ("whole", out_full)],
        None,
        [(width, f32), (width, bf16), (width, bf16)],
        sums=2,
        flops=2 * frames * width * width,
    )
    grad_frames, grad_up = lax.optimization_barrier((grad_frames, grad_up))
    grad_up = over_planes(grad_up)
    grad_heads = frames_to_heads(grad_frames)
    grad_out = lax.dot_general(mixed, grad_mid_low, (((0,), (0,)), ((), ())), preferred_element_type=f32)
    grad_out = over_cores(grad_out.astype(bf16).reshape(planes, 2, -1, width), 1)
    grad_down = jnp.concatenate(
        [v.reshape(planes, line, -1, width) for v in (grad_down, grad_out)], axis=2
    )
    grad_heads, grad_down, block_out = lax.optimization_barrier((grad_heads, grad_down, block_out))
    grad_down = over_planes(grad_down)
    grad_proj = attend_backward(
        ranges, queries, keys, projected, mixed_heads, grad_heads, logsum, cosine, sine, seg_column, seg_row
    )
    grad_proj, grad_up, grad_down = lax.optimization_barrier((grad_proj, grad_up, grad_down))
    if group > 2:
        partial = dot_nt(grad_proj, qkv_own).astype(bf16)
        grad_one = lax.psum_scatter(partial, ROW_AXES, scatter_dimension=0, tiled=True).astype(f32)
        grad_one_other = jnp.zeros((frames, width), bf16)
    else:
        away = lax.dynamic_slice_in_dim(grad_proj, (1 - core) * frames, frames, 0)
        home = lax.dynamic_slice_in_dim(grad_proj, core * frames, frames, 0)
        grad_one_other = lax.ppermute(dot_nt(away, qkv_own).astype(bf16), "core", swap)
        grad_one = dot_nt(home, qkv_own)
    over_line = lambda value: lax.psum_scatter(value, ("hi", "lo"), scatter_dimension=0, tiled=True).astype(f32)
    grad_up = over_line(grad_up)
    grad_down = over_line(grad_down)
    grad_down, grad_out = grad_down[:down_rows], grad_down[down_rows:]
    grad_in, grad_shift_one, grad_scale_one = rowwise(
        norm_one_back_kernel,
        frames,
        [("", grad_one), ("", grad_one_other), ("", resid_in), ("", grad_mid), ("", mine_column), ("row", mine_row),
         ("whole", scale_one)],
        None,
        [(width, bf16)],
        sums=2,
    )
    grad_in_home = from_rows(grad_in)
    grad_proj, grad_in = lax.optimization_barrier((grad_proj, grad_in))
    grad_qkv = lax.dot_general(normed_row, grad_proj, (((0,), (0,)), ((), ())), preferred_element_type=f32)
    grad_qkv = grad_qkv.astype(bf16)
    if group > 2:
        grad_qkv = grad_qkv.reshape(planes, 2, highs, lows, -1, 3, 1, heads_wide)
        grad_qkv = jnp.moveaxis(grad_qkv, (1, 3), (0, 1)).reshape(group, -1, 3, 1, heads_wide)
        grad_qkv = lax.all_to_all(grad_qkv, ROW_AXES, split_axis=0, concat_axis=3, tiled=True)
        grad_qkv = grad_qkv.reshape(-1, 3 * width)
        grad_qkv = lax.psum_scatter(grad_qkv, ("plane", "hi"), scatter_dimension=0, tiled=True).astype(f32)
    else:
        split = grad_qkv.reshape(planes, 2, -1, 3 * heads_wide)
        other = lax.ppermute(lax.dynamic_index_in_dim(split, 1 - core, 1, False), "core", swap)
        own = lax.dynamic_index_in_dim(split, core, 1, False)
        own, other = (v.reshape(-1, 3 * heads_wide) for v in (own, other))
        left, right = jnp.where(first_core, own, other), jnp.where(first_core, other, own)
        grad_qkv = jnp.concatenate(
            [v[:, i * heads_wide : (i + 1) * heads_wide] for i in range(3) for v in (left, right)], axis=1
        )
        grad_qkv = exchange_planes(grad_qkv.reshape(planes, -1, 3 * width))

    grad_skip_w = jnp.concatenate(
        [
            lax.dot_general(v, grad_in, (((0,), (0,)), ((), ())), preferred_element_type=f32).astype(bf16)
            for v in (x, s)
        ],
        axis=0,
    )
    grad_skip_w = exchange_planes(over_cores(grad_skip_w.reshape(planes, 2, -1, width), 1))
    grad_in_home, grad_qkv = lax.optimization_barrier((grad_in_home, grad_qkv))
    if group == 2:
        grad_qkv = exchange_line(grad_qkv)
    grad_skip_w = exchange_line(grad_skip_w)
    grad_inputs = jnp.einsum("mrfd,cd->mrfc", grad_in_home, skip_full[:width], preferred_element_type=f32).astype(bf16)
    grad_skips = jnp.einsum("mrfd,cd->mrfc", grad_in_home, skip_full[width:], preferred_element_type=f32).astype(bf16)

    grad_mod = jnp.stack([v[:labels] for v in (grad_shift_one, grad_scale_one, grad_shift_two, grad_scale_two)], axis=1)
    grad_mod = jnp.moveaxis(grad_mod.reshape(labels, devices, own_columns), 1, 0)
    grad_mod = lax.all_to_all(grad_mod, ALL_AXES, split_axis=0, concat_axis=0, tiled=True)
    grad_inputs, grad_mod, grad_up, grad_down, grad_out = lax.optimization_barrier(
        (grad_inputs, grad_mod, grad_up, grad_down, grad_out)
    )
    grad_mod = jnp.sum(grad_mod.reshape(planes, 2, highs, lows, labels, own_columns), axis=(1, 3))
    grad_mod = lax.dot_general(
        embedded.astype(f32),
        grad_mod.reshape(-1, own_columns),
        (((0,), (0,)), ((), ())),
        precision=lax.Precision.HIGHEST,
        preferred_element_type=f32,
    )
    return (
        block_out,
        grad_inputs,
        grad_skips,
        grad_skip_w,
        grad_qkv,
        grad_out,
        grad_up,
        grad_down,
        grad_mod,
    )


def solution(mesh):
    batch, wide = mesh.devices.shape

    def run(inputs, *rest):
        rows = 2 * inputs.shape[0]
        assert inputs.shape[0] == 2 and inputs.shape[1] == batch and wide % rows == 0
        fine = Mesh(mesh.devices.reshape(batch // 2, 2, rows, wide // rows), ALL_AXES)
        by_batch, by_wide = ("plane", "core"), ("hi", "lo")
        frames = P(None, by_batch, by_wide, None)
        rowed = P(None, by_batch, None)
        weight, columns = P(ALL_AXES, None), P(None, ALL_AXES)
        mapped = jax.shard_map(
            body,
            mesh=fine,
            in_specs=(frames, frames, frames, rowed, rowed) + (weight,) * 5 + (columns,),
            out_specs=(frames, frames, frames) + (weight,) * 5 + (columns,),
            check_vma=False,
        )
        return mapped(inputs, *rest)

    return run
```

```python
import functools
import math

import jax
import jax.numpy as jnp
from jax import lax
from jax.experimental import pallas as pl
from jax.experimental.pallas import tpu as pltpu
from jax.sharding import Mesh
from jax.sharding import PartitionSpec as P

HEAD_DIM = 64
TILE = 128
BLOCK = 256
ROW_TILE = 256
FEED_TILE = 256
FEED_PART = 256
VMEM_BYTES = 60 * 1024 * 1024
ROW_AXES = ("core", "lo")
LINE_AXES = ("core", "hi", "lo")
ALL_AXES = ("plane", "core", "hi", "lo")
f32 = jnp.float32
bf16 = jnp.bfloat16


def dot_nn(left, right):
    return lax.dot_general(left, right, (((1,), (0,)), ((), ())), preferred_element_type=f32)


def dot_nt(left, right):
    return lax.dot_general(left, right, (((1,), (1,)), ((), ())), preferred_element_type=f32)


def dot_tn(left, right):
    return lax.dot_general(left, right, (((0,), (0,)), ((), ())), preferred_element_type=f32)


def params(*semantics):
    return pltpu.CompilerParams(dimension_semantics=semantics, vmem_limit_bytes=VMEM_BYTES)


def cost(flops, moved, special=0):
    return pl.CostEstimate(flops=int(flops), bytes_accessed=int(moved), transcendentals=int(special))


def flat(ref):
    return ref[...].reshape(-1, ref.shape[-1])


def choose(segment_column, table_ref):
    count = table_ref.shape[0]
    picked = table_ref[count - 1 : count, :]
    for label in range(count - 2, -1, -1):
        picked = jnp.where(segment_column == label, table_ref[label : label + 1, :], picked)
    return picked


def normalise(values):
    centred = values - jnp.mean(values, axis=-1, keepdims=True)
    variance = jnp.mean(centred * centred, axis=-1, keepdims=True)
    inverse = lax.rsqrt(variance + 1e-06)
    return centred * inverse, inverse


def skip_norm_kernel(x_ref, s_ref, top_ref, bottom_ref, seg_ref, shift_ref, scale_ref, resid_ref, normed_ref):
    resid = dot_nn(x_ref[...], flat(top_ref)) + dot_nn(s_ref[...], flat(bottom_ref))
    resid_ref[...] = resid
    unit, _ = normalise(resid)
    label = seg_ref[...]
    normed = unit * (1.0 + choose(label, scale_ref)) + choose(label, shift_ref)
    normed_ref[...] = normed.astype(bf16)


def out_norm_kernel(mixed_ref, w_ref, resid_in_ref, seg_ref, shift_ref, scale_ref, resid_ref, normed_ref):
    resid = resid_in_ref[...] + dot_nn(mixed_ref[...], flat(w_ref))
    resid_ref[...] = resid
    unit, _ = normalise(resid)
    label = seg_ref[...]
    normed = unit * (1.0 + choose(label, scale_ref)) + choose(label, shift_ref)
    normed_ref[...] = normed.astype(bf16)


def segment_sums(row_labels, values, total_ref):
    members = lax.broadcasted_iota(jnp.int32, (total_ref.shape[0], row_labels.shape[1]), 0) == row_labels
    members = members.astype(f32).astype(bf16)
    high = values.astype(bf16)
    low = (values - high.astype(f32)).astype(bf16)
    total_ref[...] += dot_nn(members, high) + dot_nn(members, low)


def norm_pull(grad, resid, scale):
    unit, inverse = normalise(resid)
    inner = grad * (1.0 + scale)
    pulled = inverse * (
        inner
        - jnp.mean(inner, axis=-1, keepdims=True)
        - unit * jnp.mean(inner * unit, axis=-1, keepdims=True)
    )
    return pulled, grad * unit


def norm_two_back_kernel(
    g_ref, resid_ref, cot_ref, seg_ref, segr_ref, scale_ref, w_ref, mid_ref, low_ref, mix_ref, dshift_ref, dscale_ref
):
    @pl.when(pl.program_id(0) == 0)
    def _():
        dshift_ref[...] = jnp.zeros_like(dshift_ref)
        dscale_ref[...] = jnp.zeros_like(dscale_ref)

    grad = g_ref[...]
    pulled, by_scale = norm_pull(grad, resid_ref[...], choose(seg_ref[...], scale_ref))
    grad_mid = cot_ref[...].astype(f32) + pulled
    low = grad_mid.astype(bf16)
    mid_ref[...] = grad_mid
    low_ref[...] = low
    mix_ref[...] = dot_nt(low, flat(w_ref)).astype(bf16)
    segment_sums(segr_ref[...], grad, dshift_ref)
    segment_sums(segr_ref[...], by_scale, dscale_ref)


def norm_one_back_kernel(
    own_ref, other_ref, resid_ref, mid_ref, seg_ref, segr_ref, scale_ref, grad_ref, dshift_ref, dscale_ref
):
    @pl.when(pl.program_id(0) == 0)
    def _():
        dshift_ref[...] = jnp.zeros_like(dshift_ref)
        dscale_ref[...] = jnp.zeros_like(dscale_ref)

    grad = own_ref[...] + other_ref[...].astype(f32)
    pulled, by_scale = norm_pull(grad, resid_ref[...], choose(seg_ref[...], scale_ref))
    grad_ref[...] = (mid_ref[...] + pulled).astype(bf16)
    segment_sums(segr_ref[...], grad, dshift_ref)
    segment_sums(segr_ref[...], by_scale, dscale_ref)


def unmerge_kernel(g_ref, top_ref, bottom_ref, inputs_ref, skips_ref):
    inputs_ref[...] = dot_nt(g_ref[...], flat(top_ref)).astype(bf16)
    skips_ref[...] = dot_nt(g_ref[...], flat(bottom_ref)).astype(bf16)


def project_kernel(place_ref, x_ref, w_ref, out_ref):
    out_ref[...] = dot_nn(x_ref[...], flat(w_ref)).astype(bf16)


def project(value, gathered, begin, rows, heads_wide, member):
    length, width = value.shape
    tile = min(ROW_TILE, length)
    return pl.pallas_call(
        project_kernel,
        grid_spec=pltpu.PrefetchScalarGridSpec(
            num_scalar_prefetch=1,
            grid=(3, length // tile),
            in_specs=[
                pl.BlockSpec((tile, width), lambda t, i, r: (i, 0)),
                pl.BlockSpec((width // rows, rows, heads_wide), lambda t, i, r: (0, begin // rows + t, r[0])),
            ],
            out_specs=pl.BlockSpec((tile, heads_wide), lambda t, i, r: (i, t)),
        ),
        out_shape=jax.ShapeDtypeStruct((length, 3 * heads_wide), bf16),
        compiler_params=params("arbitrary", "arbitrary"),
        cost_estimate=cost(6 * length * width * heads_wide, 8 * length * width),
    )(member.reshape(1), value, gathered)


def rowwise(kernel, frames, blocked, outs, sums=0, flops=0, light=False):
    tile = min(ROW_TILE, frames)
    in_specs, args, moved = [], [], 0
    for kind, value in blocked:
        if kind == "row":
            in_specs.append(pl.BlockSpec((1, tile), lambda i: (0, i)))
        elif kind == "weight":
            value, block, index = value
            in_specs.append(pl.BlockSpec(block, functools.partial(lambda index, i: index, index)))
        elif kind == "whole":
            in_specs.append(pl.BlockSpec(value.shape, lambda i: (0, 0)))
        else:
            in_specs.append(pl.BlockSpec((tile, value.shape[1]), lambda i: (i, 0)))
        args.append(value)
        moved += value.size * value.dtype.itemsize
    out_specs, shapes = [], []
    for width, kind in outs:
        out_specs.append(pl.BlockSpec((tile, width), lambda i: (i, 0)))
        shapes.append(jax.ShapeDtypeStruct((frames, width), kind))
        moved += frames * width * jnp.dtype(kind).itemsize
    for _ in range(sums):
        out_specs.append(pl.BlockSpec((8, outs[0][0]), lambda i: (0, 0)))
        shapes.append(jax.ShapeDtypeStruct((8, outs[0][0]), f32))
    return pl.pallas_call(
        kernel,
        grid=(frames // tile,),
        in_specs=in_specs,
        out_specs=out_specs,
        out_shape=shapes,
        compiler_params=params("arbitrary"),
        cost_estimate=cost(1, 1) if light else cost(flops, moved),
    )(*args)


def swap_halves(values, lanes):
    half = HEAD_DIM // 2
    ahead = pltpu.roll(values, values.shape[1] - half, 1)
    behind = pltpu.roll(values, half, 1)
    return jnp.where(lanes % HEAD_DIM < half, ahead, behind)


def widen(table, width):
    return jnp.concatenate([table] * (width // table.shape[1]), axis=1)


def span(i):
    return pl.ds(pl.multiple_of(i * BLOCK, BLOCK), BLOCK)


def own_lanes(parts, lanes):
    picked = parts[0]
    for h in range(1, len(parts)):
        picked = jnp.where(lanes // HEAD_DIM == h, parts[h], picked)
    return picked


def by_count(count, most, run):
    for each in range(1, most + 1):
        pl.when(count == each)(functools.partial(run, each))


def attend_forward_kernel(
    range_ref, q_ref, k_ref, v_ref, cos_ref, sin_ref, segc_ref, segr_ref,
    out_ref, qrot_ref, krot_ref, lse_ref, seg_wide,
):
    length, width = q_ref.shape
    heads = width // HEAD_DIM
    blocks = length // BLOCK
    lanes = lax.broadcasted_iota(jnp.int32, (BLOCK, width), 1)

    def turn(i, carry):
        rows = span(i)
        cosine, sine = widen(cos_ref[rows, :], width), widen(sin_ref[rows, :], width)
        for source, target, factor in ((q_ref, qrot_ref, HEAD_DIM**-0.5), (k_ref, krot_ref, None)):
            values = source[rows, :].astype(f32)
            turned = (values * cosine + swap_halves(values, lanes) * sine).astype(bf16)
            if factor is not None:
                turned = turned * jnp.asarray(factor, bf16)
            target[rows, :] = turned
        seg_wide[rows, :] = jnp.broadcast_to(segc_ref[rows, :], (BLOCK, TILE))
        return carry

    lax.fori_loop(0, blocks, turn, 0)

    def one_query(i, carry):
        rows = span(i)

        def work(count):
            keys = pl.ds(pl.multiple_of(range_ref[0, i] * BLOCK, BLOCK), count * BLOCK)
            allowed = widen(seg_wide[rows, :], count * BLOCK) == segr_ref[:, keys]
            query = qrot_ref[rows, :]
            zero = jnp.zeros_like(query)
            mixed = []
            for h in range(heads):
                scores = dot_nt(jnp.where(lanes // HEAD_DIM == h, query, zero), krot_ref[keys, :])
                scores = jnp.where(allowed, scores, -1e30)
                highest = jnp.max(scores, axis=1, keepdims=True)
                powers = jnp.exp(scores - highest)
                totals = jnp.sum(powers, axis=1, keepdims=True)
                mixed.append(dot_nn(powers.astype(bf16), v_ref[keys, :]) * (1.0 / totals))
                logsum = jnp.broadcast_to(highest + jnp.log(totals), (BLOCK, TILE))
                lse_ref[0, h : h + 1, rows] = logsum.T[0:1]
            out_ref[rows, :] = own_lanes(mixed, lanes).astype(bf16)

        by_count(range_ref[1, i] - range_ref[0, i], blocks, work)
        return carry

    lax.fori_loop(0, blocks, one_query, 0)


def attend_forward(ranges, projected, cosine, sine, seg_column, seg_row):
    length, width = projected.shape
    width //= 3
    panels, heads = width // TILE, TILE // HEAD_DIM
    panel = lambda shift: pl.BlockSpec((length, TILE), lambda p, r: (0, shift * panels + p))
    whole = lambda shape: pl.BlockSpec(shape, lambda p, r: (0,) * len(shape))
    return pl.pallas_call(
        attend_forward_kernel,
        grid_spec=pltpu.PrefetchScalarGridSpec(
            num_scalar_prefetch=1,
            grid=(panels,),
            in_specs=[panel(0), panel(1), panel(2), whole(cosine.shape), whole(sine.shape),
                      whole(seg_column.shape), whole(seg_row.shape)],
            out_specs=[panel(0), panel(0), panel(0), pl.BlockSpec((1, heads, length), lambda p, r: (p, 0, 0))],
            scratch_shapes=[pltpu.VMEM((length, TILE), jnp.int32)],
        ),
        out_shape=[jax.ShapeDtypeStruct((length, width), bf16)] * 3
        + [jax.ShapeDtypeStruct((panels, heads, length), f32)],
        compiler_params=params("arbitrary"),
        cost_estimate=cost(8 * length * length * width, 14 * length * width, length * length * width // HEAD_DIM),
    )(ranges, projected, projected, projected, cosine, sine, seg_column, seg_row)


def attend_backward_kernel(
    range_ref, q_ref, k_ref, v_ref, out_ref, do_ref, lse_ref, cos_ref, sin_ref, segc_ref, segr_ref,
    grad_ref, dq, dk_low, dv_low, delta, seg_wide,
):
    length, width = q_ref.shape
    heads = width // HEAD_DIM
    blocks = length // BLOCK
    step = pl.program_id(1)

    @pl.when(step == 0)
    def _():
        lanes = lax.broadcasted_iota(jnp.int32, (BLOCK, width), 1)
        picker = (
            lax.broadcasted_iota(jnp.int32, (8, width), 0)
            == lax.broadcasted_iota(jnp.int32, (8, width), 1) // HEAD_DIM
        ).astype(f32)

        def prepare(i, carry):
            rows = span(i)
            product = do_ref[rows, :].astype(f32) * out_ref[rows, :].astype(f32)
            delta[:, rows] = lax.dot_general(
                picker, product, (((1,), (1,)), ((), ())),
                precision=lax.Precision.HIGHEST, preferred_element_type=f32,
            )
            dq[rows, :] = jnp.zeros((BLOCK, width), f32)
            seg_wide[rows, :] = jnp.broadcast_to(segc_ref[rows, :], (BLOCK, TILE))
            return carry

        lax.fori_loop(0, blocks, prepare, 0)

        def unturn(values, rows):
            return values * widen(cos_ref[rows, :], width) - swap_halves(values, lanes) * widen(sin_ref[rows, :], width)

        def one_key(j, carry):
            rows = span(j)

            def work(count):
                there = pl.ds(pl.multiple_of(range_ref[0, j] * BLOCK, BLOCK), count * BLOCK)
                allowed = widen(seg_wide[rows, :], count * BLOCK) == segr_ref[:, there]
                zero = jnp.zeros((BLOCK, width), bf16)
                grad_k, grad_v, grad_q = [], [], None
                for h in range(heads):
                    key = jnp.where(lanes // HEAD_DIM == h, k_ref[rows, :], zero)
                    value = jnp.where(lanes // HEAD_DIM == h, v_ref[rows, :], zero)
                    scores = dot_nt(key, q_ref[there, :]) - lse_ref[0, h : h + 1, there]
                    probability = jnp.exp(jnp.where(allowed, scores, -1e30))
                    grad_prob = dot_nt(value, do_ref[there, :])
                    grad_scores = (probability * (grad_prob - delta[h : h + 1, there])).astype(bf16)
                    grad_v.append(dot_nn(probability.astype(bf16), do_ref[there, :]))
                    grad_k.append(dot_nn(grad_scores, q_ref[there, :]))
                    part = dot_tn(grad_scores, key)
                    grad_q = part if grad_q is None else grad_q + part
                dq[there, :] += grad_q
                dk_low[rows, :] = unturn(own_lanes(grad_k, lanes), rows).astype(bf16)
                dv_low[rows, :] = own_lanes(grad_v, lanes).astype(bf16)

            by_count(range_ref[1, j] - range_ref[0, j], blocks, work)
            return carry

        lax.fori_loop(0, blocks, one_key, 0)

        def finish(i, carry):
            rows = span(i)
            grad_ref[rows, :] = unturn(dq[rows, :] * HEAD_DIM**-0.5, rows).astype(bf16)
            return carry

        lax.fori_loop(0, blocks, finish, 0)

    @pl.when(step == 1)
    def _():
        grad_ref[...] = dk_low[...]

    @pl.when(step == 2)
    def _():
        grad_ref[...] = dv_low[...]


def attend_backward(ranges, queries, keys, projected, mixed, grad_mixed, logsum, cosine, sine, seg_column, seg_row):
    length, width = queries.shape
    panels, heads = width // TILE, TILE // HEAD_DIM
    panel = lambda shift: pl.BlockSpec((length, TILE), lambda p, t, r: (0, shift * panels + p))
    whole = lambda shape: pl.BlockSpec(shape, lambda p, t, r: (0,) * len(shape))
    return pl.pallas_call(
        attend_backward_kernel,
        grid_spec=pltpu.PrefetchScalarGridSpec(
            num_scalar_prefetch=1,
            grid=(panels, 3),
            in_specs=[panel(0), panel(0), panel(2), panel(0), panel(0),
                      pl.BlockSpec((1, heads, length), lambda p, t, r: (p, 0, 0)),
                      whole(cosine.shape), whole(sine.shape), whole(seg_column.shape), whole(seg_row.shape)],
            out_specs=pl.BlockSpec((length, TILE), lambda p, t, r: (0, t * panels + p)),
            scratch_shapes=[
                pltpu.VMEM((length, TILE), f32),
                pltpu.VMEM((length, TILE), bf16),
                pltpu.VMEM((length, TILE), bf16),
                pltpu.VMEM((8, length), f32),
                pltpu.VMEM((length, TILE), jnp.int32),
            ],
        ),
        out_shape=jax.ShapeDtypeStruct((length, 3 * width), bf16),
        compiler_params=params("arbitrary", "arbitrary"),
        cost_estimate=cost(20 * length * length * width, 16 * length * width, length * length * width // HEAD_DIM),
    )(ranges, queries, keys, projected, mixed, grad_mixed, logsum, cosine, sine, seg_column, seg_row)


def gelu_and_slope(x):
    root = math.sqrt(2.0 / math.pi)
    square = x * x
    bend = jnp.tanh(x * (root + root * 0.044715 * square))
    half = 0.5 * x
    half_up = 0.5 + 0.5 * bend
    slope = half_up + half * (1.0 - bend * bend) * (root + 3.0 * root * 0.044715 * square)
    return half + half * bend, slope


def feed_kernel(
    n_ref, cot_ref, resid_ref, up_ref, down_ref, out_ref, back_ref, gup_ref, gdown_ref,
    total, n_turned, act_turned, pre,
):
    step, last = pl.program_id(0), pl.num_programs(0) - 1
    frames, width = n_ref.shape
    tile = min(FEED_TILE, frames)
    planes = gup_ref.shape[1]
    part = width // planes

    def rows_of(i):
        return pl.ds(pl.multiple_of(i * tile, tile), tile)

    @pl.when(step == 0)
    def _():
        def turn(i, carry):
            rows = rows_of(i)
            n_turned[:, rows] = n_ref[rows, :].T
            total[rows, :] = resid_ref[rows, :]
            back_ref[rows, :] = jnp.zeros((tile, width), f32)
            return carry

        lax.fori_loop(0, frames // tile, turn, 0)

    def chunk(i, carry):
        rows = rows_of(i)
        up, down = flat(up_ref), flat(down_ref)
        hidden = dot_nn(n_ref[rows, :], up)
        grad_act = dot_nt(cot_ref[rows, :], down)
        activated, slope = gelu_and_slope(hidden)
        activated = activated.astype(bf16)
        grad_pre = (grad_act * slope).astype(bf16)
        act_turned[:, rows] = activated.T
        pre[rows, :] = grad_pre
        total[rows, :] += dot_nn(activated, down)
        back_ref[rows, :] += dot_nt(grad_pre, up)
        return carry

    lax.fori_loop(0, frames // tile, chunk, 0)

    for begin in range(0, width, FEED_PART):
        grad_up = dot_nn(n_turned[begin : begin + FEED_PART, :], pre[...]).astype(bf16)
        for first in range(begin, begin + FEED_PART, part // 2):
            which, half = first // part, first % part // (part // 2)
            gup_ref[half, which] = grad_up[first - begin : first - begin + part // 2]
    piece = act_turned.shape[0]
    for begin in range(0, piece, FEED_PART):
        rows = slice(begin, begin + FEED_PART)
        gdown_ref[0, 0, rows, :] = dot_nn(act_turned[rows, :], cot_ref[...]).astype(bf16)

    @pl.when(step == last)
    def _():
        out_ref[...] = total[...].astype(bf16)


def feed_forward_and_back(normed, cot, resid, hidden, piece, w_up, w_down, planes):
    frames, width = normed.shape
    once = dict(pipeline_mode=pl.Buffered(1))
    return pl.pallas_call(
        feed_kernel,
        grid=(hidden // piece,),
        in_specs=[
            pl.BlockSpec((frames, width), lambda j: (0, 0), **once),
            pl.BlockSpec((frames, width), lambda j: (0, 0), **once),
            pl.BlockSpec((frames, width), lambda j: (0, 0), **once),
            pl.BlockSpec(*w_up[1:]),
            pl.BlockSpec(*w_down[1:]),
        ],
        out_specs=[
            pl.BlockSpec((frames, width), lambda j: (0, 0)),
            pl.BlockSpec((frames, width), lambda j: (0, 0)),
            pl.BlockSpec((2, planes, width // (2 * planes), piece), lambda j: (0, 0, 0, j)),
            pl.BlockSpec((1, 1, piece, width), lambda j: (j % 2, j // 2, 0, 0)),
        ],
        out_shape=[
            jax.ShapeDtypeStruct((frames, width), bf16),
            jax.ShapeDtypeStruct((frames, width), f32),
            jax.ShapeDtypeStruct((2, planes, width // (2 * planes), hidden), bf16),
            jax.ShapeDtypeStruct((2, planes, piece, width), bf16),
        ],
        scratch_shapes=[
            pltpu.VMEM((frames, width), f32),
            pltpu.VMEM((width, frames), bf16),
            pltpu.VMEM((piece, frames), bf16),
            pltpu.VMEM((frames, piece), bf16),
        ],
        compiler_params=params("arbitrary"),
        cost_estimate=cost(12 * frames * width * hidden, 8 * width * hidden + 16 * frames * width, frames * hidden),
    )(normed, cot, resid, w_up[0], w_down[0])


def body(inputs, skips, cotangent, segment_ids, time_steps, w_skip, w_qkv, w_out, w_up, w_down, w_mod):
    micro, _, piece, width = inputs.shape
    length = segment_ids.shape[-1]
    labels = time_steps.shape[-1]
    planes, lows, highs = lax.axis_size("plane"), lax.axis_size("lo"), lax.axis_size("hi")
    line = highs * lows
    group = 2 * lows
    devices = planes * 2 * line
    core, high, low = lax.axis_index("core"), lax.axis_index("hi"), lax.axis_index("lo")
    place = high * lows + low
    member = core * lows + low
    frames = 2 * piece
    heads_wide = width // group
    first_core = core == 0
    swap = [(0, 1), (1, 0)]

    def route(parity):
        pairs = []
        for c in range(2):
            for z in range(line):
                row = c * micro + ((z % 2) ^ parity)
                to_core, to_low = divmod(z // 2, lows)
                pairs.append((c * line + z, (to_core * highs + row) * lows + to_low))
        return pairs

    there = (route(0), route(1))
    back = tuple([(b, a) for a, b in pairs] for pairs in there)
    odd_place = place % 2
    even_row = high % 2 == 0

    def to_rows(value):
        value = value[:, 0]
        near = lax.ppermute(lax.dynamic_index_in_dim(value, odd_place, 0, False), LINE_AXES, there[0])
        far = lax.ppermute(lax.dynamic_index_in_dim(value, 1 - odd_place, 0, False), LINE_AXES, there[1])
        return jnp.concatenate([jnp.where(even_row, near, far), jnp.where(even_row, far, near)], axis=0)

    def from_rows(value):
        value = value.reshape(2, piece, width)
        near = lax.ppermute(lax.dynamic_index_in_dim(value, high % 2, 0, False), LINE_AXES, back[0])
        far = lax.ppermute(lax.dynamic_index_in_dim(value, 1 - high % 2, 0, False), LINE_AXES, back[1])
        even = odd_place == 0
        return jnp.stack([jnp.where(even, near, far), jnp.where(even, far, near)])[:, None]

    def frames_to_row(value):
        if group > 2:
            return lax.all_gather(value, ROW_AXES, axis=0, tiled=True)
        other = lax.ppermute(value, "core", swap)
        return jnp.concatenate([jnp.where(first_core, value, other), jnp.where(first_core, other, value)], axis=0)

    def heads_to_frames(value):
        if group > 2:
            return lax.all_to_all(value, ROW_AXES, split_axis=0, concat_axis=1, tiled=True)
        other = lax.ppermute(lax.dynamic_slice_in_dim(value, (1 - core) * frames, frames, 0), "core", swap)
        own = lax.dynamic_slice_in_dim(value, core * frames, frames, 0)
        return jnp.concatenate([jnp.where(first_core, own, other), jnp.where(first_core, other, own)], axis=1)

    def frames_to_heads(value):
        if group > 2:
            return lax.all_to_all(value, ROW_AXES, split_axis=1, concat_axis=0, tiled=True)
        other = lax.ppermute(lax.dynamic_slice_in_dim(value, (1 - core) * heads_wide, heads_wide, 1), "core", swap)
        own = lax.dynamic_slice_in_dim(value, core * heads_wide, heads_wide, 1)
        return jnp.concatenate([jnp.where(first_core, own, other), jnp.where(first_core, other, own)], axis=0)

    up_rows, down_rows, out_rows = w_up.shape[0], w_down.shape[0], w_out.shape[0]
    skip_rows = w_skip.shape[0]
    early = jnp.concatenate([w_skip] + [w_qkv[:, i * width : (i + 1) * width] for i in range(3)] + [w_out], axis=0)
    early = lax.all_gather(early, ALL_AXES, axis=0, tiled=True).reshape(devices, -1, width)

    labels_own = segment_ids[:, 0]
    labels_other = lax.ppermute(labels_own, "core", swap)
    labels_pick = jnp.where(core == high // micro, labels_own, labels_other)
    seg = lax.dynamic_index_in_dim(labels_pick, high % micro, 0, False)
    names = jnp.arange(labels, dtype=jnp.int32)
    starts = jnp.sum((seg[:, None] < names[None, :]).astype(jnp.int32), axis=0)
    ends = jnp.sum((seg[:, None] <= names[None, :]).astype(jnp.int32), axis=0)
    offset = jnp.sum(jnp.where(seg[:, None] == names[None, :], starts[None, :], 0), axis=1)
    where_at = jnp.arange(length, dtype=jnp.int32) - offset
    by_block = seg.reshape(-1, BLOCK)
    begin = jnp.sum(jnp.where(by_block[:, :1] == names[None, :], starts[None, :], 0), axis=1)
    finish = jnp.sum(jnp.where(by_block[:, -1:] == names[None, :], ends[None, :], 0), axis=1)
    ranges = jnp.stack([begin // BLOCK, (finish + BLOCK - 1) // BLOCK]).astype(jnp.int32)
    half = HEAD_DIM // 2
    rates = jnp.exp(-math.log(10000.0) * jnp.arange(half, dtype=f32) / half)
    angles = where_at.astype(f32)[:, None] * rates
    cosine = jnp.tile(jnp.cos(angles), (1, 4))
    sine = jnp.sin(angles)
    sine = jnp.concatenate([-sine, sine, -sine, sine], axis=1)
    seg_column, seg_row = seg[:, None], seg[None, :]
    mine = lax.dynamic_slice_in_dim(seg, member * frames, frames, 0)

    steps = lax.all_gather(time_steps[:, 0], ("plane", "core"), axis=0, tiled=True).reshape(-1)
    quarter = w_mod.shape[0] // 2
    pace = jnp.exp(-math.log(10000.0) * jnp.arange(quarter, dtype=f32) / quarter)
    turns = steps.astype(f32)[:, None] * pace
    embedded = jnp.concatenate([jnp.sin(turns), jnp.cos(turns)], axis=1).astype(bf16)
    block_mod = jnp.dot(embedded, w_mod, preferred_element_type=f32)
    own_columns = block_mod.shape[1]
    block_mod = block_mod.reshape(planes, 1, highs, 1, labels, own_columns)
    block_mod = jnp.broadcast_to(block_mod, (planes, 2, highs, lows, labels, own_columns))
    block_mod = lax.all_to_all(
        block_mod.reshape(devices, labels, own_columns), ALL_AXES, split_axis=0, concat_axis=0, tiled=True
    )
    modulation = jnp.moveaxis(block_mod, 0, 1).reshape(labels, 4, width)

    inputs, skips, modulation, seg = lax.optimization_barrier((inputs, skips, modulation, seg))
    x, s = to_rows(inputs), to_rows(skips)
    columns = w_up.shape[1] // width
    late = jnp.concatenate([w_down] + [w_up[:, i * width : (i + 1) * width] for i in range(columns)], axis=0)
    late, cotangent, x, s, modulation, cosine, sine, ranges, mine = lax.optimization_barrier(
        (late, cotangent, x, s, modulation, cosine, sine, ranges, mine)
    )
    late = lax.all_gather(late, ALL_AXES, axis=0, tiled=True).reshape(devices, -1, width)
    cot = to_rows(cotangent)
    in_place = out_rows % 16 == 0
    hidden = w_up.shape[1]
    chunk = hidden // (2 * planes)

    def weight(gathered, begin, rows, first, count):
        block = (count // rows, rows, width)
        if in_place:
            return gathered, block, (first // count, begin // rows, 0)
        taken = gathered[first // rows : (first + count) // rows, begin : begin + rows]
        return taken.reshape(1, count, width), (1, count, width), (0, 0, 0)

    skip_top, skip_bottom = (weight(early, 0, skip_rows, i * width, width) for i in range(2))
    out_weight = weight(early, skip_rows + 3 * out_rows, out_rows, 0, width)
    if in_place:
        per = width // chunk
        up_weight = (late, (devices, up_rows, chunk), lambda j: (0, down_rows // up_rows + j // per, j % per))
        down_weight = (late, (chunk // down_rows, down_rows, width), lambda j: (j, 0, 0))
    else:
        pieces = [late[:, down_rows + i * up_rows : down_rows + (i + 1) * up_rows] for i in range(columns)]
        up_full = jnp.concatenate([v.reshape(width, width) for v in pieces], axis=1)
        up_weight = (up_full[None], (1, width, chunk), lambda j: (0, 0, j))
        down_weight = (late[:, :down_rows].reshape(1, -1, width), (1, chunk, width), lambda j: (0, j, 0))

    def own_qkv(gathered):
        parts = []
        for i in range(3):
            begin = skip_rows + i * out_rows
            whole = gathered[:, begin : begin + out_rows].reshape(width, width)
            parts.append(lax.dynamic_slice_in_dim(whole, member * heads_wide, heads_wide, 1))
        return jnp.concatenate(parts, axis=1)

    mine_column, mine_row = mine[:, None], mine[None, :]
    shift_one, scale_one, shift_two, scale_two = (modulation[:, i] for i in range(4))

    resid_in, normed_one = rowwise(
        skip_norm_kernel,
        frames,
        [("", x), ("", s), ("weight", skip_top), ("weight", skip_bottom), ("", mine_column),
         ("whole", shift_one), ("whole", scale_one)],
        [(width, f32), (width, bf16)],
        flops=4 * frames * width * width,
    )
    normed_row = frames_to_row(normed_one)
    if in_place:
        projected = project(normed_row, early, skip_rows, out_rows, heads_wide, member)
    else:
        projected = jnp.dot(normed_row, own_qkv(early), preferred_element_type=f32).astype(bf16)
    mixed_heads, queries, keys, logsum = attend_forward(ranges, projected, cosine, sine, seg_column, seg_row)
    mixed = heads_to_frames(mixed_heads)
    resid_mid, normed_two = rowwise(
        out_norm_kernel,
        frames,
        [("", mixed), ("weight", out_weight), ("", resid_in), ("", mine_column), ("whole", shift_two), ("whole", scale_two)],
        [(width, f32), (width, bf16)],
        flops=2 * frames * width * width,
    )
    early, normed_two = lax.optimization_barrier((early, normed_two))
    qkv_own = own_qkv(early)
    normed_two, qkv_own = lax.optimization_barrier((normed_two, qkv_own))
    result, grad_normed_two, grad_up, grad_down = feed_forward_and_back(
        normed_two, cot, resid_mid, hidden, chunk, up_weight, down_weight, planes
    )

    def over_cores(kept, axis):
        other = lax.ppermute(lax.dynamic_index_in_dim(kept, 1 - core, axis, False), "core", swap)
        own = lax.dynamic_index_in_dim(kept, core, axis, False)
        return (own.astype(f32) + other.astype(f32)).astype(bf16)

    plane = lax.axis_index("plane")

    def exchange(value, axes, here, count):
        total = lax.dynamic_index_in_dim(value, here, 0, False).astype(f32)
        for flip in range(1, count):
            sent = lax.dynamic_index_in_dim(value, here ^ flip, 0, False)
            total += lax.ppermute(sent, axes, [(i, i ^ flip) for i in range(count)]).astype(f32)
        return total

    def exchange_planes(value):
        return exchange(value, "plane", plane, planes).astype(bf16)

    def exchange_line(value):
        return exchange(value.reshape(line, -1, value.shape[1]), ("hi", "lo"), place, line)

    def scatter(value):
        value = value.reshape(-1, value.shape[-1])
        return lax.psum_scatter(value, ("plane", "hi", "lo"), scatter_dimension=0, tiled=True)

    grad_up, grad_down = over_cores(grad_up, 0), over_cores(grad_down, 0)

    grad_mid, grad_mid_low, grad_frames, grad_shift_two, grad_scale_two = rowwise(
        norm_two_back_kernel,
        frames,
        [("", grad_normed_two), ("", resid_mid), ("", cot), ("", mine_column), ("row", mine_row),
         ("whole", scale_two), ("weight", out_weight)],
        [(width, f32), (width, bf16), (width, bf16)],
        sums=2,
        light=True,
    )
    grad_frames, grad_up = lax.optimization_barrier((grad_frames, grad_up))
    grad_up = scatter(grad_up)
    grad_heads = frames_to_heads(grad_frames)
    grad_out = lax.dot_general(mixed, grad_mid_low, (((0,), (0,)), ((), ())), preferred_element_type=f32)
    grad_out = over_cores(grad_out.astype(bf16).reshape(planes, 2, -1, width), 1)
    grad_down = jnp.concatenate(
        [v.reshape(planes, line, -1, width) for v in (grad_down, grad_out)], axis=2
    )
    grad_heads, grad_down, result = lax.optimization_barrier((grad_heads, grad_down, result))
    block_out = from_rows(result)
    grad_down = exchange_planes(grad_down.reshape(planes, -1, width))
    grad_proj = attend_backward(
        ranges, queries, keys, projected, mixed_heads, grad_heads, logsum, cosine, sine, seg_column, seg_row
    )
    grad_proj, grad_up, grad_down, block_out = lax.optimization_barrier((grad_proj, grad_up, grad_down, block_out))
    grad_down = grad_down.reshape(line, -1, width)
    grad_down = lax.all_to_all(grad_down, ("hi", "lo"), split_axis=0, concat_axis=0, tiled=True)
    if group > 2:
        partial = dot_nt(grad_proj, qkv_own).astype(bf16)
        grad_one = lax.psum_scatter(partial, ROW_AXES, scatter_dimension=0, tiled=True).astype(f32)
        grad_one_other = jnp.zeros((frames, width), bf16)
    else:
        away = lax.dynamic_slice_in_dim(grad_proj, (1 - core) * frames, frames, 0)
        home = lax.dynamic_slice_in_dim(grad_proj, core * frames, frames, 0)
        grad_one_other = lax.ppermute(dot_nt(away, qkv_own).astype(bf16), "core", swap)
        grad_one = dot_nt(home, qkv_own)
    grad_in, grad_shift_one, grad_scale_one = rowwise(
        norm_one_back_kernel,
        frames,
        [("", grad_one), ("", grad_one_other), ("", resid_in), ("", grad_mid), ("", mine_column), ("row", mine_row),
         ("whole", scale_one)],
        [(width, bf16)],
        sums=2,
    )
    grad_in_home = from_rows(grad_in)
    grad_proj, grad_in = lax.optimization_barrier((grad_proj, grad_in))
    grad_qkv = lax.dot_general(normed_row, grad_proj, (((0,), (0,)), ((), ())), preferred_element_type=f32)
    grad_qkv = grad_qkv.astype(bf16)
    if group > 2:
        grad_qkv = grad_qkv.reshape(planes, 2, highs, lows, -1, 3, 1, heads_wide)
        grad_qkv = jnp.moveaxis(grad_qkv, (1, 3), (0, 1)).reshape(group, -1, 3, 1, heads_wide)
        grad_qkv = lax.all_to_all(grad_qkv, ROW_AXES, split_axis=0, concat_axis=3, tiled=True)
        grad_qkv = grad_qkv.reshape(-1, 3 * width)
        grad_qkv = lax.psum_scatter(grad_qkv, ("plane", "hi"), scatter_dimension=0, tiled=True).astype(f32)
    else:
        split = grad_qkv.reshape(planes, 2, -1, 3 * heads_wide)
        other = lax.ppermute(lax.dynamic_index_in_dim(split, 1 - core, 1, False), "core", swap)
        own = lax.dynamic_index_in_dim(split, core, 1, False)
        own, other = (v.reshape(-1, 3 * heads_wide) for v in (own, other))
        left, right = jnp.where(first_core, own, other), jnp.where(first_core, other, own)
        grad_qkv = jnp.concatenate(
            [v[:, i * heads_wide : (i + 1) * heads_wide] for i in range(3) for v in (left, right)], axis=1
        )
        grad_qkv = exchange_planes(grad_qkv.reshape(planes, -1, 3 * width))

    grad_skip_w = jnp.concatenate(
        [
            lax.dot_general(v, grad_in, (((0,), (0,)), ((), ())), preferred_element_type=f32).astype(bf16)
            for v in (x, s)
        ],
        axis=0,
    )
    grad_skip_w = exchange_planes(over_cores(grad_skip_w.reshape(planes, 2, -1, width), 1))
    grad_in_home, grad_qkv = lax.optimization_barrier((grad_in_home, grad_qkv))
    if group == 2:
        grad_qkv = exchange_line(grad_qkv)
    grad_skip_w = exchange_line(grad_skip_w)
    grad_inputs, grad_skips = rowwise(
        unmerge_kernel,
        frames,
        [("", grad_in_home.reshape(frames, width)), ("weight", skip_top), ("weight", skip_bottom)],
        [(width, bf16), (width, bf16)],
        flops=4 * frames * width * width,
    )
    grad_inputs, grad_skips = (v.reshape(grad_in_home.shape) for v in (grad_inputs, grad_skips))

    grad_shift_one, grad_qkv = lax.optimization_barrier((grad_shift_one, grad_qkv))
    grad_mod = jnp.stack([v[:labels] for v in (grad_shift_one, grad_scale_one, grad_shift_two, grad_scale_two)], axis=1)
    grad_mod = jnp.moveaxis(grad_mod.reshape(labels, devices, own_columns), 1, 0)
    grad_mod = lax.all_to_all(grad_mod, ALL_AXES, split_axis=0, concat_axis=0, tiled=True)
    grad_inputs, grad_mod, grad_up, grad_down, grad_skip_w = lax.optimization_barrier(
        (grad_inputs, grad_mod, grad_up, grad_down, grad_skip_w)
    )
    grad_up, grad_down = grad_up.astype(f32), jnp.sum(grad_down.astype(f32), axis=0)
    grad_down, grad_out = grad_down[:down_rows], grad_down[down_rows:]
    grad_mod = jnp.sum(grad_mod.reshape(planes, 2, highs, lows, labels, own_columns), axis=(1, 3))
    grad_mod = lax.dot_general(
        embedded.astype(f32),
        grad_mod.reshape(-1, own_columns),
        (((0,), (0,)), ((), ())),
        precision=lax.Precision.HIGHEST,
        preferred_element_type=f32,
    )
    return (
        block_out,
        grad_inputs,
        grad_skips,
        grad_skip_w,
        grad_qkv,
        grad_out,
        grad_up,
        grad_down,
        grad_mod,
    )


def solution(mesh):
    batch, wide = mesh.devices.shape

    def run(inputs, *rest):
        rows = 2 * inputs.shape[0]
        assert inputs.shape[0] == 2 and inputs.shape[1] == batch and wide % rows == 0
        fine = Mesh(mesh.devices.reshape(batch // 2, 2, rows, wide // rows), ALL_AXES)
        by_batch, by_wide = ("plane", "core"), ("hi", "lo")
        frames = P(None, by_batch, by_wide, None)
        rowed = P(None, by_batch, None)
        weight, columns = P(ALL_AXES, None), P(None, ALL_AXES)
        mapped = jax.shard_map(
            body,
            mesh=fine,
            in_specs=(frames, frames, frames, rowed, rowed) + (weight,) * 5 + (columns,),
            out_specs=(frames, frames, frames) + (weight,) * 5 + (columns,),
            check_vma=False,
        )
        return mapped(inputs, *rest)

    return run
```

```python
import functools
import math

import jax
import jax.numpy as jnp
from jax import lax
from jax.experimental import pallas as pl
from jax.experimental.pallas import tpu as pltpu
from jax.sharding import Mesh
from jax.sharding import PartitionSpec as P

HEAD_DIM = 64
TILE = 128
BLOCK = 256
ROW_TILE = 256
FEED_TILE = 1024
FEED_PART = 512
VMEM_BYTES = 60 * 1024 * 1024
ROW_AXES = ("core", "lo")
LINE_AXES = ("core", "hi", "lo")
ALL_AXES = ("plane", "core", "hi", "lo")
f32 = jnp.float32
bf16 = jnp.bfloat16


def dot_nn(left, right):
    return lax.dot_general(left, right, (((1,), (0,)), ((), ())), preferred_element_type=f32)


def dot_nt(left, right):
    return lax.dot_general(left, right, (((1,), (1,)), ((), ())), preferred_element_type=f32)


def dot_tn(left, right):
    return lax.dot_general(left, right, (((0,), (0,)), ((), ())), preferred_element_type=f32)


def params(*semantics):
    return pltpu.CompilerParams(dimension_semantics=semantics, vmem_limit_bytes=VMEM_BYTES)


def cost(flops, moved, special=0):
    return pl.CostEstimate(flops=int(flops), bytes_accessed=int(moved), transcendentals=int(special))


def flat(ref):
    return ref[...].reshape(-1, ref.shape[-1])


def choose(segment_column, table_ref):
    count = table_ref.shape[0]
    picked = table_ref[count - 1 : count, :]
    for label in range(count - 2, -1, -1):
        picked = jnp.where(segment_column == label, table_ref[label : label + 1, :], picked)
    return picked


def normalise(values):
    centred = values - jnp.mean(values, axis=-1, keepdims=True)
    variance = jnp.mean(centred * centred, axis=-1, keepdims=True)
    inverse = lax.rsqrt(variance + 1e-06)
    return centred * inverse, inverse


def skip_norm_kernel(x_ref, s_ref, top_ref, bottom_ref, seg_ref, shift_ref, scale_ref, resid_ref, normed_ref):
    resid = dot_nn(x_ref[...], flat(top_ref)) + dot_nn(s_ref[...], flat(bottom_ref))
    resid_ref[...] = resid
    unit, _ = normalise(resid)
    label = seg_ref[...]
    normed = unit * (1.0 + choose(label, scale_ref)) + choose(label, shift_ref)
    normed_ref[...] = normed.astype(bf16)


def out_norm_kernel(mixed_ref, w_ref, resid_in_ref, seg_ref, shift_ref, scale_ref, resid_ref, normed_ref):
    resid = resid_in_ref[...] + dot_nn(mixed_ref[...], flat(w_ref))
    resid_ref[...] = resid
    unit, _ = normalise(resid)
    label = seg_ref[...]
    normed = unit * (1.0 + choose(label, scale_ref)) + choose(label, shift_ref)
    normed_ref[...] = normed.astype(bf16)


def segment_sums(row_labels, values, total_ref):
    members = lax.broadcasted_iota(jnp.int32, (total_ref.shape[0], row_labels.shape[1]), 0) == row_labels
    members = members.astype(f32).astype(bf16)
    high = values.astype(bf16)
    low = (values - high.astype(f32)).astype(bf16)
    total_ref[...] += dot_nn(members, high) + dot_nn(members, low)


def norm_pull(grad, resid, scale):
    unit, inverse = normalise(resid)
    inner = grad * (1.0 + scale)
    pulled = inverse * (
        inner
        - jnp.mean(inner, axis=-1, keepdims=True)
        - unit * jnp.mean(inner * unit, axis=-1, keepdims=True)
    )
    return pulled, grad * unit


def norm_two_back_kernel(
    g_ref, resid_ref, cot_ref, seg_ref, segr_ref, scale_ref, w_ref, mid_ref, low_ref, mix_ref, dshift_ref, dscale_ref
):
    @pl.when(pl.program_id(0) == 0)
    def _():
        dshift_ref[...] = jnp.zeros_like(dshift_ref)
        dscale_ref[...] = jnp.zeros_like(dscale_ref)

    grad = g_ref[...]
    pulled, by_scale = norm_pull(grad, resid_ref[...], choose(seg_ref[...], scale_ref))
    grad_mid = cot_ref[...].astype(f32) + pulled
    low = grad_mid.astype(bf16)
    mid_ref[...] = grad_mid
    low_ref[...] = low
    mix_ref[...] = dot_nt(low, flat(w_ref)).astype(bf16)
    segment_sums(segr_ref[...], grad, dshift_ref)
    segment_sums(segr_ref[...], by_scale, dscale_ref)


def norm_one_back_kernel(
    own_ref, other_ref, resid_ref, mid_ref, seg_ref, segr_ref, scale_ref, grad_ref, dshift_ref, dscale_ref
):
    @pl.when(pl.program_id(0) == 0)
    def _():
        dshift_ref[...] = jnp.zeros_like(dshift_ref)
        dscale_ref[...] = jnp.zeros_like(dscale_ref)

    grad = own_ref[...] + other_ref[...].astype(f32)
    pulled, by_scale = norm_pull(grad, resid_ref[...], choose(seg_ref[...], scale_ref))
    grad_ref[...] = (mid_ref[...] + pulled).astype(bf16)
    segment_sums(segr_ref[...], grad, dshift_ref)
    segment_sums(segr_ref[...], by_scale, dscale_ref)


def unmerge_kernel(g_ref, top_ref, bottom_ref, inputs_ref, skips_ref):
    inputs_ref[...] = dot_nt(g_ref[...], flat(top_ref)).astype(bf16)
    skips_ref[...] = dot_nt(g_ref[...], flat(bottom_ref)).astype(bf16)


def project_kernel(place_ref, x_ref, w_ref, out_ref):
    out_ref[...] = dot_nn(x_ref[...], flat(w_ref)).astype(bf16)


def project(value, gathered, begin, rows, heads_wide, member):
    length, width = value.shape
    tile = min(8 * ROW_TILE, length)
    return pl.pallas_call(
        project_kernel,
        grid_spec=pltpu.PrefetchScalarGridSpec(
            num_scalar_prefetch=1,
            grid=(3, length // tile),
            in_specs=[
                pl.BlockSpec((tile, width), lambda t, i, r: (i, 0)),
                pl.BlockSpec((width // rows, rows, heads_wide), lambda t, i, r: (0, begin // rows + t, r[0])),
            ],
            out_specs=pl.BlockSpec((tile, heads_wide), lambda t, i, r: (i, t)),
        ),
        out_shape=jax.ShapeDtypeStruct((length, 3 * heads_wide), bf16),
        compiler_params=params("arbitrary", "arbitrary"),
        cost_estimate=cost(6 * length * width * heads_wide, 8 * length * width),
    )(member.reshape(1), value, gathered)


def rowwise(kernel, frames, blocked, outs, sums=0, flops=0, light=False):
    tile = min(ROW_TILE, frames)
    in_specs, args, moved = [], [], 0
    for kind, value in blocked:
        if kind == "row":
            in_specs.append(pl.BlockSpec((1, tile), lambda i: (0, i)))
        elif kind == "weight":
            value, block, index = value
            in_specs.append(pl.BlockSpec(block, functools.partial(lambda index, i: index, index)))
        elif kind == "whole":
            in_specs.append(pl.BlockSpec(value.shape, lambda i: (0, 0)))
        else:
            in_specs.append(pl.BlockSpec((tile, value.shape[1]), lambda i: (i, 0)))
        args.append(value)
        moved += value.size * value.dtype.itemsize
    out_specs, shapes = [], []
    for width, kind in outs:
        out_specs.append(pl.BlockSpec((tile, width), lambda i: (i, 0)))
        shapes.append(jax.ShapeDtypeStruct((frames, width), kind))
        moved += frames * width * jnp.dtype(kind).itemsize
    for _ in range(sums):
        out_specs.append(pl.BlockSpec((8, outs[0][0]), lambda i: (0, 0)))
        shapes.append(jax.ShapeDtypeStruct((8, outs[0][0]), f32))
    return pl.pallas_call(
        kernel,
        grid=(frames // tile,),
        in_specs=in_specs,
        out_specs=out_specs,
        out_shape=shapes,
        compiler_params=params("arbitrary"),
        cost_estimate=cost(1, 1) if light else cost(flops, moved),
    )(*args)


def swap_halves(values, lanes):
    half = HEAD_DIM // 2
    ahead = pltpu.roll(values, values.shape[1] - half, 1)
    behind = pltpu.roll(values, half, 1)
    return jnp.where(lanes % HEAD_DIM < half, ahead, behind)


def widen(table, width):
    return jnp.concatenate([table] * (width // table.shape[1]), axis=1)


def span(i):
    return pl.ds(pl.multiple_of(i * BLOCK, BLOCK), BLOCK)


def own_lanes(parts, lanes):
    picked = parts[0]
    for h in range(1, len(parts)):
        picked = jnp.where(lanes // HEAD_DIM == h, parts[h], picked)
    return picked


def by_count(count, most, run):
    for each in range(1, most + 1):
        pl.when(count == each)(functools.partial(run, each))


def attend_forward_kernel(
    range_ref, q_ref, k_ref, v_ref, cos_ref, sin_ref, segc_ref, segr_ref,
    out_ref, qrot_ref, krot_ref, lse_ref, seg_wide,
):
    length, width = q_ref.shape
    heads = width // HEAD_DIM
    blocks = length // BLOCK
    lanes = lax.broadcasted_iota(jnp.int32, (BLOCK, width), 1)

    def turn(i, carry):
        rows = span(i)
        cosine, sine = widen(cos_ref[rows, :], width), widen(sin_ref[rows, :], width)
        for source, target, factor in ((q_ref, qrot_ref, HEAD_DIM**-0.5), (k_ref, krot_ref, None)):
            values = source[rows, :].astype(f32)
            turned = (values * cosine + swap_halves(values, lanes) * sine).astype(bf16)
            if factor is not None:
                turned = turned * jnp.asarray(factor, bf16)
            target[rows, :] = turned
        seg_wide[rows, :] = jnp.broadcast_to(segc_ref[rows, :], (BLOCK, TILE))
        return carry

    lax.fori_loop(0, blocks, turn, 0)

    def one_query(i, carry):
        rows = span(i)

        def work(count):
            keys = pl.ds(pl.multiple_of(range_ref[0, i] * BLOCK, BLOCK), count * BLOCK)
            allowed = widen(seg_wide[rows, :], count * BLOCK) == segr_ref[:, keys]
            query = qrot_ref[rows, :]
            zero = jnp.zeros_like(query)
            mixed = []
            for h in range(heads):
                scores = dot_nt(jnp.where(lanes // HEAD_DIM == h, query, zero), krot_ref[keys, :])
                scores = jnp.where(allowed, scores, -1e30)
                highest = jnp.max(scores, axis=1, keepdims=True)
                powers = jnp.exp(scores - highest)
                totals = jnp.sum(powers, axis=1, keepdims=True)
                mixed.append(dot_nn(powers.astype(bf16), v_ref[keys, :]) * (1.0 / totals))
                logsum = jnp.broadcast_to(highest + jnp.log(totals), (BLOCK, TILE))
                lse_ref[0, h : h + 1, rows] = logsum.T[0:1]
            out_ref[rows, :] = own_lanes(mixed, lanes).astype(bf16)

        by_count(range_ref[1, i] - range_ref[0, i], blocks, work)
        return carry

    lax.fori_loop(0, blocks, one_query, 0)


def attend_forward(ranges, projected, cosine, sine, seg_column, seg_row):
    length, width = projected.shape
    width //= 3
    panels, heads = width // TILE, TILE // HEAD_DIM
    panel = lambda shift: pl.BlockSpec((length, TILE), lambda p, r: (0, shift * panels + p))
    whole = lambda shape: pl.BlockSpec(shape, lambda p, r: (0,) * len(shape))
    return pl.pallas_call(
        attend_forward_kernel,
        grid_spec=pltpu.PrefetchScalarGridSpec(
            num_scalar_prefetch=1,
            grid=(panels,),
            in_specs=[panel(0), panel(1), panel(2), whole(cosine.shape), whole(sine.shape),
                      whole(seg_column.shape), whole(seg_row.shape)],
            out_specs=[panel(0), panel(0), panel(0), pl.BlockSpec((1, heads, length), lambda p, r: (p, 0, 0))],
            scratch_shapes=[pltpu.VMEM((length, TILE), jnp.int32)],
        ),
        out_shape=[jax.ShapeDtypeStruct((length, width), bf16)] * 3
        + [jax.ShapeDtypeStruct((panels, heads, length), f32)],
        compiler_params=params("arbitrary"),
        cost_estimate=cost(8 * length * length * width, 14 * length * width, length * length * width // HEAD_DIM),
    )(ranges, projected, projected, projected, cosine, sine, seg_column, seg_row)


def attend_backward_kernel(
    range_ref, q_ref, k_ref, v_ref, out_ref, do_ref, lse_ref, cos_ref, sin_ref, segc_ref, segr_ref,
    grad_ref, dq, dk_low, dv_low, delta, seg_wide,
):
    length, width = q_ref.shape
    heads = width // HEAD_DIM
    blocks = length // BLOCK
    step = pl.program_id(1)

    @pl.when(step == 0)
    def _():
        lanes = lax.broadcasted_iota(jnp.int32, (BLOCK, width), 1)
        picker = (
            lax.broadcasted_iota(jnp.int32, (8, width), 0)
            == lax.broadcasted_iota(jnp.int32, (8, width), 1) // HEAD_DIM
        ).astype(f32)

        def prepare(i, carry):
            rows = span(i)
            product = do_ref[rows, :].astype(f32) * out_ref[rows, :].astype(f32)
            delta[:, rows] = lax.dot_general(
                picker, product, (((1,), (1,)), ((), ())),
                precision=lax.Precision.HIGHEST, preferred_element_type=f32,
            )
            dq[rows, :] = jnp.zeros((BLOCK, width), f32)
            seg_wide[rows, :] = jnp.broadcast_to(segc_ref[rows, :], (BLOCK, TILE))
            return carry

        lax.fori_loop(0, blocks, prepare, 0)

        def unturn(values, rows):
            return values * widen(cos_ref[rows, :], width) - swap_halves(values, lanes) * widen(sin_ref[rows, :], width)

        def one_key(j, carry):
            rows = span(j)

            def work(count):
                there = pl.ds(pl.multiple_of(range_ref[0, j] * BLOCK, BLOCK), count * BLOCK)
                allowed = widen(seg_wide[rows, :], count * BLOCK) == segr_ref[:, there]
                zero = jnp.zeros((BLOCK, width), bf16)
                grad_k, grad_v, grad_q = [], [], None
                for h in range(heads):
                    key = jnp.where(lanes // HEAD_DIM == h, k_ref[rows, :], zero)
                    value = jnp.where(lanes // HEAD_DIM == h, v_ref[rows, :], zero)
                    scores = dot_nt(key, q_ref[there, :]) - lse_ref[0, h : h + 1, there]
                    probability = jnp.exp(jnp.where(allowed, scores, -1e30))
                    grad_prob = dot_nt(value, do_ref[there, :])
                    grad_scores = (probability * (grad_prob - delta[h : h + 1, there])).astype(bf16)
                    grad_v.append(dot_nn(probability.astype(bf16), do_ref[there, :]))
                    grad_k.append(dot_nn(grad_scores, q_ref[there, :]))
                    part = dot_tn(grad_scores, key)
                    grad_q = part if grad_q is None else grad_q + part
                dq[there, :] += grad_q
                dk_low[rows, :] = unturn(own_lanes(grad_k, lanes), rows).astype(bf16)
                dv_low[rows, :] = own_lanes(grad_v, lanes).astype(bf16)

            by_count(range_ref[1, j] - range_ref[0, j], blocks, work)
            return carry

        lax.fori_loop(0, blocks, one_key, 0)

        def finish(i, carry):
            rows = span(i)
            grad_ref[rows, :] = unturn(dq[rows, :] * HEAD_DIM**-0.5, rows).astype(bf16)
            return carry

        lax.fori_loop(0, blocks, finish, 0)

    @pl.when(step == 1)
    def _():
        grad_ref[...] = dk_low[...]

    @pl.when(step == 2)
    def _():
        grad_ref[...] = dv_low[...]


def attend_backward(ranges, queries, keys, projected, mixed, grad_mixed, logsum, cosine, sine, seg_column, seg_row):
    length, width = queries.shape
    panels, heads = width // TILE, TILE // HEAD_DIM
    panel = lambda shift: pl.BlockSpec((length, TILE), lambda p, t, r: (0, shift * panels + p))
    whole = lambda shape: pl.BlockSpec(shape, lambda p, t, r: (0,) * len(shape))
    return pl.pallas_call(
        attend_backward_kernel,
        grid_spec=pltpu.PrefetchScalarGridSpec(
            num_scalar_prefetch=1,
            grid=(panels, 3),
            in_specs=[panel(0), panel(0), panel(2), panel(0), panel(0),
                      pl.BlockSpec((1, heads, length), lambda p, t, r: (p, 0, 0)),
                      whole(cosine.shape), whole(sine.shape), whole(seg_column.shape), whole(seg_row.shape)],
            out_specs=pl.BlockSpec((length, TILE), lambda p, t, r: (0, t * panels + p)),
            scratch_shapes=[
                pltpu.VMEM((length, TILE), f32),
                pltpu.VMEM((length, TILE), bf16),
                pltpu.VMEM((length, TILE), bf16),
                pltpu.VMEM((8, length), f32),
                pltpu.VMEM((length, TILE), jnp.int32),
            ],
        ),
        out_shape=jax.ShapeDtypeStruct((length, 3 * width), bf16),
        compiler_params=params("arbitrary", "arbitrary"),
        cost_estimate=cost(20 * length * length * width, 16 * length * width, length * length * width // HEAD_DIM),
    )(ranges, queries, keys, projected, mixed, grad_mixed, logsum, cosine, sine, seg_column, seg_row)


def gelu_and_slope(x):
    root = math.sqrt(2.0 / math.pi)
    square = x * x
    bend = jnp.tanh(x * (root + root * 0.044715 * square))
    half = 0.5 * x
    half_up = 0.5 + 0.5 * bend
    slope = half_up + half * (1.0 - bend * bend) * (root + 3.0 * root * 0.044715 * square)
    return half + half * bend, slope


def feed_kernel(
    n_ref, cot_ref, resid_ref, up_ref, down_ref, out_ref, back_ref, gup_ref, gdown_ref,
    total, n_turned, act_turned, pre,
):
    step, last = pl.program_id(0), pl.num_programs(0) - 1
    frames, width = n_ref.shape
    tile = min(FEED_TILE, frames)
    planes = gup_ref.shape[1]
    part = width // planes

    def rows_of(i):
        return pl.ds(pl.multiple_of(i * tile, tile), tile)

    @pl.when(step == 0)
    def _():
        def turn(i, carry):
            rows = rows_of(i)
            n_turned[:, rows] = n_ref[rows, :].T
            total[rows, :] = resid_ref[rows, :]
            back_ref[rows, :] = jnp.zeros((tile, width), f32)
            return carry

        lax.fori_loop(0, frames // tile, turn, 0)

    def chunk(i, carry):
        rows = rows_of(i)
        up, down = flat(up_ref), flat(down_ref)
        hidden = dot_nn(n_ref[rows, :], up)
        grad_act = dot_nt(cot_ref[rows, :], down)
        activated, slope = gelu_and_slope(hidden)
        activated = activated.astype(bf16)
        grad_pre = (grad_act * slope).astype(bf16)
        act_turned[:, rows] = activated.T
        pre[rows, :] = grad_pre
        total[rows, :] += dot_nn(activated, down)
        back_ref[rows, :] += dot_nt(grad_pre, up)
        return carry

    lax.fori_loop(0, frames // tile, chunk, 0)

    for begin in range(0, width, FEED_PART):
        grad_up = dot_nn(n_turned[begin : begin + FEED_PART, :], pre[...]).astype(bf16)
        for first in range(begin, begin + FEED_PART, part // 2):
            which, half = first // part, first % part // (part // 2)
            gup_ref[half, which] = grad_up[first - begin : first - begin + part // 2]
    piece = act_turned.shape[0]
    for begin in range(0, piece, FEED_PART):
        rows = slice(begin, begin + FEED_PART)
        gdown_ref[0, 0, rows, :] = dot_nn(act_turned[rows, :], cot_ref[...]).astype(bf16)

    @pl.when(step == last)
    def _():
        out_ref[...] = total[...].astype(bf16)


def feed_forward_and_back(normed, cot, resid, hidden, piece, w_up, w_down, planes):
    frames, width = normed.shape
    once = dict(pipeline_mode=pl.Buffered(1))
    return pl.pallas_call(
        feed_kernel,
        grid=(hidden // piece,),
        in_specs=[
            pl.BlockSpec((frames, width), lambda j: (0, 0), **once),
            pl.BlockSpec((frames, width), lambda j: (0, 0), **once),
            pl.BlockSpec((frames, width), lambda j: (0, 0), **once),
            pl.BlockSpec(*w_up[1:]),
            pl.BlockSpec(*w_down[1:]),
        ],
        out_specs=[
            pl.BlockSpec((frames, width), lambda j: (0, 0)),
            pl.BlockSpec((frames, width), lambda j: (0, 0)),
            pl.BlockSpec((2, planes, width // (2 * planes), piece), lambda j: (0, 0, 0, j)),
            pl.BlockSpec((1, 1, piece, width), lambda j: (j % 2, j // 2, 0, 0)),
        ],
        out_shape=[
            jax.ShapeDtypeStruct((frames, width), bf16),
            jax.ShapeDtypeStruct((frames, width), f32),
            jax.ShapeDtypeStruct((2, planes, width // (2 * planes), hidden), bf16),
            jax.ShapeDtypeStruct((2, planes, piece, width), bf16),
        ],
        scratch_shapes=[
            pltpu.VMEM((frames, width), f32),
            pltpu.VMEM((width, frames), bf16),
            pltpu.VMEM((piece, frames), bf16),
            pltpu.VMEM((frames, piece), bf16),
        ],
        compiler_params=params("arbitrary"),
        cost_estimate=cost(12 * frames * width * hidden, 8 * width * hidden + 16 * frames * width, frames * hidden),
    )(normed, cot, resid, w_up[0], w_down[0])


def body(inputs, skips, cotangent, segment_ids, time_steps, w_skip, w_qkv, w_out, w_up, w_down, w_mod):
    micro, _, piece, width = inputs.shape
    length = segment_ids.shape[-1]
    labels = time_steps.shape[-1]
    planes, lows, highs = lax.axis_size("plane"), lax.axis_size("lo"), lax.axis_size("hi")
    line = highs * lows
    group = 2 * lows
    devices = planes * 2 * line
    core, high, low = lax.axis_index("core"), lax.axis_index("hi"), lax.axis_index("lo")
    place = high * lows + low
    member = core * lows + low
    frames = 2 * piece
    heads_wide = width // group
    first_core = core == 0
    swap = [(0, 1), (1, 0)]

    def route(parity):
        pairs = []
        for c in range(2):
            for z in range(line):
                row = c * micro + ((z % 2) ^ parity)
                to_core, to_low = divmod(z // 2, lows)
                pairs.append((c * line + z, (to_core * highs + row) * lows + to_low))
        return pairs

    there = (route(0), route(1))
    back = tuple([(b, a) for a, b in pairs] for pairs in there)
    odd_place = place % 2
    even_row = high % 2 == 0

    def to_rows(value):
        value = value[:, 0]
        near = lax.ppermute(lax.dynamic_index_in_dim(value, odd_place, 0, False), LINE_AXES, there[0])
        far = lax.ppermute(lax.dynamic_index_in_dim(value, 1 - odd_place, 0, False), LINE_AXES, there[1])
        return jnp.concatenate([jnp.where(even_row, near, far), jnp.where(even_row, far, near)], axis=0)

    def from_rows(value):
        value = value.reshape(2, piece, width)
        near = lax.ppermute(lax.dynamic_index_in_dim(value, high % 2, 0, False), LINE_AXES, back[0])
        far = lax.ppermute(lax.dynamic_index_in_dim(value, 1 - high % 2, 0, False), LINE_AXES, back[1])
        even = odd_place == 0
        return jnp.stack([jnp.where(even, near, far), jnp.where(even, far, near)])[:, None]

    def frames_to_row(value):
        if group > 2:
            return lax.all_gather(value, ROW_AXES, axis=0, tiled=True)
        other = lax.ppermute(value, "core", swap)
        return jnp.concatenate([jnp.where(first_core, value, other), jnp.where(first_core, other, value)], axis=0)

    def heads_to_frames(value):
        if group > 2:
            return lax.all_to_all(value, ROW_AXES, split_axis=0, concat_axis=1, tiled=True)
        other = lax.ppermute(lax.dynamic_slice_in_dim(value, (1 - core) * frames, frames, 0), "core", swap)
        own = lax.dynamic_slice_in_dim(value, core * frames, frames, 0)
        return jnp.concatenate([jnp.where(first_core, own, other), jnp.where(first_core, other, own)], axis=1)

    def frames_to_heads(value):
        if group > 2:
            return lax.all_to_all(value, ROW_AXES, split_axis=1, concat_axis=0, tiled=True)
        other = lax.ppermute(lax.dynamic_slice_in_dim(value, (1 - core) * heads_wide, heads_wide, 1), "core", swap)
        own = lax.dynamic_slice_in_dim(value, core * heads_wide, heads_wide, 1)
        return jnp.concatenate([jnp.where(first_core, own, other), jnp.where(first_core, other, own)], axis=0)

    def share_on_line(value):
        pieces = [value]
        for flip in range(1, line):
            pieces.append(lax.ppermute(value, ("hi", "lo"), [(i, i ^ flip) for i in range(line)]))
        pieces = jnp.stack(pieces)
        return jnp.stack([lax.dynamic_index_in_dim(pieces, place ^ i, 0, False) for i in range(line)])

    def gather_planes(value):
        return lax.all_gather(value, ("plane", "core"), axis=0, tiled=True).reshape(devices, -1, width)

    up_rows, down_rows, out_rows = w_up.shape[0], w_down.shape[0], w_out.shape[0]
    skip_rows = w_skip.shape[0]
    early = jnp.concatenate([w_skip] + [w_qkv[:, i * width : (i + 1) * width] for i in range(3)] + [w_out], axis=0)
    early_line = share_on_line(early)
    early = gather_planes(early_line)
    columns = w_up.shape[1] // width
    late = jnp.concatenate([w_down] + [w_up[:, i * width : (i + 1) * width] for i in range(columns)], axis=0)
    late_line = share_on_line(late)

    labels_own = segment_ids[:, 0]
    labels_other = lax.ppermute(labels_own, "core", swap)
    labels_pick = jnp.where(core == high // micro, labels_own, labels_other)
    seg = lax.dynamic_index_in_dim(labels_pick, high % micro, 0, False)
    names = jnp.arange(labels, dtype=jnp.int32)
    starts = jnp.sum((seg[:, None] < names[None, :]).astype(jnp.int32), axis=0)
    ends = jnp.sum((seg[:, None] <= names[None, :]).astype(jnp.int32), axis=0)
    offset = jnp.sum(jnp.where(seg[:, None] == names[None, :], starts[None, :], 0), axis=1)
    where_at = jnp.arange(length, dtype=jnp.int32) - offset
    by_block = seg.reshape(-1, BLOCK)
    begin = jnp.sum(jnp.where(by_block[:, :1] == names[None, :], starts[None, :], 0), axis=1)
    finish = jnp.sum(jnp.where(by_block[:, -1:] == names[None, :], ends[None, :], 0), axis=1)
    ranges = jnp.stack([begin // BLOCK, (finish + BLOCK - 1) // BLOCK]).astype(jnp.int32)
    half = HEAD_DIM // 2
    rates = jnp.exp(-math.log(10000.0) * jnp.arange(half, dtype=f32) / half)
    angles = where_at.astype(f32)[:, None] * rates
    cosine = jnp.tile(jnp.cos(angles), (1, 4))
    sine = jnp.sin(angles)
    sine = jnp.concatenate([-sine, sine, -sine, sine], axis=1)
    seg_column, seg_row = seg[:, None], seg[None, :]
    mine = lax.dynamic_slice_in_dim(seg, member * frames, frames, 0)

    steps = lax.all_gather(time_steps[:, 0], ("plane", "core"), axis=0, tiled=True).reshape(-1)
    quarter = w_mod.shape[0] // 2
    pace = jnp.exp(-math.log(10000.0) * jnp.arange(quarter, dtype=f32) / quarter)
    turns = steps.astype(f32)[:, None] * pace
    embedded = jnp.concatenate([jnp.sin(turns), jnp.cos(turns)], axis=1).astype(bf16)
    block_mod = jnp.dot(embedded, w_mod, preferred_element_type=f32)
    own_columns = block_mod.shape[1]
    block_mod = block_mod.reshape(planes, 1, highs, 1, labels, own_columns)
    block_mod = jnp.broadcast_to(block_mod, (planes, 2, highs, lows, labels, own_columns))
    late_line, inputs, skips, block_mod, cosine, sine, ranges, mine = lax.optimization_barrier(
        (late_line, inputs, skips, block_mod, cosine, sine, ranges, mine)
    )
    late = gather_planes(late_line)
    x, s = to_rows(inputs), to_rows(skips)
    block_mod = lax.all_to_all(
        block_mod.reshape(devices, labels, own_columns), ALL_AXES, split_axis=0, concat_axis=0, tiled=True
    )
    modulation = jnp.moveaxis(block_mod, 0, 1).reshape(labels, 4, width)

    x, s, cotangent, modulation = lax.optimization_barrier((x, s, cotangent, modulation))
    cot = to_rows(cotangent)
    in_place = out_rows % 16 == 0
    hidden = w_up.shape[1]
    chunk = hidden // (2 * planes)

    def weight(gathered, begin, rows, first, count):
        block = (count // rows, rows, width)
        if in_place:
            return gathered, block, (first // count, begin // rows, 0)
        taken = gathered[first // rows : (first + count) // rows, begin : begin + rows]
        return taken.reshape(1, count, width), (1, count, width), (0, 0, 0)

    skip_top, skip_bottom = (weight(early, 0, skip_rows, i * width, width) for i in range(2))
    out_weight = weight(early, skip_rows + 3 * out_rows, out_rows, 0, width)
    def own_qkv(gathered):
        parts = []
        for i in range(3):
            begin = skip_rows + i * out_rows
            whole = gathered[:, begin : begin + out_rows].reshape(width, width)
            parts.append(lax.dynamic_slice_in_dim(whole, member * heads_wide, heads_wide, 1))
        return jnp.concatenate(parts, axis=1)

    mine_column, mine_row = mine[:, None], mine[None, :]
    shift_one, scale_one, shift_two, scale_two = (modulation[:, i] for i in range(4))

    resid_in, normed_one = rowwise(
        skip_norm_kernel,
        frames,
        [("", x), ("", s), ("weight", skip_top), ("weight", skip_bottom), ("", mine_column),
         ("whole", shift_one), ("whole", scale_one)],
        [(width, f32), (width, bf16)],
        flops=4 * frames * width * width,
    )
    normed_row = frames_to_row(normed_one)
    if in_place:
        projected = project(normed_row, early, skip_rows, out_rows, heads_wide, member)
    else:
        projected = jnp.dot(normed_row, own_qkv(early), preferred_element_type=f32).astype(bf16)
    if in_place:
        per = width // chunk
        up_weight = (late, (devices, up_rows, chunk), lambda j: (0, down_rows // up_rows + j // per, j % per))
        down_weight = (late, (chunk // down_rows, down_rows, width), lambda j: (j, 0, 0))
    else:
        pieces = [late[:, down_rows + i * up_rows : down_rows + (i + 1) * up_rows] for i in range(columns)]
        up_full = jnp.concatenate([v.reshape(width, width) for v in pieces], axis=1)
        up_weight = (up_full[None], (1, width, chunk), lambda j: (0, 0, j))
        down_weight = (late[:, :down_rows].reshape(1, -1, width), (1, chunk, width), lambda j: (0, j, 0))
    mixed_heads, queries, keys, logsum = attend_forward(ranges, projected, cosine, sine, seg_column, seg_row)
    mixed = heads_to_frames(mixed_heads)
    resid_mid, normed_two = rowwise(
        out_norm_kernel,
        frames,
        [("", mixed), ("weight", out_weight), ("", resid_in), ("", mine_column), ("whole", shift_two), ("whole", scale_two)],
        [(width, f32), (width, bf16)],
        flops=2 * frames * width * width,
    )
    early, normed_two = lax.optimization_barrier((early, normed_two))
    qkv_own = own_qkv(early)
    normed_two, qkv_own = lax.optimization_barrier((normed_two, qkv_own))
    result, grad_normed_two, grad_up, grad_down = feed_forward_and_back(
        normed_two, cot, resid_mid, hidden, chunk, up_weight, down_weight, planes
    )

    def over_cores(kept, axis):
        other = lax.ppermute(lax.dynamic_index_in_dim(kept, 1 - core, axis, False), "core", swap)
        own = lax.dynamic_index_in_dim(kept, core, axis, False)
        return (own.astype(f32) + other.astype(f32)).astype(bf16)

    plane = lax.axis_index("plane")

    def exchange(value, axes, here, count):
        total = lax.dynamic_index_in_dim(value, here, 0, False).astype(f32)
        for flip in range(1, count):
            sent = lax.dynamic_index_in_dim(value, here ^ flip, 0, False)
            total += lax.ppermute(sent, axes, [(i, i ^ flip) for i in range(count)]).astype(f32)
        return total

    def exchange_planes(value):
        return exchange(value, "plane", plane, planes).astype(bf16)

    def exchange_line(value):
        return exchange(value.reshape(line, -1, value.shape[1]), ("hi", "lo"), place, line)

    def scatter(value):
        value = value.reshape(-1, value.shape[-1])
        return lax.psum_scatter(value, ("plane", "hi", "lo"), scatter_dimension=0, tiled=True)

    grad_up, grad_down = over_cores(grad_up, 0), over_cores(grad_down, 0)

    grad_mid, grad_mid_low, grad_frames, grad_shift_two, grad_scale_two = rowwise(
        norm_two_back_kernel,
        frames,
        [("", grad_normed_two), ("", resid_mid), ("", cot), ("", mine_column), ("row", mine_row),
         ("whole", scale_two), ("weight", out_weight)],
        [(width, f32), (width, bf16), (width, bf16)],
        sums=2,
        light=True,
    )
    grad_frames, grad_up = lax.optimization_barrier((grad_frames, grad_up))
    grad_up = scatter(grad_up)
    grad_heads = frames_to_heads(grad_frames)
    grad_out = lax.dot_general(mixed, grad_mid_low, (((0,), (0,)), ((), ())), preferred_element_type=f32)
    grad_out = over_cores(grad_out.astype(bf16).reshape(planes, 2, -1, width), 1)
    grad_down = jnp.concatenate(
        [v.reshape(planes, line, -1, width) for v in (grad_down, grad_out)], axis=2
    )
    grad_heads, grad_down, result = lax.optimization_barrier((grad_heads, grad_down, result))
    block_out = from_rows(result)
    grad_down = exchange_planes(grad_down.reshape(planes, -1, width))
    grad_proj = attend_backward(
        ranges, queries, keys, projected, mixed_heads, grad_heads, logsum, cosine, sine, seg_column, seg_row
    )
    grad_proj, grad_up, grad_down, block_out = lax.optimization_barrier((grad_proj, grad_up, grad_down, block_out))
    grad_down = grad_down.reshape(line, -1, width)
    grad_down = lax.all_to_all(grad_down, ("hi", "lo"), split_axis=0, concat_axis=0, tiled=True)
    if group > 2:
        partial = dot_nt(grad_proj, qkv_own).astype(bf16)
        grad_one = lax.psum_scatter(partial, ROW_AXES, scatter_dimension=0, tiled=True).astype(f32)
        grad_one_other = jnp.zeros((frames, width), bf16)
    else:
        away = lax.dynamic_slice_in_dim(grad_proj, (1 - core) * frames, frames, 0)
        home = lax.dynamic_slice_in_dim(grad_proj, core * frames, frames, 0)
        grad_one_other = lax.ppermute(dot_nt(away, qkv_own).astype(bf16), "core", swap)
        grad_one = dot_nt(home, qkv_own)
    grad_in, grad_shift_one, grad_scale_one = rowwise(
        norm_one_back_kernel,
        frames,
        [("", grad_one), ("", grad_one_other), ("", resid_in), ("", grad_mid), ("", mine_column), ("row", mine_row),
         ("whole", scale_one)],
        [(width, bf16)],
        sums=2,
    )
    grad_in_home = from_rows(grad_in)
    grad_proj, grad_in = lax.optimization_barrier((grad_proj, grad_in))
    grad_qkv = lax.dot_general(normed_row, grad_proj, (((0,), (0,)), ((), ())), preferred_element_type=f32)
    grad_qkv = grad_qkv.astype(bf16)
    if group > 2:
        grad_qkv = grad_qkv.reshape(planes, 2, highs, lows, -1, 3, 1, heads_wide)
        grad_qkv = jnp.moveaxis(grad_qkv, (1, 3), (0, 1)).reshape(group, -1, 3, 1, heads_wide)
        grad_qkv = lax.all_to_all(grad_qkv, ROW_AXES, split_axis=0, concat_axis=3, tiled=True)
        grad_qkv = grad_qkv.reshape(-1, 3 * width)
        grad_qkv = lax.psum_scatter(grad_qkv, ("plane", "hi"), scatter_dimension=0, tiled=True).astype(f32)
    else:
        split = grad_qkv.reshape(planes, 2, -1, 3 * heads_wide)
        other = lax.ppermute(lax.dynamic_index_in_dim(split, 1 - core, 1, False), "core", swap)
        own = lax.dynamic_index_in_dim(split, core, 1, False)
        own, other = (v.reshape(-1, 3 * heads_wide) for v in (own, other))
        left, right = jnp.where(first_core, own, other), jnp.where(first_core, other, own)
        grad_qkv = jnp.concatenate(
            [v[:, i * heads_wide : (i + 1) * heads_wide] for i in range(3) for v in (left, right)], axis=1
        )
        grad_qkv = exchange_planes(grad_qkv.reshape(planes, -1, 3 * width))

    grad_skip_w = jnp.concatenate(
        [
            lax.dot_general(v, grad_in, (((0,), (0,)), ((), ())), preferred_element_type=f32).astype(bf16)
            for v in (x, s)
        ],
        axis=0,
    )
    grad_skip_w = exchange_planes(over_cores(grad_skip_w.reshape(planes, 2, -1, width), 1))
    grad_in_home, grad_qkv = lax.optimization_barrier((grad_in_home, grad_qkv))
    if group == 2:
        grad_qkv = exchange_line(grad_qkv)
    grad_skip_w = exchange_line(grad_skip_w)
    grad_inputs, grad_skips = rowwise(
        unmerge_kernel,
        frames,
        [("", grad_in_home.reshape(frames, width)), ("weight", skip_top), ("weight", skip_bottom)],
        [(width, bf16), (width, bf16)],
        flops=4 * frames * width * width,
    )
    grad_inputs, grad_skips = (v.reshape(grad_in_home.shape) for v in (grad_inputs, grad_skips))

    grad_shift_one, grad_qkv = lax.optimization_barrier((grad_shift_one, grad_qkv))
    grad_mod = jnp.stack([v[:labels] for v in (grad_shift_one, grad_scale_one, grad_shift_two, grad_scale_two)], axis=1)
    grad_mod = jnp.moveaxis(grad_mod.reshape(labels, devices, own_columns), 1, 0)
    grad_mod = lax.all_to_all(grad_mod, ALL_AXES, split_axis=0, concat_axis=0, tiled=True)
    grad_inputs, grad_mod, grad_up, grad_down, grad_skip_w = lax.optimization_barrier(
        (grad_inputs, grad_mod, grad_up, grad_down, grad_skip_w)
    )
    grad_up, grad_down = grad_up.astype(f32), jnp.sum(grad_down.astype(f32), axis=0)
    grad_down, grad_out = grad_down[:down_rows], grad_down[down_rows:]
    grad_mod = jnp.sum(grad_mod.reshape(planes, 2, highs, lows, labels, own_columns), axis=(1, 3))
    grad_mod = lax.dot_general(
        embedded.astype(f32),
        grad_mod.reshape(-1, own_columns),
        (((0,), (0,)), ((), ())),
        precision=lax.Precision.HIGHEST,
        preferred_element_type=f32,
    )
    return (
        block_out,
        grad_inputs,
        grad_skips,
        grad_skip_w,
        grad_qkv,
        grad_out,
        grad_up,
        grad_down,
        grad_mod,
    )


def solution(mesh):
    batch, wide = mesh.devices.shape

    def run(inputs, *rest):
        rows = 2 * inputs.shape[0]
        assert inputs.shape[0] == 2 and inputs.shape[1] == batch and wide % rows == 0
        fine = Mesh(mesh.devices.reshape(batch // 2, 2, rows, wide // rows), ALL_AXES)
        by_batch, by_wide = ("plane", "core"), ("hi", "lo")
        frames = P(None, by_batch, by_wide, None)
        rowed = P(None, by_batch, None)
        weight, columns = P(ALL_AXES, None), P(None, ALL_AXES)
        mapped = jax.shard_map(
            body,
            mesh=fine,
            in_specs=(frames, frames, frames, rowed, rowed) + (weight,) * 5 + (columns,),
            out_specs=(frames, frames, frames) + (weight,) * 5 + (columns,),
            check_vma=False,
        )
        return mapped(inputs, *rest)

    return run
```

```python
import functools
import math

import jax
import jax.numpy as jnp
from jax import lax
from jax.experimental import pallas as pl
from jax.experimental.pallas import tpu as pltpu
from jax.sharding import Mesh
from jax.sharding import PartitionSpec as P

HEAD_DIM = 64
TILE = 128
BLOCK = 256
ROW_TILE = 256
FEED_TILE = 1024
FEED_PART = 512
VMEM_BYTES = 60 * 1024 * 1024
ROW_AXES = ("core", "lo")
LINE_AXES = ("core", "hi", "lo")
ALL_AXES = ("plane", "core", "hi", "lo")
f32 = jnp.float32
bf16 = jnp.bfloat16


def dot_nn(left, right):
    return lax.dot_general(left, right, (((1,), (0,)), ((), ())), preferred_element_type=f32)


def dot_nt(left, right):
    return lax.dot_general(left, right, (((1,), (1,)), ((), ())), preferred_element_type=f32)


def dot_tn(left, right):
    return lax.dot_general(left, right, (((0,), (0,)), ((), ())), preferred_element_type=f32)


def params(*semantics):
    return pltpu.CompilerParams(dimension_semantics=semantics, vmem_limit_bytes=VMEM_BYTES)


def cost(flops, moved, special=0):
    return pl.CostEstimate(flops=int(flops), bytes_accessed=int(moved), transcendentals=int(special))


def flat(ref):
    return ref[...].reshape(-1, ref.shape[-1])


def choose(segment_column, table_ref):
    count = table_ref.shape[0]
    picked = table_ref[count - 1 : count, :]
    for label in range(count - 2, -1, -1):
        picked = jnp.where(segment_column == label, table_ref[label : label + 1, :], picked)
    return picked


def normalise(values):
    centred = values - jnp.mean(values, axis=-1, keepdims=True)
    variance = jnp.mean(centred * centred, axis=-1, keepdims=True)
    inverse = lax.rsqrt(variance + 1e-06)
    return centred * inverse, inverse


def skip_norm_kernel(x_ref, s_ref, top_ref, bottom_ref, seg_ref, shift_ref, scale_ref, resid_ref, normed_ref):
    resid = dot_nn(x_ref[...], flat(top_ref)) + dot_nn(s_ref[...], flat(bottom_ref))
    resid_ref[...] = resid
    unit, _ = normalise(resid)
    label = seg_ref[...]
    normed = unit * (1.0 + choose(label, scale_ref)) + choose(label, shift_ref)
    normed_ref[...] = normed.astype(bf16)


def out_norm_kernel(mixed_ref, w_ref, resid_in_ref, seg_ref, shift_ref, scale_ref, resid_ref, normed_ref):
    resid = resid_in_ref[...] + dot_nn(mixed_ref[...], flat(w_ref))
    resid_ref[...] = resid
    unit, _ = normalise(resid)
    label = seg_ref[...]
    normed = unit * (1.0 + choose(label, scale_ref)) + choose(label, shift_ref)
    normed_ref[...] = normed.astype(bf16)


def segment_sums(row_labels, values, total_ref):
    members = lax.broadcasted_iota(jnp.int32, (total_ref.shape[0], row_labels.shape[1]), 0) == row_labels
    members = members.astype(f32).astype(bf16)
    high = values.astype(bf16)
    low = (values - high.astype(f32)).astype(bf16)
    total_ref[...] += dot_nn(members, high) + dot_nn(members, low)


def norm_pull(grad, resid, scale):
    unit, inverse = normalise(resid)
    inner = grad * (1.0 + scale)
    pulled = inverse * (
        inner
        - jnp.mean(inner, axis=-1, keepdims=True)
        - unit * jnp.mean(inner * unit, axis=-1, keepdims=True)
    )
    return pulled, grad * unit


def norm_two_back_kernel(
    g_ref, resid_ref, cot_ref, seg_ref, segr_ref, scale_ref, w_ref, mid_ref, low_ref, mix_ref, dshift_ref, dscale_ref
):
    @pl.when(pl.program_id(0) == 0)
    def _():
        dshift_ref[...] = jnp.zeros_like(dshift_ref)
        dscale_ref[...] = jnp.zeros_like(dscale_ref)

    grad = g_ref[...]
    pulled, by_scale = norm_pull(grad, resid_ref[...], choose(seg_ref[...], scale_ref))
    grad_mid = cot_ref[...].astype(f32) + pulled
    low = grad_mid.astype(bf16)
    mid_ref[...] = grad_mid
    low_ref[...] = low
    mix_ref[...] = dot_nt(low, flat(w_ref)).astype(bf16)
    segment_sums(segr_ref[...], grad, dshift_ref)
    segment_sums(segr_ref[...], by_scale, dscale_ref)


def norm_one_back_kernel(
    own_ref, other_ref, resid_ref, mid_ref, seg_ref, segr_ref, scale_ref, grad_ref, dshift_ref, dscale_ref
):
    @pl.when(pl.program_id(0) == 0)
    def _():
        dshift_ref[...] = jnp.zeros_like(dshift_ref)
        dscale_ref[...] = jnp.zeros_like(dscale_ref)

    grad = own_ref[...] + other_ref[...].astype(f32)
    pulled, by_scale = norm_pull(grad, resid_ref[...], choose(seg_ref[...], scale_ref))
    grad_ref[...] = (mid_ref[...] + pulled).astype(bf16)
    segment_sums(segr_ref[...], grad, dshift_ref)
    segment_sums(segr_ref[...], by_scale, dscale_ref)


def unmerge_kernel(g_ref, top_ref, bottom_ref, inputs_ref, skips_ref):
    inputs_ref[...] = dot_nt(g_ref[...], flat(top_ref)).astype(bf16)
    skips_ref[...] = dot_nt(g_ref[...], flat(bottom_ref)).astype(bf16)


def project_kernel(place_ref, x_ref, w_ref, out_ref):
    out_ref[...] = dot_nn(x_ref[...], flat(w_ref)).astype(bf16)


def project(value, gathered, begin, rows, heads_wide, member):
    length, width = value.shape
    tile = min(8 * ROW_TILE, length)
    return pl.pallas_call(
        project_kernel,
        grid_spec=pltpu.PrefetchScalarGridSpec(
            num_scalar_prefetch=1,
            grid=(3, length // tile),
            in_specs=[
                pl.BlockSpec((tile, width), lambda t, i, r: (i, 0)),
                pl.BlockSpec((width // rows, rows, heads_wide), lambda t, i, r: (0, begin // rows + t, r[0])),
            ],
            out_specs=pl.BlockSpec((tile, heads_wide), lambda t, i, r: (i, t)),
        ),
        out_shape=jax.ShapeDtypeStruct((length, 3 * heads_wide), bf16),
        compiler_params=params("arbitrary", "arbitrary"),
        cost_estimate=cost(1, 1),
    )(member.reshape(1), value, gathered)


def rowwise(kernel, frames, blocked, outs, sums=0, flops=0, light=False):
    tile = min(ROW_TILE, frames)
    in_specs, args, moved = [], [], 0
    for kind, value in blocked:
        if kind == "row":
            in_specs.append(pl.BlockSpec((1, tile), lambda i: (0, i)))
        elif kind == "weight":
            value, block, index = value
            in_specs.append(pl.BlockSpec(block, functools.partial(lambda index, i: index, index)))
        elif kind == "whole":
            in_specs.append(pl.BlockSpec(value.shape, lambda i: (0, 0)))
        else:
            in_specs.append(pl.BlockSpec((tile, value.shape[1]), lambda i: (i, 0)))
        args.append(value)
        moved += value.size * value.dtype.itemsize
    out_specs, shapes = [], []
    for width, kind in outs:
        out_specs.append(pl.BlockSpec((tile, width), lambda i: (i, 0)))
        shapes.append(jax.ShapeDtypeStruct((frames, width), kind))
        moved += frames * width * jnp.dtype(kind).itemsize
    for _ in range(sums):
        out_specs.append(pl.BlockSpec((8, outs[0][0]), lambda i: (0, 0)))
        shapes.append(jax.ShapeDtypeStruct((8, outs[0][0]), f32))
    return pl.pallas_call(
        kernel,
        grid=(frames // tile,),
        in_specs=in_specs,
        out_specs=out_specs,
        out_shape=shapes,
        compiler_params=params("arbitrary"),
        cost_estimate=cost(1, 1) if light else cost(flops, moved),
    )(*args)


def swap_halves(values, lanes):
    half = HEAD_DIM // 2
    ahead = pltpu.roll(values, values.shape[1] - half, 1)
    behind = pltpu.roll(values, half, 1)
    return jnp.where(lanes % HEAD_DIM < half, ahead, behind)


def widen(table, width):
    return jnp.concatenate([table] * (width // table.shape[1]), axis=1)


def span(i):
    return pl.ds(pl.multiple_of(i * BLOCK, BLOCK), BLOCK)


def own_lanes(parts, lanes):
    picked = parts[0]
    for h in range(1, len(parts)):
        picked = jnp.where(lanes // HEAD_DIM == h, parts[h], picked)
    return picked


def by_count(count, most, run):
    for each in range(1, most + 1):
        pl.when(count == each)(functools.partial(run, each))


def attend_forward_kernel(
    range_ref, q_ref, k_ref, v_ref, cos_ref, sin_ref, segc_ref, segr_ref,
    out_ref, qrot_ref, krot_ref, lse_ref, seg_wide,
):
    length, width = q_ref.shape
    heads = width // HEAD_DIM
    blocks = length // BLOCK
    lanes = lax.broadcasted_iota(jnp.int32, (BLOCK, width), 1)

    def turn(i, carry):
        rows = span(i)
        cosine, sine = widen(cos_ref[rows, :], width), widen(sin_ref[rows, :], width)
        for source, target, factor in ((q_ref, qrot_ref, HEAD_DIM**-0.5), (k_ref, krot_ref, None)):
            values = source[rows, :].astype(f32)
            turned = (values * cosine + swap_halves(values, lanes) * sine).astype(bf16)
            if factor is not None:
                turned = turned * jnp.asarray(factor, bf16)
            target[rows, :] = turned
        seg_wide[rows, :] = jnp.broadcast_to(segc_ref[rows, :], (BLOCK, TILE))
        return carry

    lax.fori_loop(0, blocks, turn, 0)

    def one_query(i, carry):
        rows = span(i)

        def work(count):
            keys = pl.ds(pl.multiple_of(range_ref[0, i] * BLOCK, BLOCK), count * BLOCK)
            allowed = widen(seg_wide[rows, :], count * BLOCK) == segr_ref[:, keys]
            query = qrot_ref[rows, :]
            zero = jnp.zeros_like(query)
            mixed = []
            for h in range(heads):
                scores = dot_nt(jnp.where(lanes // HEAD_DIM == h, query, zero), krot_ref[keys, :])
                scores = jnp.where(allowed, scores, -1e30)
                highest = jnp.max(scores, axis=1, keepdims=True)
                powers = jnp.exp(scores - highest)
                totals = jnp.sum(powers, axis=1, keepdims=True)
                mixed.append(dot_nn(powers.astype(bf16), v_ref[keys, :]) * (1.0 / totals))
                logsum = jnp.broadcast_to(highest + jnp.log(totals), (BLOCK, TILE))
                lse_ref[0, h : h + 1, rows] = logsum.T[0:1]
            out_ref[rows, :] = own_lanes(mixed, lanes).astype(bf16)

        by_count(range_ref[1, i] - range_ref[0, i], blocks, work)
        return carry

    lax.fori_loop(0, blocks, one_query, 0)


def attend_forward(ranges, projected, cosine, sine, seg_column, seg_row):
    length, width = projected.shape
    width //= 3
    panels, heads = width // TILE, TILE // HEAD_DIM
    panel = lambda shift: pl.BlockSpec((length, TILE), lambda p, r: (0, shift * panels + p))
    whole = lambda shape: pl.BlockSpec(shape, lambda p, r: (0,) * len(shape))
    return pl.pallas_call(
        attend_forward_kernel,
        grid_spec=pltpu.PrefetchScalarGridSpec(
            num_scalar_prefetch=1,
            grid=(panels,),
            in_specs=[panel(0), panel(1), panel(2), whole(cosine.shape), whole(sine.shape),
                      whole(seg_column.shape), whole(seg_row.shape)],
            out_specs=[panel(0), panel(0), panel(0), pl.BlockSpec((1, heads, length), lambda p, r: (p, 0, 0))],
            scratch_shapes=[pltpu.VMEM((length, TILE), jnp.int32)],
        ),
        out_shape=[jax.ShapeDtypeStruct((length, width), bf16)] * 3
        + [jax.ShapeDtypeStruct((panels, heads, length), f32)],
        compiler_params=params("arbitrary"),
        cost_estimate=cost(8 * length * length * width, 14 * length * width, length * length * width // HEAD_DIM),
    )(ranges, projected, projected, projected, cosine, sine, seg_column, seg_row)


def attend_backward_kernel(
    range_ref, q_ref, k_ref, v_ref, out_ref, do_ref, lse_ref, cos_ref, sin_ref, segc_ref, segr_ref,
    grad_ref, dq, dk_low, dv_low, delta, seg_wide,
):
    length, width = q_ref.shape
    heads = width // HEAD_DIM
    blocks = length // BLOCK
    step = pl.program_id(1)

    @pl.when(step == 0)
    def _():
        lanes = lax.broadcasted_iota(jnp.int32, (BLOCK, width), 1)
        picker = (
            lax.broadcasted_iota(jnp.int32, (8, width), 0)
            == lax.broadcasted_iota(jnp.int32, (8, width), 1) // HEAD_DIM
        ).astype(f32)

        def prepare(i, carry):
            rows = span(i)
            product = do_ref[rows, :].astype(f32) * out_ref[rows, :].astype(f32)
            delta[:, rows] = lax.dot_general(
                picker, product, (((1,), (1,)), ((), ())),
                precision=lax.Precision.HIGHEST, preferred_element_type=f32,
            )
            dq[:, rows] = jnp.zeros((width, BLOCK), f32)
            seg_wide[rows, :] = jnp.broadcast_to(segc_ref[rows, :], (BLOCK, TILE))
            return carry

        lax.fori_loop(0, blocks, prepare, 0)

        def unturn(values, rows):
            return values * widen(cos_ref[rows, :], width) - swap_halves(values, lanes) * widen(sin_ref[rows, :], width)

        def one_key(j, carry):
            rows = span(j)

            def work(count):
                there = pl.ds(pl.multiple_of(range_ref[0, j] * BLOCK, BLOCK), count * BLOCK)
                allowed = widen(seg_wide[rows, :], count * BLOCK) == segr_ref[:, there]
                zero = jnp.zeros((BLOCK, width), bf16)
                key, value = (
                    jnp.concatenate([jnp.where(lanes // HEAD_DIM == h, ref[rows, :], zero) for h in range(heads)], axis=0)
                    for ref in (k_ref, v_ref)
                )
                query, grad_out = q_ref[there, :], do_ref[there, :]
                found, grad_prob = dot_nt(key, query), dot_nt(value, grad_out)
                parts, lows = [], []
                for h in range(heads):
                    half = slice(h * BLOCK, (h + 1) * BLOCK)
                    scores = found[half] - lse_ref[0, h : h + 1, there]
                    part = jnp.exp(jnp.where(allowed, scores, -1e30))
                    parts.append(part.astype(bf16))
                    lows.append((part * (grad_prob[half] - delta[h : h + 1, there])).astype(bf16))
                grad_scores = jnp.concatenate(lows, axis=0)
                grad_v = dot_nn(jnp.concatenate(parts, axis=0), grad_out)
                grad_k = dot_nn(grad_scores, query)
                grad_v, grad_k = ([v[h * BLOCK : (h + 1) * BLOCK] for h in range(heads)] for v in (grad_v, grad_k))
                dq[:, there] += dot_tn(key, grad_scores)
                dk_low[rows, :] = unturn(own_lanes(grad_k, lanes), rows).astype(bf16)
                dv_low[rows, :] = own_lanes(grad_v, lanes).astype(bf16)

            by_count(range_ref[1, j] - range_ref[0, j], blocks, work)
            return carry

        lax.fori_loop(0, blocks, one_key, 0)

        def finish(i, carry):
            rows = span(i)
            grad_ref[rows, :] = unturn(dq[:, rows].T * HEAD_DIM**-0.5, rows).astype(bf16)
            return carry

        lax.fori_loop(0, blocks, finish, 0)

    @pl.when(step == 1)
    def _():
        grad_ref[...] = dk_low[...]

    @pl.when(step == 2)
    def _():
        grad_ref[...] = dv_low[...]


def attend_backward(ranges, queries, keys, projected, mixed, grad_mixed, logsum, cosine, sine, seg_column, seg_row):
    length, width = queries.shape
    panels, heads = width // TILE, TILE // HEAD_DIM
    panel = lambda shift: pl.BlockSpec((length, TILE), lambda p, t, r: (0, shift * panels + p))
    whole = lambda shape: pl.BlockSpec(shape, lambda p, t, r: (0,) * len(shape))
    return pl.pallas_call(
        attend_backward_kernel,
        grid_spec=pltpu.PrefetchScalarGridSpec(
            num_scalar_prefetch=1,
            grid=(panels, 3),
            in_specs=[panel(0), panel(0), panel(2), panel(0), panel(0),
                      pl.BlockSpec((1, heads, length), lambda p, t, r: (p, 0, 0)),
                      whole(cosine.shape), whole(sine.shape), whole(seg_column.shape), whole(seg_row.shape)],
            out_specs=pl.BlockSpec((length, TILE), lambda p, t, r: (0, t * panels + p)),
            scratch_shapes=[
                pltpu.VMEM((TILE, length), f32),
                pltpu.VMEM((length, TILE), bf16),
                pltpu.VMEM((length, TILE), bf16),
                pltpu.VMEM((8, length), f32),
                pltpu.VMEM((length, TILE), jnp.int32),
            ],
        ),
        out_shape=jax.ShapeDtypeStruct((length, 3 * width), bf16),
        compiler_params=params("arbitrary", "arbitrary"),
        cost_estimate=cost(20 * length * length * width, 16 * length * width, length * length * width // HEAD_DIM),
    )(ranges, queries, keys, projected, mixed, grad_mixed, logsum, cosine, sine, seg_column, seg_row)


def gelu_and_slope(x):
    root = math.sqrt(2.0 / math.pi)
    square = x * x
    bend = jnp.tanh(x * (root + root * 0.044715 * square))
    half = 0.5 * x
    half_up = 0.5 + 0.5 * bend
    slope = half_up + half * (1.0 - bend * bend) * (root + 3.0 * root * 0.044715 * square)
    return half + half * bend, slope


def feed_kernel(
    core_ref, n_ref, cot_ref, resid_ref, up_ref, down_ref, out_ref, back_ref,
    gup_own_ref, gup_other_ref, gdown_own_ref, gdown_other_ref, total, n_turned, act_turned, pre,
):
    step, last = pl.program_id(0), pl.num_programs(0) - 1
    core = core_ref[0]
    frames, width = n_ref.shape
    tile = min(FEED_TILE, frames)
    planes = gup_own_ref.shape[0]
    part = width // planes

    def rows_of(i):
        return pl.ds(pl.multiple_of(i * tile, tile), tile)

    @pl.when(step == 0)
    def _():
        def turn(i, carry):
            rows = rows_of(i)
            n_turned[:, rows] = n_ref[rows, :].T
            total[rows, :] = resid_ref[rows, :]
            back_ref[rows, :] = jnp.zeros((tile, width), f32)
            return carry

        lax.fori_loop(0, frames // tile, turn, 0)

    def chunk(i, carry):
        rows = rows_of(i)
        up, down = flat(up_ref), flat(down_ref)
        hidden = dot_nn(n_ref[rows, :], up)
        grad_act = dot_nt(cot_ref[rows, :], down)
        activated, slope = gelu_and_slope(hidden)
        activated = activated.astype(bf16)
        grad_pre = (grad_act * slope).astype(bf16)
        act_turned[:, rows] = activated.T
        pre[rows, :] = grad_pre
        total[rows, :] += dot_nn(activated, down)
        back_ref[rows, :] += dot_nt(grad_pre, up)
        return carry

    lax.fori_loop(0, frames // tile, chunk, 0)

    for begin in range(0, width, FEED_PART):
        grad_up = dot_nn(n_turned[begin : begin + FEED_PART, :], pre[...]).astype(bf16)
        for first in range(begin, begin + FEED_PART, part // 2):
            which, half = first // part, first % part // (part // 2)
            kept = grad_up[first - begin : first - begin + part // 2]
            pl.when(core == half)(functools.partial(gup_own_ref.__setitem__, which, kept))
            pl.when(core != half)(functools.partial(gup_other_ref.__setitem__, which, kept))
    piece = act_turned.shape[0]
    for begin in range(0, piece, FEED_PART):
        rows = slice(begin, begin + FEED_PART)
        kept = dot_nn(act_turned[rows, :], cot_ref[...]).astype(bf16)
        pl.when(core == step % 2)(functools.partial(gdown_own_ref.__setitem__, (0, rows), kept))
        pl.when(core != step % 2)(functools.partial(gdown_other_ref.__setitem__, (0, rows), kept))

    @pl.when(step == last)
    def _():
        out_ref[...] = total[...].astype(bf16)


def feed_forward_and_back(core, normed, cot, resid, hidden, piece, w_up, w_down, planes):
    frames, width = normed.shape
    whole = lambda: pl.BlockSpec((frames, width), lambda j, r: (0, 0), pipeline_mode=pl.Buffered(1))
    weight = lambda w: pl.BlockSpec(w[1], lambda j, r: w[2](j))
    up_block = pl.BlockSpec((planes, width // (2 * planes), piece), lambda j, r: (0, 0, j))
    down_block = pl.BlockSpec((1, piece, width), lambda j, r: (j // 2, 0, 0))
    return pl.pallas_call(
        feed_kernel,
        grid_spec=pltpu.PrefetchScalarGridSpec(
            num_scalar_prefetch=1,
            grid=(hidden // piece,),
            in_specs=[whole(), whole(), whole(), weight(w_up), weight(w_down)],
            out_specs=[pl.BlockSpec((frames, width), lambda j, r: (0, 0))] * 2 + [up_block] * 2 + [down_block] * 2,
            scratch_shapes=[
                pltpu.VMEM((frames, width), f32),
                pltpu.VMEM((width, frames), bf16),
                pltpu.VMEM((piece, frames), bf16),
                pltpu.VMEM((frames, piece), bf16),
            ],
        ),
        out_shape=[jax.ShapeDtypeStruct((frames, width), bf16), jax.ShapeDtypeStruct((frames, width), f32)]
        + [jax.ShapeDtypeStruct((planes, width // (2 * planes), hidden), bf16)] * 2
        + [jax.ShapeDtypeStruct((planes, piece, width), bf16)] * 2,
        compiler_params=params("arbitrary"),
        cost_estimate=cost(12 * frames * width * hidden, 8 * width * hidden + 16 * frames * width, frames * hidden),
    )(core.reshape(1), normed, cot, resid, w_up[0], w_down[0])


def body(inputs, skips, cotangent, segment_ids, time_steps, w_skip, w_qkv, w_out, w_up, w_down, w_mod):
    micro, _, piece, width = inputs.shape
    length = segment_ids.shape[-1]
    labels = time_steps.shape[-1]
    planes, lows, highs = lax.axis_size("plane"), lax.axis_size("lo"), lax.axis_size("hi")
    line = highs * lows
    group = 2 * lows
    devices = planes * 2 * line
    core, high, low = lax.axis_index("core"), lax.axis_index("hi"), lax.axis_index("lo")
    place = high * lows + low
    member = core * lows + low
    frames = 2 * piece
    heads_wide = width // group
    first_core = core == 0
    swap = [(0, 1), (1, 0)]

    def route(parity):
        pairs = []
        for c in range(2):
            for z in range(line):
                row = c * micro + ((z % 2) ^ parity)
                to_core, to_low = divmod(z // 2, lows)
                pairs.append((c * line + z, (to_core * highs + row) * lows + to_low))
        return pairs

    there = (route(0), route(1))
    back = tuple([(b, a) for a, b in pairs] for pairs in there)
    odd_place = place % 2
    even_row = high % 2 == 0

    def to_rows(value):
        value = value[:, 0]
        near = lax.ppermute(lax.dynamic_index_in_dim(value, odd_place, 0, False), LINE_AXES, there[0])
        far = lax.ppermute(lax.dynamic_index_in_dim(value, 1 - odd_place, 0, False), LINE_AXES, there[1])
        return jnp.concatenate([jnp.where(even_row, near, far), jnp.where(even_row, far, near)], axis=0)

    def from_rows(value):
        value = value.reshape(2, piece, width)
        near = lax.ppermute(lax.dynamic_index_in_dim(value, high % 2, 0, False), LINE_AXES, back[0])
        far = lax.ppermute(lax.dynamic_index_in_dim(value, 1 - high % 2, 0, False), LINE_AXES, back[1])
        even = odd_place == 0
        return jnp.stack([jnp.where(even, near, far), jnp.where(even, far, near)])[:, None]

    def frames_to_row(value):
        if group > 2:
            return lax.all_gather(value, ROW_AXES, axis=0, tiled=True)
        other = lax.ppermute(value, "core", swap)
        return jnp.concatenate([jnp.where(first_core, value, other), jnp.where(first_core, other, value)], axis=0)

    def heads_to_frames(value):
        if group > 2:
            return lax.all_to_all(value, ROW_AXES, split_axis=0, concat_axis=1, tiled=True)
        other = lax.ppermute(lax.dynamic_slice_in_dim(value, (1 - core) * frames, frames, 0), "core", swap)
        own = lax.dynamic_slice_in_dim(value, core * frames, frames, 0)
        return jnp.concatenate([jnp.where(first_core, own, other), jnp.where(first_core, other, own)], axis=1)

    def frames_to_heads(value):
        if group > 2:
            return lax.all_to_all(value, ROW_AXES, split_axis=1, concat_axis=0, tiled=True)
        other = lax.ppermute(lax.dynamic_slice_in_dim(value, (1 - core) * heads_wide, heads_wide, 1), "core", swap)
        own = lax.dynamic_slice_in_dim(value, core * heads_wide, heads_wide, 1)
        return jnp.concatenate([jnp.where(first_core, own, other), jnp.where(first_core, other, own)], axis=0)

    def share_on_line(value):
        pieces = [value]
        for flip in range(1, line):
            pieces.append(lax.ppermute(value, ("hi", "lo"), [(i, i ^ flip) for i in range(line)]))
        pieces = jnp.stack(pieces)
        return jnp.stack([lax.dynamic_index_in_dim(pieces, place ^ i, 0, False) for i in range(line)])

    def gather_planes(value):
        return lax.all_gather(value, ("plane", "core"), axis=0, tiled=True).reshape(devices, -1, width)

    up_rows, down_rows, out_rows = w_up.shape[0], w_down.shape[0], w_out.shape[0]
    skip_rows = w_skip.shape[0]
    early = jnp.concatenate([w_skip] + [w_qkv[:, i * width : (i + 1) * width] for i in range(3)] + [w_out], axis=0)
    early_line = share_on_line(early)
    columns = w_up.shape[1] // width
    late = jnp.concatenate([w_down] + [w_up[:, i * width : (i + 1) * width] for i in range(columns)], axis=0)

    labels_own = segment_ids[:, 0]
    labels_other = lax.ppermute(labels_own, "core", swap)
    labels_pick = jnp.where(core == high // micro, labels_own, labels_other)
    seg = lax.dynamic_index_in_dim(labels_pick, high % micro, 0, False)
    names = jnp.arange(labels, dtype=jnp.int32)
    starts = jnp.sum((seg[:, None] < names[None, :]).astype(jnp.int32), axis=0)
    ends = jnp.sum((seg[:, None] <= names[None, :]).astype(jnp.int32), axis=0)
    offset = jnp.sum(jnp.where(seg[:, None] == names[None, :], starts[None, :], 0), axis=1)
    where_at = jnp.arange(length, dtype=jnp.int32) - offset
    by_block = seg.reshape(-1, BLOCK)
    begin = jnp.sum(jnp.where(by_block[:, :1] == names[None, :], starts[None, :], 0), axis=1)
    finish = jnp.sum(jnp.where(by_block[:, -1:] == names[None, :], ends[None, :], 0), axis=1)
    ranges = jnp.stack([begin // BLOCK, (finish + BLOCK - 1) // BLOCK]).astype(jnp.int32)
    half = HEAD_DIM // 2
    rates = jnp.exp(-math.log(10000.0) * jnp.arange(half, dtype=f32) / half)
    angles = where_at.astype(f32)[:, None] * rates
    cosine = jnp.tile(jnp.cos(angles), (1, 4))
    sine = jnp.sin(angles)
    sine = jnp.concatenate([-sine, sine, -sine, sine], axis=1)
    seg_column, seg_row = seg[:, None], seg[None, :]
    mine = lax.dynamic_slice_in_dim(seg, member * frames, frames, 0)

    steps = lax.all_gather(time_steps[:, 0], ("plane", "core"), axis=0, tiled=True).reshape(-1)
    quarter = w_mod.shape[0] // 2
    pace = jnp.exp(-math.log(10000.0) * jnp.arange(quarter, dtype=f32) / quarter)
    turns = steps.astype(f32)[:, None] * pace
    embedded = jnp.concatenate([jnp.sin(turns), jnp.cos(turns)], axis=1).astype(bf16)
    block_mod = jnp.dot(embedded, w_mod, preferred_element_type=f32)
    own_columns = block_mod.shape[1]
    block_mod = block_mod.reshape(planes, 1, highs, 1, labels, own_columns)
    block_mod = jnp.broadcast_to(block_mod, (planes, 2, highs, lows, labels, own_columns))
    block_mod = lax.all_to_all(
        block_mod.reshape(devices, labels, own_columns), ALL_AXES, split_axis=0, concat_axis=0, tiled=True
    )
    modulation = jnp.moveaxis(block_mod, 0, 1).reshape(labels, 4, width)

    early_line, inputs, skips, modulation, cosine, sine, ranges, mine = lax.optimization_barrier(
        (early_line, inputs, skips, modulation, cosine, sine, ranges, mine)
    )
    early = gather_planes(early_line)
    x, s = to_rows(inputs), to_rows(skips)
    late, s = lax.optimization_barrier((late, s))
    late = lax.all_gather(late, ("hi", "lo"), axis=0, tiled=True)
    in_place = out_rows % 16 == 0
    hidden = w_up.shape[1]
    chunk = hidden // (2 * planes)

    def weight(gathered, begin, rows, first, count):
        block = (count // rows, rows, width)
        if in_place:
            return gathered, block, (first // count, begin // rows, 0)
        taken = gathered[first // rows : (first + count) // rows, begin : begin + rows]
        return taken.reshape(1, count, width), (1, count, width), (0, 0, 0)

    skip_top, skip_bottom = (weight(early, 0, skip_rows, i * width, width) for i in range(2))
    out_weight = weight(early, skip_rows + 3 * out_rows, out_rows, 0, width)
    def own_qkv(gathered):
        parts = []
        for i in range(3):
            begin = skip_rows + i * out_rows
            whole = gathered[:, begin : begin + out_rows].reshape(width, width)
            parts.append(lax.dynamic_slice_in_dim(whole, member * heads_wide, heads_wide, 1))
        return jnp.concatenate(parts, axis=1)

    mine_column, mine_row = mine[:, None], mine[None, :]
    shift_one, scale_one, shift_two, scale_two = (modulation[:, i] for i in range(4))

    resid_in, normed_one = rowwise(
        skip_norm_kernel,
        frames,
        [("", x), ("", s), ("weight", skip_top), ("weight", skip_bottom), ("", mine_column),
         ("whole", shift_one), ("whole", scale_one)],
        [(width, f32), (width, bf16)],
        light=True,
    )
    normed_row = frames_to_row(normed_one)
    if in_place:
        projected = project(normed_row, early, skip_rows, out_rows, heads_wide, member)
    else:
        projected = jnp.dot(normed_row, own_qkv(early), preferred_element_type=f32).astype(bf16)
    projected, late, cotangent = lax.optimization_barrier((projected, late, cotangent))
    late = gather_planes(late)
    cot = to_rows(cotangent)
    if in_place:
        per = width // chunk
        up_weight = (late, (devices, up_rows, chunk), lambda j: (0, down_rows // up_rows + j // per, j % per))
        down_weight = (late, (chunk // down_rows, down_rows, width), lambda j: (j, 0, 0))
    else:
        pieces = [late[:, down_rows + i * up_rows : down_rows + (i + 1) * up_rows] for i in range(columns)]
        up_full = jnp.concatenate([v.reshape(width, width) for v in pieces], axis=1)
        up_weight = (up_full[None], (1, width, chunk), lambda j: (0, 0, j))
        down_weight = (late[:, :down_rows].reshape(1, -1, width), (1, chunk, width), lambda j: (0, j, 0))
    mixed_heads, queries, keys, logsum = attend_forward(ranges, projected, cosine, sine, seg_column, seg_row)
    mixed = heads_to_frames(mixed_heads)
    resid_mid, normed_two = rowwise(
        out_norm_kernel,
        frames,
        [("", mixed), ("weight", out_weight), ("", resid_in), ("", mine_column), ("whole", shift_two), ("whole", scale_two)],
        [(width, f32), (width, bf16)],
        flops=2 * frames * width * width,
    )
    early, normed_two = lax.optimization_barrier((early, normed_two))
    qkv_own = own_qkv(early)
    normed_two, qkv_own = lax.optimization_barrier((normed_two, qkv_own))
    result, grad_normed_two, *up_halves, own_down, other_down = feed_forward_and_back(
        core, normed_two, cot, resid_mid, hidden, chunk, up_weight, down_weight, planes
    )

    def over_cores(kept, axis):
        other = lax.ppermute(lax.dynamic_index_in_dim(kept, 1 - core, axis, False), "core", swap)
        own = lax.dynamic_index_in_dim(kept, core, axis, False)
        return (own.astype(f32) + other.astype(f32)).astype(bf16)

    plane = lax.axis_index("plane")

    def exchange(value, axes, here, count):
        total = lax.dynamic_index_in_dim(value, here, 0, False).astype(f32)
        for flip in range(1, count):
            sent = lax.dynamic_index_in_dim(value, here ^ flip, 0, False)
            total += lax.ppermute(sent, axes, [(i, i ^ flip) for i in range(count)]).astype(f32)
        return total

    def exchange_planes(value):
        return exchange(value, "plane", plane, planes).astype(bf16)

    def exchange_line(value):
        return exchange(value.reshape(line, -1, value.shape[1]), ("hi", "lo"), place, line)

    def scatter(value):
        value = value.reshape(-1, value.shape[-1])
        return lax.psum_scatter(value, ("plane", "hi", "lo"), scatter_dimension=0, tiled=True)

    def add_other(own, other):
        return (own.astype(f32) + lax.ppermute(other, "core", swap).astype(f32)).astype(bf16)

    grad_up, grad_down = add_other(*up_halves), add_other(own_down, other_down)

    grad_mid, grad_mid_low, grad_frames, grad_shift_two, grad_scale_two = rowwise(
        norm_two_back_kernel,
        frames,
        [("", grad_normed_two), ("", resid_mid), ("", cot), ("", mine_column), ("row", mine_row),
         ("whole", scale_two), ("weight", out_weight)],
        [(width, f32), (width, bf16), (width, bf16)],
        sums=2,
        light=True,
    )
    grad_frames, grad_up = lax.optimization_barrier((grad_frames, grad_up))
    grad_up = scatter(grad_up)
    grad_heads = frames_to_heads(grad_frames)
    grad_out = lax.dot_general(mixed, grad_mid_low, (((0,), (0,)), ((), ())), preferred_element_type=f32)
    grad_out = over_cores(grad_out.astype(bf16).reshape(planes, 2, -1, width), 1)
    grad_down = jnp.concatenate(
        [v.reshape(planes, line, -1, width) for v in (grad_down, grad_out)], axis=2
    )
    grad_heads, grad_down, result = lax.optimization_barrier((grad_heads, grad_down, result))
    block_out = from_rows(result)
    grad_down = exchange_planes(grad_down.reshape(planes, -1, width))
    grad_proj = attend_backward(
        ranges, queries, keys, projected, mixed_heads, grad_heads, logsum, cosine, sine, seg_column, seg_row
    )
    grad_proj, grad_down, block_out = lax.optimization_barrier((grad_proj, grad_down, block_out))
    grad_down = exchange_line(grad_down)
    grad_qkv = lax.dot_general(normed_row, grad_proj, (((0,), (0,)), ((), ())), preferred_element_type=f32)
    grad_qkv = grad_qkv.astype(bf16)
    grad_proj, grad_qkv = lax.optimization_barrier((grad_proj, grad_qkv))
    if group > 2:
        grad_qkv = grad_qkv.reshape(planes, 2, highs, lows, -1, 3, 1, heads_wide)
        grad_qkv = jnp.moveaxis(grad_qkv, (1, 3), (0, 1)).reshape(group, -1, 3, 1, heads_wide)
        grad_qkv = lax.all_to_all(grad_qkv, ROW_AXES, split_axis=0, concat_axis=3, tiled=True)
        grad_qkv = grad_qkv.reshape(-1, 3 * width)
        partial = dot_nt(grad_proj, qkv_own).astype(bf16)
        grad_one = lax.psum_scatter(partial, ROW_AXES, scatter_dimension=0, tiled=True).astype(f32)
        grad_one_other = jnp.zeros((frames, width), bf16)
    else:
        split = grad_qkv.reshape(planes, 2, -1, 3 * heads_wide)
        other = lax.ppermute(lax.dynamic_index_in_dim(split, 1 - core, 1, False), "core", swap)
        own = lax.dynamic_index_in_dim(split, core, 1, False)
        own, other = (v.reshape(-1, 3 * heads_wide) for v in (own, other))
        left, right = jnp.where(first_core, own, other), jnp.where(first_core, other, own)
        grad_qkv = jnp.concatenate(
            [v[:, i * heads_wide : (i + 1) * heads_wide] for i in range(3) for v in (left, right)], axis=1
        )
        away = lax.dynamic_slice_in_dim(grad_proj, (1 - core) * frames, frames, 0)
        home = lax.dynamic_slice_in_dim(grad_proj, core * frames, frames, 0)
        grad_one_other = lax.ppermute(dot_nt(away, qkv_own).astype(bf16), "core", swap)
        grad_one = dot_nt(home, qkv_own)
    grad_one, grad_qkv, grad_up = lax.optimization_barrier((grad_one, grad_qkv, grad_up))
    if group > 2:
        grad_qkv = lax.psum_scatter(grad_qkv, ("plane", "hi"), scatter_dimension=0, tiled=True).astype(f32)
    else:
        grad_qkv = lax.psum_scatter(grad_qkv, "plane", scatter_dimension=0, tiled=True)
    grad_in, grad_shift_one, grad_scale_one = rowwise(
        norm_one_back_kernel,
        frames,
        [("", grad_one), ("", grad_one_other), ("", resid_in), ("", grad_mid), ("", mine_column), ("row", mine_row),
         ("whole", scale_one)],
        [(width, bf16)],
        sums=2,
    )
    grad_in, grad_down = lax.optimization_barrier((grad_in, grad_down))
    grad_in_home = from_rows(grad_in)
    grad_skip_w = jnp.concatenate(
        [
            lax.dot_general(v, grad_in, (((0,), (0,)), ((), ())), preferred_element_type=f32).astype(bf16)
            for v in (x, s)
        ],
        axis=0,
    )
    grad_skip_w = exchange_planes(over_cores(grad_skip_w.reshape(planes, 2, -1, width), 1))
    grad_in_home, grad_qkv = lax.optimization_barrier((grad_in_home, grad_qkv))
    if group == 2:
        grad_qkv = exchange_line(grad_qkv)
    grad_inputs, grad_skips = rowwise(
        unmerge_kernel,
        frames,
        [("", grad_in_home.reshape(frames, width)), ("weight", skip_top), ("weight", skip_bottom)],
        [(width, bf16), (width, bf16)],
        flops=4 * frames * width * width,
    )
    grad_inputs, grad_skips = (v.reshape(grad_in_home.shape) for v in (grad_inputs, grad_skips))

    grad_shift_one, grad_skip_w = lax.optimization_barrier((grad_shift_one, grad_skip_w))
    grad_skip_w = exchange_line(grad_skip_w)
    grad_mod = jnp.stack([v[:labels] for v in (grad_shift_one, grad_scale_one, grad_shift_two, grad_scale_two)], axis=1)
    grad_mod = jnp.moveaxis(grad_mod.reshape(labels, devices, own_columns), 1, 0)
    grad_mod = lax.all_to_all(grad_mod, ALL_AXES, split_axis=0, concat_axis=0, tiled=True)
    grad_inputs, grad_mod, grad_up, grad_skip_w = lax.optimization_barrier(
        (grad_inputs, grad_mod, grad_up, grad_skip_w)
    )
    grad_up = grad_up.astype(f32)
    grad_down, grad_out = grad_down[:down_rows], grad_down[down_rows:]
    grad_mod = jnp.sum(grad_mod.reshape(planes, 2, highs, lows, labels, own_columns), axis=(1, 3))
    grad_mod = lax.dot_general(
        embedded.astype(f32),
        grad_mod.reshape(-1, own_columns),
        (((0,), (0,)), ((), ())),
        precision=lax.Precision.HIGHEST,
        preferred_element_type=f32,
    )
    return (
        block_out,
        grad_inputs,
        grad_skips,
        grad_skip_w,
        grad_qkv,
        grad_out,
        grad_up,
        grad_down,
        grad_mod,
    )


def solution(mesh):
    batch, wide = mesh.devices.shape

    def run(inputs, *rest):
        rows = 2 * inputs.shape[0]
        assert inputs.shape[0] == 2 and inputs.shape[1] == batch and wide % rows == 0
        fine = Mesh(mesh.devices.reshape(batch // 2, 2, rows, wide // rows), ALL_AXES)
        by_batch, by_wide = ("plane", "core"), ("hi", "lo")
        frames = P(None, by_batch, by_wide, None)
        rowed = P(None, by_batch, None)
        weight, columns = P(ALL_AXES, None), P(None, ALL_AXES)
        mapped = jax.shard_map(
            body,
            mesh=fine,
            in_specs=(frames, frames, frames, rowed, rowed) + (weight,) * 5 + (columns,),
            out_specs=(frames, frames, frames) + (weight,) * 5 + (columns,),
            check_vma=False,
        )
        return mapped(inputs, *rest)

    return run
```

```python
import functools
import math

import jax
import jax.numpy as jnp
from jax import lax
from jax.experimental import pallas as pl
from jax.experimental.pallas import tpu as pltpu
from jax.sharding import Mesh
from jax.sharding import PartitionSpec as P

HEAD_DIM = 64
TILE = 128
BLOCK = 256
ROW_TILE = 256
FEED_TILE = 1024
FEED_PART = 512
VMEM_BYTES = 60 * 1024 * 1024
ROW_AXES = ("core", "lo")
LINE_AXES = ("core", "hi", "lo")
ALL_AXES = ("plane", "core", "hi", "lo")
f32 = jnp.float32
bf16 = jnp.bfloat16


def dot_nn(left, right):
    return lax.dot_general(left, right, (((1,), (0,)), ((), ())), preferred_element_type=f32)


def dot_nt(left, right):
    return lax.dot_general(left, right, (((1,), (1,)), ((), ())), preferred_element_type=f32)


def dot_tn(left, right):
    return lax.dot_general(left, right, (((0,), (0,)), ((), ())), preferred_element_type=f32)


def params(*semantics):
    return pltpu.CompilerParams(dimension_semantics=semantics, vmem_limit_bytes=VMEM_BYTES)


def cost(flops, moved, special=0):
    return pl.CostEstimate(flops=int(flops), bytes_accessed=int(moved), transcendentals=int(special))


def flat(ref):
    return ref[...].reshape(-1, ref.shape[-1])


def choose(segment_column, table_ref):
    count = table_ref.shape[0]
    picked = table_ref[count - 1 : count, :]
    for label in range(count - 2, -1, -1):
        picked = jnp.where(segment_column == label, table_ref[label : label + 1, :], picked)
    return picked


def normalise(values):
    centred = values - jnp.mean(values, axis=-1, keepdims=True)
    variance = jnp.mean(centred * centred, axis=-1, keepdims=True)
    inverse = lax.rsqrt(variance + 1e-06)
    return centred * inverse, inverse


def merge_kernel(x_ref, s_ref, top_ref, bottom_ref, resid_ref):
    resid = dot_nn(x_ref[...], flat(top_ref)) + dot_nn(s_ref[...], flat(bottom_ref))
    resid_ref[...] = resid.astype(bf16)


def norm_kernel(resid_ref, seg_ref, shift_ref, scale_ref, normed_ref):
    unit, _ = normalise(resid_ref[...].astype(f32))
    label = seg_ref[...]
    normed = unit * (1.0 + choose(label, scale_ref)) + choose(label, shift_ref)
    normed_ref[...] = normed.astype(bf16)


def out_norm_kernel(mixed_ref, w_ref, resid_in_ref, seg_ref, shift_ref, scale_ref, resid_ref, normed_ref):
    resid = resid_in_ref[...].astype(f32) + dot_nn(mixed_ref[...], flat(w_ref))
    resid_ref[...] = resid
    unit, _ = normalise(resid)
    label = seg_ref[...]
    normed = unit * (1.0 + choose(label, scale_ref)) + choose(label, shift_ref)
    normed_ref[...] = normed.astype(bf16)


def segment_sums(row_labels, values, total_ref):
    members = lax.broadcasted_iota(jnp.int32, (total_ref.shape[0], row_labels.shape[1]), 0) == row_labels
    members = members.astype(f32).astype(bf16)
    high = values.astype(bf16)
    low = (values - high.astype(f32)).astype(bf16)
    total_ref[...] += dot_nn(members, high) + dot_nn(members, low)


def norm_pull(grad, resid, scale):
    unit, inverse = normalise(resid)
    inner = grad * (1.0 + scale)
    pulled = inverse * (
        inner
        - jnp.mean(inner, axis=-1, keepdims=True)
        - unit * jnp.mean(inner * unit, axis=-1, keepdims=True)
    )
    return pulled, grad * unit


def norm_two_back_kernel(
    g_ref, resid_ref, cot_ref, seg_ref, segr_ref, scale_ref, w_ref, mid_ref, low_ref, mix_ref, dshift_ref, dscale_ref
):
    @pl.when(pl.program_id(0) == 0)
    def _():
        dshift_ref[...] = jnp.zeros_like(dshift_ref)
        dscale_ref[...] = jnp.zeros_like(dscale_ref)

    grad = g_ref[...]
    pulled, by_scale = norm_pull(grad, resid_ref[...], choose(seg_ref[...], scale_ref))
    grad_mid = cot_ref[...].astype(f32) + pulled
    low = grad_mid.astype(bf16)
    mid_ref[...] = grad_mid
    low_ref[...] = low
    mix_ref[...] = dot_nt(low, flat(w_ref)).astype(bf16)
    segment_sums(segr_ref[...], grad, dshift_ref)
    segment_sums(segr_ref[...], by_scale, dscale_ref)


def norm_one_back_kernel(
    own_ref, other_ref, resid_ref, mid_ref, seg_ref, segr_ref, scale_ref, grad_ref, dshift_ref, dscale_ref
):
    @pl.when(pl.program_id(0) == 0)
    def _():
        dshift_ref[...] = jnp.zeros_like(dshift_ref)
        dscale_ref[...] = jnp.zeros_like(dscale_ref)

    grad = own_ref[...] + other_ref[...].astype(f32)
    pulled, by_scale = norm_pull(grad, resid_ref[...].astype(f32), choose(seg_ref[...], scale_ref))
    grad_ref[...] = (mid_ref[...] + pulled).astype(bf16)
    segment_sums(segr_ref[...], grad, dshift_ref)
    segment_sums(segr_ref[...], by_scale, dscale_ref)


def unmerge_kernel(g_ref, top_ref, bottom_ref, inputs_ref, skips_ref):
    inputs_ref[...] = dot_nt(g_ref[...], flat(top_ref)).astype(bf16)
    skips_ref[...] = dot_nt(g_ref[...], flat(bottom_ref)).astype(bf16)


def project_kernel(place_ref, x_ref, w_ref, out_ref):
    out_ref[...] = dot_nn(x_ref[...], flat(w_ref)).astype(bf16)


def project(value, gathered, begin, rows, heads_wide, member):
    length, width = value.shape
    tile = min(8 * ROW_TILE, length)
    return pl.pallas_call(
        project_kernel,
        grid_spec=pltpu.PrefetchScalarGridSpec(
            num_scalar_prefetch=1,
            grid=(3, length // tile),
            in_specs=[
                pl.BlockSpec((tile, width), lambda t, i, r: (i, 0)),
                pl.BlockSpec((width // rows, rows, heads_wide), lambda t, i, r: (0, begin // rows + t, r[0])),
            ],
            out_specs=pl.BlockSpec((tile, heads_wide), lambda t, i, r: (i, t)),
        ),
        out_shape=jax.ShapeDtypeStruct((length, 3 * heads_wide), bf16),
        compiler_params=params("arbitrary", "arbitrary"),
        cost_estimate=cost(1, 1),
    )(member.reshape(1), value, gathered)


def rowwise(kernel, frames, blocked, outs, sums=0, flops=0, light=False):
    tile = min(ROW_TILE, frames)
    in_specs, args, moved = [], [], 0
    for kind, value in blocked:
        if kind == "row":
            in_specs.append(pl.BlockSpec((1, tile), lambda i: (0, i)))
        elif kind == "weight":
            value, block, index = value
            in_specs.append(pl.BlockSpec(block, functools.partial(lambda index, i: index, index)))
        elif kind == "whole":
            in_specs.append(pl.BlockSpec(value.shape, lambda i: (0, 0)))
        else:
            in_specs.append(pl.BlockSpec((tile, value.shape[1]), lambda i: (i, 0)))
        args.append(value)
        moved += value.size * value.dtype.itemsize
    out_specs, shapes = [], []
    for width, kind in outs:
        out_specs.append(pl.BlockSpec((tile, width), lambda i: (i, 0)))
        shapes.append(jax.ShapeDtypeStruct((frames, width), kind))
        moved += frames * width * jnp.dtype(kind).itemsize
    for _ in range(sums):
        out_specs.append(pl.BlockSpec((8, outs[0][0]), lambda i: (0, 0)))
        shapes.append(jax.ShapeDtypeStruct((8, outs[0][0]), f32))
    return pl.pallas_call(
        kernel,
        grid=(frames // tile,),
        in_specs=in_specs,
        out_specs=out_specs,
        out_shape=shapes,
        compiler_params=params("arbitrary"),
        cost_estimate=cost(1, 1) if light else cost(flops, moved),
    )(*args)


def swap_halves(values, lanes):
    half = HEAD_DIM // 2
    ahead = pltpu.roll(values, values.shape[1] - half, 1)
    behind = pltpu.roll(values, half, 1)
    return jnp.where(lanes % HEAD_DIM < half, ahead, behind)


def widen(table, width):
    return jnp.concatenate([table] * (width // table.shape[1]), axis=1)


def span(i):
    return pl.ds(pl.multiple_of(i * BLOCK, BLOCK), BLOCK)


def own_lanes(parts, lanes):
    picked = parts[0]
    for h in range(1, len(parts)):
        picked = jnp.where(lanes // HEAD_DIM == h, parts[h], picked)
    return picked


def by_count(count, most, run):
    for each in range(1, most + 1):
        pl.when(count == each)(functools.partial(run, each))


def attend_forward_kernel(
    range_ref, q_ref, k_ref, v_ref, cos_ref, sin_ref, segc_ref, segr_ref,
    out_ref, qrot_ref, krot_ref, lse_ref, seg_wide,
):
    length, width = q_ref.shape
    heads = width // HEAD_DIM
    blocks = length // BLOCK
    lanes = lax.broadcasted_iota(jnp.int32, (BLOCK, width), 1)

    def turn(i, carry):
        rows = span(i)
        cosine, sine = widen(cos_ref[rows, :], width), widen(sin_ref[rows, :], width)
        for source, target, factor in ((q_ref, qrot_ref, HEAD_DIM**-0.5), (k_ref, krot_ref, None)):
            values = source[rows, :].astype(f32)
            turned = (values * cosine + swap_halves(values, lanes) * sine).astype(bf16)
            if factor is not None:
                turned = turned * jnp.asarray(factor, bf16)
            target[rows, :] = turned
        seg_wide[rows, :] = jnp.broadcast_to(segc_ref[rows, :], (BLOCK, TILE))
        return carry

    lax.fori_loop(0, blocks, turn, 0)

    def one_query(i, carry):
        rows = span(i)

        def work(count):
            keys = pl.ds(pl.multiple_of(range_ref[0, i] * BLOCK, BLOCK), count * BLOCK)
            allowed = widen(seg_wide[rows, :], count * BLOCK) == segr_ref[:, keys]
            query = qrot_ref[rows, :]
            zero = jnp.zeros_like(query)
            mixed = []
            for h in range(heads):
                scores = dot_nt(jnp.where(lanes // HEAD_DIM == h, query, zero), krot_ref[keys, :])
                scores = jnp.where(allowed, scores, -1e30)
                highest = jnp.max(scores, axis=1, keepdims=True)
                powers = jnp.exp(scores - highest)
                totals = jnp.sum(powers, axis=1, keepdims=True)
                mixed.append(dot_nn(powers.astype(bf16), v_ref[keys, :]) * (1.0 / totals))
                logsum = jnp.broadcast_to(highest + jnp.log(totals), (BLOCK, TILE))
                lse_ref[0, h : h + 1, rows] = logsum.T[0:1]
            out_ref[rows, :] = own_lanes(mixed, lanes).astype(bf16)

        by_count(range_ref[1, i] - range_ref[0, i], blocks, work)
        return carry

    lax.fori_loop(0, blocks, one_query, 0)


def attend_forward(ranges, projected, cosine, sine, seg_column, seg_row):
    length, width = projected.shape
    width //= 3
    panels, heads = width // TILE, TILE // HEAD_DIM
    panel = lambda shift: pl.BlockSpec((length, TILE), lambda p, r: (0, shift * panels + p))
    whole = lambda shape: pl.BlockSpec(shape, lambda p, r: (0,) * len(shape))
    return pl.pallas_call(
        attend_forward_kernel,
        grid_spec=pltpu.PrefetchScalarGridSpec(
            num_scalar_prefetch=1,
            grid=(panels,),
            in_specs=[panel(0), panel(1), panel(2), whole(cosine.shape), whole(sine.shape),
                      whole(seg_column.shape), whole(seg_row.shape)],
            out_specs=[panel(0), panel(0), panel(0), pl.BlockSpec((1, heads, length), lambda p, r: (p, 0, 0))],
            scratch_shapes=[pltpu.VMEM((length, TILE), jnp.int32)],
        ),
        out_shape=[jax.ShapeDtypeStruct((length, width), bf16)] * 3
        + [jax.ShapeDtypeStruct((panels, heads, length), f32)],
        compiler_params=params("arbitrary"),
        cost_estimate=cost(8 * length * length * width, 14 * length * width, length * length * width // HEAD_DIM),
    )(ranges, projected, projected, projected, cosine, sine, seg_column, seg_row)


def attend_backward_kernel(
    range_ref, q_ref, k_ref, v_ref, out_ref, do_ref, lse_ref, cos_ref, sin_ref, segc_ref, segr_ref,
    grad_ref, dq, dk_low, dv_low, delta, seg_wide,
):
    length, width = q_ref.shape
    heads = width // HEAD_DIM
    blocks = length // BLOCK
    step = pl.program_id(1)

    @pl.when(step == 0)
    def _():
        lanes = lax.broadcasted_iota(jnp.int32, (BLOCK, width), 1)
        picker = (
            lax.broadcasted_iota(jnp.int32, (8, width), 0)
            == lax.broadcasted_iota(jnp.int32, (8, width), 1) // HEAD_DIM
        ).astype(f32)

        def prepare(i, carry):
            rows = span(i)
            product = do_ref[rows, :].astype(f32) * out_ref[rows, :].astype(f32)
            delta[:, rows] = lax.dot_general(
                picker, product, (((1,), (1,)), ((), ())),
                precision=lax.Precision.HIGHEST, preferred_element_type=f32,
            )
            dq[:, rows] = jnp.zeros((width, BLOCK), f32)
            seg_wide[rows, :] = jnp.broadcast_to(segc_ref[rows, :], (BLOCK, TILE))
            return carry

        lax.fori_loop(0, blocks, prepare, 0)

        def unturn(values, rows):
            return values * widen(cos_ref[rows, :], width) - swap_halves(values, lanes) * widen(sin_ref[rows, :], width)

        def one_key(j, carry):
            rows = span(j)

            def work(count):
                there = pl.ds(pl.multiple_of(range_ref[0, j] * BLOCK, BLOCK), count * BLOCK)
                allowed = widen(seg_wide[rows, :], count * BLOCK) == segr_ref[:, there]
                zero = jnp.zeros((BLOCK, width), bf16)
                key, value = (
                    jnp.concatenate([jnp.where(lanes // HEAD_DIM == h, ref[rows, :], zero) for h in range(heads)], axis=0)
                    for ref in (k_ref, v_ref)
                )
                query, grad_out = q_ref[there, :], do_ref[there, :]
                found, grad_prob = dot_nt(key, query), dot_nt(value, grad_out)
                parts, lows = [], []
                for h in range(heads):
                    half = slice(h * BLOCK, (h + 1) * BLOCK)
                    scores = found[half] - lse_ref[0, h : h + 1, there]
                    part = jnp.exp(jnp.where(allowed, scores, -1e30))
                    parts.append(part.astype(bf16))
                    lows.append((part * (grad_prob[half] - delta[h : h + 1, there])).astype(bf16))
                grad_scores = jnp.concatenate(lows, axis=0)
                grad_v = dot_nn(jnp.concatenate(parts, axis=0), grad_out)
                grad_k = dot_nn(grad_scores, query)
                grad_v, grad_k = ([v[h * BLOCK : (h + 1) * BLOCK] for h in range(heads)] for v in (grad_v, grad_k))
                dq[:, there] += dot_tn(key, grad_scores)
                dk_low[rows, :] = unturn(own_lanes(grad_k, lanes), rows).astype(bf16)
                dv_low[rows, :] = own_lanes(grad_v, lanes).astype(bf16)

            by_count(range_ref[1, j] - range_ref[0, j], blocks, work)
            return carry

        lax.fori_loop(0, blocks, one_key, 0)

        def finish(i, carry):
            rows = span(i)
            grad_ref[rows, :] = unturn(dq[:, rows].T * HEAD_DIM**-0.5, rows).astype(bf16)
            return carry

        lax.fori_loop(0, blocks, finish, 0)

    @pl.when(step == 1)
    def _():
        grad_ref[...] = dk_low[...]

    @pl.when(step == 2)
    def _():
        grad_ref[...] = dv_low[...]


def attend_backward(ranges, queries, keys, projected, mixed, grad_mixed, logsum, cosine, sine, seg_column, seg_row):
    length, width = queries.shape
    panels, heads = width // TILE, TILE // HEAD_DIM
    panel = lambda shift: pl.BlockSpec((length, TILE), lambda p, t, r: (0, shift * panels + p))
    whole = lambda shape: pl.BlockSpec(shape, lambda p, t, r: (0,) * len(shape))
    return pl.pallas_call(
        attend_backward_kernel,
        grid_spec=pltpu.PrefetchScalarGridSpec(
            num_scalar_prefetch=1,
            grid=(panels, 3),
            in_specs=[panel(0), panel(0), panel(2), panel(0), panel(0),
                      pl.BlockSpec((1, heads, length), lambda p, t, r: (p, 0, 0)),
                      whole(cosine.shape), whole(sine.shape), whole(seg_column.shape), whole(seg_row.shape)],
            out_specs=pl.BlockSpec((length, TILE), lambda p, t, r: (0, t * panels + p)),
            scratch_shapes=[
                pltpu.VMEM((TILE, length), f32),
                pltpu.VMEM((length, TILE), bf16),
                pltpu.VMEM((length, TILE), bf16),
                pltpu.VMEM((8, length), f32),
                pltpu.VMEM((length, TILE), jnp.int32),
            ],
        ),
        out_shape=jax.ShapeDtypeStruct((length, 3 * width), bf16),
        compiler_params=params("arbitrary", "arbitrary"),
        cost_estimate=cost(20 * length * length * width, 16 * length * width, length * length * width // HEAD_DIM),
    )(ranges, queries, keys, projected, mixed, grad_mixed, logsum, cosine, sine, seg_column, seg_row)


def gelu_and_slope(x):
    root = math.sqrt(2.0 / math.pi)
    square = x * x
    bend = jnp.tanh(x * (root + root * 0.044715 * square))
    half = 0.5 * x
    half_up = 0.5 + 0.5 * bend
    slope = half_up + half * (1.0 - bend * bend) * (root + 3.0 * root * 0.044715 * square)
    return half + half * bend, slope


def feed_kernel(
    core_ref, n_ref, cot_ref, resid_ref, up_ref, down_ref, out_ref, back_ref,
    gup_own_ref, gup_other_ref, gdown_own_ref, gdown_other_ref, total, n_turned, act_turned, pre,
):
    step, last = pl.program_id(0), pl.num_programs(0) - 1
    core = core_ref[0]
    frames, width = n_ref.shape
    tile = min(FEED_TILE, frames)
    planes = gup_own_ref.shape[0]
    part = width // planes

    def rows_of(i):
        return pl.ds(pl.multiple_of(i * tile, tile), tile)

    @pl.when(step == 0)
    def _():
        def turn(i, carry):
            rows = rows_of(i)
            n_turned[:, rows] = n_ref[rows, :].T
            total[rows, :] = resid_ref[rows, :]
            back_ref[rows, :] = jnp.zeros((tile, width), f32)
            return carry

        lax.fori_loop(0, frames // tile, turn, 0)

    def chunk(i, carry):
        rows = rows_of(i)
        up, down = flat(up_ref), flat(down_ref)
        hidden = dot_nn(n_ref[rows, :], up)
        grad_act = dot_nt(cot_ref[rows, :], down)
        activated, slope = gelu_and_slope(hidden)
        activated = activated.astype(bf16)
        grad_pre = (grad_act * slope).astype(bf16)
        act_turned[:, rows] = activated.T
        pre[rows, :] = grad_pre
        total[rows, :] += dot_nn(activated, down)
        back_ref[rows, :] += dot_nt(grad_pre, up)
        return carry

    lax.fori_loop(0, frames // tile, chunk, 0)

    for begin in range(0, width, FEED_PART):
        grad_up = dot_nn(n_turned[begin : begin + FEED_PART, :], pre[...]).astype(bf16)
        for first in range(begin, begin + FEED_PART, part // 2):
            which, half = first // part, first % part // (part // 2)
            kept = grad_up[first - begin : first - begin + part // 2]
            pl.when(core == half)(functools.partial(gup_own_ref.__setitem__, which, kept))
            pl.when(core != half)(functools.partial(gup_other_ref.__setitem__, which, kept))
    piece = act_turned.shape[0]
    for begin in range(0, piece, FEED_PART):
        rows = slice(begin, begin + FEED_PART)
        kept = dot_nn(act_turned[rows, :], cot_ref[...]).astype(bf16)
        pl.when(core == step % 2)(functools.partial(gdown_own_ref.__setitem__, (0, rows), kept))
        pl.when(core != step % 2)(functools.partial(gdown_other_ref.__setitem__, (0, rows), kept))

    @pl.when(step == last)
    def _():
        out_ref[...] = total[...].astype(bf16)


def feed_forward_and_back(core, normed, cot, resid, hidden, piece, w_up, w_down, planes):
    frames, width = normed.shape
    whole = lambda: pl.BlockSpec((frames, width), lambda j, r: (0, 0), pipeline_mode=pl.Buffered(1))
    weight = lambda w: pl.BlockSpec(w[1], lambda j, r: w[2](j))
    up_block = pl.BlockSpec((planes, width // (2 * planes), piece), lambda j, r: (0, 0, j))
    down_block = pl.BlockSpec((1, piece, width), lambda j, r: (j // 2, 0, 0))
    return pl.pallas_call(
        feed_kernel,
        grid_spec=pltpu.PrefetchScalarGridSpec(
            num_scalar_prefetch=1,
            grid=(hidden // piece,),
            in_specs=[whole(), whole(), whole(), weight(w_up), weight(w_down)],
            out_specs=[pl.BlockSpec((frames, width), lambda j, r: (0, 0))] * 2 + [up_block] * 2 + [down_block] * 2,
            scratch_shapes=[
                pltpu.VMEM((frames, width), f32),
                pltpu.VMEM((width, frames), bf16),
                pltpu.VMEM((piece, frames), bf16),
                pltpu.VMEM((frames, piece), bf16),
            ],
        ),
        out_shape=[jax.ShapeDtypeStruct((frames, width), bf16), jax.ShapeDtypeStruct((frames, width), f32)]
        + [jax.ShapeDtypeStruct((planes, width // (2 * planes), hidden), bf16)] * 2
        + [jax.ShapeDtypeStruct((planes, piece, width), bf16)] * 2,
        compiler_params=params("arbitrary"),
        cost_estimate=cost(12 * frames * width * hidden, 8 * width * hidden + 16 * frames * width, frames * hidden),
    )(core.reshape(1), normed, cot, resid, w_up[0], w_down[0])


def body(inputs, skips, cotangent, segment_ids, time_steps, w_skip, w_qkv, w_out, w_up, w_down, w_mod):
    micro, _, piece, width = inputs.shape
    length = segment_ids.shape[-1]
    labels = time_steps.shape[-1]
    planes, lows, highs = lax.axis_size("plane"), lax.axis_size("lo"), lax.axis_size("hi")
    line = highs * lows
    group = 2 * lows
    devices = planes * 2 * line
    core, high, low = lax.axis_index("core"), lax.axis_index("hi"), lax.axis_index("lo")
    place = high * lows + low
    member = core * lows + low
    frames = 2 * piece
    heads_wide = width // group
    first_core = core == 0
    swap = [(0, 1), (1, 0)]

    def route(parity):
        pairs = []
        for c in range(2):
            for z in range(line):
                row = c * micro + ((z % 2) ^ parity)
                to_core, to_low = divmod(z // 2, lows)
                pairs.append((c * line + z, (to_core * highs + row) * lows + to_low))
        return pairs

    there = (route(0), route(1))
    back = tuple([(b, a) for a, b in pairs] for pairs in there)
    odd_place = place % 2
    even_row = high % 2 == 0

    def to_rows(value):
        value = value[:, 0]
        near = lax.ppermute(lax.dynamic_index_in_dim(value, odd_place, 0, False), LINE_AXES, there[0])
        far = lax.ppermute(lax.dynamic_index_in_dim(value, 1 - odd_place, 0, False), LINE_AXES, there[1])
        return jnp.concatenate([jnp.where(even_row, near, far), jnp.where(even_row, far, near)], axis=0)

    def from_rows(value):
        value = value.reshape(2, piece, width)
        near = lax.ppermute(lax.dynamic_index_in_dim(value, high % 2, 0, False), LINE_AXES, back[0])
        far = lax.ppermute(lax.dynamic_index_in_dim(value, 1 - high % 2, 0, False), LINE_AXES, back[1])
        even = odd_place == 0
        return jnp.stack([jnp.where(even, near, far), jnp.where(even, far, near)])[:, None]

    def frames_to_row(value):
        if group > 2:
            return lax.all_gather(value, ROW_AXES, axis=0, tiled=True)
        other = lax.ppermute(value, "core", swap)
        return jnp.concatenate([jnp.where(first_core, value, other), jnp.where(first_core, other, value)], axis=0)

    def heads_to_frames(value):
        if group > 2:
            return lax.all_to_all(value, ROW_AXES, split_axis=0, concat_axis=1, tiled=True)
        other = lax.ppermute(lax.dynamic_slice_in_dim(value, (1 - core) * frames, frames, 0), "core", swap)
        own = lax.dynamic_slice_in_dim(value, core * frames, frames, 0)
        return jnp.concatenate([jnp.where(first_core, own, other), jnp.where(first_core, other, own)], axis=1)

    def frames_to_heads(value):
        if group > 2:
            return lax.all_to_all(value, ROW_AXES, split_axis=1, concat_axis=0, tiled=True)
        other = lax.ppermute(lax.dynamic_slice_in_dim(value, (1 - core) * heads_wide, heads_wide, 1), "core", swap)
        own = lax.dynamic_slice_in_dim(value, core * heads_wide, heads_wide, 1)
        return jnp.concatenate([jnp.where(first_core, own, other), jnp.where(first_core, other, own)], axis=0)

    def share_on_line(value):
        pieces = [value]
        for flip in range(1, line):
            pieces.append(lax.ppermute(value, ("hi", "lo"), [(i, i ^ flip) for i in range(line)]))
        pieces = jnp.stack(pieces)
        return jnp.stack([lax.dynamic_index_in_dim(pieces, place ^ i, 0, False) for i in range(line)])

    def gather_planes(value):
        return lax.all_gather(value, ("plane", "core"), axis=0, tiled=True).reshape(devices, -1, width)

    up_rows, down_rows, out_rows = w_up.shape[0], w_down.shape[0], w_out.shape[0]
    skip_rows = w_skip.shape[0]
    columns = w_up.shape[1] // width
    middle = jnp.concatenate([w_qkv[:, i * width : (i + 1) * width] for i in range(3)] + [w_out], axis=0)
    late = jnp.concatenate([w_down] + [w_up[:, i * width : (i + 1) * width] for i in range(columns)], axis=0)
    early = share_on_line(w_skip)
    early, middle = lax.optimization_barrier((early, middle))
    early = gather_planes(early)
    middle = share_on_line(middle)
    middle, late, time_steps = lax.optimization_barrier((middle, late, time_steps))
    middle = gather_planes(middle)
    late = share_on_line(late)

    labels_own = segment_ids[:, 0]
    labels_other = lax.ppermute(labels_own, "core", swap)
    labels_pick = jnp.where(core == high // micro, labels_own, labels_other)
    seg = lax.dynamic_index_in_dim(labels_pick, high % micro, 0, False)
    names = jnp.arange(labels, dtype=jnp.int32)
    starts = jnp.sum((seg[:, None] < names[None, :]).astype(jnp.int32), axis=0)
    ends = jnp.sum((seg[:, None] <= names[None, :]).astype(jnp.int32), axis=0)
    offset = jnp.sum(jnp.where(seg[:, None] == names[None, :], starts[None, :], 0), axis=1)
    where_at = jnp.arange(length, dtype=jnp.int32) - offset
    by_block = seg.reshape(-1, BLOCK)
    begin = jnp.sum(jnp.where(by_block[:, :1] == names[None, :], starts[None, :], 0), axis=1)
    finish = jnp.sum(jnp.where(by_block[:, -1:] == names[None, :], ends[None, :], 0), axis=1)
    ranges = jnp.stack([begin // BLOCK, (finish + BLOCK - 1) // BLOCK]).astype(jnp.int32)
    half = HEAD_DIM // 2
    rates = jnp.exp(-math.log(10000.0) * jnp.arange(half, dtype=f32) / half)
    angles = where_at.astype(f32)[:, None] * rates
    cosine = jnp.tile(jnp.cos(angles), (1, 4))
    sine = jnp.sin(angles)
    sine = jnp.concatenate([-sine, sine, -sine, sine], axis=1)
    seg_column, seg_row = seg[:, None], seg[None, :]
    mine = lax.dynamic_slice_in_dim(seg, member * frames, frames, 0)

    steps = lax.all_gather(time_steps[:, 0], ("plane", "core"), axis=0, tiled=True).reshape(-1)
    quarter = w_mod.shape[0] // 2
    pace = jnp.exp(-math.log(10000.0) * jnp.arange(quarter, dtype=f32) / quarter)
    turns = steps.astype(f32)[:, None] * pace
    embedded = jnp.concatenate([jnp.sin(turns), jnp.cos(turns)], axis=1).astype(bf16)
    block_mod = jnp.dot(embedded, w_mod, preferred_element_type=f32)
    own_columns = block_mod.shape[1]
    block_mod = block_mod.reshape(planes, 1, highs, 1, labels, own_columns)
    block_mod = jnp.broadcast_to(block_mod, (planes, 2, highs, lows, labels, own_columns))
    block_mod = lax.all_to_all(
        block_mod.reshape(devices, labels, own_columns), ALL_AXES, split_axis=0, concat_axis=0, tiled=True
    )
    modulation = jnp.moveaxis(block_mod, 0, 1).reshape(labels, 4, width)

    in_place = out_rows % 16 == 0
    hidden = w_up.shape[1]
    chunk = hidden // (2 * planes)

    def weight(gathered, begin, rows, first, count):
        block = (count // rows, rows, width)
        if in_place:
            return gathered, block, (first // count, begin // rows, 0)
        taken = gathered[first // rows : (first + count) // rows, begin : begin + rows]
        return taken.reshape(1, count, width), (1, count, width), (0, 0, 0)

    skip_top, skip_bottom = (weight(early, 0, skip_rows, i * width, width) for i in range(2))
    out_weight = weight(middle, 3 * out_rows, out_rows, 0, width)
    def own_qkv(gathered):
        parts = []
        for i in range(3):
            whole = gathered[:, i * out_rows : (i + 1) * out_rows].reshape(width, width)
            parts.append(lax.dynamic_slice_in_dim(whole, member * heads_wide, heads_wide, 1))
        return jnp.concatenate(parts, axis=1)

    mine_column, mine_row = mine[:, None], mine[None, :]
    shift_one, scale_one, shift_two, scale_two = (modulation[:, i] for i in range(4))

    x, s = (v.reshape(frames, width) for v in (inputs, skips))
    (resid_in,) = rowwise(
        merge_kernel, frames, [("", x), ("", s), ("weight", skip_top), ("weight", skip_bottom)], [(width, bf16)], light=True
    )
    resid_in = to_rows(resid_in.reshape(inputs.shape))
    resid_in, late, cotangent, modulation, cosine, sine, ranges = lax.optimization_barrier(
        (resid_in, late, cotangent, modulation, cosine, sine, ranges)
    )
    (normed_one,) = rowwise(
        norm_kernel,
        frames,
        [("", resid_in), ("", mine_column), ("whole", shift_one), ("whole", scale_one)],
        [(width, bf16)],
        light=True,
    )
    normed_row = frames_to_row(normed_one)
    if in_place:
        projected = project(normed_row, middle, 0, out_rows, heads_wide, member)
    else:
        projected = jnp.dot(normed_row, own_qkv(middle), preferred_element_type=f32).astype(bf16)
    late = gather_planes(late)
    cot = to_rows(cotangent)
    if in_place:
        per = width // chunk
        up_weight = (late, (devices, up_rows, chunk), lambda j: (0, down_rows // up_rows + j // per, j % per))
        down_weight = (late, (chunk // down_rows, down_rows, width), lambda j: (j, 0, 0))
    else:
        pieces = [late[:, down_rows + i * up_rows : down_rows + (i + 1) * up_rows] for i in range(columns)]
        up_full = jnp.concatenate([v.reshape(width, width) for v in pieces], axis=1)
        up_weight = (up_full[None], (1, width, chunk), lambda j: (0, 0, j))
        down_weight = (late[:, :down_rows].reshape(1, -1, width), (1, chunk, width), lambda j: (0, j, 0))
    mixed_heads, queries, keys, logsum = attend_forward(ranges, projected, cosine, sine, seg_column, seg_row)
    mixed = heads_to_frames(mixed_heads)
    resid_mid, normed_two = rowwise(
        out_norm_kernel,
        frames,
        [("", mixed), ("weight", out_weight), ("", resid_in), ("", mine_column), ("whole", shift_two), ("whole", scale_two)],
        [(width, f32), (width, bf16)],
        flops=2 * frames * width * width,
    )
    middle, normed_two = lax.optimization_barrier((middle, normed_two))
    qkv_own = own_qkv(middle)
    normed_two, qkv_own = lax.optimization_barrier((normed_two, qkv_own))
    result, grad_normed_two, *up_halves, own_down, other_down = feed_forward_and_back(
        core, normed_two, cot, resid_mid, hidden, chunk, up_weight, down_weight, planes
    )

    def over_cores(kept, axis):
        other = lax.ppermute(lax.dynamic_index_in_dim(kept, 1 - core, axis, False), "core", swap)
        own = lax.dynamic_index_in_dim(kept, core, axis, False)
        return (own.astype(f32) + other.astype(f32)).astype(bf16)

    plane = lax.axis_index("plane")

    def exchange(value, axes, here, count):
        total = lax.dynamic_index_in_dim(value, here, 0, False).astype(f32)
        for flip in range(1, count):
            sent = lax.dynamic_index_in_dim(value, here ^ flip, 0, False)
            total += lax.ppermute(sent, axes, [(i, i ^ flip) for i in range(count)]).astype(f32)
        return total

    def exchange_planes(value):
        return exchange(value, "plane", plane, planes).astype(bf16)

    def exchange_line(value):
        return exchange(value.reshape(line, -1, value.shape[-1]), ("hi", "lo"), place, line)

    def scatter(value):
        value = value.reshape(-1, value.shape[-1])
        return lax.psum_scatter(value, "plane", scatter_dimension=0, tiled=True)

    def add_other(own, other):
        return (own.astype(f32) + lax.ppermute(other, "core", swap).astype(f32)).astype(bf16)

    grad_up, grad_down = add_other(*up_halves), add_other(own_down, other_down)

    grad_mid, grad_mid_low, grad_frames, grad_shift_two, grad_scale_two = rowwise(
        norm_two_back_kernel,
        frames,
        [("", grad_normed_two), ("", resid_mid), ("", cot), ("", mine_column), ("row", mine_row),
         ("whole", scale_two), ("weight", out_weight)],
        [(width, f32), (width, bf16), (width, bf16)],
        sums=2,
        light=True,
    )
    grad_frames, grad_up = lax.optimization_barrier((grad_frames, grad_up))
    grad_up = scatter(grad_up)
    grad_heads = frames_to_heads(grad_frames)
    grad_out = lax.dot_general(mixed, grad_mid_low, (((0,), (0,)), ((), ())), preferred_element_type=f32)
    grad_out = over_cores(grad_out.astype(bf16).reshape(planes, 2, -1, width), 1)
    grad_down = jnp.concatenate(
        [v.reshape(planes, line, -1, width) for v in (grad_down, grad_out)], axis=2
    )
    grad_heads, grad_down, result = lax.optimization_barrier((grad_heads, grad_down, result))
    block_out = from_rows(result)
    grad_down = exchange_planes(grad_down.reshape(planes, -1, width))
    grad_proj = attend_backward(
        ranges, queries, keys, projected, mixed_heads, grad_heads, logsum, cosine, sine, seg_column, seg_row
    )
    grad_proj, grad_up, grad_down, block_out = lax.optimization_barrier((grad_proj, grad_up, grad_down, block_out))
    grad_down = jnp.concatenate(
        [grad_up[:, i * width : (i + 1) * width].reshape(line, -1, width) for i in range(columns)]
        + [grad_down.reshape(line, -1, width)],
        axis=1,
    )
    grad_down = lax.psum_scatter(grad_down.reshape(-1, width), ("hi", "lo"), scatter_dimension=0, tiled=True)
    grad_qkv = lax.dot_general(normed_row, grad_proj, (((0,), (0,)), ((), ())), preferred_element_type=f32)
    grad_qkv = grad_qkv.astype(bf16)
    grad_proj, grad_qkv = lax.optimization_barrier((grad_proj, grad_qkv))
    if group > 2:
        grad_qkv = grad_qkv.reshape(planes, 2, highs, lows, -1, 3, 1, heads_wide)
        grad_qkv = jnp.moveaxis(grad_qkv, (1, 3), (0, 1)).reshape(group, -1, 3, 1, heads_wide)
        grad_qkv = lax.all_to_all(grad_qkv, ROW_AXES, split_axis=0, concat_axis=3, tiled=True)
        grad_qkv = grad_qkv.reshape(-1, 3 * width)
        partial = dot_nt(grad_proj, qkv_own).astype(bf16)
        grad_one = lax.psum_scatter(partial, ROW_AXES, scatter_dimension=0, tiled=True).astype(f32)
        grad_one_other = jnp.zeros((frames, width), bf16)
    else:
        split = grad_qkv.reshape(planes, 2, -1, 3 * heads_wide)
        other = lax.ppermute(lax.dynamic_index_in_dim(split, 1 - core, 1, False), "core", swap)
        own = lax.dynamic_index_in_dim(split, core, 1, False)
        own, other = (v.reshape(-1, 3 * heads_wide) for v in (own, other))
        left, right = jnp.where(first_core, own, other), jnp.where(first_core, other, own)
        grad_qkv = jnp.concatenate(
            [v[:, i * heads_wide : (i + 1) * heads_wide] for i in range(3) for v in (left, right)], axis=1
        )
        away = lax.dynamic_slice_in_dim(grad_proj, (1 - core) * frames, frames, 0)
        home = lax.dynamic_slice_in_dim(grad_proj, core * frames, frames, 0)
        grad_one_other = lax.ppermute(dot_nt(away, qkv_own).astype(bf16), "core", swap)
        grad_one = dot_nt(home, qkv_own)
    grad_one, grad_qkv = lax.optimization_barrier((grad_one, grad_qkv))
    if group > 2:
        grad_qkv = lax.psum_scatter(grad_qkv, ("plane", "hi"), scatter_dimension=0, tiled=True).astype(f32)
    else:
        grad_qkv = exchange_planes(grad_qkv.reshape(planes, -1, 3 * width))
    grad_in, grad_shift_one, grad_scale_one = rowwise(
        norm_one_back_kernel,
        frames,
        [("", grad_one), ("", grad_one_other), ("", resid_in), ("", grad_mid), ("", mine_column), ("row", mine_row),
         ("whole", scale_one)],
        [(width, bf16)],
        sums=2,
    )
    grad_in_home = from_rows(grad_in)
    grad_in_home, grad_qkv, grad_down = lax.optimization_barrier((grad_in_home, grad_qkv, grad_down))
    if group == 2:
        grad_qkv = exchange_line(grad_qkv)
    home = grad_in_home.reshape(frames, width)
    grad_skip_w = jnp.concatenate(
        [
            lax.dot_general(v, home, (((0,), (0,)), ((), ())), preferred_element_type=f32).astype(bf16)
            for v in (x, s)
        ],
        axis=0,
    )
    grad_skip_w = exchange_planes(over_cores(grad_skip_w.reshape(planes, 2, -1, width), 1))
    grad_inputs, grad_skips = rowwise(
        unmerge_kernel,
        frames,
        [("", home), ("weight", skip_top), ("weight", skip_bottom)],
        [(width, bf16), (width, bf16)],
        flops=4 * frames * width * width,
    )
    grad_inputs, grad_skips = (v.reshape(grad_in_home.shape) for v in (grad_inputs, grad_skips))

    grad_shift_one, grad_skip_w = lax.optimization_barrier((grad_shift_one, grad_skip_w))
    grad_skip_w = exchange_line(grad_skip_w)
    grad_mod = jnp.stack([v[:labels] for v in (grad_shift_one, grad_scale_one, grad_shift_two, grad_scale_two)], axis=1)
    grad_mod = jnp.moveaxis(grad_mod.reshape(labels, devices, own_columns), 1, 0)
    grad_mod = lax.all_to_all(grad_mod, ALL_AXES, split_axis=0, concat_axis=0, tiled=True)
    grad_inputs, grad_mod, grad_skip_w = lax.optimization_barrier((grad_inputs, grad_mod, grad_skip_w))
    taken = columns * up_rows
    grad_down = grad_down.astype(f32)
    grad_up = jnp.concatenate([grad_down[i * up_rows : (i + 1) * up_rows] for i in range(columns)], axis=1)
    grad_down, grad_out = grad_down[taken : taken + down_rows], grad_down[taken + down_rows :]
    grad_mod = jnp.sum(grad_mod.reshape(planes, 2, highs, lows, labels, own_columns), axis=(1, 3))
    grad_mod = lax.dot_general(
        embedded.astype(f32),
        grad_mod.reshape(-1, own_columns),
        (((0,), (0,)), ((), ())),
        precision=lax.Precision.HIGHEST,
        preferred_element_type=f32,
    )
    return (
        block_out,
        grad_inputs,
        grad_skips,
        grad_skip_w,
        grad_qkv,
        grad_out,
        grad_up,
        grad_down,
        grad_mod,
    )


def solution(mesh):
    batch, wide = mesh.devices.shape

    def run(inputs, *rest):
        rows = 2 * inputs.shape[0]
        assert inputs.shape[0] == 2 and inputs.shape[1] == batch and wide % rows == 0
        fine = Mesh(mesh.devices.reshape(batch // 2, 2, rows, wide // rows), ALL_AXES)
        by_batch, by_wide = ("plane", "core"), ("hi", "lo")
        frames = P(None, by_batch, by_wide, None)
        rowed = P(None, by_batch, None)
        weight, columns = P(ALL_AXES, None), P(None, ALL_AXES)
        mapped = jax.shard_map(
            body,
            mesh=fine,
            in_specs=(frames, frames, frames, rowed, rowed) + (weight,) * 5 + (columns,),
            out_specs=(frames, frames, frames) + (weight,) * 5 + (columns,),
            check_vma=False,
        )
        return mapped(inputs, *rest)

    return run
```

```python
import functools
import math

import jax
import jax.numpy as jnp
from jax import lax
from jax.experimental import pallas as pl
from jax.experimental.pallas import tpu as pltpu
from jax.sharding import Mesh
from jax.sharding import PartitionSpec as P

HEAD_DIM = 64
TILE = 128
BLOCK = 256
ROW_TILE = 256
FEED_TILE = 1024
FEED_PART = 512
VMEM_BYTES = 60 * 1024 * 1024
ROW_AXES = ("core", "lo")
LINE_AXES = ("core", "hi", "lo")
ALL_AXES = ("plane", "core", "hi", "lo")
f32 = jnp.float32
bf16 = jnp.bfloat16


def dot_nn(left, right):
    return lax.dot_general(left, right, (((1,), (0,)), ((), ())), preferred_element_type=f32)


def dot_nt(left, right):
    return lax.dot_general(left, right, (((1,), (1,)), ((), ())), preferred_element_type=f32)


def dot_tn(left, right):
    return lax.dot_general(left, right, (((0,), (0,)), ((), ())), preferred_element_type=f32)


def params(*semantics):
    return pltpu.CompilerParams(dimension_semantics=semantics, vmem_limit_bytes=VMEM_BYTES)


def cost(flops, moved, special=0):
    return pl.CostEstimate(flops=int(flops), bytes_accessed=int(moved), transcendentals=int(special))


def flat(ref):
    return ref[...].reshape(-1, ref.shape[-1])


def choose(segment_column, table_ref):
    count = table_ref.shape[0]
    picked = table_ref[count - 1 : count, :]
    for label in range(count - 2, -1, -1):
        picked = jnp.where(segment_column == label, table_ref[label : label + 1, :], picked)
    return picked


def normalise(values):
    centred = values - jnp.mean(values, axis=-1, keepdims=True)
    variance = jnp.mean(centred * centred, axis=-1, keepdims=True)
    inverse = lax.rsqrt(variance + 1e-06)
    return centred * inverse, inverse


def merge_kernel(x_ref, s_ref, top_ref, bottom_ref, resid_ref):
    resid = dot_nn(x_ref[...], flat(top_ref)) + dot_nn(s_ref[...], flat(bottom_ref))
    resid_ref[...] = resid.astype(bf16)


def norm_kernel(resid_ref, seg_ref, shift_ref, scale_ref, normed_ref):
    unit, _ = normalise(resid_ref[...].astype(f32))
    label = seg_ref[...]
    normed = unit * (1.0 + choose(label, scale_ref)) + choose(label, shift_ref)
    normed_ref[...] = normed.astype(bf16)


def out_norm_kernel(mixed_ref, w_ref, resid_in_ref, seg_ref, shift_ref, scale_ref, resid_ref, normed_ref):
    resid = resid_in_ref[...].astype(f32) + dot_nn(mixed_ref[...], flat(w_ref))
    resid_ref[...] = resid
    unit, _ = normalise(resid)
    label = seg_ref[...]
    normed = unit * (1.0 + choose(label, scale_ref)) + choose(label, shift_ref)
    normed_ref[...] = normed.astype(bf16)


def segment_sums(row_labels, values, total_ref):
    members = lax.broadcasted_iota(jnp.int32, (total_ref.shape[0], row_labels.shape[1]), 0) == row_labels
    members = members.astype(f32).astype(bf16)
    high = values.astype(bf16)
    low = (values - high.astype(f32)).astype(bf16)
    total_ref[...] += dot_nn(members, high) + dot_nn(members, low)


def norm_pull(grad, resid, scale):
    unit, inverse = normalise(resid)
    inner = grad * (1.0 + scale)
    pulled = inverse * (
        inner
        - jnp.mean(inner, axis=-1, keepdims=True)
        - unit * jnp.mean(inner * unit, axis=-1, keepdims=True)
    )
    return pulled, grad * unit


def norm_two_back_kernel(
    g_ref, resid_ref, cot_ref, seg_ref, segr_ref, scale_ref, w_ref, mid_ref, low_ref, mix_ref, dshift_ref, dscale_ref
):
    @pl.when(pl.program_id(0) == 0)
    def _():
        dshift_ref[...] = jnp.zeros_like(dshift_ref)
        dscale_ref[...] = jnp.zeros_like(dscale_ref)

    grad = g_ref[...]
    pulled, by_scale = norm_pull(grad, resid_ref[...], choose(seg_ref[...], scale_ref))
    grad_mid = cot_ref[...].astype(f32) + pulled
    low = grad_mid.astype(bf16)
    mid_ref[...] = grad_mid
    low_ref[...] = low
    mix_ref[...] = dot_nt(low, flat(w_ref)).astype(bf16)
    segment_sums(segr_ref[...], grad, dshift_ref)
    segment_sums(segr_ref[...], by_scale, dscale_ref)


def norm_one_back_kernel(
    own_ref, other_ref, resid_ref, mid_ref, seg_ref, segr_ref, scale_ref, grad_ref, dshift_ref, dscale_ref
):
    @pl.when(pl.program_id(0) == 0)
    def _():
        dshift_ref[...] = jnp.zeros_like(dshift_ref)
        dscale_ref[...] = jnp.zeros_like(dscale_ref)

    grad = own_ref[...] + other_ref[...].astype(f32)
    pulled, by_scale = norm_pull(grad, resid_ref[...].astype(f32), choose(seg_ref[...], scale_ref))
    grad_ref[...] = (mid_ref[...] + pulled).astype(bf16)
    segment_sums(segr_ref[...], grad, dshift_ref)
    segment_sums(segr_ref[...], by_scale, dscale_ref)


def unmerge_kernel(g_ref, top_ref, bottom_ref, inputs_ref, skips_ref):
    inputs_ref[...] = dot_nt(g_ref[...], flat(top_ref)).astype(bf16)
    skips_ref[...] = dot_nt(g_ref[...], flat(bottom_ref)).astype(bf16)


def project_kernel(place_ref, x_ref, w_ref, out_ref):
    out_ref[...] = dot_nn(x_ref[...], flat(w_ref)).astype(bf16)


def project(value, gathered, begin, rows, heads_wide, member):
    length, width = value.shape
    tile = min(8 * ROW_TILE, length)
    return pl.pallas_call(
        project_kernel,
        grid_spec=pltpu.PrefetchScalarGridSpec(
            num_scalar_prefetch=1,
            grid=(3, length // tile),
            in_specs=[
                pl.BlockSpec((tile, width), lambda t, i, r: (i, 0)),
                pl.BlockSpec((width // rows, rows, heads_wide), lambda t, i, r: (0, begin // rows + t, r[0])),
            ],
            out_specs=pl.BlockSpec((tile, heads_wide), lambda t, i, r: (i, t)),
        ),
        out_shape=jax.ShapeDtypeStruct((length, 3 * heads_wide), bf16),
        compiler_params=params("arbitrary", "arbitrary"),
        cost_estimate=cost(1, 1),
    )(member.reshape(1), value, gathered)


def pull_project_kernel(place_ref, dq_ref, dk_ref, dv_ref, q_ref, k_ref, v_ref, out_ref):
    total = dot_nt(dq_ref[...], flat(q_ref))
    total += dot_nt(dk_ref[...], flat(k_ref))
    total += dot_nt(dv_ref[...], flat(v_ref))
    out_ref[...] = total.astype(out_ref.dtype)


def pull_project(grad_proj, gathered, rows, heads_wide, member, frames, half, kind):
    width = gathered.shape[2]
    tile = min(2 * ROW_TILE, frames)
    steps = frames // tile
    grads = [
        pl.BlockSpec((tile, heads_wide), functools.partial(lambda t, i, r: (r[1] * steps + i, t), t)) for t in range(3)
    ]
    weights = [
        pl.BlockSpec((width // rows, rows, heads_wide), functools.partial(lambda t, i, r: (0, t, r[0]), t))
        for t in range(3)
    ]
    return pl.pallas_call(
        pull_project_kernel,
        grid_spec=pltpu.PrefetchScalarGridSpec(
            num_scalar_prefetch=1,
            grid=(steps,),
            in_specs=grads + weights,
            out_specs=pl.BlockSpec((tile, width), lambda i, r: (i, 0)),
        ),
        out_shape=jax.ShapeDtypeStruct((frames, width), kind),
        compiler_params=params("arbitrary"),
        cost_estimate=cost(6 * frames * width * heads_wide, 8 * frames * width),
    )(jnp.stack([member, half]).astype(jnp.int32), *[grad_proj] * 3, *[gathered] * 3)


def rowwise(kernel, frames, blocked, outs, sums=0, flops=0, light=False):
    tile = min(ROW_TILE, frames)
    in_specs, args, moved = [], [], 0
    for kind, value in blocked:
        if kind == "row":
            in_specs.append(pl.BlockSpec((1, tile), lambda i: (0, i)))
        elif kind == "weight":
            value, block, index = value
            in_specs.append(pl.BlockSpec(block, functools.partial(lambda index, i: index, index)))
        elif kind == "whole":
            in_specs.append(pl.BlockSpec(value.shape, lambda i: (0, 0)))
        else:
            in_specs.append(pl.BlockSpec((tile, value.shape[1]), lambda i: (i, 0)))
        args.append(value)
        moved += value.size * value.dtype.itemsize
    out_specs, shapes = [], []
    for width, kind in outs:
        out_specs.append(pl.BlockSpec((tile, width), lambda i: (i, 0)))
        shapes.append(jax.ShapeDtypeStruct((frames, width), kind))
        moved += frames * width * jnp.dtype(kind).itemsize
    for _ in range(sums):
        out_specs.append(pl.BlockSpec((8, outs[0][0]), lambda i: (0, 0)))
        shapes.append(jax.ShapeDtypeStruct((8, outs[0][0]), f32))
    return pl.pallas_call(
        kernel,
        grid=(frames // tile,),
        in_specs=in_specs,
        out_specs=out_specs,
        out_shape=shapes,
        compiler_params=params("arbitrary"),
        cost_estimate=cost(1, 1) if light else cost(flops, moved),
    )(*args)


def swap_halves(values, lanes):
    half = HEAD_DIM // 2
    ahead = pltpu.roll(values, values.shape[1] - half, 1)
    behind = pltpu.roll(values, half, 1)
    return jnp.where(lanes % HEAD_DIM < half, ahead, behind)


def widen(table, width):
    return jnp.concatenate([table] * (width // table.shape[1]), axis=1)


def span(i):
    return pl.ds(pl.multiple_of(i * BLOCK, BLOCK), BLOCK)


def own_lanes(parts, lanes):
    picked = parts[0]
    for h in range(1, len(parts)):
        picked = jnp.where(lanes // HEAD_DIM == h, parts[h], picked)
    return picked


def by_count(count, most, run):
    for each in range(1, most + 1):
        pl.when(count == each)(functools.partial(run, each))


def attend_forward_kernel(
    range_ref, q_ref, k_ref, v_ref, cos_ref, sin_ref, segc_ref, segr_ref,
    out_ref, qrot_ref, krot_ref, lse_ref, seg_wide,
):
    length, width = q_ref.shape
    heads = width // HEAD_DIM
    blocks = length // BLOCK
    lanes = lax.broadcasted_iota(jnp.int32, (BLOCK, width), 1)

    def turn(i, carry):
        rows = span(i)
        cosine, sine = widen(cos_ref[rows, :], width), widen(sin_ref[rows, :], width)
        for source, target, factor in ((q_ref, qrot_ref, HEAD_DIM**-0.5), (k_ref, krot_ref, None)):
            values = source[rows, :].astype(f32)
            turned = (values * cosine + swap_halves(values, lanes) * sine).astype(bf16)
            if factor is not None:
                turned = turned * jnp.asarray(factor, bf16)
            target[rows, :] = turned
        seg_wide[rows, :] = jnp.broadcast_to(segc_ref[rows, :], (BLOCK, TILE))
        return carry

    lax.fori_loop(0, blocks, turn, 0)

    def one_query(i, carry):
        rows = span(i)

        def work(count):
            keys = pl.ds(pl.multiple_of(range_ref[0, i] * BLOCK, BLOCK), count * BLOCK)
            allowed = widen(seg_wide[rows, :], count * BLOCK) == segr_ref[:, keys]
            query = qrot_ref[rows, :]
            zero = jnp.zeros_like(query)
            mixed = []
            for h in range(heads):
                scores = dot_nt(jnp.where(lanes // HEAD_DIM == h, query, zero), krot_ref[keys, :])
                scores = jnp.where(allowed, scores, -1e30)
                highest = jnp.max(scores, axis=1, keepdims=True)
                powers = jnp.exp(scores - highest)
                totals = jnp.sum(powers, axis=1, keepdims=True)
                mixed.append(dot_nn(powers.astype(bf16), v_ref[keys, :]) * (1.0 / totals))
                logsum = jnp.broadcast_to(highest + jnp.log(totals), (BLOCK, TILE))
                lse_ref[0, h : h + 1, rows] = logsum.T[0:1]
            out_ref[rows, :] = own_lanes(mixed, lanes).astype(bf16)

        by_count(range_ref[1, i] - range_ref[0, i], blocks, work)
        return carry

    lax.fori_loop(0, blocks, one_query, 0)


def attend_forward(ranges, projected, cosine, sine, seg_column, seg_row):
    length, width = projected.shape
    width //= 3
    panels, heads = width // TILE, TILE // HEAD_DIM
    panel = lambda shift: pl.BlockSpec((length, TILE), lambda p, r: (0, shift * panels + p))
    whole = lambda shape: pl.BlockSpec(shape, lambda p, r: (0,) * len(shape))
    return pl.pallas_call(
        attend_forward_kernel,
        grid_spec=pltpu.PrefetchScalarGridSpec(
            num_scalar_prefetch=1,
            grid=(panels,),
            in_specs=[panel(0), panel(1), panel(2), whole(cosine.shape), whole(sine.shape),
                      whole(seg_column.shape), whole(seg_row.shape)],
            out_specs=[panel(0), panel(0), panel(0), pl.BlockSpec((1, heads, length), lambda p, r: (p, 0, 0))],
            scratch_shapes=[pltpu.VMEM((length, TILE), jnp.int32)],
        ),
        out_shape=[jax.ShapeDtypeStruct((length, width), bf16)] * 3
        + [jax.ShapeDtypeStruct((panels, heads, length), f32)],
        compiler_params=params("arbitrary"),
        cost_estimate=cost(8 * length * length * width, 14 * length * width, length * length * width // HEAD_DIM),
    )(ranges, projected, projected, projected, cosine, sine, seg_column, seg_row)


def attend_backward_kernel(
    range_ref, q_ref, k_ref, v_ref, out_ref, do_ref, lse_ref, cos_ref, sin_ref, segc_ref, segr_ref,
    grad_ref, dq, dk_low, dv_low, delta, seg_wide,
):
    length, width = q_ref.shape
    heads = width // HEAD_DIM
    blocks = length // BLOCK
    step = pl.program_id(1)

    @pl.when(step == 0)
    def _():
        lanes = lax.broadcasted_iota(jnp.int32, (BLOCK, width), 1)
        picker = (
            lax.broadcasted_iota(jnp.int32, (8, width), 0)
            == lax.broadcasted_iota(jnp.int32, (8, width), 1) // HEAD_DIM
        ).astype(f32)

        def prepare(i, carry):
            rows = span(i)
            product = do_ref[rows, :].astype(f32) * out_ref[rows, :].astype(f32)
            delta[:, rows] = lax.dot_general(
                picker, product, (((1,), (1,)), ((), ())),
                precision=lax.Precision.HIGHEST, preferred_element_type=f32,
            )
            dq[:, rows] = jnp.zeros((width, BLOCK), f32)
            seg_wide[rows, :] = jnp.broadcast_to(segc_ref[rows, :], (BLOCK, TILE))
            return carry

        lax.fori_loop(0, blocks, prepare, 0)

        def unturn(values, rows):
            return values * widen(cos_ref[rows, :], width) - swap_halves(values, lanes) * widen(sin_ref[rows, :], width)

        def one_key(j, carry):
            rows = span(j)

            def work(count):
                there = pl.ds(pl.multiple_of(range_ref[0, j] * BLOCK, BLOCK), count * BLOCK)
                allowed = widen(seg_wide[rows, :], count * BLOCK) == segr_ref[:, there]
                zero = jnp.zeros((BLOCK, width), bf16)
                key, value = (
                    jnp.concatenate([jnp.where(lanes // HEAD_DIM == h, ref[rows, :], zero) for h in range(heads)], axis=0)
                    for ref in (k_ref, v_ref)
                )
                query, grad_out = q_ref[there, :], do_ref[there, :]
                found, grad_prob = dot_nt(key, query), dot_nt(value, grad_out)
                parts, lows = [], []
                for h in range(heads):
                    half = slice(h * BLOCK, (h + 1) * BLOCK)
                    scores = found[half] - lse_ref[0, h : h + 1, there]
                    part = jnp.exp(jnp.where(allowed, scores, -1e30))
                    parts.append(part.astype(bf16))
                    lows.append((part * (grad_prob[half] - delta[h : h + 1, there])).astype(bf16))
                grad_scores = jnp.concatenate(lows, axis=0)
                grad_v = dot_nn(jnp.concatenate(parts, axis=0), grad_out)
                grad_k = dot_nn(grad_scores, query)
                grad_v, grad_k = ([v[h * BLOCK : (h + 1) * BLOCK] for h in range(heads)] for v in (grad_v, grad_k))
                dq[:, there] += dot_tn(key, grad_scores)
                dk_low[rows, :] = unturn(own_lanes(grad_k, lanes), rows).astype(bf16)
                dv_low[rows, :] = own_lanes(grad_v, lanes).astype(bf16)

            by_count(range_ref[1, j] - range_ref[0, j], blocks, work)
            return carry

        lax.fori_loop(0, blocks, one_key, 0)

        def finish(i, carry):
            rows = span(i)
            grad_ref[rows, :] = unturn(dq[:, rows].T * HEAD_DIM**-0.5, rows).astype(bf16)
            return carry

        lax.fori_loop(0, blocks, finish, 0)

    @pl.when(step == 1)
    def _():
        grad_ref[...] = dk_low[...]

    @pl.when(step == 2)
    def _():
        grad_ref[...] = dv_low[...]


def attend_backward(ranges, queries, keys, projected, mixed, grad_mixed, logsum, cosine, sine, seg_column, seg_row):
    length, width = queries.shape
    panels, heads = width // TILE, TILE // HEAD_DIM
    panel = lambda shift: pl.BlockSpec((length, TILE), lambda p, t, r: (0, shift * panels + p))
    whole = lambda shape: pl.BlockSpec(shape, lambda p, t, r: (0,) * len(shape))
    return pl.pallas_call(
        attend_backward_kernel,
        grid_spec=pltpu.PrefetchScalarGridSpec(
            num_scalar_prefetch=1,
            grid=(panels, 3),
            in_specs=[panel(0), panel(0), panel(2), panel(0), panel(0),
                      pl.BlockSpec((1, heads, length), lambda p, t, r: (p, 0, 0)),
                      whole(cosine.shape), whole(sine.shape), whole(seg_column.shape), whole(seg_row.shape)],
            out_specs=pl.BlockSpec((length, TILE), lambda p, t, r: (0, t * panels + p)),
            scratch_shapes=[
                pltpu.VMEM((TILE, length), f32),
                pltpu.VMEM((length, TILE), bf16),
                pltpu.VMEM((length, TILE), bf16),
                pltpu.VMEM((8, length), f32),
                pltpu.VMEM((length, TILE), jnp.int32),
            ],
        ),
        out_shape=jax.ShapeDtypeStruct((length, 3 * width), bf16),
        compiler_params=params("arbitrary", "arbitrary"),
        cost_estimate=cost(20 * length * length * width, 16 * length * width, length * length * width // HEAD_DIM),
    )(ranges, queries, keys, projected, mixed, grad_mixed, logsum, cosine, sine, seg_column, seg_row)


def gelu_and_slope(x):
    root = math.sqrt(2.0 / math.pi)
    square = x * x
    bend = jnp.tanh(x * (root + root * 0.044715 * square))
    half = 0.5 * x
    half_up = 0.5 + 0.5 * bend
    slope = half_up + half * (1.0 - bend * bend) * (root + 3.0 * root * 0.044715 * square)
    return half + half * bend, slope


def feed_kernel(
    core_ref, n_ref, cot_ref, resid_ref, up_ref, down_ref, out_ref, back_ref,
    gup_ref, gdown_own_ref, gdown_other_ref, total, n_turned, act_turned, pre,
):
    step, last = pl.program_id(0), pl.num_programs(0) - 1
    core = core_ref[0]
    frames, width = n_ref.shape
    tile = min(FEED_TILE, frames)

    def rows_of(i):
        return pl.ds(pl.multiple_of(i * tile, tile), tile)

    @pl.when(step == 0)
    def _():
        def turn(i, carry):
            rows = rows_of(i)
            n_turned[:, rows] = n_ref[rows, :].T
            total[rows, :] = resid_ref[rows, :]
            back_ref[rows, :] = jnp.zeros((tile, width), f32)
            return carry

        lax.fori_loop(0, frames // tile, turn, 0)

    def chunk(i, carry):
        rows = rows_of(i)
        up, down = flat(up_ref), flat(down_ref)
        hidden = dot_nn(n_ref[rows, :], up)
        grad_act = dot_nt(cot_ref[rows, :], down)
        activated, slope = gelu_and_slope(hidden)
        activated = activated.astype(bf16)
        grad_pre = (grad_act * slope).astype(bf16)
        act_turned[:, rows] = activated.T
        pre[rows, :] = grad_pre
        total[rows, :] += dot_nn(activated, down)
        back_ref[rows, :] += dot_nt(grad_pre, up)
        return carry

    lax.fori_loop(0, frames // tile, chunk, 0)

    for begin in range(0, width, FEED_PART):
        rows = slice(begin, begin + FEED_PART)
        gup_ref[rows, :] = dot_nn(n_turned[rows, :], pre[...]).astype(bf16)
    piece = act_turned.shape[0]
    for begin in range(0, piece, FEED_PART):
        rows = slice(begin, begin + FEED_PART)
        kept = dot_nn(act_turned[rows, :], cot_ref[...]).astype(bf16)
        pl.when(core == step % 2)(functools.partial(gdown_own_ref.__setitem__, (0, rows), kept))
        pl.when(core != step % 2)(functools.partial(gdown_other_ref.__setitem__, (0, rows), kept))

    @pl.when(step == last)
    def _():
        out_ref[...] = total[...].astype(bf16)


def feed_forward_and_back(core, normed, cot, resid, hidden, piece, w_up, w_down, planes):
    frames, width = normed.shape
    whole = lambda: pl.BlockSpec((frames, width), lambda j, r: (0, 0), pipeline_mode=pl.Buffered(1))
    weight = lambda w: pl.BlockSpec(w[1], lambda j, r: w[2](j))
    up_block = pl.BlockSpec((width, piece), lambda j, r: (0, j))
    down_block = pl.BlockSpec((1, piece, width), lambda j, r: (j // 2, 0, 0))
    return pl.pallas_call(
        feed_kernel,
        grid_spec=pltpu.PrefetchScalarGridSpec(
            num_scalar_prefetch=1,
            grid=(hidden // piece,),
            in_specs=[whole(), whole(), whole(), weight(w_up), weight(w_down)],
            out_specs=[pl.BlockSpec((frames, width), lambda j, r: (0, 0))] * 2 + [up_block] + [down_block] * 2,
            scratch_shapes=[
                pltpu.VMEM((frames, width), f32),
                pltpu.VMEM((width, frames), bf16),
                pltpu.VMEM((piece, frames), bf16),
                pltpu.VMEM((frames, piece), bf16),
            ],
        ),
        out_shape=[jax.ShapeDtypeStruct((frames, width), bf16), jax.ShapeDtypeStruct((frames, width), f32)]
        + [jax.ShapeDtypeStruct((width, hidden), bf16)]
        + [jax.ShapeDtypeStruct((planes, piece, width), bf16)] * 2,
        compiler_params=params("arbitrary"),
        cost_estimate=cost(12 * frames * width * hidden, 8 * width * hidden + 16 * frames * width, frames * hidden),
    )(core.reshape(1), normed, cot, resid, w_up[0], w_down[0])


def body(inputs, skips, cotangent, segment_ids, time_steps, w_skip, w_qkv, w_out, w_up, w_down, w_mod):
    micro, _, piece, width = inputs.shape
    length = segment_ids.shape[-1]
    labels = time_steps.shape[-1]
    planes, lows, highs = lax.axis_size("plane"), lax.axis_size("lo"), lax.axis_size("hi")
    line = highs * lows
    group = 2 * lows
    devices = planes * 2 * line
    core, high, low = lax.axis_index("core"), lax.axis_index("hi"), lax.axis_index("lo")
    place = high * lows + low
    member = core * lows + low
    frames = 2 * piece
    heads_wide = width // group
    first_core = core == 0
    swap = [(0, 1), (1, 0)]

    def route(parity):
        pairs = []
        for c in range(2):
            for z in range(line):
                row = c * micro + ((z % 2) ^ parity)
                to_core, to_low = divmod(z // 2, lows)
                pairs.append((c * line + z, (to_core * highs + row) * lows + to_low))
        return pairs

    there = (route(0), route(1))
    back = tuple([(b, a) for a, b in pairs] for pairs in there)
    odd_place = place % 2
    even_row = high % 2 == 0

    def to_rows(value):
        value = value[:, 0]
        near = lax.ppermute(lax.dynamic_index_in_dim(value, odd_place, 0, False), LINE_AXES, there[0])
        far = lax.ppermute(lax.dynamic_index_in_dim(value, 1 - odd_place, 0, False), LINE_AXES, there[1])
        return jnp.concatenate([jnp.where(even_row, near, far), jnp.where(even_row, far, near)], axis=0)

    def from_rows(value):
        value = value.reshape(2, piece, width)
        near = lax.ppermute(lax.dynamic_index_in_dim(value, high % 2, 0, False), LINE_AXES, back[0])
        far = lax.ppermute(lax.dynamic_index_in_dim(value, 1 - high % 2, 0, False), LINE_AXES, back[1])
        even = odd_place == 0
        return jnp.stack([jnp.where(even, near, far), jnp.where(even, far, near)])[:, None]

    def frames_to_row(value):
        if group > 2:
            return lax.all_gather(value, ROW_AXES, axis=0, tiled=True)
        other = lax.ppermute(value, "core", swap)
        return jnp.concatenate([jnp.where(first_core, value, other), jnp.where(first_core, other, value)], axis=0)

    def heads_to_frames(value):
        if group > 2:
            return lax.all_to_all(value, ROW_AXES, split_axis=0, concat_axis=1, tiled=True)
        other = lax.ppermute(lax.dynamic_slice_in_dim(value, (1 - core) * frames, frames, 0), "core", swap)
        own = lax.dynamic_slice_in_dim(value, core * frames, frames, 0)
        return jnp.concatenate([jnp.where(first_core, own, other), jnp.where(first_core, other, own)], axis=1)

    def frames_to_heads(value):
        if group > 2:
            return lax.all_to_all(value, ROW_AXES, split_axis=1, concat_axis=0, tiled=True)
        other = lax.ppermute(lax.dynamic_slice_in_dim(value, (1 - core) * heads_wide, heads_wide, 1), "core", swap)
        own = lax.dynamic_slice_in_dim(value, core * heads_wide, heads_wide, 1)
        return jnp.concatenate([jnp.where(first_core, own, other), jnp.where(first_core, other, own)], axis=0)

    def share_on_line(value):
        pieces = [value]
        for flip in range(1, line):
            pieces.append(lax.ppermute(value, ("hi", "lo"), [(i, i ^ flip) for i in range(line)]))
        pieces = jnp.stack(pieces)
        return jnp.stack([lax.dynamic_index_in_dim(pieces, place ^ i, 0, False) for i in range(line)])

    def gather_planes(value):
        return lax.all_gather(value, ("plane", "core"), axis=0, tiled=True).reshape(devices, -1, width)

    up_rows, down_rows, out_rows = w_up.shape[0], w_down.shape[0], w_out.shape[0]
    skip_rows = w_skip.shape[0]
    columns = w_up.shape[1] // width
    middle = jnp.concatenate([w_qkv[:, i * width : (i + 1) * width] for i in range(3)] + [w_out], axis=0)
    late = jnp.concatenate([w_down] + [w_up[:, i * width : (i + 1) * width] for i in range(columns)], axis=0)
    early = share_on_line(w_skip)
    early, middle, late = lax.optimization_barrier((early, middle, late))
    early = gather_planes(early)
    middle, late = share_on_line(middle), share_on_line(late)
    middle = gather_planes(middle)

    labels_own = segment_ids[:, 0]
    labels_other = lax.ppermute(labels_own, "core", swap)
    labels_pick = jnp.where(core == high // micro, labels_own, labels_other)
    seg = lax.dynamic_index_in_dim(labels_pick, high % micro, 0, False)
    names = jnp.arange(labels, dtype=jnp.int32)
    starts = jnp.sum((seg[:, None] < names[None, :]).astype(jnp.int32), axis=0)
    ends = jnp.sum((seg[:, None] <= names[None, :]).astype(jnp.int32), axis=0)
    offset = jnp.sum(jnp.where(seg[:, None] == names[None, :], starts[None, :], 0), axis=1)
    where_at = jnp.arange(length, dtype=jnp.int32) - offset
    by_block = seg.reshape(-1, BLOCK)
    begin = jnp.sum(jnp.where(by_block[:, :1] == names[None, :], starts[None, :], 0), axis=1)
    finish = jnp.sum(jnp.where(by_block[:, -1:] == names[None, :], ends[None, :], 0), axis=1)
    ranges = jnp.stack([begin // BLOCK, (finish + BLOCK - 1) // BLOCK]).astype(jnp.int32)
    half = HEAD_DIM // 2
    rates = jnp.exp(-math.log(10000.0) * jnp.arange(half, dtype=f32) / half)
    angles = where_at.astype(f32)[:, None] * rates
    cosine = jnp.tile(jnp.cos(angles), (1, 4))
    sine = jnp.sin(angles)
    sine = jnp.concatenate([-sine, sine, -sine, sine], axis=1)
    seg_column, seg_row = seg[:, None], seg[None, :]
    mine = lax.dynamic_slice_in_dim(seg, member * frames, frames, 0)

    steps = lax.all_gather(time_steps[:, 0], ("plane", "core"), axis=0, tiled=True).reshape(-1)
    quarter = w_mod.shape[0] // 2
    pace = jnp.exp(-math.log(10000.0) * jnp.arange(quarter, dtype=f32) / quarter)
    turns = steps.astype(f32)[:, None] * pace
    embedded = jnp.concatenate([jnp.sin(turns), jnp.cos(turns)], axis=1).astype(bf16)
    block_mod = jnp.dot(embedded, w_mod, preferred_element_type=f32)
    own_columns = block_mod.shape[1]
    block_mod = block_mod.reshape(planes, 1, highs, 1, labels, own_columns)
    block_mod = jnp.broadcast_to(block_mod, (planes, 2, highs, lows, labels, own_columns))
    block_mod = lax.all_to_all(
        block_mod.reshape(devices, labels, own_columns), ALL_AXES, split_axis=0, concat_axis=0, tiled=True
    )
    modulation = jnp.moveaxis(block_mod, 0, 1).reshape(labels, 4, width)

    in_place = out_rows % 16 == 0
    hidden = w_up.shape[1]
    chunk = hidden // (2 * planes)

    def weight(gathered, begin, rows, first, count):
        block = (count // rows, rows, width)
        if in_place:
            return gathered, block, (first // count, begin // rows, 0)
        taken = gathered[first // rows : (first + count) // rows, begin : begin + rows]
        return taken.reshape(1, count, width), (1, count, width), (0, 0, 0)

    skip_top, skip_bottom = (weight(early, 0, skip_rows, i * width, width) for i in range(2))
    out_weight = weight(middle, 3 * out_rows, out_rows, 0, width)
    def own_qkv(gathered):
        parts = []
        for i in range(3):
            whole = gathered[:, i * out_rows : (i + 1) * out_rows].reshape(width, width)
            parts.append(lax.dynamic_slice_in_dim(whole, member * heads_wide, heads_wide, 1))
        return jnp.concatenate(parts, axis=1)

    mine_column, mine_row = mine[:, None], mine[None, :]
    shift_one, scale_one, shift_two, scale_two = (modulation[:, i] for i in range(4))

    x, s = (v.reshape(frames, width) for v in (inputs, skips))
    (resid_in,) = rowwise(
        merge_kernel, frames, [("", x), ("", s), ("weight", skip_top), ("weight", skip_bottom)], [(width, bf16)], light=True
    )
    resid_in = to_rows(resid_in.reshape(inputs.shape))
    resid_in, late, cotangent, modulation, cosine, sine, ranges = lax.optimization_barrier(
        (resid_in, late, cotangent, modulation, cosine, sine, ranges)
    )
    (normed_one,) = rowwise(
        norm_kernel,
        frames,
        [("", resid_in), ("", mine_column), ("whole", shift_one), ("whole", scale_one)],
        [(width, bf16)],
        light=True,
    )
    normed_row = frames_to_row(normed_one)
    if in_place:
        projected = project(normed_row, middle, 0, out_rows, heads_wide, member)
    else:
        projected = jnp.dot(normed_row, own_qkv(middle), preferred_element_type=f32).astype(bf16)
    late = gather_planes(late)
    cot = to_rows(cotangent)
    if in_place:
        per = width // chunk
        up_weight = (late, (devices, up_rows, chunk), lambda j: (0, down_rows // up_rows + j // per, j % per))
        down_weight = (late, (chunk // down_rows, down_rows, width), lambda j: (j, 0, 0))
    else:
        pieces = [late[:, down_rows + i * up_rows : down_rows + (i + 1) * up_rows] for i in range(columns)]
        up_full = jnp.concatenate([v.reshape(width, width) for v in pieces], axis=1)
        up_weight = (up_full[None], (1, width, chunk), lambda j: (0, 0, j))
        down_weight = (late[:, :down_rows].reshape(1, -1, width), (1, chunk, width), lambda j: (0, j, 0))
    mixed_heads, queries, keys, logsum = attend_forward(ranges, projected, cosine, sine, seg_column, seg_row)
    mixed = heads_to_frames(mixed_heads)
    resid_mid, normed_two = rowwise(
        out_norm_kernel,
        frames,
        [("", mixed), ("weight", out_weight), ("", resid_in), ("", mine_column), ("whole", shift_two), ("whole", scale_two)],
        [(width, f32), (width, bf16)],
        flops=2 * frames * width * width,
    )
    result, grad_normed_two, grad_up, own_down, other_down = feed_forward_and_back(
        core, normed_two, cot, resid_mid, hidden, chunk, up_weight, down_weight, planes
    )

    def over_cores(kept, axis):
        other = lax.ppermute(lax.dynamic_index_in_dim(kept, 1 - core, axis, False), "core", swap)
        own = lax.dynamic_index_in_dim(kept, core, axis, False)
        return (own.astype(f32) + other.astype(f32)).astype(bf16)

    plane = lax.axis_index("plane")

    def exchange(value, axes, here, count):
        total = lax.dynamic_index_in_dim(value, here, 0, False).astype(f32)
        for flip in range(1, count):
            sent = lax.dynamic_index_in_dim(value, here ^ flip, 0, False)
            total += lax.ppermute(sent, axes, [(i, i ^ flip) for i in range(count)]).astype(f32)
        return total

    def exchange_planes(value):
        return exchange(value, "plane", plane, planes).astype(bf16)

    def exchange_line(value):
        return exchange(value.reshape(line, -1, value.shape[-1]), ("hi", "lo"), place, line)

    def add_other(own, other):
        return (own.astype(f32) + lax.ppermute(other, "core", swap).astype(f32)).astype(bf16)

    grad_up = lax.psum_scatter(grad_up, ("plane", "core"), scatter_dimension=0, tiled=True)
    grad_down = add_other(own_down, other_down)

    grad_mid, grad_mid_low, grad_frames, grad_shift_two, grad_scale_two = rowwise(
        norm_two_back_kernel,
        frames,
        [("", grad_normed_two), ("", resid_mid), ("", cot), ("", mine_column), ("row", mine_row),
         ("whole", scale_two), ("weight", out_weight)],
        [(width, f32), (width, bf16), (width, bf16)],
        sums=2,
        light=True,
    )
    grad_heads = frames_to_heads(grad_frames)
    grad_out = lax.dot_general(mixed, grad_mid_low, (((0,), (0,)), ((), ())), preferred_element_type=f32)
    grad_out = over_cores(grad_out.astype(bf16).reshape(planes, 2, -1, width), 1)
    grad_down = jnp.concatenate(
        [v.reshape(planes, line, -1, width) for v in (grad_down, grad_out)], axis=2
    )
    grad_heads, grad_down, result = lax.optimization_barrier((grad_heads, grad_down, result))
    block_out = from_rows(result)
    grad_down = exchange_planes(grad_down.reshape(planes, -1, width))
    grad_proj = attend_backward(
        ranges, queries, keys, projected, mixed_heads, grad_heads, logsum, cosine, sine, seg_column, seg_row
    )
    grad_proj, grad_up, grad_down, block_out = lax.optimization_barrier((grad_proj, grad_up, grad_down, block_out))
    grad_down = jnp.concatenate(
        [grad_up[:, i * width : (i + 1) * width].reshape(line, -1, width) for i in range(columns)]
        + [grad_down.reshape(line, -1, width)],
        axis=1,
    )
    grad_down = lax.psum_scatter(grad_down.reshape(-1, width), ("hi", "lo"), scatter_dimension=0, tiled=True)
    grad_qkv = lax.dot_general(normed_row, grad_proj, (((0,), (0,)), ((), ())), preferred_element_type=f32)
    grad_qkv = grad_qkv.astype(bf16)
    grad_proj, grad_qkv = lax.optimization_barrier((grad_proj, grad_qkv))
    if group > 2:
        grad_qkv = grad_qkv.reshape(planes, 2, highs, lows, -1, 3, 1, heads_wide)
        grad_qkv = jnp.moveaxis(grad_qkv, (1, 3), (0, 1)).reshape(group, -1, 3, 1, heads_wide)
        grad_qkv = lax.all_to_all(grad_qkv, ROW_AXES, split_axis=0, concat_axis=3, tiled=True)
        grad_qkv = grad_qkv.reshape(-1, 3 * width)
        partial = dot_nt(grad_proj, own_qkv(middle)).astype(bf16)
        grad_one = lax.psum_scatter(partial, ROW_AXES, scatter_dimension=0, tiled=True).astype(f32)
        grad_one_other = jnp.zeros((frames, width), bf16)
    else:
        split = grad_qkv.reshape(planes, 2, -1, 3 * heads_wide)
        other = lax.ppermute(lax.dynamic_index_in_dim(split, 1 - core, 1, False), "core", swap)
        own = lax.dynamic_index_in_dim(split, core, 1, False)
        own, other = (v.reshape(-1, 3 * heads_wide) for v in (own, other))
        left, right = jnp.where(first_core, own, other), jnp.where(first_core, other, own)
        grad_qkv = jnp.concatenate(
            [v[:, i * heads_wide : (i + 1) * heads_wide] for i in range(3) for v in (left, right)], axis=1
        )
        if in_place:
            pull = functools.partial(pull_project, grad_proj, middle, out_rows, heads_wide, member, frames)
            away, home = pull(1 - core, bf16), pull(core, f32)
        else:
            qkv_own = own_qkv(middle)
            away = lax.dynamic_slice_in_dim(grad_proj, (1 - core) * frames, frames, 0)
            home = lax.dynamic_slice_in_dim(grad_proj, core * frames, frames, 0)
            away, home = dot_nt(away, qkv_own).astype(bf16), dot_nt(home, qkv_own)
        grad_one_other = lax.ppermute(away, "core", swap)
        grad_one = home
    grad_one, grad_qkv = lax.optimization_barrier((grad_one, grad_qkv))
    if group > 2:
        grad_qkv = lax.psum_scatter(grad_qkv, ("plane", "hi"), scatter_dimension=0, tiled=True).astype(f32)
    else:
        grad_qkv = grad_qkv.reshape(planes, -1, 3 * width)
        grad_qkv = lax.all_to_all(grad_qkv, "plane", split_axis=0, concat_axis=0, tiled=True)
        grad_qkv = jnp.sum(grad_qkv.astype(f32), axis=0).astype(bf16)
    grad_in, grad_shift_one, grad_scale_one = rowwise(
        norm_one_back_kernel,
        frames,
        [("", grad_one), ("", grad_one_other), ("", resid_in), ("", grad_mid), ("", mine_column), ("row", mine_row),
         ("whole", scale_one)],
        [(width, bf16)],
        sums=2,
    )
    grad_in_home = from_rows(grad_in)
    grad_in_home, grad_qkv, grad_down = lax.optimization_barrier((grad_in_home, grad_qkv, grad_down))
    if group == 2:
        grad_qkv = grad_qkv.reshape(line, -1, 3 * width)
        grad_qkv = lax.all_to_all(grad_qkv, ("hi", "lo"), split_axis=0, concat_axis=0, tiled=True)
        grad_qkv = jnp.sum(grad_qkv.astype(f32), axis=0)
    home = grad_in_home.reshape(frames, width)
    grad_skip_w = jnp.concatenate(
        [
            lax.dot_general(v, home, (((0,), (0,)), ((), ())), preferred_element_type=f32).astype(bf16)
            for v in (x, s)
        ],
        axis=0,
    )
    grad_skip_w = exchange_planes(over_cores(grad_skip_w.reshape(planes, 2, -1, width), 1))
    grad_inputs, grad_skips = rowwise(
        unmerge_kernel,
        frames,
        [("", home), ("weight", skip_top), ("weight", skip_bottom)],
        [(width, bf16), (width, bf16)],
        flops=4 * frames * width * width,
    )
    grad_inputs, grad_skips = (v.reshape(grad_in_home.shape) for v in (grad_inputs, grad_skips))

    grad_shift_one, grad_skip_w = lax.optimization_barrier((grad_shift_one, grad_skip_w))
    grad_skip_w = exchange_line(grad_skip_w)
    grad_mod = jnp.stack([v[:labels] for v in (grad_shift_one, grad_scale_one, grad_shift_two, grad_scale_two)], axis=1)
    grad_mod = jnp.moveaxis(grad_mod.reshape(labels, devices, own_columns), 1, 0)
    grad_mod = lax.all_to_all(grad_mod, ALL_AXES, split_axis=0, concat_axis=0, tiled=True)
    grad_inputs, grad_mod, grad_skip_w = lax.optimization_barrier((grad_inputs, grad_mod, grad_skip_w))
    taken = columns * up_rows
    grad_down = grad_down.astype(f32)
    grad_up = jnp.concatenate([grad_down[i * up_rows : (i + 1) * up_rows] for i in range(columns)], axis=1)
    grad_down, grad_out = grad_down[taken : taken + down_rows], grad_down[taken + down_rows :]
    grad_mod = jnp.sum(grad_mod.reshape(planes, 2, highs, lows, labels, own_columns), axis=(1, 3))
    grad_mod = lax.dot_general(
        embedded.astype(f32),
        grad_mod.reshape(-1, own_columns),
        (((0,), (0,)), ((), ())),
        precision=lax.Precision.HIGHEST,
        preferred_element_type=f32,
    )
    return (
        block_out,
        grad_inputs,
        grad_skips,
        grad_skip_w,
        grad_qkv,
        grad_out,
        grad_up,
        grad_down,
        grad_mod,
    )


def solution(mesh):
    batch, wide = mesh.devices.shape

    def run(inputs, *rest):
        rows = 2 * inputs.shape[0]
        assert inputs.shape[0] == 2 and inputs.shape[1] == batch and wide % rows == 0
        fine = Mesh(mesh.devices.reshape(batch // 2, 2, rows, wide // rows), ALL_AXES)
        by_batch, by_wide = ("plane", "core"), ("hi", "lo")
        frames = P(None, by_batch, by_wide, None)
        rowed = P(None, by_batch, None)
        weight, columns = P(ALL_AXES, None), P(None, ALL_AXES)
        mapped = jax.shard_map(
            body,
            mesh=fine,
            in_specs=(frames, frames, frames, rowed, rowed) + (weight,) * 5 + (columns,),
            out_specs=(frames, frames, frames) + (weight,) * 5 + (columns,),
            check_vma=False,
        )
        return mapped(inputs, *rest)

    return run
```

```python
import functools
import math

import jax
import jax.numpy as jnp
from jax import lax
from jax.experimental import pallas as pl
from jax.experimental.pallas import tpu as pltpu
from jax.sharding import Mesh
from jax.sharding import PartitionSpec as P

HEAD_DIM = 64
TILE = 128
BLOCK = 256
ROW_TILE = 256
FEED_TILE = 1024
FEED_PART = 512
VMEM_BYTES = 60 * 1024 * 1024
ROW_AXES = ("core", "lo")
LINE_AXES = ("core", "hi", "lo")
ALL_AXES = ("plane", "core", "hi", "lo")
f32 = jnp.float32
bf16 = jnp.bfloat16


def dot_nn(left, right):
    return lax.dot_general(left, right, (((1,), (0,)), ((), ())), preferred_element_type=f32)


def dot_nt(left, right):
    return lax.dot_general(left, right, (((1,), (1,)), ((), ())), preferred_element_type=f32)


def dot_tn(left, right):
    return lax.dot_general(left, right, (((0,), (0,)), ((), ())), preferred_element_type=f32)


def params(*semantics):
    return pltpu.CompilerParams(dimension_semantics=semantics, vmem_limit_bytes=VMEM_BYTES)


def cost(flops, moved, special=0):
    return pl.CostEstimate(flops=int(flops), bytes_accessed=int(moved), transcendentals=int(special))


def flat(ref):
    return ref[...].reshape(-1, ref.shape[-1])


def choose(segment_column, table_ref):
    count = table_ref.shape[0]
    picked = table_ref[count - 1 : count, :]
    for label in range(count - 2, -1, -1):
        picked = jnp.where(segment_column == label, table_ref[label : label + 1, :], picked)
    return picked


def normalise(values):
    centred = values - jnp.mean(values, axis=-1, keepdims=True)
    variance = jnp.mean(centred * centred, axis=-1, keepdims=True)
    inverse = lax.rsqrt(variance + 1e-06)
    return centred * inverse, inverse


def merge_kernel(x_ref, s_ref, top_ref, bottom_ref, resid_ref):
    resid = dot_nn(x_ref[...], flat(top_ref)) + dot_nn(s_ref[...], flat(bottom_ref))
    resid_ref[...] = resid.astype(bf16)


def norm_kernel(resid_ref, seg_ref, shift_ref, scale_ref, normed_ref):
    unit, _ = normalise(resid_ref[...].astype(f32))
    label = seg_ref[...]
    normed = unit * (1.0 + choose(label, scale_ref)) + choose(label, shift_ref)
    normed_ref[...] = normed.astype(bf16)


def out_norm_kernel(mixed_ref, w_ref, resid_in_ref, seg_ref, shift_ref, scale_ref, resid_ref, normed_ref):
    resid = resid_in_ref[...].astype(f32) + dot_nn(mixed_ref[...], flat(w_ref))
    resid_ref[...] = resid
    unit, _ = normalise(resid)
    label = seg_ref[...]
    normed = unit * (1.0 + choose(label, scale_ref)) + choose(label, shift_ref)
    normed_ref[...] = normed.astype(bf16)


def segment_sums(row_labels, values, total_ref):
    members = lax.broadcasted_iota(jnp.int32, (total_ref.shape[0], row_labels.shape[1]), 0) == row_labels
    members = members.astype(f32).astype(bf16)
    high = values.astype(bf16)
    low = (values - high.astype(f32)).astype(bf16)
    total_ref[...] += dot_nn(members, high) + dot_nn(members, low)


def norm_pull(grad, resid, scale):
    unit, inverse = normalise(resid)
    inner = grad * (1.0 + scale)
    pulled = inverse * (
        inner
        - jnp.mean(inner, axis=-1, keepdims=True)
        - unit * jnp.mean(inner * unit, axis=-1, keepdims=True)
    )
    return pulled, grad * unit


def norm_two_back_kernel(
    g_ref, resid_ref, cot_ref, seg_ref, segr_ref, scale_ref, w_ref, mid_ref, low_ref, mix_ref, dshift_ref, dscale_ref
):
    @pl.when(pl.program_id(0) == 0)
    def _():
        dshift_ref[...] = jnp.zeros_like(dshift_ref)
        dscale_ref[...] = jnp.zeros_like(dscale_ref)

    grad = g_ref[...]
    pulled, by_scale = norm_pull(grad, resid_ref[...], choose(seg_ref[...], scale_ref))
    grad_mid = cot_ref[...].astype(f32) + pulled
    low = grad_mid.astype(bf16)
    mid_ref[...] = grad_mid
    low_ref[...] = low
    mix_ref[...] = dot_nt(low, flat(w_ref)).astype(bf16)
    segment_sums(segr_ref[...], grad, dshift_ref)
    segment_sums(segr_ref[...], by_scale, dscale_ref)


def norm_one_back_kernel(
    own_ref, other_ref, resid_ref, mid_ref, seg_ref, segr_ref, scale_ref, grad_ref, dshift_ref, dscale_ref
):
    @pl.when(pl.program_id(0) == 0)
    def _():
        dshift_ref[...] = jnp.zeros_like(dshift_ref)
        dscale_ref[...] = jnp.zeros_like(dscale_ref)

    grad = own_ref[...] + other_ref[...].astype(f32)
    pulled, by_scale = norm_pull(grad, resid_ref[...].astype(f32), choose(seg_ref[...], scale_ref))
    grad_ref[...] = (mid_ref[...] + pulled).astype(bf16)
    segment_sums(segr_ref[...], grad, dshift_ref)
    segment_sums(segr_ref[...], by_scale, dscale_ref)


def unmerge_kernel(g_ref, top_ref, bottom_ref, inputs_ref, skips_ref):
    inputs_ref[...] = dot_nt(g_ref[...], flat(top_ref)).astype(bf16)
    skips_ref[...] = dot_nt(g_ref[...], flat(bottom_ref)).astype(bf16)


def project_kernel(place_ref, x_ref, w_ref, out_ref):
    out_ref[...] = dot_nn(x_ref[...], flat(w_ref)).astype(bf16)


def project(value, gathered, begin, rows, heads_wide, member):
    length, width = value.shape
    tile = min(8 * ROW_TILE, length)
    return pl.pallas_call(
        project_kernel,
        grid_spec=pltpu.PrefetchScalarGridSpec(
            num_scalar_prefetch=1,
            grid=(3, length // tile),
            in_specs=[
                pl.BlockSpec((tile, width), lambda t, i, r: (i, 0)),
                pl.BlockSpec((width // rows, rows, heads_wide), lambda t, i, r: (0, begin // rows + t, r[0])),
            ],
            out_specs=pl.BlockSpec((tile, heads_wide), lambda t, i, r: (i, t)),
        ),
        out_shape=jax.ShapeDtypeStruct((length, 3 * heads_wide), bf16),
        compiler_params=params("arbitrary", "arbitrary"),
        cost_estimate=cost(1, 1),
    )(member.reshape(1), value, gathered)


def pull_project_kernel(place_ref, dq_ref, dk_ref, dv_ref, q_ref, k_ref, v_ref, out_ref):
    total = dot_nt(dq_ref[...], flat(q_ref))
    total += dot_nt(dk_ref[...], flat(k_ref))
    total += dot_nt(dv_ref[...], flat(v_ref))
    out_ref[...] = total.astype(out_ref.dtype)


def pull_project(grad_proj, gathered, rows, heads_wide, member, frames, half, kind):
    width = gathered.shape[2]
    tile = min(2 * ROW_TILE, frames)
    steps = frames // tile
    grads = [
        pl.BlockSpec((tile, heads_wide), functools.partial(lambda t, i, r: (r[1] * steps + i, t), t)) for t in range(3)
    ]
    weights = [
        pl.BlockSpec((width // rows, rows, heads_wide), functools.partial(lambda t, i, r: (0, t, r[0]), t))
        for t in range(3)
    ]
    return pl.pallas_call(
        pull_project_kernel,
        grid_spec=pltpu.PrefetchScalarGridSpec(
            num_scalar_prefetch=1,
            grid=(steps,),
            in_specs=grads + weights,
            out_specs=pl.BlockSpec((tile, width), lambda i, r: (i, 0)),
        ),
        out_shape=jax.ShapeDtypeStruct((frames, width), kind),
        compiler_params=params("arbitrary"),
        cost_estimate=cost(6 * frames * width * heads_wide, 8 * frames * width),
    )(jnp.stack([member, half]).astype(jnp.int32), *[grad_proj] * 3, *[gathered] * 3)


def rowwise(kernel, frames, blocked, outs, sums=0, flops=0, light=False):
    tile = min(ROW_TILE, frames)
    in_specs, args, moved = [], [], 0
    for kind, value in blocked:
        if kind == "row":
            in_specs.append(pl.BlockSpec((1, tile), lambda i: (0, i)))
        elif kind == "weight":
            value, block, index = value
            in_specs.append(pl.BlockSpec(block, functools.partial(lambda index, i: index, index)))
        elif kind == "whole":
            in_specs.append(pl.BlockSpec(value.shape, lambda i: (0, 0)))
        else:
            in_specs.append(pl.BlockSpec((tile, value.shape[1]), lambda i: (i, 0)))
        args.append(value)
        moved += value.size * value.dtype.itemsize
    out_specs, shapes = [], []
    for width, kind in outs:
        out_specs.append(pl.BlockSpec((tile, width), lambda i: (i, 0)))
        shapes.append(jax.ShapeDtypeStruct((frames, width), kind))
        moved += frames * width * jnp.dtype(kind).itemsize
    for _ in range(sums):
        out_specs.append(pl.BlockSpec((8, outs[0][0]), lambda i: (0, 0)))
        shapes.append(jax.ShapeDtypeStruct((8, outs[0][0]), f32))
    return pl.pallas_call(
        kernel,
        grid=(frames // tile,),
        in_specs=in_specs,
        out_specs=out_specs,
        out_shape=shapes,
        compiler_params=params("arbitrary"),
        cost_estimate=cost(1, 1) if light else cost(flops, moved),
    )(*args)


def swap_halves(values, lanes):
    half = HEAD_DIM // 2
    ahead = pltpu.roll(values, values.shape[1] - half, 1)
    behind = pltpu.roll(values, half, 1)
    return jnp.where(lanes % HEAD_DIM < half, ahead, behind)


def widen(table, width):
    return jnp.concatenate([table] * (width // table.shape[1]), axis=1)


def span(i):
    return pl.ds(pl.multiple_of(i * BLOCK, BLOCK), BLOCK)


def own_lanes(parts, lanes):
    picked = parts[0]
    for h in range(1, len(parts)):
        picked = jnp.where(lanes // HEAD_DIM == h, parts[h], picked)
    return picked


def by_count(count, most, run):
    for each in range(1, most + 1):
        pl.when(count == each)(functools.partial(run, each))


def attend_forward_kernel(
    range_ref, q_ref, k_ref, v_ref, cos_ref, sin_ref, segc_ref, segr_ref,
    out_ref, qrot_ref, krot_ref, lse_ref, seg_wide,
):
    length, width = q_ref.shape
    heads = width // HEAD_DIM
    blocks = length // BLOCK
    lanes = lax.broadcasted_iota(jnp.int32, (BLOCK, width), 1)

    def turn(i, carry):
        rows = span(i)
        cosine, sine = widen(cos_ref[rows, :], width), widen(sin_ref[rows, :], width)
        for source, target, factor in ((q_ref, qrot_ref, HEAD_DIM**-0.5), (k_ref, krot_ref, None)):
            values = source[rows, :].astype(f32)
            turned = (values * cosine + swap_halves(values, lanes) * sine).astype(bf16)
            if factor is not None:
                turned = turned * jnp.asarray(factor, bf16)
            target[rows, :] = turned
        seg_wide[rows, :] = jnp.broadcast_to(segc_ref[rows, :], (BLOCK, TILE))
        return carry

    lax.fori_loop(0, blocks, turn, 0)

    def one_query(i, carry):
        rows = span(i)

        def work(count):
            keys = pl.ds(pl.multiple_of(range_ref[0, i] * BLOCK, BLOCK), count * BLOCK)
            allowed = widen(seg_wide[rows, :], count * BLOCK) == segr_ref[:, keys]
            query = qrot_ref[rows, :]
            zero = jnp.zeros_like(query)
            mixed = []
            for h in range(heads):
                scores = dot_nt(jnp.where(lanes // HEAD_DIM == h, query, zero), krot_ref[keys, :])
                scores = jnp.where(allowed, scores, -1e30)
                highest = jnp.max(scores, axis=1, keepdims=True)
                powers = jnp.exp(scores - highest)
                totals = jnp.sum(powers, axis=1, keepdims=True)
                mixed.append(dot_nn(powers.astype(bf16), v_ref[keys, :]) * (1.0 / totals))
                logsum = jnp.broadcast_to(highest + jnp.log(totals), (BLOCK, TILE))
                lse_ref[0, h : h + 1, rows] = logsum.T[0:1]
            out_ref[rows, :] = own_lanes(mixed, lanes).astype(bf16)

        by_count(range_ref[1, i] - range_ref[0, i], blocks, work)
        return carry

    lax.fori_loop(0, blocks, one_query, 0)


def attend_forward(ranges, projected, cosine, sine, seg_column, seg_row):
    length, width = projected.shape
    width //= 3
    panels, heads = width // TILE, TILE // HEAD_DIM
    panel = lambda shift: pl.BlockSpec((length, TILE), lambda p, r: (0, shift * panels + p))
    whole = lambda shape: pl.BlockSpec(shape, lambda p, r: (0,) * len(shape))
    return pl.pallas_call(
        attend_forward_kernel,
        grid_spec=pltpu.PrefetchScalarGridSpec(
            num_scalar_prefetch=1,
            grid=(panels,),
            in_specs=[panel(0), panel(1), panel(2), whole(cosine.shape), whole(sine.shape),
                      whole(seg_column.shape), whole(seg_row.shape)],
            out_specs=[panel(0), panel(0), panel(0), pl.BlockSpec((1, heads, length), lambda p, r: (p, 0, 0))],
            scratch_shapes=[pltpu.VMEM((length, TILE), jnp.int32)],
        ),
        out_shape=[jax.ShapeDtypeStruct((length, width), bf16)] * 3
        + [jax.ShapeDtypeStruct((panels, heads, length), f32)],
        compiler_params=params("arbitrary"),
        cost_estimate=cost(8 * length * length * width, 14 * length * width, length * length * width // HEAD_DIM),
    )(ranges, projected, projected, projected, cosine, sine, seg_column, seg_row)


def attend_backward_kernel(
    range_ref, q_ref, k_ref, v_ref, out_ref, do_ref, lse_ref, cos_ref, sin_ref, segc_ref, segr_ref,
    grad_ref, dq, dk_low, dv_low, delta, seg_wide,
):
    length, width = q_ref.shape
    heads = width // HEAD_DIM
    blocks = length // BLOCK
    step = pl.program_id(1)

    @pl.when(step == 0)
    def _():
        lanes = lax.broadcasted_iota(jnp.int32, (BLOCK, width), 1)
        picker = (
            lax.broadcasted_iota(jnp.int32, (8, width), 0)
            == lax.broadcasted_iota(jnp.int32, (8, width), 1) // HEAD_DIM
        ).astype(f32)

        def prepare(i, carry):
            rows = span(i)
            product = do_ref[rows, :].astype(f32) * out_ref[rows, :].astype(f32)
            delta[:, rows] = lax.dot_general(
                picker, product, (((1,), (1,)), ((), ())),
                precision=lax.Precision.HIGHEST, preferred_element_type=f32,
            )
            dq[:, rows] = jnp.zeros((width, BLOCK), f32)
            seg_wide[rows, :] = jnp.broadcast_to(segc_ref[rows, :], (BLOCK, TILE))
            return carry

        lax.fori_loop(0, blocks, prepare, 0)

        def unturn(values, rows):
            return values * widen(cos_ref[rows, :], width) - swap_halves(values, lanes) * widen(sin_ref[rows, :], width)

        def one_key(j, carry):
            rows = span(j)

            def work(count):
                there = pl.ds(pl.multiple_of(range_ref[0, j] * BLOCK, BLOCK), count * BLOCK)
                allowed = widen(seg_wide[rows, :], count * BLOCK) == segr_ref[:, there]
                zero = jnp.zeros((BLOCK, width), bf16)
                key, value = (
                    jnp.concatenate([jnp.where(lanes // HEAD_DIM == h, ref[rows, :], zero) for h in range(heads)], axis=0)
                    for ref in (k_ref, v_ref)
                )
                query, grad_out = q_ref[there, :], do_ref[there, :]
                found, grad_prob = dot_nt(key, query), dot_nt(value, grad_out)
                parts, lows = [], []
                for h in range(heads):
                    half = slice(h * BLOCK, (h + 1) * BLOCK)
                    scores = found[half] - lse_ref[0, h : h + 1, there]
                    part = jnp.exp(jnp.where(allowed, scores, -1e30))
                    parts.append(part.astype(bf16))
                    lows.append((part * (grad_prob[half] - delta[h : h + 1, there])).astype(bf16))
                grad_scores = jnp.concatenate(lows, axis=0)
                grad_v = dot_nn(jnp.concatenate(parts, axis=0), grad_out)
                grad_k = dot_nn(grad_scores, query)
                grad_v, grad_k = ([v[h * BLOCK : (h + 1) * BLOCK] for h in range(heads)] for v in (grad_v, grad_k))
                dq[:, there] += dot_tn(key, grad_scores)
                dk_low[rows, :] = unturn(own_lanes(grad_k, lanes), rows).astype(bf16)
                dv_low[rows, :] = own_lanes(grad_v, lanes).astype(bf16)

            by_count(range_ref[1, j] - range_ref[0, j], blocks, work)
            return carry

        lax.fori_loop(0, blocks, one_key, 0)

        def finish(i, carry):
            rows = span(i)
            grad_ref[rows, :] = unturn(dq[:, rows].T * HEAD_DIM**-0.5, rows).astype(bf16)
            return carry

        lax.fori_loop(0, blocks, finish, 0)

    @pl.when(step == 1)
    def _():
        grad_ref[...] = dk_low[...]

    @pl.when(step == 2)
    def _():
        grad_ref[...] = dv_low[...]


def attend_backward(ranges, queries, keys, projected, mixed, grad_mixed, logsum, cosine, sine, seg_column, seg_row):
    length, width = queries.shape
    panels, heads = width // TILE, TILE // HEAD_DIM
    panel = lambda shift: pl.BlockSpec((length, TILE), lambda p, t, r: (0, shift * panels + p))
    whole = lambda shape: pl.BlockSpec(shape, lambda p, t, r: (0,) * len(shape))
    return pl.pallas_call(
        attend_backward_kernel,
        grid_spec=pltpu.PrefetchScalarGridSpec(
            num_scalar_prefetch=1,
            grid=(panels, 3),
            in_specs=[panel(0), panel(0), panel(2), panel(0), panel(0),
                      pl.BlockSpec((1, heads, length), lambda p, t, r: (p, 0, 0)),
                      whole(cosine.shape), whole(sine.shape), whole(seg_column.shape), whole(seg_row.shape)],
            out_specs=pl.BlockSpec((length, TILE), lambda p, t, r: (0, t * panels + p)),
            scratch_shapes=[
                pltpu.VMEM((TILE, length), f32),
                pltpu.VMEM((length, TILE), bf16),
                pltpu.VMEM((length, TILE), bf16),
                pltpu.VMEM((8, length), f32),
                pltpu.VMEM((length, TILE), jnp.int32),
            ],
        ),
        out_shape=jax.ShapeDtypeStruct((length, 3 * width), bf16),
        compiler_params=params("arbitrary", "arbitrary"),
        cost_estimate=cost(20 * length * length * width, 16 * length * width, length * length * width // HEAD_DIM),
    )(ranges, queries, keys, projected, mixed, grad_mixed, logsum, cosine, sine, seg_column, seg_row)


def gelu_and_slope(x):
    root = math.sqrt(2.0 / math.pi)
    square = x * x
    bend = jnp.tanh(x * (root + root * 0.044715 * square))
    half = 0.5 * x
    half_up = 0.5 + 0.5 * bend
    slope = half_up + half * (1.0 - bend * bend) * (root + 3.0 * root * 0.044715 * square)
    return half + half * bend, slope


def feed_kernel(
    n_ref, cot_ref, resid_ref, up_ref, down_ref, out_ref, back_ref, gup_ref, gdown_ref,
    total, n_turned, act_turned, pre,
):
    step, last = pl.program_id(0), pl.num_programs(0) - 1
    frames, width = n_ref.shape
    tile = min(FEED_TILE, frames)

    def rows_of(i):
        return pl.ds(pl.multiple_of(i * tile, tile), tile)

    @pl.when(step == 0)
    def _():
        def turn(i, carry):
            rows = rows_of(i)
            n_turned[:, rows] = n_ref[rows, :].T
            total[rows, :] = resid_ref[rows, :]
            back_ref[rows, :] = jnp.zeros((tile, width), f32)
            return carry

        lax.fori_loop(0, frames // tile, turn, 0)

    def chunk(i, carry):
        rows = rows_of(i)
        up, down = flat(up_ref), flat(down_ref)
        hidden = dot_nn(n_ref[rows, :], up)
        grad_act = dot_nt(cot_ref[rows, :], down)
        activated, slope = gelu_and_slope(hidden)
        activated = activated.astype(bf16)
        grad_pre = (grad_act * slope).astype(bf16)
        act_turned[:, rows] = activated.T
        pre[rows, :] = grad_pre
        total[rows, :] += dot_nn(activated, down)
        back_ref[rows, :] += dot_nt(grad_pre, up)
        return carry

    lax.fori_loop(0, frames // tile, chunk, 0)

    for begin in range(0, width, FEED_PART):
        rows = slice(begin, begin + FEED_PART)
        gup_ref[rows, :] = dot_nn(n_turned[rows, :], pre[...]).astype(bf16)
    piece = act_turned.shape[0]
    for begin in range(0, piece, FEED_PART):
        rows = slice(begin, begin + FEED_PART)
        gdown_ref[rows, :] = dot_nn(act_turned[rows, :], cot_ref[...]).astype(bf16)

    @pl.when(step == last)
    def _():
        out_ref[...] = total[...].astype(bf16)


def feed_forward_and_back(normed, cot, resid, hidden, piece, w_up, w_down):
    frames, width = normed.shape
    whole = lambda: pl.BlockSpec((frames, width), lambda j: (0, 0), pipeline_mode=pl.Buffered(1))
    return pl.pallas_call(
        feed_kernel,
        grid=(hidden // piece,),
        in_specs=[whole(), whole(), whole(), pl.BlockSpec(*w_up[1:]), pl.BlockSpec(*w_down[1:])],
        out_specs=[pl.BlockSpec((frames, width), lambda j: (0, 0))] * 2
        + [pl.BlockSpec((width, piece), lambda j: (0, j)), pl.BlockSpec((piece, width), lambda j: (j, 0))],
        out_shape=[
            jax.ShapeDtypeStruct((frames, width), bf16),
            jax.ShapeDtypeStruct((frames, width), f32),
            jax.ShapeDtypeStruct((width, hidden), bf16),
            jax.ShapeDtypeStruct((hidden, width), bf16),
        ],
        scratch_shapes=[
            pltpu.VMEM((frames, width), f32),
            pltpu.VMEM((width, frames), bf16),
            pltpu.VMEM((piece, frames), bf16),
            pltpu.VMEM((frames, piece), bf16),
        ],
        compiler_params=params("arbitrary"),
        cost_estimate=cost(12 * frames * width * hidden, 8 * width * hidden + 16 * frames * width, frames * hidden),
    )(normed, cot, resid, w_up[0], w_down[0])


def body(inputs, skips, cotangent, segment_ids, time_steps, w_skip, w_qkv, w_out, w_up, w_down, w_mod):
    micro, _, piece, width = inputs.shape
    length = segment_ids.shape[-1]
    labels = time_steps.shape[-1]
    planes, lows, highs = lax.axis_size("plane"), lax.axis_size("lo"), lax.axis_size("hi")
    line = highs * lows
    group = 2 * lows
    devices = planes * 2 * line
    core, high, low = lax.axis_index("core"), lax.axis_index("hi"), lax.axis_index("lo")
    place = high * lows + low
    member = core * lows + low
    frames = 2 * piece
    heads_wide = width // group
    first_core = core == 0
    swap = [(0, 1), (1, 0)]

    def route(parity):
        pairs = []
        for c in range(2):
            for z in range(line):
                row = c * micro + ((z % 2) ^ parity)
                to_core, to_low = divmod(z // 2, lows)
                pairs.append((c * line + z, (to_core * highs + row) * lows + to_low))
        return pairs

    there = (route(0), route(1))
    back = tuple([(b, a) for a, b in pairs] for pairs in there)
    odd_place = place % 2
    even_row = high % 2 == 0

    def to_rows(value):
        value = value[:, 0]
        near = lax.ppermute(lax.dynamic_index_in_dim(value, odd_place, 0, False), LINE_AXES, there[0])
        far = lax.ppermute(lax.dynamic_index_in_dim(value, 1 - odd_place, 0, False), LINE_AXES, there[1])
        return jnp.concatenate([jnp.where(even_row, near, far), jnp.where(even_row, far, near)], axis=0)

    def from_rows(value):
        value = value.reshape(2, piece, width)
        near = lax.ppermute(lax.dynamic_index_in_dim(value, high % 2, 0, False), LINE_AXES, back[0])
        far = lax.ppermute(lax.dynamic_index_in_dim(value, 1 - high % 2, 0, False), LINE_AXES, back[1])
        even = odd_place == 0
        return jnp.stack([jnp.where(even, near, far), jnp.where(even, far, near)])[:, None]

    def frames_to_row(value):
        if group > 2:
            return lax.all_gather(value, ROW_AXES, axis=0, tiled=True)
        other = lax.ppermute(value, "core", swap)
        return jnp.concatenate([jnp.where(first_core, value, other), jnp.where(first_core, other, value)], axis=0)

    def heads_to_frames(value):
        if group > 2:
            return lax.all_to_all(value, ROW_AXES, split_axis=0, concat_axis=1, tiled=True)
        other = lax.ppermute(lax.dynamic_slice_in_dim(value, (1 - core) * frames, frames, 0), "core", swap)
        own = lax.dynamic_slice_in_dim(value, core * frames, frames, 0)
        return jnp.concatenate([jnp.where(first_core, own, other), jnp.where(first_core, other, own)], axis=1)

    def frames_to_heads(value):
        if group > 2:
            return lax.all_to_all(value, ROW_AXES, split_axis=1, concat_axis=0, tiled=True)
        other = lax.ppermute(lax.dynamic_slice_in_dim(value, (1 - core) * heads_wide, heads_wide, 1), "core", swap)
        own = lax.dynamic_slice_in_dim(value, core * heads_wide, heads_wide, 1)
        return jnp.concatenate([jnp.where(first_core, own, other), jnp.where(first_core, other, own)], axis=0)

    def share_on_line(value):
        pieces = [value]
        for flip in range(1, line):
            pieces.append(lax.ppermute(value, ("hi", "lo"), [(i, i ^ flip) for i in range(line)]))
        pieces = jnp.stack(pieces)
        return jnp.stack([lax.dynamic_index_in_dim(pieces, place ^ i, 0, False) for i in range(line)])

    def gather_planes(value):
        return lax.all_gather(value, ("plane", "core"), axis=0, tiled=True).reshape(devices, -1, width)

    up_rows, down_rows, out_rows = w_up.shape[0], w_down.shape[0], w_out.shape[0]
    skip_rows = w_skip.shape[0]
    columns = w_up.shape[1] // width
    middle = jnp.concatenate([w_qkv[:, i * width : (i + 1) * width] for i in range(3)] + [w_out], axis=0)
    late = jnp.concatenate([w_down] + [w_up[:, i * width : (i + 1) * width] for i in range(columns)], axis=0)
    early = share_on_line(w_skip)
    early, middle, late = lax.optimization_barrier((early, middle, late))
    early = gather_planes(early)
    middle, late = share_on_line(middle), share_on_line(late)
    middle = gather_planes(middle)

    labels_own = segment_ids[:, 0]
    labels_other = lax.ppermute(labels_own, "core", swap)
    labels_pick = jnp.where(core == high // micro, labels_own, labels_other)
    seg = lax.dynamic_index_in_dim(labels_pick, high % micro, 0, False)
    names = jnp.arange(labels, dtype=jnp.int32)
    starts = jnp.sum((seg[:, None] < names[None, :]).astype(jnp.int32), axis=0)
    ends = jnp.sum((seg[:, None] <= names[None, :]).astype(jnp.int32), axis=0)
    offset = jnp.sum(jnp.where(seg[:, None] == names[None, :], starts[None, :], 0), axis=1)
    where_at = jnp.arange(length, dtype=jnp.int32) - offset
    by_block = seg.reshape(-1, BLOCK)
    begin = jnp.sum(jnp.where(by_block[:, :1] == names[None, :], starts[None, :], 0), axis=1)
    finish = jnp.sum(jnp.where(by_block[:, -1:] == names[None, :], ends[None, :], 0), axis=1)
    ranges = jnp.stack([begin // BLOCK, (finish + BLOCK - 1) // BLOCK]).astype(jnp.int32)
    half = HEAD_DIM // 2
    rates = jnp.exp(-math.log(10000.0) * jnp.arange(half, dtype=f32) / half)
    angles = where_at.astype(f32)[:, None] * rates
    cosine = jnp.tile(jnp.cos(angles), (1, 4))
    sine = jnp.sin(angles)
    sine = jnp.concatenate([-sine, sine, -sine, sine], axis=1)
    seg_column, seg_row = seg[:, None], seg[None, :]
    mine = lax.dynamic_slice_in_dim(seg, member * frames, frames, 0)

    steps = lax.all_gather(time_steps[:, 0], ("plane", "core"), axis=0, tiled=True).reshape(-1)
    quarter = w_mod.shape[0] // 2
    pace = jnp.exp(-math.log(10000.0) * jnp.arange(quarter, dtype=f32) / quarter)
    turns = steps.astype(f32)[:, None] * pace
    embedded = jnp.concatenate([jnp.sin(turns), jnp.cos(turns)], axis=1).astype(bf16)
    block_mod = jnp.dot(embedded, w_mod, preferred_element_type=f32)
    own_columns = block_mod.shape[1]
    block_mod = block_mod.reshape(planes, 1, highs, 1, labels, own_columns)
    block_mod = jnp.broadcast_to(block_mod, (planes, 2, highs, lows, labels, own_columns))
    block_mod = lax.all_to_all(
        block_mod.reshape(devices, labels, own_columns), ALL_AXES, split_axis=0, concat_axis=0, tiled=True
    )
    modulation = jnp.moveaxis(block_mod, 0, 1).reshape(labels, 4, width)

    in_place = out_rows % 16 == 0
    hidden = w_up.shape[1]
    chunk = hidden // (2 * planes)

    def weight(gathered, begin, rows, first, count):
        block = (count // rows, rows, width)
        if in_place:
            return gathered, block, (first // count, begin // rows, 0)
        taken = gathered[first // rows : (first + count) // rows, begin : begin + rows]
        return taken.reshape(1, count, width), (1, count, width), (0, 0, 0)

    skip_top, skip_bottom = (weight(early, 0, skip_rows, i * width, width) for i in range(2))
    out_weight = weight(middle, 3 * out_rows, out_rows, 0, width)
    def own_qkv(gathered):
        parts = []
        for i in range(3):
            whole = gathered[:, i * out_rows : (i + 1) * out_rows].reshape(width, width)
            parts.append(lax.dynamic_slice_in_dim(whole, member * heads_wide, heads_wide, 1))
        return jnp.concatenate(parts, axis=1)

    mine_column, mine_row = mine[:, None], mine[None, :]
    shift_one, scale_one, shift_two, scale_two = (modulation[:, i] for i in range(4))

    x, s = (v.reshape(frames, width) for v in (inputs, skips))
    (resid_in,) = rowwise(
        merge_kernel, frames, [("", x), ("", s), ("weight", skip_top), ("weight", skip_bottom)], [(width, bf16)], light=True
    )
    resid_in = to_rows(resid_in.reshape(inputs.shape))
    resid_in, late, cotangent, modulation, cosine, sine, ranges = lax.optimization_barrier(
        (resid_in, late, cotangent, modulation, cosine, sine, ranges)
    )
    (normed_one,) = rowwise(
        norm_kernel,
        frames,
        [("", resid_in), ("", mine_column), ("whole", shift_one), ("whole", scale_one)],
        [(width, bf16)],
        light=True,
    )
    normed_row = frames_to_row(normed_one)
    if in_place:
        projected = project(normed_row, middle, 0, out_rows, heads_wide, member)
    else:
        projected = jnp.dot(normed_row, own_qkv(middle), preferred_element_type=f32).astype(bf16)
    late = gather_planes(late)
    cot = to_rows(cotangent)
    if in_place:
        per = width // chunk
        up_weight = (late, (devices, up_rows, chunk), lambda j: (0, down_rows // up_rows + j // per, j % per))
        down_weight = (late, (chunk // down_rows, down_rows, width), lambda j: (j, 0, 0))
    else:
        pieces = [late[:, down_rows + i * up_rows : down_rows + (i + 1) * up_rows] for i in range(columns)]
        up_full = jnp.concatenate([v.reshape(width, width) for v in pieces], axis=1)
        up_weight = (up_full[None], (1, width, chunk), lambda j: (0, 0, j))
        down_weight = (late[:, :down_rows].reshape(1, -1, width), (1, chunk, width), lambda j: (0, j, 0))
    mixed_heads, queries, keys, logsum = attend_forward(ranges, projected, cosine, sine, seg_column, seg_row)
    mixed = heads_to_frames(mixed_heads)
    resid_mid, normed_two = rowwise(
        out_norm_kernel,
        frames,
        [("", mixed), ("weight", out_weight), ("", resid_in), ("", mine_column), ("whole", shift_two), ("whole", scale_two)],
        [(width, f32), (width, bf16)],
        flops=2 * frames * width * width,
    )
    result, grad_normed_two, grad_up, grad_down = feed_forward_and_back(
        normed_two, cot, resid_mid, hidden, chunk, up_weight, down_weight
    )

    def over_cores(kept, axis):
        other = lax.ppermute(lax.dynamic_index_in_dim(kept, 1 - core, axis, False), "core", swap)
        own = lax.dynamic_index_in_dim(kept, core, axis, False)
        return (own.astype(f32) + other.astype(f32)).astype(bf16)

    plane = lax.axis_index("plane")

    def exchange(value, axes, here, count):
        total = lax.dynamic_index_in_dim(value, here, 0, False).astype(f32)
        for flip in range(1, count):
            sent = lax.dynamic_index_in_dim(value, here ^ flip, 0, False)
            total += lax.ppermute(sent, axes, [(i, i ^ flip) for i in range(count)]).astype(f32)
        return total

    def exchange_planes(value):
        return exchange(value, "plane", plane, planes).astype(bf16)

    def exchange_line(value):
        return exchange(value.reshape(line, -1, value.shape[-1]), ("hi", "lo"), place, line)

    grad_up, grad_down = (
        lax.psum_scatter(v, ("plane", "core"), scatter_dimension=0, tiled=True) for v in (grad_up, grad_down)
    )

    grad_mid, grad_mid_low, grad_frames, grad_shift_two, grad_scale_two = rowwise(
        norm_two_back_kernel,
        frames,
        [("", grad_normed_two), ("", resid_mid), ("", cot), ("", mine_column), ("row", mine_row),
         ("whole", scale_two), ("weight", out_weight)],
        [(width, f32), (width, bf16), (width, bf16)],
        sums=2,
        light=True,
    )
    grad_heads = frames_to_heads(grad_frames)
    grad_out = lax.dot_general(mixed, grad_mid_low, (((0,), (0,)), ((), ())), preferred_element_type=f32)
    grad_out = over_cores(grad_out.astype(bf16).reshape(planes, 2, -1, width), 1)
    grad_heads, grad_out, result = lax.optimization_barrier((grad_heads, grad_out, result))
    block_out = from_rows(result)
    grad_proj = attend_backward(
        ranges, queries, keys, projected, mixed_heads, grad_heads, logsum, cosine, sine, seg_column, seg_row
    )
    grad_proj, block_out = lax.optimization_barrier((grad_proj, block_out))
    grad_qkv = lax.dot_general(normed_row, grad_proj, (((0,), (0,)), ((), ())), preferred_element_type=f32)
    grad_qkv = grad_qkv.astype(bf16)
    grad_proj, grad_qkv = lax.optimization_barrier((grad_proj, grad_qkv))
    if group > 2:
        grad_qkv = grad_qkv.reshape(planes, 2, highs, lows, -1, 3, 1, heads_wide)
        grad_qkv = jnp.moveaxis(grad_qkv, (1, 3), (0, 1)).reshape(group, -1, 3, 1, heads_wide)
        grad_qkv = lax.all_to_all(grad_qkv, ROW_AXES, split_axis=0, concat_axis=3, tiled=True)
        grad_qkv = grad_qkv.reshape(-1, 3 * width)
        partial = dot_nt(grad_proj, own_qkv(middle)).astype(bf16)
        grad_one = lax.psum_scatter(partial, ROW_AXES, scatter_dimension=0, tiled=True).astype(f32)
        grad_one_other = jnp.zeros((frames, width), bf16)
    else:
        split = grad_qkv.reshape(planes, 2, -1, 3 * heads_wide)
        other = lax.ppermute(lax.dynamic_index_in_dim(split, 1 - core, 1, False), "core", swap)
        own = lax.dynamic_index_in_dim(split, core, 1, False)
        own, other = (v.reshape(-1, 3 * heads_wide) for v in (own, other))
        left, right = jnp.where(first_core, own, other), jnp.where(first_core, other, own)
        grad_qkv = jnp.concatenate(
            [v[:, i * heads_wide : (i + 1) * heads_wide] for i in range(3) for v in (left, right)], axis=1
        )
        if in_place:
            pull = functools.partial(pull_project, grad_proj, middle, out_rows, heads_wide, member, frames)
            away, home = pull(1 - core, bf16), pull(core, f32)
        else:
            qkv_own = own_qkv(middle)
            away = lax.dynamic_slice_in_dim(grad_proj, (1 - core) * frames, frames, 0)
            home = lax.dynamic_slice_in_dim(grad_proj, core * frames, frames, 0)
            away, home = dot_nt(away, qkv_own).astype(bf16), dot_nt(home, qkv_own)
        grad_one_other = lax.ppermute(away, "core", swap)
        grad_one = home
    grad_one, grad_qkv = lax.optimization_barrier((grad_one, grad_qkv))
    if group > 2:
        grad_qkv = lax.psum_scatter(grad_qkv, ("plane", "hi"), scatter_dimension=0, tiled=True).astype(f32)
    else:
        grad_qkv = jnp.concatenate([grad_qkv.reshape(planes, -1, 3 * width), grad_out], axis=2)
        grad_qkv = exchange_planes(grad_qkv)
    grad_in, grad_shift_one, grad_scale_one = rowwise(
        norm_one_back_kernel,
        frames,
        [("", grad_one), ("", grad_one_other), ("", resid_in), ("", grad_mid), ("", mine_column), ("row", mine_row),
         ("whole", scale_one)],
        [(width, bf16)],
        sums=2,
    )
    grad_in_home = from_rows(grad_in)
    grad_mod = jnp.stack([v[:labels] for v in (grad_shift_one, grad_scale_one, grad_shift_two, grad_scale_two)], axis=1)
    grad_mod = jnp.moveaxis(grad_mod.reshape(labels, devices, own_columns), 1, 0)
    grad_mod = lax.all_to_all(grad_mod, ALL_AXES, split_axis=0, concat_axis=0, tiled=True)
    grad_in_home, grad_qkv, grad_up, grad_down, grad_mod = lax.optimization_barrier(
        (grad_in_home, grad_qkv, grad_up, grad_down, grad_mod)
    )
    both = jnp.concatenate(
        [grad_up[:, i * width : (i + 1) * width].reshape(line, -1, width) for i in range(columns)]
        + [grad_down.reshape(line, -1, width)],
        axis=1,
    )
    both = lax.psum_scatter(both.reshape(-1, width), ("hi", "lo"), scatter_dimension=0, tiled=True).astype(f32)
    taken = columns * up_rows
    grad_up = jnp.concatenate([both[i * up_rows : (i + 1) * up_rows] for i in range(columns)], axis=1)
    grad_down = both[taken:]
    if group == 2:
        grad_qkv = grad_qkv.reshape(line, -1, 4 * width)
        grad_qkv = lax.all_to_all(grad_qkv, ("hi", "lo"), split_axis=0, concat_axis=0, tiled=True)
        grad_qkv = jnp.sum(grad_qkv.astype(f32), axis=0)
        grad_qkv, grad_out = grad_qkv[:, : 3 * width], grad_qkv[:, 3 * width :]
    else:
        grad_out = exchange_line(exchange_planes(grad_out))
    home = grad_in_home.reshape(frames, width)
    grad_skip_w = jnp.concatenate(
        [
            lax.dot_general(v, home, (((0,), (0,)), ((), ())), preferred_element_type=f32).astype(bf16)
            for v in (x, s)
        ],
        axis=0,
    )
    grad_skip_w = exchange_planes(over_cores(grad_skip_w.reshape(planes, 2, -1, width), 1))
    grad_inputs, grad_skips = rowwise(
        unmerge_kernel,
        frames,
        [("", home), ("weight", skip_top), ("weight", skip_bottom)],
        [(width, bf16), (width, bf16)],
        flops=4 * frames * width * width,
    )
    grad_inputs, grad_skips = (v.reshape(grad_in_home.shape) for v in (grad_inputs, grad_skips))

    grad_skip_w = exchange_line(grad_skip_w)
    grad_mod = jnp.sum(grad_mod.reshape(planes, 2, highs, lows, labels, own_columns), axis=(1, 3))
    grad_mod = lax.dot_general(
        embedded.astype(f32),
        grad_mod.reshape(-1, own_columns),
        (((0,), (0,)), ((), ())),
        precision=lax.Precision.HIGHEST,
        preferred_element_type=f32,
    )
    return (
        block_out,
        grad_inputs,
        grad_skips,
        grad_skip_w,
        grad_qkv,
        grad_out,
        grad_up,
        grad_down,
        grad_mod,
    )


def solution(mesh):
    batch, wide = mesh.devices.shape

    def run(inputs, *rest):
        rows = 2 * inputs.shape[0]
        assert inputs.shape[0] == 2 and inputs.shape[1] == batch and wide % rows == 0
        fine = Mesh(mesh.devices.reshape(batch // 2, 2, rows, wide // rows), ALL_AXES)
        by_batch, by_wide = ("plane", "core"), ("hi", "lo")
        frames = P(None, by_batch, by_wide, None)
        rowed = P(None, by_batch, None)
        weight, columns = P(ALL_AXES, None), P(None, ALL_AXES)
        mapped = jax.shard_map(
            body,
            mesh=fine,
            in_specs=(frames, frames, frames, rowed, rowed) + (weight,) * 5 + (columns,),
            out_specs=(frames, frames, frames) + (weight,) * 5 + (columns,),
            check_vma=False,
        )
        return mapped(inputs, *rest)

    return run
```

```python
import functools
import math

import jax
import jax.numpy as jnp
from jax import lax
from jax.experimental import pallas as pl
from jax.experimental.pallas import tpu as pltpu
from jax.sharding import Mesh
from jax.sharding import PartitionSpec as P

HEAD_DIM = 64
TILE = 128
BLOCK = 256
ROW_TILE = 256
FEED_TILE = 1024
FEED_PART = 512
VMEM_BYTES = 60 * 1024 * 1024
ROW_AXES = ("core", "lo")
LINE_AXES = ("core", "hi", "lo")
ALL_AXES = ("plane", "core", "hi", "lo")
f32 = jnp.float32
bf16 = jnp.bfloat16


def dot_nn(left, right):
    return lax.dot_general(left, right, (((1,), (0,)), ((), ())), preferred_element_type=f32)


def dot_nt(left, right):
    return lax.dot_general(left, right, (((1,), (1,)), ((), ())), preferred_element_type=f32)


def dot_tn(left, right):
    return lax.dot_general(left, right, (((0,), (0,)), ((), ())), preferred_element_type=f32)


def params(*semantics):
    return pltpu.CompilerParams(dimension_semantics=semantics, vmem_limit_bytes=VMEM_BYTES)


def cost(flops, moved, special=0):
    return pl.CostEstimate(flops=int(flops), bytes_accessed=int(moved), transcendentals=int(special))


def flat(ref):
    return ref[...].reshape(-1, ref.shape[-1])


def choose(segment_column, table_ref):
    count = table_ref.shape[0]
    picked = table_ref[count - 1 : count, :]
    for label in range(count - 2, -1, -1):
        picked = jnp.where(segment_column == label, table_ref[label : label + 1, :], picked)
    return picked


def normalise(values):
    centred = values - jnp.mean(values, axis=-1, keepdims=True)
    variance = jnp.mean(centred * centred, axis=-1, keepdims=True)
    inverse = lax.rsqrt(variance + 1e-06)
    return centred * inverse, inverse


def merge_kernel(x_ref, s_ref, top_ref, bottom_ref, resid_ref):
    resid = dot_nn(x_ref[...], flat(top_ref)) + dot_nn(s_ref[...], flat(bottom_ref))
    resid_ref[...] = resid.astype(bf16)


def norm_kernel(resid_ref, seg_ref, shift_ref, scale_ref, normed_ref):
    unit, _ = normalise(resid_ref[...].astype(f32))
    label = seg_ref[...]
    normed = unit * (1.0 + choose(label, scale_ref)) + choose(label, shift_ref)
    normed_ref[...] = normed.astype(bf16)


def out_norm_kernel(mixed_ref, w_ref, resid_in_ref, seg_ref, shift_ref, scale_ref, resid_ref, normed_ref):
    resid = resid_in_ref[...].astype(f32) + dot_nn(mixed_ref[...], flat(w_ref))
    resid_ref[...] = resid
    unit, _ = normalise(resid)
    label = seg_ref[...]
    normed = unit * (1.0 + choose(label, scale_ref)) + choose(label, shift_ref)
    normed_ref[...] = normed.astype(bf16)


def segment_sums(row_labels, values, total_ref):
    members = lax.broadcasted_iota(jnp.int32, (total_ref.shape[0], row_labels.shape[1]), 0) == row_labels
    members = members.astype(f32).astype(bf16)
    high = values.astype(bf16)
    low = (values - high.astype(f32)).astype(bf16)
    total_ref[...] += dot_nn(members, high) + dot_nn(members, low)


def norm_pull(grad, resid, scale):
    unit, inverse = normalise(resid)
    inner = grad * (1.0 + scale)
    pulled = inverse * (
        inner
        - jnp.mean(inner, axis=-1, keepdims=True)
        - unit * jnp.mean(inner * unit, axis=-1, keepdims=True)
    )
    return pulled, grad * unit


def norm_two_back_kernel(
    g_ref, resid_ref, cot_ref, seg_ref, segr_ref, scale_ref, w_ref, mid_ref, low_ref, mix_ref, dshift_ref, dscale_ref
):
    @pl.when(pl.program_id(0) == 0)
    def _():
        dshift_ref[...] = jnp.zeros_like(dshift_ref)
        dscale_ref[...] = jnp.zeros_like(dscale_ref)

    grad = g_ref[...]
    pulled, by_scale = norm_pull(grad, resid_ref[...], choose(seg_ref[...], scale_ref))
    grad_mid = cot_ref[...].astype(f32) + pulled
    low = grad_mid.astype(bf16)
    mid_ref[...] = grad_mid
    low_ref[...] = low
    mix_ref[...] = dot_nt(low, flat(w_ref)).astype(bf16)
    segment_sums(segr_ref[...], grad, dshift_ref)
    segment_sums(segr_ref[...], by_scale, dscale_ref)


def norm_one_back_kernel(
    own_ref, other_ref, resid_ref, mid_ref, seg_ref, segr_ref, scale_ref, grad_ref, dshift_ref, dscale_ref
):
    @pl.when(pl.program_id(0) == 0)
    def _():
        dshift_ref[...] = jnp.zeros_like(dshift_ref)
        dscale_ref[...] = jnp.zeros_like(dscale_ref)

    grad = own_ref[...] + other_ref[...].astype(f32)
    pulled, by_scale = norm_pull(grad, resid_ref[...].astype(f32), choose(seg_ref[...], scale_ref))
    grad_ref[...] = (mid_ref[...] + pulled).astype(bf16)
    segment_sums(segr_ref[...], grad, dshift_ref)
    segment_sums(segr_ref[...], by_scale, dscale_ref)


def unmerge_kernel(g_ref, top_ref, bottom_ref, inputs_ref, skips_ref):
    inputs_ref[...] = dot_nt(g_ref[...], flat(top_ref)).astype(bf16)
    skips_ref[...] = dot_nt(g_ref[...], flat(bottom_ref)).astype(bf16)


def project_kernel(place_ref, x_ref, w_ref, out_ref):
    out_ref[...] = dot_nn(x_ref[...], flat(w_ref)).astype(bf16)


def project(value, gathered, begin, rows, heads_wide, member):
    length, width = value.shape
    tile = min(8 * ROW_TILE, length)
    return pl.pallas_call(
        project_kernel,
        grid_spec=pltpu.PrefetchScalarGridSpec(
            num_scalar_prefetch=1,
            grid=(3, length // tile),
            in_specs=[
                pl.BlockSpec((tile, width), lambda t, i, r: (i, 0)),
                pl.BlockSpec((width // rows, rows, heads_wide), lambda t, i, r: (0, begin // rows + t, r[0])),
            ],
            out_specs=pl.BlockSpec((tile, heads_wide), lambda t, i, r: (i, t)),
        ),
        out_shape=jax.ShapeDtypeStruct((length, 3 * heads_wide), bf16),
        compiler_params=params("arbitrary", "arbitrary"),
        cost_estimate=cost(1, 1),
    )(member.reshape(1), value, gathered)


def pull_project_kernel(place_ref, dq_ref, dk_ref, dv_ref, q_ref, k_ref, v_ref, out_ref):
    total = dot_nt(dq_ref[...], flat(q_ref))
    total += dot_nt(dk_ref[...], flat(k_ref))
    total += dot_nt(dv_ref[...], flat(v_ref))
    out_ref[...] = total.astype(out_ref.dtype)


def pull_project(grad_proj, gathered, rows, heads_wide, member, frames, half, kind):
    width = gathered.shape[2]
    tile = min(2 * ROW_TILE, frames)
    steps = frames // tile
    grads = [
        pl.BlockSpec((tile, heads_wide), functools.partial(lambda t, i, r: (r[1] * steps + i, t), t)) for t in range(3)
    ]
    weights = [
        pl.BlockSpec((width // rows, rows, heads_wide), functools.partial(lambda t, i, r: (0, t, r[0]), t))
        for t in range(3)
    ]
    return pl.pallas_call(
        pull_project_kernel,
        grid_spec=pltpu.PrefetchScalarGridSpec(
            num_scalar_prefetch=1,
            grid=(steps,),
            in_specs=grads + weights,
            out_specs=pl.BlockSpec((tile, width), lambda i, r: (i, 0)),
        ),
        out_shape=jax.ShapeDtypeStruct((frames, width), kind),
        compiler_params=params("arbitrary"),
        cost_estimate=cost(6 * frames * width * heads_wide, 8 * frames * width),
    )(jnp.stack([member, half]).astype(jnp.int32), *[grad_proj] * 3, *[gathered] * 3)


def rowwise(kernel, frames, blocked, outs, sums=0, flops=0, light=False):
    tile = min(ROW_TILE, frames)
    in_specs, args, moved = [], [], 0
    for kind, value in blocked:
        if kind == "row":
            in_specs.append(pl.BlockSpec((1, tile), lambda i: (0, i)))
        elif kind == "weight":
            value, block, index = value
            in_specs.append(pl.BlockSpec(block, functools.partial(lambda index, i: index, index)))
        elif kind == "whole":
            in_specs.append(pl.BlockSpec(value.shape, lambda i: (0, 0)))
        else:
            in_specs.append(pl.BlockSpec((tile, value.shape[1]), lambda i: (i, 0)))
        args.append(value)
        moved += value.size * value.dtype.itemsize
    out_specs, shapes = [], []
    for width, kind in outs:
        out_specs.append(pl.BlockSpec((tile, width), lambda i: (i, 0)))
        shapes.append(jax.ShapeDtypeStruct((frames, width), kind))
        moved += frames * width * jnp.dtype(kind).itemsize
    for _ in range(sums):
        out_specs.append(pl.BlockSpec((8, outs[0][0]), lambda i: (0, 0)))
        shapes.append(jax.ShapeDtypeStruct((8, outs[0][0]), f32))
    return pl.pallas_call(
        kernel,
        grid=(frames // tile,),
        in_specs=in_specs,
        out_specs=out_specs,
        out_shape=shapes,
        compiler_params=params("arbitrary"),
        cost_estimate=cost(1, 1) if light else cost(flops, moved),
    )(*args)


def swap_halves(values, lanes):
    half = HEAD_DIM // 2
    ahead = pltpu.roll(values, values.shape[1] - half, 1)
    behind = pltpu.roll(values, half, 1)
    return jnp.where(lanes % HEAD_DIM < half, ahead, behind)


def widen(table, width):
    return jnp.concatenate([table] * (width // table.shape[1]), axis=1)


def span(i):
    return pl.ds(pl.multiple_of(i * BLOCK, BLOCK), BLOCK)


def own_lanes(parts, lanes):
    picked = parts[0]
    for h in range(1, len(parts)):
        picked = jnp.where(lanes // HEAD_DIM == h, parts[h], picked)
    return picked


def by_count(count, most, run):
    for each in range(1, most + 1):
        pl.when(count == each)(functools.partial(run, each))


def attend_forward_kernel(
    range_ref, q_ref, k_ref, v_ref, cos_ref, sin_ref, segc_ref, segr_ref,
    out_ref, qrot_ref, krot_ref, lse_ref, seg_wide,
):
    length, width = q_ref.shape
    heads = width // HEAD_DIM
    blocks = length // BLOCK
    lanes = lax.broadcasted_iota(jnp.int32, (BLOCK, width), 1)

    def turn(i, carry):
        rows = span(i)
        cosine, sine = widen(cos_ref[rows, :], width), widen(sin_ref[rows, :], width)
        for source, target, factor in ((q_ref, qrot_ref, HEAD_DIM**-0.5), (k_ref, krot_ref, None)):
            values = source[rows, :].astype(f32)
            turned = (values * cosine + swap_halves(values, lanes) * sine).astype(bf16)
            if factor is not None:
                turned = turned * jnp.asarray(factor, bf16)
            target[rows, :] = turned
        seg_wide[rows, :] = jnp.broadcast_to(segc_ref[rows, :], (BLOCK, TILE))
        return carry

    lax.fori_loop(0, blocks, turn, 0)

    def one_query(i, carry):
        rows = span(i)

        def work(count):
            keys = pl.ds(pl.multiple_of(range_ref[0, i] * BLOCK, BLOCK), count * BLOCK)
            allowed = widen(seg_wide[rows, :], count * BLOCK) == segr_ref[:, keys]
            query = qrot_ref[rows, :]
            zero = jnp.zeros_like(query)
            mixed = []
            for h in range(heads):
                scores = dot_nt(jnp.where(lanes // HEAD_DIM == h, query, zero), krot_ref[keys, :])
                scores = jnp.where(allowed, scores, -1e30)
                highest = jnp.max(scores, axis=1, keepdims=True)
                powers = jnp.exp(scores - highest)
                totals = jnp.sum(powers, axis=1, keepdims=True)
                mixed.append(dot_nn(powers.astype(bf16), v_ref[keys, :]) * (1.0 / totals))
                logsum = jnp.broadcast_to(highest + jnp.log(totals), (BLOCK, TILE))
                lse_ref[0, h : h + 1, rows] = logsum.T[0:1]
            out_ref[rows, :] = own_lanes(mixed, lanes).astype(bf16)

        by_count(range_ref[1, i] - range_ref[0, i], blocks, work)
        return carry

    lax.fori_loop(0, blocks, one_query, 0)


def attend_forward(ranges, projected, cosine, sine, seg_column, seg_row):
    length, width = projected.shape
    width //= 3
    panels, heads = width // TILE, TILE // HEAD_DIM
    panel = lambda shift: pl.BlockSpec((length, TILE), lambda p, r: (0, shift * panels + p))
    whole = lambda shape: pl.BlockSpec(shape, lambda p, r: (0,) * len(shape))
    return pl.pallas_call(
        attend_forward_kernel,
        grid_spec=pltpu.PrefetchScalarGridSpec(
            num_scalar_prefetch=1,
            grid=(panels,),
            in_specs=[panel(0), panel(1), panel(2), whole(cosine.shape), whole(sine.shape),
                      whole(seg_column.shape), whole(seg_row.shape)],
            out_specs=[panel(0), panel(0), panel(0), pl.BlockSpec((1, heads, length), lambda p, r: (p, 0, 0))],
            scratch_shapes=[pltpu.VMEM((length, TILE), jnp.int32)],
        ),
        out_shape=[jax.ShapeDtypeStruct((length, width), bf16)] * 3
        + [jax.ShapeDtypeStruct((panels, heads, length), f32)],
        compiler_params=params("arbitrary"),
        cost_estimate=cost(8 * length * length * width, 14 * length * width, length * length * width // HEAD_DIM),
    )(ranges, projected, projected, projected, cosine, sine, seg_column, seg_row)


def attend_backward_kernel(
    range_ref, q_ref, k_ref, v_ref, out_ref, do_ref, lse_ref, cos_ref, sin_ref, segc_ref, segr_ref,
    grad_ref, dq, dk_low, dv_low, delta, seg_wide,
):
    length, width = q_ref.shape
    heads = width // HEAD_DIM
    blocks = length // BLOCK
    step = pl.program_id(1)

    @pl.when(step == 0)
    def _():
        lanes = lax.broadcasted_iota(jnp.int32, (BLOCK, width), 1)
        picker = (
            lax.broadcasted_iota(jnp.int32, (8, width), 0)
            == lax.broadcasted_iota(jnp.int32, (8, width), 1) // HEAD_DIM
        ).astype(f32)

        def prepare(i, carry):
            rows = span(i)
            product = do_ref[rows, :].astype(f32) * out_ref[rows, :].astype(f32)
            delta[:, rows] = lax.dot_general(
                picker, product, (((1,), (1,)), ((), ())),
                precision=lax.Precision.HIGHEST, preferred_element_type=f32,
            )
            dq[:, rows] = jnp.zeros((width, BLOCK), f32)
            seg_wide[rows, :] = jnp.broadcast_to(segc_ref[rows, :], (BLOCK, TILE))
            return carry

        lax.fori_loop(0, blocks, prepare, 0)

        def unturn(values, rows):
            return values * widen(cos_ref[rows, :], width) - swap_halves(values, lanes) * widen(sin_ref[rows, :], width)

        def one_key(j, carry):
            rows = span(j)

            def work(count):
                there = pl.ds(pl.multiple_of(range_ref[0, j] * BLOCK, BLOCK), count * BLOCK)
                allowed = widen(seg_wide[rows, :], count * BLOCK) == segr_ref[:, there]
                zero = jnp.zeros((BLOCK, width), bf16)
                key, value = (
                    jnp.concatenate([jnp.where(lanes // HEAD_DIM == h, ref[rows, :], zero) for h in range(heads)], axis=0)
                    for ref in (k_ref, v_ref)
                )
                query, grad_out = q_ref[there, :], do_ref[there, :]
                found, grad_prob = dot_nt(key, query), dot_nt(value, grad_out)
                parts, lows = [], []
                for h in range(heads):
                    half = slice(h * BLOCK, (h + 1) * BLOCK)
                    scores = found[half] - lse_ref[0, h : h + 1, there]
                    part = jnp.exp(jnp.where(allowed, scores, -1e30))
                    parts.append(part.astype(bf16))
                    lows.append((part * (grad_prob[half] - delta[h : h + 1, there])).astype(bf16))
                grad_scores = jnp.concatenate(lows, axis=0)
                grad_v = dot_nn(jnp.concatenate(parts, axis=0), grad_out)
                grad_k = dot_nn(grad_scores, query)
                grad_v, grad_k = ([v[h * BLOCK : (h + 1) * BLOCK] for h in range(heads)] for v in (grad_v, grad_k))
                dq[:, there] += dot_tn(key, grad_scores)
                dk_low[rows, :] = unturn(own_lanes(grad_k, lanes), rows).astype(bf16)
                dv_low[rows, :] = own_lanes(grad_v, lanes).astype(bf16)

            by_count(range_ref[1, j] - range_ref[0, j], blocks, work)
            return carry

        lax.fori_loop(0, blocks, one_key, 0)

        def finish(i, carry):
            rows = span(i)
            grad_ref[rows, :] = unturn(dq[:, rows].T * HEAD_DIM**-0.5, rows).astype(bf16)
            return carry

        lax.fori_loop(0, blocks, finish, 0)

    @pl.when(step == 1)
    def _():
        grad_ref[...] = dk_low[...]

    @pl.when(step == 2)
    def _():
        grad_ref[...] = dv_low[...]


def attend_backward(ranges, queries, keys, projected, mixed, grad_mixed, logsum, cosine, sine, seg_column, seg_row):
    length, width = queries.shape
    panels, heads = width // TILE, TILE // HEAD_DIM
    panel = lambda shift: pl.BlockSpec((length, TILE), lambda p, t, r: (0, shift * panels + p))
    whole = lambda shape: pl.BlockSpec(shape, lambda p, t, r: (0,) * len(shape))
    return pl.pallas_call(
        attend_backward_kernel,
        grid_spec=pltpu.PrefetchScalarGridSpec(
            num_scalar_prefetch=1,
            grid=(panels, 3),
            in_specs=[panel(0), panel(0), panel(2), panel(0), panel(0),
                      pl.BlockSpec((1, heads, length), lambda p, t, r: (p, 0, 0)),
                      whole(cosine.shape), whole(sine.shape), whole(seg_column.shape), whole(seg_row.shape)],
            out_specs=pl.BlockSpec((length, TILE), lambda p, t, r: (0, t * panels + p)),
            scratch_shapes=[
                pltpu.VMEM((TILE, length), f32),
                pltpu.VMEM((length, TILE), bf16),
                pltpu.VMEM((length, TILE), bf16),
                pltpu.VMEM((8, length), f32),
                pltpu.VMEM((length, TILE), jnp.int32),
            ],
        ),
        out_shape=jax.ShapeDtypeStruct((length, 3 * width), bf16),
        compiler_params=params("arbitrary", "arbitrary"),
        cost_estimate=cost(20 * length * length * width, 16 * length * width, length * length * width // HEAD_DIM),
    )(ranges, queries, keys, projected, mixed, grad_mixed, logsum, cosine, sine, seg_column, seg_row)


def gelu_and_slope(x):
    root = math.sqrt(2.0 / math.pi)
    square = x * x
    bend = jnp.tanh(x * (root + root * 0.044715 * square))
    half = 0.5 * x
    half_up = 0.5 + 0.5 * bend
    slope = half_up + half * (1.0 - bend * bend) * (root + 3.0 * root * 0.044715 * square)
    return half + half * bend, slope


def feed_kernel(
    n_ref, cot_ref, resid_ref, up_ref, down_ref, out_ref, back_ref, gup_ref, gdown_ref,
    total, n_turned, act_turned, pre,
):
    step, last = pl.program_id(0), pl.num_programs(0) - 1
    frames, width = n_ref.shape
    tile = min(FEED_TILE, frames)

    def rows_of(i):
        return pl.ds(pl.multiple_of(i * tile, tile), tile)

    @pl.when(step == 0)
    def _():
        def turn(i, carry):
            rows = rows_of(i)
            n_turned[:, rows] = n_ref[rows, :].T
            total[rows, :] = resid_ref[rows, :]
            back_ref[rows, :] = jnp.zeros((tile, width), f32)
            return carry

        lax.fori_loop(0, frames // tile, turn, 0)

    def chunk(i, carry):
        rows = rows_of(i)
        up, down = flat(up_ref), flat(down_ref)
        hidden = dot_nn(n_ref[rows, :], up)
        grad_act = dot_nt(cot_ref[rows, :], down)
        activated, slope = gelu_and_slope(hidden)
        activated = activated.astype(bf16)
        grad_pre = (grad_act * slope).astype(bf16)
        act_turned[:, rows] = activated.T
        pre[rows, :] = grad_pre
        total[rows, :] += dot_nn(activated, down)
        back_ref[rows, :] += dot_nt(grad_pre, up)
        return carry

    lax.fori_loop(0, frames // tile, chunk, 0)

    for begin in range(0, width, FEED_PART):
        rows = slice(begin, begin + FEED_PART)
        gup_ref[rows, :] = dot_nn(n_turned[rows, :], pre[...]).astype(bf16)
    piece = act_turned.shape[0]
    for begin in range(0, piece, FEED_PART):
        rows = slice(begin, begin + FEED_PART)
        gdown_ref[rows, :] = dot_nn(act_turned[rows, :], cot_ref[...]).astype(bf16)

    @pl.when(step == last)
    def _():
        out_ref[...] = total[...].astype(bf16)


def feed_forward_and_back(normed, cot, resid, hidden, piece, w_up, w_down):
    frames, width = normed.shape
    whole = lambda: pl.BlockSpec((frames, width), lambda j: (0, 0), pipeline_mode=pl.Buffered(1))
    return pl.pallas_call(
        feed_kernel,
        grid=(hidden // piece,),
        in_specs=[whole(), whole(), whole(), pl.BlockSpec(*w_up[1:]), pl.BlockSpec(*w_down[1:])],
        out_specs=[pl.BlockSpec((frames, width), lambda j: (0, 0))] * 2
        + [pl.BlockSpec((width, piece), lambda j: (0, j)), pl.BlockSpec((piece, width), lambda j: (j, 0))],
        out_shape=[
            jax.ShapeDtypeStruct((frames, width), bf16),
            jax.ShapeDtypeStruct((frames, width), f32),
            jax.ShapeDtypeStruct((width, hidden), bf16),
            jax.ShapeDtypeStruct((hidden, width), bf16),
        ],
        scratch_shapes=[
            pltpu.VMEM((frames, width), f32),
            pltpu.VMEM((width, frames), bf16),
            pltpu.VMEM((piece, frames), bf16),
            pltpu.VMEM((frames, piece), bf16),
        ],
        compiler_params=params("arbitrary"),
        cost_estimate=cost(12 * frames * width * hidden, 8 * width * hidden + 16 * frames * width, frames * hidden),
    )(normed, cot, resid, w_up[0], w_down[0])


def body(inputs, skips, cotangent, segment_ids, time_steps, w_skip, w_qkv, w_out, w_up, w_down, w_mod):
    micro, _, piece, width = inputs.shape
    length = segment_ids.shape[-1]
    labels = time_steps.shape[-1]
    planes, lows, highs = lax.axis_size("plane"), lax.axis_size("lo"), lax.axis_size("hi")
    line = highs * lows
    group = 2 * lows
    devices = planes * 2 * line
    core, high, low = lax.axis_index("core"), lax.axis_index("hi"), lax.axis_index("lo")
    place = high * lows + low
    member = core * lows + low
    frames = 2 * piece
    heads_wide = width // group
    first_core = core == 0
    swap = [(0, 1), (1, 0)]

    def route(parity):
        pairs = []
        for c in range(2):
            for z in range(line):
                row = c * micro + ((z % 2) ^ parity)
                to_core, to_low = divmod(z // 2, lows)
                pairs.append((c * line + z, (to_core * highs + row) * lows + to_low))
        return pairs

    there = (route(0), route(1))
    back = tuple([(b, a) for a, b in pairs] for pairs in there)
    odd_place = place % 2
    even_row = high % 2 == 0

    def to_rows(value):
        value = value[:, 0]
        near = lax.ppermute(lax.dynamic_index_in_dim(value, odd_place, 0, False), LINE_AXES, there[0])
        far = lax.ppermute(lax.dynamic_index_in_dim(value, 1 - odd_place, 0, False), LINE_AXES, there[1])
        return jnp.concatenate([jnp.where(even_row, near, far), jnp.where(even_row, far, near)], axis=0)

    def from_rows(value):
        value = value.reshape(2, piece, width)
        near = lax.ppermute(lax.dynamic_index_in_dim(value, high % 2, 0, False), LINE_AXES, back[0])
        far = lax.ppermute(lax.dynamic_index_in_dim(value, 1 - high % 2, 0, False), LINE_AXES, back[1])
        even = odd_place == 0
        return jnp.stack([jnp.where(even, near, far), jnp.where(even, far, near)])[:, None]

    def frames_to_row(value):
        if group > 2:
            return lax.all_gather(value, ROW_AXES, axis=0, tiled=True)
        other = lax.ppermute(value, "core", swap)
        return jnp.concatenate([jnp.where(first_core, value, other), jnp.where(first_core, other, value)], axis=0)

    def heads_to_frames(value):
        if group > 2:
            return lax.all_to_all(value, ROW_AXES, split_axis=0, concat_axis=1, tiled=True)
        other = lax.ppermute(lax.dynamic_slice_in_dim(value, (1 - core) * frames, frames, 0), "core", swap)
        own = lax.dynamic_slice_in_dim(value, core * frames, frames, 0)
        return jnp.concatenate([jnp.where(first_core, own, other), jnp.where(first_core, other, own)], axis=1)

    def frames_to_heads(value):
        if group > 2:
            return lax.all_to_all(value, ROW_AXES, split_axis=1, concat_axis=0, tiled=True)
        other = lax.ppermute(lax.dynamic_slice_in_dim(value, (1 - core) * heads_wide, heads_wide, 1), "core", swap)
        own = lax.dynamic_slice_in_dim(value, core * heads_wide, heads_wide, 1)
        return jnp.concatenate([jnp.where(first_core, own, other), jnp.where(first_core, other, own)], axis=0)

    def share_on_line(value):
        pieces = [value]
        for flip in range(1, line):
            pieces.append(lax.ppermute(value, ("hi", "lo"), [(i, i ^ flip) for i in range(line)]))
        pieces = jnp.stack(pieces)
        return jnp.stack([lax.dynamic_index_in_dim(pieces, place ^ i, 0, False) for i in range(line)])

    def gather_planes(value):
        return lax.all_gather(value, ("plane", "core"), axis=0, tiled=True).reshape(devices, -1, width)

    up_rows, down_rows, out_rows = w_up.shape[0], w_down.shape[0], w_out.shape[0]
    skip_rows = w_skip.shape[0]
    columns = w_up.shape[1] // width
    middle = jnp.concatenate([w_qkv[:, i * width : (i + 1) * width] for i in range(3)] + [w_out], axis=0)
    late = jnp.concatenate([w_down] + [w_up[:, i * width : (i + 1) * width] for i in range(columns)], axis=0)
    early = share_on_line(w_skip)
    early, middle, late = lax.optimization_barrier((early, middle, late))
    early = gather_planes(early)
    middle, late = share_on_line(middle), share_on_line(late)
    middle = gather_planes(middle)

    in_place = out_rows % 16 == 0
    hidden = w_up.shape[1]
    chunk = hidden // (2 * planes)

    def weight(gathered, begin, rows, first, count):
        block = (count // rows, rows, width)
        if in_place:
            return gathered, block, (first // count, begin // rows, 0)
        taken = gathered[first // rows : (first + count) // rows, begin : begin + rows]
        return taken.reshape(1, count, width), (1, count, width), (0, 0, 0)

    skip_top, skip_bottom = (weight(early, 0, skip_rows, i * width, width) for i in range(2))
    out_weight = weight(middle, 3 * out_rows, out_rows, 0, width)
    x, s = (v.reshape(frames, width) for v in (inputs, skips))
    (resid_in,) = rowwise(
        merge_kernel, frames, [("", x), ("", s), ("weight", skip_top), ("weight", skip_bottom)], [(width, bf16)], light=True
    )
    stacked = jnp.concatenate([x, s], axis=1)
    resid_in, segment_ids, time_steps = lax.optimization_barrier((resid_in, segment_ids, time_steps))

    labels_own = segment_ids[:, 0]
    labels_other = lax.ppermute(labels_own, "core", swap)
    labels_pick = jnp.where(core == high // micro, labels_own, labels_other)
    seg = lax.dynamic_index_in_dim(labels_pick, high % micro, 0, False)
    names = jnp.arange(labels, dtype=jnp.int32)
    starts = jnp.sum((seg[:, None] < names[None, :]).astype(jnp.int32), axis=0)
    ends = jnp.sum((seg[:, None] <= names[None, :]).astype(jnp.int32), axis=0)
    offset = jnp.sum(jnp.where(seg[:, None] == names[None, :], starts[None, :], 0), axis=1)
    where_at = jnp.arange(length, dtype=jnp.int32) - offset
    by_block = seg.reshape(-1, BLOCK)
    begin = jnp.sum(jnp.where(by_block[:, :1] == names[None, :], starts[None, :], 0), axis=1)
    finish = jnp.sum(jnp.where(by_block[:, -1:] == names[None, :], ends[None, :], 0), axis=1)
    ranges = jnp.stack([begin // BLOCK, (finish + BLOCK - 1) // BLOCK]).astype(jnp.int32)
    half = HEAD_DIM // 2
    rates = jnp.exp(-math.log(10000.0) * jnp.arange(half, dtype=f32) / half)
    angles = where_at.astype(f32)[:, None] * rates
    cosine = jnp.tile(jnp.cos(angles), (1, 4))
    sine = jnp.sin(angles)
    sine = jnp.concatenate([-sine, sine, -sine, sine], axis=1)
    seg_column, seg_row = seg[:, None], seg[None, :]
    mine = lax.dynamic_slice_in_dim(seg, member * frames, frames, 0)

    steps = lax.all_gather(time_steps[:, 0], ("plane", "core"), axis=0, tiled=True).reshape(-1)
    quarter = w_mod.shape[0] // 2
    pace = jnp.exp(-math.log(10000.0) * jnp.arange(quarter, dtype=f32) / quarter)
    turns = steps.astype(f32)[:, None] * pace
    embedded = jnp.concatenate([jnp.sin(turns), jnp.cos(turns)], axis=1).astype(bf16)
    block_mod = jnp.dot(embedded, w_mod, preferred_element_type=f32)
    own_columns = block_mod.shape[1]
    block_mod = block_mod.reshape(planes, 1, highs, 1, labels, own_columns)
    block_mod = jnp.broadcast_to(block_mod, (planes, 2, highs, lows, labels, own_columns))
    block_mod = lax.all_to_all(
        block_mod.reshape(devices, labels, own_columns), ALL_AXES, split_axis=0, concat_axis=0, tiled=True
    )
    modulation = jnp.moveaxis(block_mod, 0, 1).reshape(labels, 4, width)

    def own_qkv(gathered):
        parts = []
        for i in range(3):
            whole = gathered[:, i * out_rows : (i + 1) * out_rows].reshape(width, width)
            parts.append(lax.dynamic_slice_in_dim(whole, member * heads_wide, heads_wide, 1))
        return jnp.concatenate(parts, axis=1)

    mine_column, mine_row = mine[:, None], mine[None, :]
    shift_one, scale_one, shift_two, scale_two = (modulation[:, i] for i in range(4))

    resid_in = to_rows(resid_in.reshape(inputs.shape))
    resid_in, late, cotangent, stacked, modulation, cosine, sine, ranges = lax.optimization_barrier(
        (resid_in, late, cotangent, stacked, modulation, cosine, sine, ranges)
    )
    (normed_one,) = rowwise(
        norm_kernel,
        frames,
        [("", resid_in), ("", mine_column), ("whole", shift_one), ("whole", scale_one)],
        [(width, bf16)],
        light=True,
    )
    normed_row = frames_to_row(normed_one)
    if in_place:
        projected = project(normed_row, middle, 0, out_rows, heads_wide, member)
    else:
        projected = jnp.dot(normed_row, own_qkv(middle), preferred_element_type=f32).astype(bf16)
    late = gather_planes(late)
    cot = to_rows(cotangent)
    if in_place:
        per = width // chunk
        up_weight = (late, (devices, up_rows, chunk), lambda j: (0, down_rows // up_rows + j // per, j % per))
        down_weight = (late, (chunk // down_rows, down_rows, width), lambda j: (j, 0, 0))
    else:
        pieces = [late[:, down_rows + i * up_rows : down_rows + (i + 1) * up_rows] for i in range(columns)]
        up_full = jnp.concatenate([v.reshape(width, width) for v in pieces], axis=1)
        up_weight = (up_full[None], (1, width, chunk), lambda j: (0, 0, j))
        down_weight = (late[:, :down_rows].reshape(1, -1, width), (1, chunk, width), lambda j: (0, j, 0))
    mixed_heads, queries, keys, logsum = attend_forward(ranges, projected, cosine, sine, seg_column, seg_row)
    mixed = heads_to_frames(mixed_heads)
    resid_mid, normed_two = rowwise(
        out_norm_kernel,
        frames,
        [("", mixed), ("weight", out_weight), ("", resid_in), ("", mine_column), ("whole", shift_two), ("whole", scale_two)],
        [(width, f32), (width, bf16)],
        flops=2 * frames * width * width,
    )
    result, grad_normed_two, grad_up, grad_down = feed_forward_and_back(
        normed_two, cot, resid_mid, hidden, chunk, up_weight, down_weight
    )

    def over_cores(kept, axis):
        other = lax.ppermute(lax.dynamic_index_in_dim(kept, 1 - core, axis, False), "core", swap)
        own = lax.dynamic_index_in_dim(kept, core, axis, False)
        return (own.astype(f32) + other.astype(f32)).astype(bf16)

    plane = lax.axis_index("plane")

    def exchange(value, axes, here, count):
        total = lax.dynamic_index_in_dim(value, here, 0, False).astype(f32)
        for flip in range(1, count):
            sent = lax.dynamic_index_in_dim(value, here ^ flip, 0, False)
            total += lax.ppermute(sent, axes, [(i, i ^ flip) for i in range(count)]).astype(f32)
        return total

    def exchange_planes(value):
        return exchange(value, "plane", plane, planes).astype(bf16)

    def exchange_line(value):
        return exchange(value.reshape(line, -1, value.shape[-1]), ("hi", "lo"), place, line)

    grad_up, grad_down = (
        lax.psum_scatter(v, ("plane", "core"), scatter_dimension=0, tiled=True) for v in (grad_up, grad_down)
    )

    grad_mid, grad_mid_low, grad_frames, grad_shift_two, grad_scale_two = rowwise(
        norm_two_back_kernel,
        frames,
        [("", grad_normed_two), ("", resid_mid), ("", cot), ("", mine_column), ("row", mine_row),
         ("whole", scale_two), ("weight", out_weight)],
        [(width, f32), (width, bf16), (width, bf16)],
        sums=2,
        light=True,
    )
    grad_heads = frames_to_heads(grad_frames)
    grad_out = lax.dot_general(mixed, grad_mid_low, (((0,), (0,)), ((), ())), preferred_element_type=f32)
    grad_out = over_cores(grad_out.astype(bf16).reshape(planes, 2, -1, width), 1)
    grad_heads, grad_out, result = lax.optimization_barrier((grad_heads, grad_out, result))
    block_out = from_rows(result)
    grad_proj = attend_backward(
        ranges, queries, keys, projected, mixed_heads, grad_heads, logsum, cosine, sine, seg_column, seg_row
    )
    grad_proj, block_out, grad_up = lax.optimization_barrier((grad_proj, block_out, grad_up))
    grad_up = lax.psum_scatter(grad_up, ("hi", "lo"), scatter_dimension=0, tiled=True)
    grad_qkv = lax.dot_general(normed_row, grad_proj, (((0,), (0,)), ((), ())), preferred_element_type=f32)
    grad_qkv = grad_qkv.astype(bf16)
    grad_proj, grad_qkv = lax.optimization_barrier((grad_proj, grad_qkv))
    if group > 2:
        grad_qkv = grad_qkv.reshape(planes, 2, highs, lows, -1, 3, 1, heads_wide)
        grad_qkv = jnp.moveaxis(grad_qkv, (1, 3), (0, 1)).reshape(group, -1, 3, 1, heads_wide)
        grad_qkv = lax.all_to_all(grad_qkv, ROW_AXES, split_axis=0, concat_axis=3, tiled=True)
        grad_qkv = grad_qkv.reshape(-1, 3 * width)
        partial = dot_nt(grad_proj, own_qkv(middle)).astype(bf16)
        grad_one = lax.psum_scatter(partial, ROW_AXES, scatter_dimension=0, tiled=True).astype(f32)
        grad_one_other = jnp.zeros((frames, width), bf16)
    else:
        split = grad_qkv.reshape(planes, 2, -1, 3 * heads_wide)
        other = lax.ppermute(lax.dynamic_index_in_dim(split, 1 - core, 1, False), "core", swap)
        own = lax.dynamic_index_in_dim(split, core, 1, False)
        own, other = (v.reshape(-1, 3 * heads_wide) for v in (own, other))
        left, right = jnp.where(first_core, own, other), jnp.where(first_core, other, own)
        grad_qkv = jnp.concatenate(
            [v[:, i * heads_wide : (i + 1) * heads_wide] for i in range(3) for v in (left, right)], axis=1
        )
        if in_place:
            pull = functools.partial(pull_project, grad_proj, middle, out_rows, heads_wide, member, frames)
            away, home = pull(1 - core, bf16), pull(core, f32)
        else:
            qkv_own = own_qkv(middle)
            away = lax.dynamic_slice_in_dim(grad_proj, (1 - core) * frames, frames, 0)
            home = lax.dynamic_slice_in_dim(grad_proj, core * frames, frames, 0)
            away, home = dot_nt(away, qkv_own).astype(bf16), dot_nt(home, qkv_own)
        grad_one_other = lax.ppermute(away, "core", swap)
        grad_one = home
    grad_one, grad_qkv = lax.optimization_barrier((grad_one, grad_qkv))
    if group > 2:
        grad_qkv = lax.psum_scatter(grad_qkv, ("plane", "hi"), scatter_dimension=0, tiled=True).astype(f32)
    else:
        grad_qkv = jnp.concatenate([grad_qkv.reshape(planes, -1, 3 * width), grad_out], axis=2)
        grad_qkv = exchange_planes(grad_qkv)
    grad_in, grad_shift_one, grad_scale_one = rowwise(
        norm_one_back_kernel,
        frames,
        [("", grad_one), ("", grad_one_other), ("", resid_in), ("", grad_mid), ("", mine_column), ("row", mine_row),
         ("whole", scale_one)],
        [(width, bf16)],
        sums=2,
    )
    grad_in_home = from_rows(grad_in)
    grad_mod = jnp.stack([v[:labels] for v in (grad_shift_one, grad_scale_one, grad_shift_two, grad_scale_two)], axis=1)
    grad_mod = jnp.moveaxis(grad_mod.reshape(labels, devices, own_columns), 1, 0)
    grad_mod = lax.all_to_all(grad_mod, ALL_AXES, split_axis=0, concat_axis=0, tiled=True)
    grad_in_home, grad_qkv, grad_down, grad_mod = lax.optimization_barrier((grad_in_home, grad_qkv, grad_down, grad_mod))
    grad_down = lax.psum_scatter(grad_down, ("hi", "lo"), scatter_dimension=0, tiled=True)
    grad_up, grad_down = grad_up.astype(f32), grad_down.astype(f32)
    if group == 2:
        grad_qkv = grad_qkv.reshape(line, -1, 4 * width)
        grad_qkv = lax.all_to_all(grad_qkv, ("hi", "lo"), split_axis=0, concat_axis=0, tiled=True)
        grad_qkv = jnp.sum(grad_qkv.astype(f32), axis=0)
        grad_qkv, grad_out = grad_qkv[:, : 3 * width], grad_qkv[:, 3 * width :]
    else:
        grad_out = exchange_line(exchange_planes(grad_out))
    home = grad_in_home.reshape(frames, width)
    grad_skip_w = lax.dot_general(stacked, home, (((0,), (0,)), ((), ())), preferred_element_type=f32).astype(bf16)
    grad_skip_w = exchange_planes(over_cores(grad_skip_w.reshape(planes, 2, -1, width), 1))
    grad_inputs, grad_skips = rowwise(
        unmerge_kernel,
        frames,
        [("", home), ("weight", skip_top), ("weight", skip_bottom)],
        [(width, bf16), (width, bf16)],
        flops=4 * frames * width * width,
    )
    grad_inputs, grad_skips = (v.reshape(grad_in_home.shape) for v in (grad_inputs, grad_skips))

    grad_skip_w = exchange_line(grad_skip_w)
    grad_mod = jnp.sum(grad_mod.reshape(planes, 2, highs, lows, labels, own_columns), axis=(1, 3))
    grad_mod = lax.dot_general(
        embedded.astype(f32),
        grad_mod.reshape(-1, own_columns),
        (((0,), (0,)), ((), ())),
        precision=lax.Precision.HIGHEST,
        preferred_element_type=f32,
    )
    return (
        block_out,
        grad_inputs,
        grad_skips,
        grad_skip_w,
        grad_qkv,
        grad_out,
        grad_up,
        grad_down,
        grad_mod,
    )


def solution(mesh):
    batch, wide = mesh.devices.shape

    def run(inputs, *rest):
        rows = 2 * inputs.shape[0]
        assert inputs.shape[0] == 2 and inputs.shape[1] == batch and wide % rows == 0
        fine = Mesh(mesh.devices.reshape(batch // 2, 2, rows, wide // rows), ALL_AXES)
        by_batch, by_wide = ("plane", "core"), ("hi", "lo")
        frames = P(None, by_batch, by_wide, None)
        rowed = P(None, by_batch, None)
        weight, columns = P(ALL_AXES, None), P(None, ALL_AXES)
        mapped = jax.shard_map(
            body,
            mesh=fine,
            in_specs=(frames, frames, frames, rowed, rowed) + (weight,) * 5 + (columns,),
            out_specs=(frames, frames, frames) + (weight,) * 5 + (columns,),
            check_vma=False,
        )
        return mapped(inputs, *rest)

    return run
```

```python
import functools
import math

import jax
import jax.numpy as jnp
from jax import lax
from jax.experimental import pallas as pl
from jax.experimental.pallas import tpu as pltpu
from jax.sharding import Mesh
from jax.sharding import PartitionSpec as P

HEAD_DIM = 64
TILE = 128
BLOCK = 256
ROW_TILE = 256
FEED_TILE = 1024
FEED_PART = 512
VMEM_BYTES = 60 * 1024 * 1024
ROW_AXES = ("core", "lo")
LINE_AXES = ("core", "hi", "lo")
ALL_AXES = ("plane", "core", "hi", "lo")
f32 = jnp.float32
bf16 = jnp.bfloat16


def dot_nn(left, right):
    return lax.dot_general(left, right, (((1,), (0,)), ((), ())), preferred_element_type=f32)


def dot_nt(left, right):
    return lax.dot_general(left, right, (((1,), (1,)), ((), ())), preferred_element_type=f32)


def dot_tn(left, right):
    return lax.dot_general(left, right, (((0,), (0,)), ((), ())), preferred_element_type=f32)


def params(*semantics):
    return pltpu.CompilerParams(dimension_semantics=semantics, vmem_limit_bytes=VMEM_BYTES)


def cost(flops, moved, special=0):
    return pl.CostEstimate(flops=int(flops), bytes_accessed=int(moved), transcendentals=int(special))


def flat(ref):
    return ref[...].reshape(-1, ref.shape[-1])


def choose(segment_column, table_ref):
    count = table_ref.shape[0]
    picked = table_ref[count - 1 : count, :]
    for label in range(count - 2, -1, -1):
        picked = jnp.where(segment_column == label, table_ref[label : label + 1, :], picked)
    return picked


def normalise(values):
    centred = values - jnp.mean(values, axis=-1, keepdims=True)
    variance = jnp.mean(centred * centred, axis=-1, keepdims=True)
    inverse = lax.rsqrt(variance + 1e-06)
    return centred * inverse, inverse


def merge_kernel(x_ref, s_ref, top_ref, bottom_ref, resid_ref):
    resid = dot_nn(x_ref[...], flat(top_ref)) + dot_nn(s_ref[...], flat(bottom_ref))
    resid_ref[...] = resid.astype(bf16)


def norm_kernel(resid_ref, seg_ref, shift_ref, scale_ref, normed_ref):
    unit, _ = normalise(resid_ref[...].astype(f32))
    label = seg_ref[...]
    normed = unit * (1.0 + choose(label, scale_ref)) + choose(label, shift_ref)
    normed_ref[...] = normed.astype(bf16)


def out_norm_kernel(mixed_ref, w_ref, resid_in_ref, seg_ref, shift_ref, scale_ref, resid_ref, normed_ref):
    resid = resid_in_ref[...].astype(f32) + dot_nn(mixed_ref[...], flat(w_ref))
    resid_ref[...] = resid
    unit, _ = normalise(resid)
    label = seg_ref[...]
    normed = unit * (1.0 + choose(label, scale_ref)) + choose(label, shift_ref)
    normed_ref[...] = normed.astype(bf16)


def segment_sums(row_labels, values, total_ref):
    members = lax.broadcasted_iota(jnp.int32, (total_ref.shape[0], row_labels.shape[1]), 0) == row_labels
    members = members.astype(f32).astype(bf16)
    high = values.astype(bf16)
    low = (values - high.astype(f32)).astype(bf16)
    total_ref[...] += dot_nn(members, high) + dot_nn(members, low)


def norm_pull(grad, resid, scale):
    unit, inverse = normalise(resid)
    inner = grad * (1.0 + scale)
    pulled = inverse * (
        inner
        - jnp.mean(inner, axis=-1, keepdims=True)
        - unit * jnp.mean(inner * unit, axis=-1, keepdims=True)
    )
    return pulled, grad * unit


def norm_two_back_kernel(
    g_ref, resid_ref, cot_ref, seg_ref, segr_ref, scale_ref, w_ref, mid_ref, low_ref, mix_ref, dshift_ref, dscale_ref
):
    @pl.when(pl.program_id(0) == 0)
    def _():
        dshift_ref[...] = jnp.zeros_like(dshift_ref)
        dscale_ref[...] = jnp.zeros_like(dscale_ref)

    grad = g_ref[...]
    pulled, by_scale = norm_pull(grad, resid_ref[...], choose(seg_ref[...], scale_ref))
    grad_mid = cot_ref[...].astype(f32) + pulled
    low = grad_mid.astype(bf16)
    mid_ref[...] = grad_mid
    low_ref[...] = low
    mix_ref[...] = dot_nt(low, flat(w_ref)).astype(bf16)
    segment_sums(segr_ref[...], grad, dshift_ref)
    segment_sums(segr_ref[...], by_scale, dscale_ref)


def norm_one_back_kernel(
    own_ref, other_ref, resid_ref, mid_ref, seg_ref, segr_ref, scale_ref, grad_ref, dshift_ref, dscale_ref
):
    @pl.when(pl.program_id(0) == 0)
    def _():
        dshift_ref[...] = jnp.zeros_like(dshift_ref)
        dscale_ref[...] = jnp.zeros_like(dscale_ref)

    grad = own_ref[...] + other_ref[...].astype(f32)
    pulled, by_scale = norm_pull(grad, resid_ref[...].astype(f32), choose(seg_ref[...], scale_ref))
    grad_ref[...] = (mid_ref[...] + pulled).astype(bf16)
    segment_sums(segr_ref[...], grad, dshift_ref)
    segment_sums(segr_ref[...], by_scale, dscale_ref)


def unmerge_kernel(g_ref, top_ref, bottom_ref, inputs_ref, skips_ref):
    inputs_ref[...] = dot_nt(g_ref[...], flat(top_ref)).astype(bf16)
    skips_ref[...] = dot_nt(g_ref[...], flat(bottom_ref)).astype(bf16)


def project_kernel(place_ref, x_ref, w_ref, out_ref):
    out_ref[...] = dot_nn(x_ref[...], flat(w_ref)).astype(bf16)


def project(value, gathered, begin, rows, heads_wide, member):
    length, width = value.shape
    tile = min(8 * ROW_TILE, length)
    return pl.pallas_call(
        project_kernel,
        grid_spec=pltpu.PrefetchScalarGridSpec(
            num_scalar_prefetch=1,
            grid=(3, length // tile),
            in_specs=[
                pl.BlockSpec((tile, width), lambda t, i, r: (i, 0)),
                pl.BlockSpec((width // rows, rows, heads_wide), lambda t, i, r: (0, begin // rows + t, r[0])),
            ],
            out_specs=pl.BlockSpec((tile, heads_wide), lambda t, i, r: (i, t)),
        ),
        out_shape=jax.ShapeDtypeStruct((length, 3 * heads_wide), bf16),
        compiler_params=params("arbitrary", "arbitrary"),
        cost_estimate=cost(1, 1),
    )(member.reshape(1), value, gathered)


def pull_project_kernel(place_ref, dq_ref, dk_ref, dv_ref, q_ref, k_ref, v_ref, out_ref):
    total = dot_nt(dq_ref[...], flat(q_ref))
    total += dot_nt(dk_ref[...], flat(k_ref))
    total += dot_nt(dv_ref[...], flat(v_ref))
    out_ref[...] = total.astype(out_ref.dtype)


def pull_project(grad_proj, gathered, rows, heads_wide, member, frames, half, kind):
    width = gathered.shape[2]
    tile = min(2 * ROW_TILE, frames)
    steps = frames // tile
    grads = [
        pl.BlockSpec((tile, heads_wide), functools.partial(lambda t, i, r: (r[1] * steps + i, t), t)) for t in range(3)
    ]
    weights = [
        pl.BlockSpec((width // rows, rows, heads_wide), functools.partial(lambda t, i, r: (0, t, r[0]), t))
        for t in range(3)
    ]
    return pl.pallas_call(
        pull_project_kernel,
        grid_spec=pltpu.PrefetchScalarGridSpec(
            num_scalar_prefetch=1,
            grid=(steps,),
            in_specs=grads + weights,
            out_specs=pl.BlockSpec((tile, width), lambda i, r: (i, 0)),
        ),
        out_shape=jax.ShapeDtypeStruct((frames, width), kind),
        compiler_params=params("arbitrary"),
        cost_estimate=cost(6 * frames * width * heads_wide, 8 * frames * width),
    )(jnp.stack([member, half]).astype(jnp.int32), *[grad_proj] * 3, *[gathered] * 3)


def rowwise(kernel, frames, blocked, outs, sums=0, flops=0, light=False):
    tile = min(ROW_TILE, frames)
    in_specs, args, moved = [], [], 0
    for kind, value in blocked:
        if kind == "row":
            in_specs.append(pl.BlockSpec((1, tile), lambda i: (0, i)))
        elif kind == "weight":
            value, block, index = value
            in_specs.append(pl.BlockSpec(block, functools.partial(lambda index, i: index, index)))
        elif kind == "whole":
            in_specs.append(pl.BlockSpec(value.shape, lambda i: (0, 0)))
        else:
            in_specs.append(pl.BlockSpec((tile, value.shape[1]), lambda i: (i, 0)))
        args.append(value)
        moved += value.size * value.dtype.itemsize
    out_specs, shapes = [], []
    for width, kind in outs:
        out_specs.append(pl.BlockSpec((tile, width), lambda i: (i, 0)))
        shapes.append(jax.ShapeDtypeStruct((frames, width), kind))
        moved += frames * width * jnp.dtype(kind).itemsize
    for _ in range(sums):
        out_specs.append(pl.BlockSpec((8, outs[0][0]), lambda i: (0, 0)))
        shapes.append(jax.ShapeDtypeStruct((8, outs[0][0]), f32))
    return pl.pallas_call(
        kernel,
        grid=(frames // tile,),
        in_specs=in_specs,
        out_specs=out_specs,
        out_shape=shapes,
        compiler_params=params("arbitrary"),
        cost_estimate=cost(1, 1) if light else cost(flops, moved),
    )(*args)


def swap_halves(values, lanes):
    half = HEAD_DIM // 2
    ahead = pltpu.roll(values, values.shape[1] - half, 1)
    behind = pltpu.roll(values, half, 1)
    return jnp.where(lanes % HEAD_DIM < half, ahead, behind)


def widen(table, width):
    return jnp.concatenate([table] * (width // table.shape[1]), axis=1)


def span(i):
    return pl.ds(pl.multiple_of(i * BLOCK, BLOCK), BLOCK)


def own_lanes(parts, lanes):
    picked = parts[0]
    for h in range(1, len(parts)):
        picked = jnp.where(lanes // HEAD_DIM == h, parts[h], picked)
    return picked


def by_count(count, most, run):
    for each in range(1, most + 1):
        pl.when(count == each)(functools.partial(run, each))


def attend_forward_kernel(
    range_ref, q_ref, k_ref, v_ref, cos_ref, sin_ref, segc_ref, segr_ref,
    out_ref, qrot_ref, krot_ref, lse_ref, seg_wide,
):
    length, width = q_ref.shape
    heads = width // HEAD_DIM
    blocks = length // BLOCK
    lanes = lax.broadcasted_iota(jnp.int32, (BLOCK, width), 1)

    def turn(i, carry):
        rows = span(i)
        cosine, sine = widen(cos_ref[rows, :], width), widen(sin_ref[rows, :], width)
        for source, target, factor in ((q_ref, qrot_ref, HEAD_DIM**-0.5), (k_ref, krot_ref, None)):
            values = source[rows, :].astype(f32)
            turned = (values * cosine + swap_halves(values, lanes) * sine).astype(bf16)
            if factor is not None:
                turned = turned * jnp.asarray(factor, bf16)
            target[rows, :] = turned
        seg_wide[rows, :] = jnp.broadcast_to(segc_ref[rows, :], (BLOCK, TILE))
        return carry

    lax.fori_loop(0, blocks, turn, 0)

    def one_query(i, carry):
        rows = span(i)

        def work(count):
            keys = pl.ds(pl.multiple_of(range_ref[0, i] * BLOCK, BLOCK), count * BLOCK)
            allowed = widen(seg_wide[rows, :], count * BLOCK) == segr_ref[:, keys]
            query = qrot_ref[rows, :]
            zero = jnp.zeros_like(query)
            mixed = []
            for h in range(heads):
                scores = dot_nt(jnp.where(lanes // HEAD_DIM == h, query, zero), krot_ref[keys, :])
                scores = jnp.where(allowed, scores, -1e30)
                highest = jnp.max(scores, axis=1, keepdims=True)
                powers = jnp.exp(scores - highest)
                totals = jnp.sum(powers, axis=1, keepdims=True)
                mixed.append(dot_nn(powers.astype(bf16), v_ref[keys, :]) * (1.0 / totals))
                logsum = jnp.broadcast_to(highest + jnp.log(totals), (BLOCK, TILE))
                lse_ref[0, h : h + 1, rows] = logsum.T[0:1]
            out_ref[rows, :] = own_lanes(mixed, lanes).astype(bf16)

        by_count(range_ref[1, i] - range_ref[0, i], blocks, work)
        return carry

    lax.fori_loop(0, blocks, one_query, 0)


def attend_forward(ranges, projected, cosine, sine, seg_column, seg_row):
    length, width = projected.shape
    width //= 3
    panels, heads = width // TILE, TILE // HEAD_DIM
    panel = lambda shift: pl.BlockSpec((length, TILE), lambda p, r: (0, shift * panels + p))
    whole = lambda shape: pl.BlockSpec(shape, lambda p, r: (0,) * len(shape))
    return pl.pallas_call(
        attend_forward_kernel,
        grid_spec=pltpu.PrefetchScalarGridSpec(
            num_scalar_prefetch=1,
            grid=(panels,),
            in_specs=[panel(0), panel(1), panel(2), whole(cosine.shape), whole(sine.shape),
                      whole(seg_column.shape), whole(seg_row.shape)],
            out_specs=[panel(0), panel(0), panel(0), pl.BlockSpec((1, heads, length), lambda p, r: (p, 0, 0))],
            scratch_shapes=[pltpu.VMEM((length, TILE), jnp.int32)],
        ),
        out_shape=[jax.ShapeDtypeStruct((length, width), bf16)] * 3
        + [jax.ShapeDtypeStruct((panels, heads, length), f32)],
        compiler_params=params("arbitrary"),
        cost_estimate=cost(8 * length * length * width, 14 * length * width, length * length * width // HEAD_DIM),
    )(ranges, projected, projected, projected, cosine, sine, seg_column, seg_row)


def attend_backward_kernel(
    range_ref, q_ref, k_ref, v_ref, out_ref, do_ref, lse_ref, cos_ref, sin_ref, segc_ref, segr_ref,
    grad_ref, dq, dk_low, dv_low, delta, seg_wide,
):
    length, width = q_ref.shape
    heads = width // HEAD_DIM
    blocks = length // BLOCK
    step = pl.program_id(1)

    @pl.when(step == 0)
    def _():
        lanes = lax.broadcasted_iota(jnp.int32, (BLOCK, width), 1)
        picker = (
            lax.broadcasted_iota(jnp.int32, (8, width), 0)
            == lax.broadcasted_iota(jnp.int32, (8, width), 1) // HEAD_DIM
        ).astype(f32)

        def prepare(i, carry):
            rows = span(i)
            product = do_ref[rows, :].astype(f32) * out_ref[rows, :].astype(f32)
            delta[:, rows] = lax.dot_general(
                picker, product, (((1,), (1,)), ((), ())),
                precision=lax.Precision.HIGHEST, preferred_element_type=f32,
            )
            dq[:, rows] = jnp.zeros((width, BLOCK), f32)
            seg_wide[rows, :] = jnp.broadcast_to(segc_ref[rows, :], (BLOCK, TILE))
            return carry

        lax.fori_loop(0, blocks, prepare, 0)

        def unturn(values, rows):
            return values * widen(cos_ref[rows, :], width) - swap_halves(values, lanes) * widen(sin_ref[rows, :], width)

        def one_key(j, carry):
            rows = span(j)

            def work(count):
                there = pl.ds(pl.multiple_of(range_ref[0, j] * BLOCK, BLOCK), count * BLOCK)
                allowed = widen(seg_wide[rows, :], count * BLOCK) == segr_ref[:, there]
                zero = jnp.zeros((BLOCK, width), bf16)
                key, value = (
                    jnp.concatenate([jnp.where(lanes // HEAD_DIM == h, ref[rows, :], zero) for h in range(heads)], axis=0)
                    for ref in (k_ref, v_ref)
                )
                query, grad_out = q_ref[there, :], do_ref[there, :]
                found, grad_prob = dot_nt(key, query), dot_nt(value, grad_out)
                parts, lows = [], []
                for h in range(heads):
                    half = slice(h * BLOCK, (h + 1) * BLOCK)
                    scores = found[half] - lse_ref[0, h : h + 1, there]
                    part = jnp.exp(jnp.where(allowed, scores, -1e30))
                    parts.append(part.astype(bf16))
                    lows.append((part * (grad_prob[half] - delta[h : h + 1, there])).astype(bf16))
                grad_scores = jnp.concatenate(lows, axis=0)
                grad_v = dot_nn(jnp.concatenate(parts, axis=0), grad_out)
                grad_k = dot_nn(grad_scores, query)
                grad_v, grad_k = ([v[h * BLOCK : (h + 1) * BLOCK] for h in range(heads)] for v in (grad_v, grad_k))
                dq[:, there] += dot_tn(key, grad_scores)
                dk_low[rows, :] = unturn(own_lanes(grad_k, lanes), rows).astype(bf16)
                dv_low[rows, :] = own_lanes(grad_v, lanes).astype(bf16)

            by_count(range_ref[1, j] - range_ref[0, j], blocks, work)
            return carry

        lax.fori_loop(0, blocks, one_key, 0)

        def finish(i, carry):
            rows = span(i)
            grad_ref[rows, :] = unturn(dq[:, rows].T * HEAD_DIM**-0.5, rows).astype(bf16)
            return carry

        lax.fori_loop(0, blocks, finish, 0)

    @pl.when(step == 1)
    def _():
        grad_ref[...] = dk_low[...]

    @pl.when(step == 2)
    def _():
        grad_ref[...] = dv_low[...]


def attend_backward(ranges, queries, keys, projected, mixed, grad_mixed, logsum, cosine, sine, seg_column, seg_row):
    length, width = queries.shape
    panels, heads = width // TILE, TILE // HEAD_DIM
    panel = lambda shift: pl.BlockSpec((length, TILE), lambda p, t, r: (0, shift * panels + p))
    whole = lambda shape: pl.BlockSpec(shape, lambda p, t, r: (0,) * len(shape))
    return pl.pallas_call(
        attend_backward_kernel,
        grid_spec=pltpu.PrefetchScalarGridSpec(
            num_scalar_prefetch=1,
            grid=(panels, 3),
            in_specs=[panel(0), panel(0), panel(2), panel(0), panel(0),
                      pl.BlockSpec((1, heads, length), lambda p, t, r: (p, 0, 0)),
                      whole(cosine.shape), whole(sine.shape), whole(seg_column.shape), whole(seg_row.shape)],
            out_specs=pl.BlockSpec((length, TILE), lambda p, t, r: (0, t * panels + p)),
            scratch_shapes=[
                pltpu.VMEM((TILE, length), f32),
                pltpu.VMEM((length, TILE), bf16),
                pltpu.VMEM((length, TILE), bf16),
                pltpu.VMEM((8, length), f32),
                pltpu.VMEM((length, TILE), jnp.int32),
            ],
        ),
        out_shape=jax.ShapeDtypeStruct((length, 3 * width), bf16),
        compiler_params=params("arbitrary", "arbitrary"),
        cost_estimate=cost(20 * length * length * width, 16 * length * width, length * length * width // HEAD_DIM),
    )(ranges, queries, keys, projected, mixed, grad_mixed, logsum, cosine, sine, seg_column, seg_row)


def gelu_and_slope(x):
    root = math.sqrt(2.0 / math.pi)
    square = x * x
    bend = jnp.tanh(x * (root + root * 0.044715 * square))
    half = 0.5 * x
    half_up = 0.5 + 0.5 * bend
    slope = half_up + half * (1.0 - bend * bend) * (root + 3.0 * root * 0.044715 * square)
    return half + half * bend, slope


def feed_kernel(
    n_ref, cot_ref, resid_ref, up_ref, down_ref, out_ref, back_ref, gup_ref, gdown_ref,
    total, n_turned, act_turned, pre,
):
    step, last = pl.program_id(0), pl.num_programs(0) - 1
    frames, width = n_ref.shape
    tile = min(FEED_TILE, frames)

    def rows_of(i):
        return pl.ds(pl.multiple_of(i * tile, tile), tile)

    @pl.when(step == 0)
    def _():
        def turn(i, carry):
            rows = rows_of(i)
            n_turned[:, rows] = n_ref[rows, :].T
            total[rows, :] = resid_ref[rows, :]
            back_ref[rows, :] = jnp.zeros((tile, width), f32)
            return carry

        lax.fori_loop(0, frames // tile, turn, 0)

    def chunk(i, carry):
        rows = rows_of(i)
        up, down = flat(up_ref), flat(down_ref)
        hidden = dot_nn(n_ref[rows, :], up)
        grad_act = dot_nt(cot_ref[rows, :], down)
        activated, slope = gelu_and_slope(hidden)
        activated = activated.astype(bf16)
        grad_pre = (grad_act * slope).astype(bf16)
        act_turned[:, rows] = activated.T
        pre[rows, :] = grad_pre
        total[rows, :] += dot_nn(activated, down)
        back_ref[rows, :] += dot_nt(grad_pre, up)
        return carry

    lax.fori_loop(0, frames // tile, chunk, 0)

    for begin in range(0, width, FEED_PART):
        rows = slice(begin, begin + FEED_PART)
        gup_ref[rows, :] = dot_nn(n_turned[rows, :], pre[...]).astype(bf16)
    piece = act_turned.shape[0]
    for begin in range(0, piece, FEED_PART):
        rows = slice(begin, begin + FEED_PART)
        gdown_ref[rows, :] = dot_nn(act_turned[rows, :], cot_ref[...]).astype(bf16)

    @pl.when(step == last)
    def _():
        out_ref[...] = total[...].astype(bf16)


def feed_forward_and_back(normed, cot, resid, hidden, piece, w_up, w_down):
    frames, width = normed.shape
    whole = lambda: pl.BlockSpec((frames, width), lambda j: (0, 0), pipeline_mode=pl.Buffered(1))
    return pl.pallas_call(
        feed_kernel,
        grid=(hidden // piece,),
        in_specs=[whole(), whole(), whole(), pl.BlockSpec(*w_up[1:]), pl.BlockSpec(*w_down[1:])],
        out_specs=[pl.BlockSpec((frames, width), lambda j: (0, 0))] * 2
        + [pl.BlockSpec((width, piece), lambda j: (0, j)), pl.BlockSpec((piece, width), lambda j: (j, 0))],
        out_shape=[
            jax.ShapeDtypeStruct((frames, width), bf16),
            jax.ShapeDtypeStruct((frames, width), f32),
            jax.ShapeDtypeStruct((width, hidden), bf16),
            jax.ShapeDtypeStruct((hidden, width), bf16),
        ],
        scratch_shapes=[
            pltpu.VMEM((frames, width), f32),
            pltpu.VMEM((width, frames), bf16),
            pltpu.VMEM((piece, frames), bf16),
            pltpu.VMEM((frames, piece), bf16),
        ],
        compiler_params=params("arbitrary"),
        cost_estimate=cost(12 * frames * width * hidden, 8 * width * hidden + 16 * frames * width, frames * hidden),
    )(normed, cot, resid, w_up[0], w_down[0])


def body(inputs, skips, cotangent, segment_ids, time_steps, w_skip, w_qkv, w_out, w_up, w_down, w_mod):
    micro, _, piece, width = inputs.shape
    length = segment_ids.shape[-1]
    labels = time_steps.shape[-1]
    planes, lows, highs = lax.axis_size("plane"), lax.axis_size("lo"), lax.axis_size("hi")
    line = highs * lows
    group = 2 * lows
    devices = planes * 2 * line
    core, high, low = lax.axis_index("core"), lax.axis_index("hi"), lax.axis_index("lo")
    place = high * lows + low
    member = core * lows + low
    frames = 2 * piece
    heads_wide = width // group
    first_core = core == 0
    swap = [(0, 1), (1, 0)]

    def route(parity):
        pairs = []
        for c in range(2):
            for z in range(line):
                row = c * micro + ((z % 2) ^ parity)
                to_core, to_low = divmod(z // 2, lows)
                pairs.append((c * line + z, (to_core * highs + row) * lows + to_low))
        return pairs

    there = (route(0), route(1))
    back = tuple([(b, a) for a, b in pairs] for pairs in there)
    odd_place = place % 2
    even_row = high % 2 == 0

    def to_rows(value):
        value = value[:, 0]
        near = lax.ppermute(lax.dynamic_index_in_dim(value, odd_place, 0, False), LINE_AXES, there[0])
        far = lax.ppermute(lax.dynamic_index_in_dim(value, 1 - odd_place, 0, False), LINE_AXES, there[1])
        return jnp.concatenate([jnp.where(even_row, near, far), jnp.where(even_row, far, near)], axis=0)

    def from_rows(value):
        value = value.reshape(2, piece, width)
        near = lax.ppermute(lax.dynamic_index_in_dim(value, high % 2, 0, False), LINE_AXES, back[0])
        far = lax.ppermute(lax.dynamic_index_in_dim(value, 1 - high % 2, 0, False), LINE_AXES, back[1])
        even = odd_place == 0
        return jnp.stack([jnp.where(even, near, far), jnp.where(even, far, near)])[:, None]

    def frames_to_row(value):
        if group > 2:
            return lax.all_gather(value, ROW_AXES, axis=0, tiled=True)
        other = lax.ppermute(value, "core", swap)
        return jnp.concatenate([jnp.where(first_core, value, other), jnp.where(first_core, other, value)], axis=0)

    def heads_to_frames(value):
        if group > 2:
            return lax.all_to_all(value, ROW_AXES, split_axis=0, concat_axis=1, tiled=True)
        other = lax.ppermute(lax.dynamic_slice_in_dim(value, (1 - core) * frames, frames, 0), "core", swap)
        own = lax.dynamic_slice_in_dim(value, core * frames, frames, 0)
        return jnp.concatenate([jnp.where(first_core, own, other), jnp.where(first_core, other, own)], axis=1)

    def frames_to_heads(value):
        if group > 2:
            return lax.all_to_all(value, ROW_AXES, split_axis=1, concat_axis=0, tiled=True)
        other = lax.ppermute(lax.dynamic_slice_in_dim(value, (1 - core) * heads_wide, heads_wide, 1), "core", swap)
        own = lax.dynamic_slice_in_dim(value, core * heads_wide, heads_wide, 1)
        return jnp.concatenate([jnp.where(first_core, own, other), jnp.where(first_core, other, own)], axis=0)

    def share_on_line(value):
        pieces = [value]
        for flip in range(1, line):
            pieces.append(lax.ppermute(value, ("hi", "lo"), [(i, i ^ flip) for i in range(line)]))
        pieces = jnp.stack(pieces)
        return jnp.stack([lax.dynamic_index_in_dim(pieces, place ^ i, 0, False) for i in range(line)])

    def gather_planes(value):
        return lax.all_gather(value, ("plane", "core"), axis=0, tiled=True).reshape(devices, -1, width)

    up_rows, down_rows, out_rows = w_up.shape[0], w_down.shape[0], w_out.shape[0]
    skip_rows = w_skip.shape[0]
    columns = w_up.shape[1] // width
    middle = jnp.concatenate([w_qkv[:, i * width : (i + 1) * width] for i in range(3)] + [w_out], axis=0)
    late = jnp.concatenate([w_down] + [w_up[:, i * width : (i + 1) * width] for i in range(columns)], axis=0)
    early = share_on_line(w_skip)
    early, middle, late = lax.optimization_barrier((early, middle, late))
    early = gather_planes(early)
    middle, late = share_on_line(middle), share_on_line(late)
    middle = gather_planes(middle)

    in_place = out_rows % 16 == 0
    hidden = w_up.shape[1]
    chunk = hidden // (2 * planes)

    def weight(gathered, begin, rows, first, count):
        block = (count // rows, rows, width)
        if in_place:
            return gathered, block, (first // count, begin // rows, 0)
        taken = gathered[first // rows : (first + count) // rows, begin : begin + rows]
        return taken.reshape(1, count, width), (1, count, width), (0, 0, 0)

    skip_top, skip_bottom = (weight(early, 0, skip_rows, i * width, width) for i in range(2))
    out_weight = weight(middle, 3 * out_rows, out_rows, 0, width)
    x, s = (v.reshape(frames, width) for v in (inputs, skips))
    (resid_in,) = rowwise(
        merge_kernel, frames, [("", x), ("", s), ("weight", skip_top), ("weight", skip_bottom)], [(width, bf16)], light=True
    )
    stacked = jnp.concatenate([x, s], axis=1)

    labels_own = segment_ids[:, 0]
    labels_other = lax.ppermute(labels_own, "core", swap)
    labels_pick = jnp.where(core == high // micro, labels_own, labels_other)
    seg = lax.dynamic_index_in_dim(labels_pick, high % micro, 0, False)
    names = jnp.arange(labels, dtype=jnp.int32)
    starts = jnp.sum((seg[:, None] < names[None, :]).astype(jnp.int32), axis=0)
    ends = jnp.sum((seg[:, None] <= names[None, :]).astype(jnp.int32), axis=0)
    offset = jnp.sum(jnp.where(seg[:, None] == names[None, :], starts[None, :], 0), axis=1)
    where_at = jnp.arange(length, dtype=jnp.int32) - offset
    by_block = seg.reshape(-1, BLOCK)
    begin = jnp.sum(jnp.where(by_block[:, :1] == names[None, :], starts[None, :], 0), axis=1)
    finish = jnp.sum(jnp.where(by_block[:, -1:] == names[None, :], ends[None, :], 0), axis=1)
    ranges = jnp.stack([begin // BLOCK, (finish + BLOCK - 1) // BLOCK]).astype(jnp.int32)
    half = HEAD_DIM // 2
    rates = jnp.exp(-math.log(10000.0) * jnp.arange(half, dtype=f32) / half)
    angles = where_at.astype(f32)[:, None] * rates
    cosine = jnp.tile(jnp.cos(angles), (1, 4))
    sine = jnp.sin(angles)
    sine = jnp.concatenate([-sine, sine, -sine, sine], axis=1)
    seg_column, seg_row = seg[:, None], seg[None, :]
    mine = lax.dynamic_slice_in_dim(seg, member * frames, frames, 0)

    steps = lax.all_gather(time_steps[:, 0], ("plane", "core"), axis=0, tiled=True).reshape(-1)
    quarter = w_mod.shape[0] // 2
    pace = jnp.exp(-math.log(10000.0) * jnp.arange(quarter, dtype=f32) / quarter)
    turns = steps.astype(f32)[:, None] * pace
    embedded = jnp.concatenate([jnp.sin(turns), jnp.cos(turns)], axis=1).astype(bf16)
    block_mod = jnp.dot(embedded, w_mod, preferred_element_type=f32)
    own_columns = block_mod.shape[1]
    block_mod = block_mod.reshape(planes, 1, highs, 1, labels, own_columns)
    block_mod = jnp.broadcast_to(block_mod, (planes, 2, highs, lows, labels, own_columns))
    block_mod = lax.all_to_all(
        block_mod.reshape(devices, labels, own_columns), ALL_AXES, split_axis=0, concat_axis=0, tiled=True
    )
    modulation = jnp.moveaxis(block_mod, 0, 1).reshape(labels, 4, width)

    def own_qkv(gathered):
        parts = []
        for i in range(3):
            whole = gathered[:, i * out_rows : (i + 1) * out_rows].reshape(width, width)
            parts.append(lax.dynamic_slice_in_dim(whole, member * heads_wide, heads_wide, 1))
        return jnp.concatenate(parts, axis=1)

    mine_column, mine_row = mine[:, None], mine[None, :]
    shift_one, scale_one, shift_two, scale_two = (modulation[:, i] for i in range(4))

    resid_in = to_rows(resid_in.reshape(inputs.shape))
    resid_in, late, cotangent, stacked, modulation, cosine, sine, ranges = lax.optimization_barrier(
        (resid_in, late, cotangent, stacked, modulation, cosine, sine, ranges)
    )
    (normed_one,) = rowwise(
        norm_kernel,
        frames,
        [("", resid_in), ("", mine_column), ("whole", shift_one), ("whole", scale_one)],
        [(width, bf16)],
        light=True,
    )
    normed_row = frames_to_row(normed_one)
    if in_place:
        projected = project(normed_row, middle, 0, out_rows, heads_wide, member)
    else:
        projected = jnp.dot(normed_row, own_qkv(middle), preferred_element_type=f32).astype(bf16)
    late = gather_planes(late)
    cot = to_rows(cotangent)
    if in_place:
        per = width // chunk
        up_weight = (late, (devices, up_rows, chunk), lambda j: (0, down_rows // up_rows + j // per, j % per))
        down_weight = (late, (chunk // down_rows, down_rows, width), lambda j: (j, 0, 0))
    else:
        pieces = [late[:, down_rows + i * up_rows : down_rows + (i + 1) * up_rows] for i in range(columns)]
        up_full = jnp.concatenate([v.reshape(width, width) for v in pieces], axis=1)
        up_weight = (up_full[None], (1, width, chunk), lambda j: (0, 0, j))
        down_weight = (late[:, :down_rows].reshape(1, -1, width), (1, chunk, width), lambda j: (0, j, 0))
    mixed_heads, queries, keys, logsum = attend_forward(ranges, projected, cosine, sine, seg_column, seg_row)
    mixed = heads_to_frames(mixed_heads)
    resid_mid, normed_two = rowwise(
        out_norm_kernel,
        frames,
        [("", mixed), ("weight", out_weight), ("", resid_in), ("", mine_column), ("whole", shift_two), ("whole", scale_two)],
        [(width, f32), (width, bf16)],
        flops=2 * frames * width * width,
    )
    result, grad_normed_two, grad_up, grad_down = feed_forward_and_back(
        normed_two, cot, resid_mid, hidden, chunk, up_weight, down_weight
    )

    def over_cores(kept, axis):
        other = lax.ppermute(lax.dynamic_index_in_dim(kept, 1 - core, axis, False), "core", swap)
        own = lax.dynamic_index_in_dim(kept, core, axis, False)
        return (own.astype(f32) + other.astype(f32)).astype(bf16)

    plane = lax.axis_index("plane")

    def exchange(value, axes, here, count):
        total = lax.dynamic_index_in_dim(value, here, 0, False).astype(f32)
        for flip in range(1, count):
            sent = lax.dynamic_index_in_dim(value, here ^ flip, 0, False)
            total += lax.ppermute(sent, axes, [(i, i ^ flip) for i in range(count)]).astype(f32)
        return total

    def exchange_planes(value):
        return exchange(value, "plane", plane, planes).astype(bf16)

    def exchange_line(value):
        return exchange(value.reshape(line, -1, value.shape[-1]), ("hi", "lo"), place, line)

    grad_up, grad_down = (
        lax.psum_scatter(v, ("plane", "core"), scatter_dimension=0, tiled=True) for v in (grad_up, grad_down)
    )

    grad_mid, grad_mid_low, grad_frames, grad_shift_two, grad_scale_two = rowwise(
        norm_two_back_kernel,
        frames,
        [("", grad_normed_two), ("", resid_mid), ("", cot), ("", mine_column), ("row", mine_row),
         ("whole", scale_two), ("weight", out_weight)],
        [(width, f32), (width, bf16), (width, bf16)],
        sums=2,
        light=True,
    )
    grad_heads = frames_to_heads(grad_frames)
    grad_out = lax.dot_general(mixed, grad_mid_low, (((0,), (0,)), ((), ())), preferred_element_type=f32)
    grad_out = over_cores(grad_out.astype(bf16).reshape(planes, 2, -1, width), 1)
    grad_heads, grad_out, result = lax.optimization_barrier((grad_heads, grad_out, result))
    block_out = from_rows(result)
    grad_proj = attend_backward(
        ranges, queries, keys, projected, mixed_heads, grad_heads, logsum, cosine, sine, seg_column, seg_row
    )
    grad_proj, block_out, grad_up = lax.optimization_barrier((grad_proj, block_out, grad_up))
    grad_up = lax.psum_scatter(grad_up, ("hi", "lo"), scatter_dimension=0, tiled=True)
    grad_qkv = lax.dot_general(normed_row, grad_proj, (((0,), (0,)), ((), ())), preferred_element_type=f32)
    grad_qkv = grad_qkv.astype(bf16)
    grad_proj, grad_qkv = lax.optimization_barrier((grad_proj, grad_qkv))
    if group > 2:
        grad_qkv = grad_qkv.reshape(planes, 2, highs, lows, -1, 3, 1, heads_wide)
        grad_qkv = jnp.moveaxis(grad_qkv, (1, 3), (0, 1)).reshape(group, -1, 3, 1, heads_wide)
        grad_qkv = lax.all_to_all(grad_qkv, ROW_AXES, split_axis=0, concat_axis=3, tiled=True)
        grad_qkv = grad_qkv.reshape(-1, 3 * width)
        partial = dot_nt(grad_proj, own_qkv(middle)).astype(bf16)
        grad_one = lax.psum_scatter(partial, ROW_AXES, scatter_dimension=0, tiled=True).astype(f32)
        grad_one_other = jnp.zeros((frames, width), bf16)
    else:
        split = grad_qkv.reshape(planes, 2, -1, 3 * heads_wide)
        other = lax.ppermute(lax.dynamic_index_in_dim(split, 1 - core, 1, False), "core", swap)
        own = lax.dynamic_index_in_dim(split, core, 1, False)
        own, other = (v.reshape(-1, 3 * heads_wide) for v in (own, other))
        left, right = jnp.where(first_core, own, other), jnp.where(first_core, other, own)
        grad_qkv = jnp.concatenate(
            [v[:, i * heads_wide : (i + 1) * heads_wide] for i in range(3) for v in (left, right)], axis=1
        )
        if in_place:
            pull = functools.partial(pull_project, grad_proj, middle, out_rows, heads_wide, member, frames)
            away, home = pull(1 - core, bf16), pull(core, f32)
        else:
            qkv_own = own_qkv(middle)
            away = lax.dynamic_slice_in_dim(grad_proj, (1 - core) * frames, frames, 0)
            home = lax.dynamic_slice_in_dim(grad_proj, core * frames, frames, 0)
            away, home = dot_nt(away, qkv_own).astype(bf16), dot_nt(home, qkv_own)
        grad_one_other = lax.ppermute(away, "core", swap)
        grad_one = home
    grad_one, grad_qkv = lax.optimization_barrier((grad_one, grad_qkv))
    if group > 2:
        grad_qkv = lax.psum_scatter(grad_qkv, ("plane", "hi"), scatter_dimension=0, tiled=True).astype(f32)
    else:
        grad_qkv = jnp.concatenate([grad_qkv.reshape(planes, -1, 3 * width), grad_out], axis=2)
        grad_qkv = exchange_planes(grad_qkv)
    grad_in, grad_shift_one, grad_scale_one = rowwise(
        norm_one_back_kernel,
        frames,
        [("", grad_one), ("", grad_one_other), ("", resid_in), ("", grad_mid), ("", mine_column), ("row", mine_row),
         ("whole", scale_one)],
        [(width, bf16)],
        sums=2,
    )
    grad_in_home = from_rows(grad_in)
    grad_mod = jnp.stack([v[:labels] for v in (grad_shift_one, grad_scale_one, grad_shift_two, grad_scale_two)], axis=1)
    grad_mod = jnp.moveaxis(grad_mod.reshape(labels, devices, own_columns), 1, 0)
    grad_mod = lax.all_to_all(grad_mod, ALL_AXES, split_axis=0, concat_axis=0, tiled=True)
    grad_in_home, grad_qkv, grad_down, grad_mod = lax.optimization_barrier((grad_in_home, grad_qkv, grad_down, grad_mod))
    grad_down = lax.psum_scatter(grad_down, ("hi", "lo"), scatter_dimension=0, tiled=True)
    grad_up, grad_down = grad_up.astype(f32), grad_down.astype(f32)
    if group == 2:
        grad_qkv = grad_qkv.reshape(line, -1, 4 * width)
        grad_qkv = lax.all_to_all(grad_qkv, ("hi", "lo"), split_axis=0, concat_axis=0, tiled=True)
        grad_qkv = jnp.sum(grad_qkv.astype(f32), axis=0)
        grad_qkv, grad_out = grad_qkv[:, : 3 * width], grad_qkv[:, 3 * width :]
    else:
        grad_out = exchange_line(exchange_planes(grad_out))
    home = grad_in_home.reshape(frames, width)
    grad_skip_w = lax.dot_general(stacked, home, (((0,), (0,)), ((), ())), preferred_element_type=f32).astype(bf16)
    grad_skip_w = exchange_planes(over_cores(grad_skip_w.reshape(planes, 2, -1, width), 1))
    grad_inputs, grad_skips = rowwise(
        unmerge_kernel,
        frames,
        [("", home), ("weight", skip_top), ("weight", skip_bottom)],
        [(width, bf16), (width, bf16)],
        flops=4 * frames * width * width,
    )
    grad_inputs, grad_skips = (v.reshape(grad_in_home.shape) for v in (grad_inputs, grad_skips))

    grad_skip_w = exchange_line(grad_skip_w)
    grad_mod = jnp.sum(grad_mod.reshape(planes, 2, highs, lows, labels, own_columns), axis=(1, 3))
    grad_mod = lax.dot_general(
        embedded.astype(f32),
        grad_mod.reshape(-1, own_columns),
        (((0,), (0,)), ((), ())),
        precision=lax.Precision.HIGHEST,
        preferred_element_type=f32,
    )
    return (
        block_out,
        grad_inputs,
        grad_skips,
        grad_skip_w,
        grad_qkv,
        grad_out,
        grad_up,
        grad_down,
        grad_mod,
    )


def solution(mesh):
    batch, wide = mesh.devices.shape

    def run(inputs, *rest):
        rows = 2 * inputs.shape[0]
        assert inputs.shape[0] == 2 and inputs.shape[1] == batch and wide % rows == 0
        fine = Mesh(mesh.devices.reshape(batch // 2, 2, rows, wide // rows), ALL_AXES)
        by_batch, by_wide = ("plane", "core"), ("hi", "lo")
        frames = P(None, by_batch, by_wide, None)
        rowed = P(None, by_batch, None)
        weight, columns = P(ALL_AXES, None), P(None, ALL_AXES)
        mapped = jax.shard_map(
            body,
            mesh=fine,
            in_specs=(frames, frames, frames, rowed, rowed) + (weight,) * 5 + (columns,),
            out_specs=(frames, frames, frames) + (weight,) * 5 + (columns,),
            check_vma=False,
        )
        return mapped(inputs, *rest)

    return run
```

```python
import functools
import math

import jax
import jax.numpy as jnp
from jax import lax
from jax.experimental import pallas as pl
from jax.experimental.pallas import tpu as pltpu
from jax.sharding import Mesh
from jax.sharding import PartitionSpec as P

HEAD_DIM = 64
TILE = 128
BLOCK = 256
ROW_TILE = 256
FEED_TILE = 1024
FEED_PART = 512
VMEM_BYTES = 60 * 1024 * 1024
ROW_AXES = ("core", "lo")
LINE_AXES = ("core", "hi", "lo")
ALL_AXES = ("plane", "core", "hi", "lo")
f32 = jnp.float32
bf16 = jnp.bfloat16


def dot_nn(left, right):
    return lax.dot_general(left, right, (((1,), (0,)), ((), ())), preferred_element_type=f32)


def dot_nt(left, right):
    return lax.dot_general(left, right, (((1,), (1,)), ((), ())), preferred_element_type=f32)


def dot_tn(left, right):
    return lax.dot_general(left, right, (((0,), (0,)), ((), ())), preferred_element_type=f32)


def params(*semantics):
    return pltpu.CompilerParams(dimension_semantics=semantics, vmem_limit_bytes=VMEM_BYTES)


def cost(flops, moved, special=0):
    return pl.CostEstimate(flops=int(flops), bytes_accessed=int(moved), transcendentals=int(special))


def flat(ref):
    return ref[...].reshape(-1, ref.shape[-1])


def choose(segment_column, table_ref):
    count = table_ref.shape[0]
    picked = table_ref[count - 1 : count, :]
    for label in range(count - 2, -1, -1):
        picked = jnp.where(segment_column == label, table_ref[label : label + 1, :], picked)
    return picked


def normalise(values):
    centred = values - jnp.mean(values, axis=-1, keepdims=True)
    variance = jnp.mean(centred * centred, axis=-1, keepdims=True)
    inverse = lax.rsqrt(variance + 1e-06)
    return centred * inverse, inverse


def merge_kernel(x_ref, s_ref, top_ref, bottom_ref, resid_ref):
    resid = dot_nn(x_ref[...], flat(top_ref)) + dot_nn(s_ref[...], flat(bottom_ref))
    resid_ref[...] = resid.astype(bf16)


def norm_kernel(resid_ref, seg_ref, shift_ref, scale_ref, normed_ref):
    unit, _ = normalise(resid_ref[...].astype(f32))
    label = seg_ref[...]
    normed = unit * (1.0 + choose(label, scale_ref)) + choose(label, shift_ref)
    normed_ref[...] = normed.astype(bf16)


def out_norm_kernel(mixed_ref, w_ref, resid_in_ref, seg_ref, shift_ref, scale_ref, resid_ref, normed_ref):
    resid = resid_in_ref[...].astype(f32) + dot_nn(mixed_ref[...], flat(w_ref))
    resid_ref[...] = resid
    unit, _ = normalise(resid)
    label = seg_ref[...]
    normed = unit * (1.0 + choose(label, scale_ref)) + choose(label, shift_ref)
    normed_ref[...] = normed.astype(bf16)


def segment_sums(row_labels, values, total_ref):
    members = lax.broadcasted_iota(jnp.int32, (total_ref.shape[0], row_labels.shape[1]), 0) == row_labels
    members = members.astype(f32).astype(bf16)
    high = values.astype(bf16)
    low = (values - high.astype(f32)).astype(bf16)
    total_ref[...] += dot_nn(members, high) + dot_nn(members, low)


def norm_pull(grad, resid, scale):
    unit, inverse = normalise(resid)
    inner = grad * (1.0 + scale)
    pulled = inverse * (
        inner
        - jnp.mean(inner, axis=-1, keepdims=True)
        - unit * jnp.mean(inner * unit, axis=-1, keepdims=True)
    )
    return pulled, grad * unit


def norm_two_back_kernel(
    g_ref, resid_ref, cot_ref, seg_ref, segr_ref, scale_ref, w_ref, mid_ref, low_ref, mix_ref, dshift_ref, dscale_ref
):
    @pl.when(pl.program_id(0) == 0)
    def _():
        dshift_ref[...] = jnp.zeros_like(dshift_ref)
        dscale_ref[...] = jnp.zeros_like(dscale_ref)

    grad = g_ref[...]
    pulled, by_scale = norm_pull(grad, resid_ref[...], choose(seg_ref[...], scale_ref))
    grad_mid = cot_ref[...].astype(f32) + pulled
    low = grad_mid.astype(bf16)
    mid_ref[...] = grad_mid
    low_ref[...] = low
    mix_ref[...] = dot_nt(low, flat(w_ref)).astype(bf16)
    segment_sums(segr_ref[...], grad, dshift_ref)
    segment_sums(segr_ref[...], by_scale, dscale_ref)


def norm_one_back_kernel(
    own_ref, other_ref, resid_ref, mid_ref, seg_ref, segr_ref, scale_ref, grad_ref, dshift_ref, dscale_ref
):
    @pl.when(pl.program_id(0) == 0)
    def _():
        dshift_ref[...] = jnp.zeros_like(dshift_ref)
        dscale_ref[...] = jnp.zeros_like(dscale_ref)

    grad = own_ref[...] + other_ref[...].astype(f32)
    pulled, by_scale = norm_pull(grad, resid_ref[...].astype(f32), choose(seg_ref[...], scale_ref))
    grad_ref[...] = (mid_ref[...] + pulled).astype(bf16)
    segment_sums(segr_ref[...], grad, dshift_ref)
    segment_sums(segr_ref[...], by_scale, dscale_ref)


def unmerge_kernel(g_ref, top_ref, bottom_ref, inputs_ref, skips_ref):
    inputs_ref[...] = dot_nt(g_ref[...], flat(top_ref)).astype(bf16)
    skips_ref[...] = dot_nt(g_ref[...], flat(bottom_ref)).astype(bf16)


def project_kernel(place_ref, x_ref, w_ref, out_ref):
    out_ref[...] = dot_nn(x_ref[...], flat(w_ref)).astype(bf16)


def project(value, gathered, begin, rows, heads_wide, member):
    length, width = value.shape
    tile = min(8 * ROW_TILE, length)
    return pl.pallas_call(
        project_kernel,
        grid_spec=pltpu.PrefetchScalarGridSpec(
            num_scalar_prefetch=1,
            grid=(3, length // tile),
            in_specs=[
                pl.BlockSpec((tile, width), lambda t, i, r: (i, 0)),
                pl.BlockSpec((width // rows, rows, heads_wide), lambda t, i, r: (0, begin // rows + t, r[0])),
            ],
            out_specs=pl.BlockSpec((tile, heads_wide), lambda t, i, r: (i, t)),
        ),
        out_shape=jax.ShapeDtypeStruct((length, 3 * heads_wide), bf16),
        compiler_params=params("arbitrary", "arbitrary"),
        cost_estimate=cost(1, 1),
    )(member.reshape(1), value, gathered)


def pull_project_kernel(place_ref, dq_ref, dk_ref, dv_ref, q_ref, k_ref, v_ref, out_ref):
    total = dot_nt(dq_ref[...], flat(q_ref))
    total += dot_nt(dk_ref[...], flat(k_ref))
    total += dot_nt(dv_ref[...], flat(v_ref))
    out_ref[...] = total.astype(out_ref.dtype)


def pull_project(grad_proj, gathered, rows, heads_wide, member, frames, half, kind):
    width = gathered.shape[2]
    tile = min(2 * ROW_TILE, frames)
    steps = frames // tile
    grads = [
        pl.BlockSpec((tile, heads_wide), functools.partial(lambda t, i, r: (r[1] * steps + i, t), t)) for t in range(3)
    ]
    weights = [
        pl.BlockSpec((width // rows, rows, heads_wide), functools.partial(lambda t, i, r: (0, t, r[0]), t))
        for t in range(3)
    ]
    return pl.pallas_call(
        pull_project_kernel,
        grid_spec=pltpu.PrefetchScalarGridSpec(
            num_scalar_prefetch=1,
            grid=(steps,),
            in_specs=grads + weights,
            out_specs=pl.BlockSpec((tile, width), lambda i, r: (i, 0)),
        ),
        out_shape=jax.ShapeDtypeStruct((frames, width), kind),
        compiler_params=params("arbitrary"),
        cost_estimate=cost(6 * frames * width * heads_wide, 8 * frames * width),
    )(jnp.stack([member, half]).astype(jnp.int32), *[grad_proj] * 3, *[gathered] * 3)


def rowwise(kernel, frames, blocked, outs, sums=0, flops=0, light=False):
    tile = min(ROW_TILE, frames)
    in_specs, args, moved = [], [], 0
    for kind, value in blocked:
        if kind == "row":
            in_specs.append(pl.BlockSpec((1, tile), lambda i: (0, i)))
        elif kind == "weight":
            value, block, index = value
            in_specs.append(pl.BlockSpec(block, functools.partial(lambda index, i: index, index)))
        elif kind == "whole":
            in_specs.append(pl.BlockSpec(value.shape, lambda i: (0, 0)))
        else:
            in_specs.append(pl.BlockSpec((tile, value.shape[1]), lambda i: (i, 0)))
        args.append(value)
        moved += value.size * value.dtype.itemsize
    out_specs, shapes = [], []
    for width, kind in outs:
        out_specs.append(pl.BlockSpec((tile, width), lambda i: (i, 0)))
        shapes.append(jax.ShapeDtypeStruct((frames, width), kind))
        moved += frames * width * jnp.dtype(kind).itemsize
    for _ in range(sums):
        out_specs.append(pl.BlockSpec((8, outs[0][0]), lambda i: (0, 0)))
        shapes.append(jax.ShapeDtypeStruct((8, outs[0][0]), f32))
    return pl.pallas_call(
        kernel,
        grid=(frames // tile,),
        in_specs=in_specs,
        out_specs=out_specs,
        out_shape=shapes,
        compiler_params=params("arbitrary"),
        cost_estimate=cost(1, 1) if light else cost(flops, moved),
    )(*args)


def swap_halves(values, lanes):
    half = HEAD_DIM // 2
    ahead = pltpu.roll(values, values.shape[1] - half, 1)
    behind = pltpu.roll(values, half, 1)
    return jnp.where(lanes % HEAD_DIM < half, ahead, behind)


def widen(table, width):
    return jnp.concatenate([table] * (width // table.shape[1]), axis=1)


def span(i):
    return pl.ds(pl.multiple_of(i * BLOCK, BLOCK), BLOCK)


def own_lanes(parts, lanes):
    picked = parts[0]
    for h in range(1, len(parts)):
        picked = jnp.where(lanes // HEAD_DIM == h, parts[h], picked)
    return picked


def by_count(count, most, run):
    for each in range(1, most + 1):
        pl.when(count == each)(functools.partial(run, each))


def attend_forward_kernel(
    range_ref, q_ref, k_ref, v_ref, cos_ref, sin_ref, segc_ref, segr_ref,
    out_ref, qrot_ref, krot_ref, lse_ref, seg_wide,
):
    length, width = q_ref.shape
    heads = width // HEAD_DIM
    blocks = length // BLOCK
    lanes = lax.broadcasted_iota(jnp.int32, (BLOCK, width), 1)

    def turn(i, carry):
        rows = span(i)
        cosine, sine = widen(cos_ref[rows, :], width), widen(sin_ref[rows, :], width)
        for source, target, factor in ((q_ref, qrot_ref, HEAD_DIM**-0.5), (k_ref, krot_ref, None)):
            values = source[rows, :].astype(f32)
            turned = (values * cosine + swap_halves(values, lanes) * sine).astype(bf16)
            if factor is not None:
                turned = turned * jnp.asarray(factor, bf16)
            target[rows, :] = turned
        seg_wide[rows, :] = jnp.broadcast_to(segc_ref[rows, :], (BLOCK, TILE))
        return carry

    lax.fori_loop(0, blocks, turn, 0)

    def one_query(i, carry):
        rows = span(i)

        def work(count):
            keys = pl.ds(pl.multiple_of(range_ref[0, i] * BLOCK, BLOCK), count * BLOCK)
            allowed = widen(seg_wide[rows, :], count * BLOCK) == segr_ref[:, keys]
            query = qrot_ref[rows, :]
            zero = jnp.zeros_like(query)
            mixed = []
            for h in range(heads):
                scores = dot_nt(jnp.where(lanes // HEAD_DIM == h, query, zero), krot_ref[keys, :])
                scores = jnp.where(allowed, scores, -1e30)
                highest = jnp.max(scores, axis=1, keepdims=True)
                powers = jnp.exp(scores - highest)
                totals = jnp.sum(powers, axis=1, keepdims=True)
                mixed.append(dot_nn(powers.astype(bf16), v_ref[keys, :]) * (1.0 / totals))
                logsum = jnp.broadcast_to(highest + jnp.log(totals), (BLOCK, TILE))
                lse_ref[0, h : h + 1, rows] = logsum.T[0:1]
            out_ref[rows, :] = own_lanes(mixed, lanes).astype(bf16)

        by_count(range_ref[1, i] - range_ref[0, i], blocks, work)
        return carry

    lax.fori_loop(0, blocks, one_query, 0)


def attend_forward(ranges, projected, cosine, sine, seg_column, seg_row):
    length, width = projected.shape
    width //= 3
    panels, heads = width // TILE, TILE // HEAD_DIM
    panel = lambda shift: pl.BlockSpec((length, TILE), lambda p, r: (0, shift * panels + p))
    whole = lambda shape: pl.BlockSpec(shape, lambda p, r: (0,) * len(shape))
    return pl.pallas_call(
        attend_forward_kernel,
        grid_spec=pltpu.PrefetchScalarGridSpec(
            num_scalar_prefetch=1,
            grid=(panels,),
            in_specs=[panel(0), panel(1), panel(2), whole(cosine.shape), whole(sine.shape),
                      whole(seg_column.shape), whole(seg_row.shape)],
            out_specs=[panel(0), panel(0), panel(0), pl.BlockSpec((1, heads, length), lambda p, r: (p, 0, 0))],
            scratch_shapes=[pltpu.VMEM((length, TILE), jnp.int32)],
        ),
        out_shape=[jax.ShapeDtypeStruct((length, width), bf16)] * 3
        + [jax.ShapeDtypeStruct((panels, heads, length), f32)],
        compiler_params=params("arbitrary"),
        cost_estimate=cost(8 * length * length * width, 14 * length * width, length * length * width // HEAD_DIM),
    )(ranges, projected, projected, projected, cosine, sine, seg_column, seg_row)


def attend_backward_kernel(
    range_ref, q_ref, k_ref, v_ref, out_ref, do_ref, lse_ref, cos_ref, sin_ref, segc_ref, segr_ref,
    grad_ref, dq, dk_low, dv_low, delta, seg_wide,
):
    length, width = q_ref.shape
    heads = width // HEAD_DIM
    blocks = length // BLOCK
    step = pl.program_id(1)

    @pl.when(step == 0)
    def _():
        lanes = lax.broadcasted_iota(jnp.int32, (BLOCK, width), 1)
        picker = (
            lax.broadcasted_iota(jnp.int32, (8, width), 0)
            == lax.broadcasted_iota(jnp.int32, (8, width), 1) // HEAD_DIM
        ).astype(f32)

        def prepare(i, carry):
            rows = span(i)
            product = do_ref[rows, :].astype(f32) * out_ref[rows, :].astype(f32)
            delta[:, rows] = lax.dot_general(
                picker, product, (((1,), (1,)), ((), ())),
                precision=lax.Precision.HIGHEST, preferred_element_type=f32,
            )
            dq[:, rows] = jnp.zeros((width, BLOCK), f32)
            seg_wide[rows, :] = jnp.broadcast_to(segc_ref[rows, :], (BLOCK, TILE))
            return carry

        lax.fori_loop(0, blocks, prepare, 0)

        def unturn(values, rows):
            return values * widen(cos_ref[rows, :], width) - swap_halves(values, lanes) * widen(sin_ref[rows, :], width)

        def one_key(j, carry):
            rows = span(j)

            def work(count):
                there = pl.ds(pl.multiple_of(range_ref[0, j] * BLOCK, BLOCK), count * BLOCK)
                allowed = widen(seg_wide[rows, :], count * BLOCK) == segr_ref[:, there]
                zero = jnp.zeros((BLOCK, width), bf16)
                key, value = (
                    jnp.concatenate([jnp.where(lanes // HEAD_DIM == h, ref[rows, :], zero) for h in range(heads)], axis=0)
                    for ref in (k_ref, v_ref)
                )
                query, grad_out = q_ref[there, :], do_ref[there, :]
                found, grad_prob = dot_nt(key, query), dot_nt(value, grad_out)
                parts, lows = [], []
                for h in range(heads):
                    half = slice(h * BLOCK, (h + 1) * BLOCK)
                    scores = found[half] - lse_ref[0, h : h + 1, there]
                    part = jnp.exp(jnp.where(allowed, scores, -1e30))
                    parts.append(part.astype(bf16))
                    lows.append((part * (grad_prob[half] - delta[h : h + 1, there])).astype(bf16))
                grad_scores = jnp.concatenate(lows, axis=0)
                grad_v = dot_nn(jnp.concatenate(parts, axis=0), grad_out)
                grad_k = dot_nn(grad_scores, query)
                grad_v, grad_k = ([v[h * BLOCK : (h + 1) * BLOCK] for h in range(heads)] for v in (grad_v, grad_k))
                dq[:, there] += dot_tn(key, grad_scores)
                dk_low[rows, :] = unturn(own_lanes(grad_k, lanes), rows).astype(bf16)
                dv_low[rows, :] = own_lanes(grad_v, lanes).astype(bf16)

            by_count(range_ref[1, j] - range_ref[0, j], blocks, work)
            return carry

        lax.fori_loop(0, blocks, one_key, 0)

        def finish(i, carry):
            rows = span(i)
            grad_ref[rows, :] = unturn(dq[:, rows].T * HEAD_DIM**-0.5, rows).astype(bf16)
            return carry

        lax.fori_loop(0, blocks, finish, 0)

    @pl.when(step == 1)
    def _():
        grad_ref[...] = dk_low[...]

    @pl.when(step == 2)
    def _():
        grad_ref[...] = dv_low[...]


def attend_backward(ranges, queries, keys, projected, mixed, grad_mixed, logsum, cosine, sine, seg_column, seg_row):
    length, width = queries.shape
    panels, heads = width // TILE, TILE // HEAD_DIM
    panel = lambda shift: pl.BlockSpec((length, TILE), lambda p, t, r: (0, shift * panels + p))
    whole = lambda shape: pl.BlockSpec(shape, lambda p, t, r: (0,) * len(shape))
    return pl.pallas_call(
        attend_backward_kernel,
        grid_spec=pltpu.PrefetchScalarGridSpec(
            num_scalar_prefetch=1,
            grid=(panels, 3),
            in_specs=[panel(0), panel(0), panel(2), panel(0), panel(0),
                      pl.BlockSpec((1, heads, length), lambda p, t, r: (p, 0, 0)),
                      whole(cosine.shape), whole(sine.shape), whole(seg_column.shape), whole(seg_row.shape)],
            out_specs=pl.BlockSpec((length, TILE), lambda p, t, r: (0, t * panels + p)),
            scratch_shapes=[
                pltpu.VMEM((TILE, length), f32),
                pltpu.VMEM((length, TILE), bf16),
                pltpu.VMEM((length, TILE), bf16),
                pltpu.VMEM((8, length), f32),
                pltpu.VMEM((length, TILE), jnp.int32),
            ],
        ),
        out_shape=jax.ShapeDtypeStruct((length, 3 * width), bf16),
        compiler_params=params("arbitrary", "arbitrary"),
        cost_estimate=cost(20 * length * length * width, 16 * length * width, length * length * width // HEAD_DIM),
    )(ranges, queries, keys, projected, mixed, grad_mixed, logsum, cosine, sine, seg_column, seg_row)


def gelu_and_slope(x):
    root = math.sqrt(2.0 / math.pi)
    square = x * x
    bend = jnp.tanh(x * (root + root * 0.044715 * square))
    half = 0.5 * x
    half_up = 0.5 + 0.5 * bend
    slope = half_up + half * (1.0 - bend * bend) * (root + 3.0 * root * 0.044715 * square)
    return half + half * bend, slope


def feed_kernel(
    n_ref, cot_ref, resid_ref, up_ref, down_ref, out_ref, back_ref, gup_ref, gdown_ref,
    total, n_turned, act_turned, pre,
):
    step, last = pl.program_id(0), pl.num_programs(0) - 1
    frames, width = n_ref.shape
    tile = min(FEED_TILE, frames)

    def rows_of(i):
        return pl.ds(pl.multiple_of(i * tile, tile), tile)

    @pl.when(step == 0)
    def _():
        def turn(i, carry):
            rows = rows_of(i)
            n_turned[:, rows] = n_ref[rows, :].T
            total[rows, :] = resid_ref[rows, :]
            back_ref[rows, :] = jnp.zeros((tile, width), f32)
            return carry

        lax.fori_loop(0, frames // tile, turn, 0)

    def chunk(i, carry):
        rows = rows_of(i)
        up, down = flat(up_ref), flat(down_ref)
        hidden = dot_nn(n_ref[rows, :], up)
        grad_act = dot_nt(cot_ref[rows, :], down)
        activated, slope = gelu_and_slope(hidden)
        activated = activated.astype(bf16)
        grad_pre = (grad_act * slope).astype(bf16)
        act_turned[:, rows] = activated.T
        pre[rows, :] = grad_pre
        total[rows, :] += dot_nn(activated, down)
        back_ref[rows, :] += dot_nt(grad_pre, up)
        return carry

    lax.fori_loop(0, frames // tile, chunk, 0)

    for begin in range(0, width, FEED_PART):
        rows = slice(begin, begin + FEED_PART)
        gup_ref[rows, :] = dot_nn(n_turned[rows, :], pre[...]).astype(bf16)
    piece = act_turned.shape[0]
    for begin in range(0, piece, FEED_PART):
        rows = slice(begin, begin + FEED_PART)
        gdown_ref[rows, :] = dot_nn(act_turned[rows, :], cot_ref[...]).astype(bf16)

    @pl.when(step == last)
    def _():
        out_ref[...] = total[...].astype(bf16)


def feed_forward_and_back(normed, cot, resid, hidden, piece, w_up, w_down):
    frames, width = normed.shape
    whole = lambda: pl.BlockSpec((frames, width), lambda j: (0, 0), pipeline_mode=pl.Buffered(1))
    return pl.pallas_call(
        feed_kernel,
        grid=(hidden // piece,),
        in_specs=[whole(), whole(), whole(), pl.BlockSpec(*w_up[1:]), pl.BlockSpec(*w_down[1:])],
        out_specs=[pl.BlockSpec((frames, width), lambda j: (0, 0))] * 2
        + [pl.BlockSpec((width, piece), lambda j: (0, j)), pl.BlockSpec((piece, width), lambda j: (j, 0))],
        out_shape=[
            jax.ShapeDtypeStruct((frames, width), bf16),
            jax.ShapeDtypeStruct((frames, width), f32),
            jax.ShapeDtypeStruct((width, hidden), bf16),
            jax.ShapeDtypeStruct((hidden, width), bf16),
        ],
        scratch_shapes=[
            pltpu.VMEM((frames, width), f32),
            pltpu.VMEM((width, frames), bf16),
            pltpu.VMEM((piece, frames), bf16),
            pltpu.VMEM((frames, piece), bf16),
        ],
        compiler_params=params("arbitrary"),
        cost_estimate=cost(12 * frames * width * hidden, 8 * width * hidden + 16 * frames * width, frames * hidden),
    )(normed, cot, resid, w_up[0], w_down[0])


def body(inputs, skips, cotangent, segment_ids, time_steps, w_skip, w_qkv, w_out, w_up, w_down, w_mod):
    micro, _, piece, width = inputs.shape
    length = segment_ids.shape[-1]
    labels = time_steps.shape[-1]
    planes, lows, highs = lax.axis_size("plane"), lax.axis_size("lo"), lax.axis_size("hi")
    line = highs * lows
    group = 2 * lows
    devices = planes * 2 * line
    core, high, low = lax.axis_index("core"), lax.axis_index("hi"), lax.axis_index("lo")
    place = high * lows + low
    member = core * lows + low
    frames = 2 * piece
    heads_wide = width // group
    first_core = core == 0
    swap = [(0, 1), (1, 0)]

    def route(parity):
        pairs = []
        for c in range(2):
            for z in range(line):
                row = c * micro + ((z % 2) ^ parity)
                to_core, to_low = divmod(z // 2, lows)
                pairs.append((c * line + z, (to_core * highs + row) * lows + to_low))
        return pairs

    there = (route(0), route(1))
    back = tuple([(b, a) for a, b in pairs] for pairs in there)
    odd_place = place % 2
    even_row = high % 2 == 0

    def to_rows(value):
        value = value[:, 0]
        near = lax.ppermute(lax.dynamic_index_in_dim(value, odd_place, 0, False), LINE_AXES, there[0])
        far = lax.ppermute(lax.dynamic_index_in_dim(value, 1 - odd_place, 0, False), LINE_AXES, there[1])
        return jnp.concatenate([jnp.where(even_row, near, far), jnp.where(even_row, far, near)], axis=0)

    def from_rows(value):
        value = value.reshape(2, piece, width)
        near = lax.ppermute(lax.dynamic_index_in_dim(value, high % 2, 0, False), LINE_AXES, back[0])
        far = lax.ppermute(lax.dynamic_index_in_dim(value, 1 - high % 2, 0, False), LINE_AXES, back[1])
        even = odd_place == 0
        return jnp.stack([jnp.where(even, near, far), jnp.where(even, far, near)])[:, None]

    def frames_to_row(value):
        if group > 2:
            return lax.all_gather(value, ROW_AXES, axis=0, tiled=True)
        other = lax.ppermute(value, "core", swap)
        return jnp.concatenate([jnp.where(first_core, value, other), jnp.where(first_core, other, value)], axis=0)

    def heads_to_frames(value):
        if group > 2:
            return lax.all_to_all(value, ROW_AXES, split_axis=0, concat_axis=1, tiled=True)
        other = lax.ppermute(lax.dynamic_slice_in_dim(value, (1 - core) * frames, frames, 0), "core", swap)
        own = lax.dynamic_slice_in_dim(value, core * frames, frames, 0)
        return jnp.concatenate([jnp.where(first_core, own, other), jnp.where(first_core, other, own)], axis=1)

    def frames_to_heads(value):
        if group > 2:
            return lax.all_to_all(value, ROW_AXES, split_axis=1, concat_axis=0, tiled=True)
        other = lax.ppermute(lax.dynamic_slice_in_dim(value, (1 - core) * heads_wide, heads_wide, 1), "core", swap)
        own = lax.dynamic_slice_in_dim(value, core * heads_wide, heads_wide, 1)
        return jnp.concatenate([jnp.where(first_core, own, other), jnp.where(first_core, other, own)], axis=0)

    def share_on_line(value):
        pieces = [value]
        for flip in range(1, line):
            pieces.append(lax.ppermute(value, ("hi", "lo"), [(i, i ^ flip) for i in range(line)]))
        pieces = jnp.stack(pieces)
        return jnp.stack([lax.dynamic_index_in_dim(pieces, place ^ i, 0, False) for i in range(line)])

    def gather_planes(value):
        return lax.all_gather(value, ("plane", "core"), axis=0, tiled=True).reshape(devices, -1, width)

    up_rows, down_rows, out_rows = w_up.shape[0], w_down.shape[0], w_out.shape[0]
    skip_rows = w_skip.shape[0]
    columns = w_up.shape[1] // width
    middle = jnp.concatenate([w_qkv[:, i * width : (i + 1) * width] for i in range(3)] + [w_out], axis=0)
    late = jnp.concatenate([w_down] + [w_up[:, i * width : (i + 1) * width] for i in range(columns)], axis=0)
    early = share_on_line(w_skip)
    early, middle, late = lax.optimization_barrier((early, middle, late))
    early = gather_planes(early)
    middle, late = share_on_line(middle), share_on_line(late)
    middle = gather_planes(middle)

    in_place = out_rows % 16 == 0
    hidden = w_up.shape[1]
    chunk = hidden // (2 * planes)

    def weight(gathered, begin, rows, first, count):
        block = (count // rows, rows, width)
        if in_place:
            return gathered, block, (first // count, begin // rows, 0)
        taken = gathered[first // rows : (first + count) // rows, begin : begin + rows]
        return taken.reshape(1, count, width), (1, count, width), (0, 0, 0)

    skip_top, skip_bottom = (weight(early, 0, skip_rows, i * width, width) for i in range(2))
    out_weight = weight(middle, 3 * out_rows, out_rows, 0, width)
    x, s = (v.reshape(frames, width) for v in (inputs, skips))
    (resid_in,) = rowwise(
        merge_kernel, frames, [("", x), ("", s), ("weight", skip_top), ("weight", skip_bottom)], [(width, bf16)], light=True
    )
    stacked = jnp.concatenate([x, s], axis=1)

    labels_own = segment_ids[:, 0]
    labels_other = lax.ppermute(labels_own, "core", swap)
    labels_pick = jnp.where(core == high // micro, labels_own, labels_other)
    seg = lax.dynamic_index_in_dim(labels_pick, high % micro, 0, False)
    names = jnp.arange(labels, dtype=jnp.int32)
    starts = jnp.sum((seg[:, None] < names[None, :]).astype(jnp.int32), axis=0)
    ends = jnp.sum((seg[:, None] <= names[None, :]).astype(jnp.int32), axis=0)
    offset = jnp.sum(jnp.where(seg[:, None] == names[None, :], starts[None, :], 0), axis=1)
    where_at = jnp.arange(length, dtype=jnp.int32) - offset
    by_block = seg.reshape(-1, BLOCK)
    begin = jnp.sum(jnp.where(by_block[:, :1] == names[None, :], starts[None, :], 0), axis=1)
    finish = jnp.sum(jnp.where(by_block[:, -1:] == names[None, :], ends[None, :], 0), axis=1)
    ranges = jnp.stack([begin // BLOCK, (finish + BLOCK - 1) // BLOCK]).astype(jnp.int32)
    half = HEAD_DIM // 2
    rates = jnp.exp(-math.log(10000.0) * jnp.arange(half, dtype=f32) / half)
    angles = where_at.astype(f32)[:, None] * rates
    cosine = jnp.tile(jnp.cos(angles), (1, 4))
    sine = jnp.sin(angles)
    sine = jnp.concatenate([-sine, sine, -sine, sine], axis=1)
    seg_column, seg_row = seg[:, None], seg[None, :]
    mine = lax.dynamic_slice_in_dim(seg, member * frames, frames, 0)

    steps = lax.all_gather(time_steps[:, 0], ("plane", "core"), axis=0, tiled=True).reshape(-1)
    quarter = w_mod.shape[0] // 2
    pace = jnp.exp(-math.log(10000.0) * jnp.arange(quarter, dtype=f32) / quarter)
    turns = steps.astype(f32)[:, None] * pace
    embedded = jnp.concatenate([jnp.sin(turns), jnp.cos(turns)], axis=1).astype(bf16)
    block_mod = jnp.dot(embedded, w_mod, preferred_element_type=f32)
    own_columns = block_mod.shape[1]
    block_mod = block_mod.reshape(planes, 1, highs, 1, labels, own_columns)
    block_mod = jnp.broadcast_to(block_mod, (planes, 2, highs, lows, labels, own_columns))
    block_mod = lax.all_to_all(
        block_mod.reshape(devices, labels, own_columns), ALL_AXES, split_axis=0, concat_axis=0, tiled=True
    )
    modulation = jnp.moveaxis(block_mod, 0, 1).reshape(labels, 4, width)

    def own_qkv(gathered):
        parts = []
        for i in range(3):
            whole = gathered[:, i * out_rows : (i + 1) * out_rows].reshape(width, width)
            parts.append(lax.dynamic_slice_in_dim(whole, member * heads_wide, heads_wide, 1))
        return jnp.concatenate(parts, axis=1)

    mine_column, mine_row = mine[:, None], mine[None, :]
    shift_one, scale_one, shift_two, scale_two = (modulation[:, i] for i in range(4))

    resid_in = to_rows(resid_in.reshape(inputs.shape))
    resid_in, late, cotangent, stacked, modulation, cosine, sine, ranges = lax.optimization_barrier(
        (resid_in, late, cotangent, stacked, modulation, cosine, sine, ranges)
    )
    (normed_one,) = rowwise(
        norm_kernel,
        frames,
        [("", resid_in), ("", mine_column), ("whole", shift_one), ("whole", scale_one)],
        [(width, bf16)],
        light=True,
    )
    normed_row = frames_to_row(normed_one)
    if in_place:
        projected = project(normed_row, middle, 0, out_rows, heads_wide, member)
    else:
        projected = jnp.dot(normed_row, own_qkv(middle), preferred_element_type=f32).astype(bf16)
    late = gather_planes(late)
    cot = to_rows(cotangent)
    if in_place:
        per = width // chunk
        up_weight = (late, (devices, up_rows, chunk), lambda j: (0, down_rows // up_rows + j // per, j % per))
        down_weight = (late, (chunk // down_rows, down_rows, width), lambda j: (j, 0, 0))
    else:
        pieces = [late[:, down_rows + i * up_rows : down_rows + (i + 1) * up_rows] for i in range(columns)]
        up_full = jnp.concatenate([v.reshape(width, width) for v in pieces], axis=1)
        up_weight = (up_full[None], (1, width, chunk), lambda j: (0, 0, j))
        down_weight = (late[:, :down_rows].reshape(1, -1, width), (1, chunk, width), lambda j: (0, j, 0))
    mixed_heads, queries, keys, logsum = attend_forward(ranges, projected, cosine, sine, seg_column, seg_row)
    mixed = heads_to_frames(mixed_heads)
    resid_mid, normed_two = rowwise(
        out_norm_kernel,
        frames,
        [("", mixed), ("weight", out_weight), ("", resid_in), ("", mine_column), ("whole", shift_two), ("whole", scale_two)],
        [(width, f32), (width, bf16)],
        flops=2 * frames * width * width,
    )
    result, grad_normed_two, grad_up, grad_down = feed_forward_and_back(
        normed_two, cot, resid_mid, hidden, chunk, up_weight, down_weight
    )

    def over_cores(kept, axis):
        other = lax.ppermute(lax.dynamic_index_in_dim(kept, 1 - core, axis, False), "core", swap)
        own = lax.dynamic_index_in_dim(kept, core, axis, False)
        return (own.astype(f32) + other.astype(f32)).astype(bf16)

    plane = lax.axis_index("plane")

    def exchange(value, axes, here, count):
        total = lax.dynamic_index_in_dim(value, here, 0, False).astype(f32)
        for flip in range(1, count):
            sent = lax.dynamic_index_in_dim(value, here ^ flip, 0, False)
            total += lax.ppermute(sent, axes, [(i, i ^ flip) for i in range(count)]).astype(f32)
        return total

    def exchange_planes(value):
        return exchange(value, "plane", plane, planes).astype(bf16)

    def exchange_line(value):
        return exchange(value.reshape(line, -1, value.shape[-1]), ("hi", "lo"), place, line)

    grad_up, grad_down = (
        lax.psum_scatter(v, ("plane", "core"), scatter_dimension=0, tiled=True) for v in (grad_up, grad_down)
    )

    grad_mid, grad_mid_low, grad_frames, grad_shift_two, grad_scale_two = rowwise(
        norm_two_back_kernel,
        frames,
        [("", grad_normed_two), ("", resid_mid), ("", cot), ("", mine_column), ("row", mine_row),
         ("whole", scale_two), ("weight", out_weight)],
        [(width, f32), (width, bf16), (width, bf16)],
        sums=2,
        light=True,
    )
    grad_heads = frames_to_heads(grad_frames)
    grad_out = lax.dot_general(mixed, grad_mid_low, (((0,), (0,)), ((), ())), preferred_element_type=f32)
    grad_out = over_cores(grad_out.astype(bf16).reshape(planes, 2, -1, width), 1)
    grad_heads, grad_out, result = lax.optimization_barrier((grad_heads, grad_out, result))
    block_out = from_rows(result)
    grad_proj = attend_backward(
        ranges, queries, keys, projected, mixed_heads, grad_heads, logsum, cosine, sine, seg_column, seg_row
    )
    grad_proj, block_out, grad_up = lax.optimization_barrier((grad_proj, block_out, grad_up))
    grad_up = lax.psum_scatter(grad_up, ("hi", "lo"), scatter_dimension=0, tiled=True)
    if group > 2:
        partial = dot_nt(grad_proj, own_qkv(middle)).astype(bf16)
        grad_one = lax.psum_scatter(partial, ROW_AXES, scatter_dimension=0, tiled=True).astype(f32)
        grad_one_other = jnp.zeros((frames, width), bf16)
    else:
        if in_place:
            pull = functools.partial(pull_project, grad_proj, middle, out_rows, heads_wide, member, frames)
            away, home = pull(1 - core, bf16), pull(core, f32)
        else:
            qkv_own = own_qkv(middle)
            away = lax.dynamic_slice_in_dim(grad_proj, (1 - core) * frames, frames, 0)
            home = lax.dynamic_slice_in_dim(grad_proj, core * frames, frames, 0)
            away, home = dot_nt(away, qkv_own).astype(bf16), dot_nt(home, qkv_own)
        grad_one_other = lax.ppermute(away, "core", swap)
        grad_one = home
    grad_in, grad_shift_one, grad_scale_one = rowwise(
        norm_one_back_kernel,
        frames,
        [("", grad_one), ("", grad_one_other), ("", resid_in), ("", grad_mid), ("", mine_column), ("row", mine_row),
         ("whole", scale_one)],
        [(width, bf16)],
        sums=2,
    )
    grad_in_home = from_rows(grad_in)
    grad_proj, grad_in = lax.optimization_barrier((grad_proj, grad_in))
    grad_qkv = lax.dot_general(normed_row, grad_proj, (((0,), (0,)), ((), ())), preferred_element_type=f32)
    grad_qkv = grad_qkv.astype(bf16)
    if group > 2:
        grad_qkv = grad_qkv.reshape(planes, 2, highs, lows, -1, 3, 1, heads_wide)
        grad_qkv = jnp.moveaxis(grad_qkv, (1, 3), (0, 1)).reshape(group, -1, 3, 1, heads_wide)
        grad_qkv = lax.all_to_all(grad_qkv, ROW_AXES, split_axis=0, concat_axis=3, tiled=True)
        grad_qkv = grad_qkv.reshape(-1, 3 * width)
        grad_qkv = lax.psum_scatter(grad_qkv, ("plane", "hi"), scatter_dimension=0, tiled=True).astype(f32)
    else:
        split = grad_qkv.reshape(planes, 2, -1, 3 * heads_wide)
        other = lax.ppermute(lax.dynamic_index_in_dim(split, 1 - core, 1, False), "core", swap)
        own = lax.dynamic_index_in_dim(split, core, 1, False)
        own, other = (v.reshape(-1, 3 * heads_wide) for v in (own, other))
        left, right = jnp.where(first_core, own, other), jnp.where(first_core, other, own)
        grad_qkv = jnp.concatenate(
            [v[:, i * heads_wide : (i + 1) * heads_wide] for i in range(3) for v in (left, right)], axis=1
        )
        grad_qkv = jnp.concatenate([grad_qkv.reshape(planes, -1, 3 * width), grad_out], axis=2)
        grad_qkv = exchange_planes(grad_qkv)
    grad_mod = jnp.stack([v[:labels] for v in (grad_shift_one, grad_scale_one, grad_shift_two, grad_scale_two)], axis=1)
    grad_mod = jnp.moveaxis(grad_mod.reshape(labels, devices, own_columns), 1, 0)
    grad_mod = lax.all_to_all(grad_mod, ALL_AXES, split_axis=0, concat_axis=0, tiled=True)
    grad_in_home, grad_qkv, grad_down, grad_mod = lax.optimization_barrier((grad_in_home, grad_qkv, grad_down, grad_mod))
    grad_down = lax.psum_scatter(grad_down, ("hi", "lo"), scatter_dimension=0, tiled=True)
    grad_up, grad_down = grad_up.astype(f32), grad_down.astype(f32)
    if group == 2:
        grad_qkv = grad_qkv.reshape(line, -1, 4 * width)
        grad_qkv = lax.all_to_all(grad_qkv, ("hi", "lo"), split_axis=0, concat_axis=0, tiled=True)
        grad_qkv = jnp.sum(grad_qkv.astype(f32), axis=0)
        grad_qkv, grad_out = grad_qkv[:, : 3 * width], grad_qkv[:, 3 * width :]
    else:
        grad_out = exchange_line(exchange_planes(grad_out))
    home = grad_in_home.reshape(frames, width)
    grad_skip_w = lax.dot_general(stacked, home, (((0,), (0,)), ((), ())), preferred_element_type=f32).astype(bf16)
    grad_skip_w = exchange_planes(over_cores(grad_skip_w.reshape(planes, 2, -1, width), 1))
    grad_inputs, grad_skips = rowwise(
        unmerge_kernel,
        frames,
        [("", home), ("weight", skip_top), ("weight", skip_bottom)],
        [(width, bf16), (width, bf16)],
        flops=4 * frames * width * width,
    )
    grad_inputs, grad_skips = (v.reshape(grad_in_home.shape) for v in (grad_inputs, grad_skips))

    grad_skip_w = exchange_line(grad_skip_w)
    grad_mod = jnp.sum(grad_mod.reshape(planes, 2, highs, lows, labels, own_columns), axis=(1, 3))
    grad_mod = lax.dot_general(
        embedded.astype(f32),
        grad_mod.reshape(-1, own_columns),
        (((0,), (0,)), ((), ())),
        precision=lax.Precision.HIGHEST,
        preferred_element_type=f32,
    )
    return (
        block_out,
        grad_inputs,
        grad_skips,
        grad_skip_w,
        grad_qkv,
        grad_out,
        grad_up,
        grad_down,
        grad_mod,
    )


def solution(mesh):
    batch, wide = mesh.devices.shape

    def run(inputs, *rest):
        rows = 2 * inputs.shape[0]
        assert inputs.shape[0] == 2 and inputs.shape[1] == batch and wide % rows == 0
        fine = Mesh(mesh.devices.reshape(batch // 2, 2, rows, wide // rows), ALL_AXES)
        by_batch, by_wide = ("plane", "core"), ("hi", "lo")
        frames = P(None, by_batch, by_wide, None)
        rowed = P(None, by_batch, None)
        weight, columns = P(ALL_AXES, None), P(None, ALL_AXES)
        mapped = jax.shard_map(
            body,
            mesh=fine,
            in_specs=(frames, frames, frames, rowed, rowed) + (weight,) * 5 + (columns,),
            out_specs=(frames, frames, frames) + (weight,) * 5 + (columns,),
            check_vma=False,
        )
        return mapped(inputs, *rest)

    return run
```

```python
import functools
import math

import jax
import jax.numpy as jnp
from jax import lax
from jax.experimental import pallas as pl
from jax.experimental.pallas import tpu as pltpu
from jax.sharding import Mesh
from jax.sharding import PartitionSpec as P

HEAD_DIM = 64
TILE = 128
BLOCK = 256
ROW_TILE = 256
FEED_TILE = 1024
FEED_PART = 512
VMEM_BYTES = 60 * 1024 * 1024
ROW_AXES = ("core", "lo")
LINE_AXES = ("core", "hi", "lo")
ALL_AXES = ("plane", "core", "hi", "lo")
f32 = jnp.float32
bf16 = jnp.bfloat16


def dot_nn(left, right):
    return lax.dot_general(left, right, (((1,), (0,)), ((), ())), preferred_element_type=f32)


def dot_nt(left, right):
    return lax.dot_general(left, right, (((1,), (1,)), ((), ())), preferred_element_type=f32)


def dot_tn(left, right):
    return lax.dot_general(left, right, (((0,), (0,)), ((), ())), preferred_element_type=f32)


def params(*semantics):
    return pltpu.CompilerParams(dimension_semantics=semantics, vmem_limit_bytes=VMEM_BYTES)


def cost(flops, moved, special=0):
    return pl.CostEstimate(flops=int(flops), bytes_accessed=int(moved), transcendentals=int(special))


def flat(ref):
    return ref[...].reshape(-1, ref.shape[-1])


def choose(segment_column, table_ref):
    count = table_ref.shape[0]
    picked = table_ref[count - 1 : count, :]
    for label in range(count - 2, -1, -1):
        picked = jnp.where(segment_column == label, table_ref[label : label + 1, :], picked)
    return picked


def normalise(values):
    centred = values - jnp.mean(values, axis=-1, keepdims=True)
    variance = jnp.mean(centred * centred, axis=-1, keepdims=True)
    inverse = lax.rsqrt(variance + 1e-06)
    return centred * inverse, inverse


def merge_kernel(x_ref, s_ref, top_ref, bottom_ref, resid_ref):
    resid = dot_nn(x_ref[...], flat(top_ref)) + dot_nn(s_ref[...], flat(bottom_ref))
    resid_ref[...] = resid.astype(bf16)


def norm_kernel(resid_ref, seg_ref, shift_ref, scale_ref, normed_ref):
    unit, _ = normalise(resid_ref[...].astype(f32))
    label = seg_ref[...]
    normed = unit * (1.0 + choose(label, scale_ref)) + choose(label, shift_ref)
    normed_ref[...] = normed.astype(bf16)


def out_norm_kernel(mixed_ref, w_ref, resid_in_ref, seg_ref, shift_ref, scale_ref, resid_ref, normed_ref):
    resid = resid_in_ref[...].astype(f32) + dot_nn(mixed_ref[...], flat(w_ref))
    resid_ref[...] = resid
    unit, _ = normalise(resid)
    label = seg_ref[...]
    normed = unit * (1.0 + choose(label, scale_ref)) + choose(label, shift_ref)
    normed_ref[...] = normed.astype(bf16)


def segment_sums(row_labels, values, total_ref):
    members = lax.broadcasted_iota(jnp.int32, (total_ref.shape[0], row_labels.shape[1]), 0) == row_labels
    members = members.astype(f32).astype(bf16)
    high = values.astype(bf16)
    low = (values - high.astype(f32)).astype(bf16)
    total_ref[...] += dot_nn(members, high) + dot_nn(members, low)


def norm_pull(grad, resid, scale):
    unit, inverse = normalise(resid)
    inner = grad * (1.0 + scale)
    pulled = inverse * (
        inner
        - jnp.mean(inner, axis=-1, keepdims=True)
        - unit * jnp.mean(inner * unit, axis=-1, keepdims=True)
    )
    return pulled, grad * unit


def norm_two_back_kernel(
    g_ref, resid_ref, cot_ref, seg_ref, segr_ref, scale_ref, w_ref, mid_ref, low_ref, mix_ref, dshift_ref, dscale_ref
):
    @pl.when(pl.program_id(0) == 0)
    def _():
        dshift_ref[...] = jnp.zeros_like(dshift_ref)
        dscale_ref[...] = jnp.zeros_like(dscale_ref)

    grad = g_ref[...]
    pulled, by_scale = norm_pull(grad, resid_ref[...], choose(seg_ref[...], scale_ref))
    grad_mid = cot_ref[...].astype(f32) + pulled
    low = grad_mid.astype(bf16)
    mid_ref[...] = grad_mid
    low_ref[...] = low
    mix_ref[...] = dot_nt(low, flat(w_ref)).astype(bf16)
    segment_sums(segr_ref[...], grad, dshift_ref)
    segment_sums(segr_ref[...], by_scale, dscale_ref)


def norm_one_back_kernel(
    own_ref, other_ref, resid_ref, mid_ref, seg_ref, segr_ref, scale_ref, grad_ref, dshift_ref, dscale_ref
):
    @pl.when(pl.program_id(0) == 0)
    def _():
        dshift_ref[...] = jnp.zeros_like(dshift_ref)
        dscale_ref[...] = jnp.zeros_like(dscale_ref)

    grad = own_ref[...] + other_ref[...].astype(f32)
    pulled, by_scale = norm_pull(grad, resid_ref[...].astype(f32), choose(seg_ref[...], scale_ref))
    grad_ref[...] = (mid_ref[...] + pulled).astype(bf16)
    segment_sums(segr_ref[...], grad, dshift_ref)
    segment_sums(segr_ref[...], by_scale, dscale_ref)


def unmerge_kernel(g_ref, top_ref, bottom_ref, inputs_ref, skips_ref):
    inputs_ref[...] = dot_nt(g_ref[...], flat(top_ref)).astype(bf16)
    skips_ref[...] = dot_nt(g_ref[...], flat(bottom_ref)).astype(bf16)


def project_kernel(place_ref, x_ref, w_ref, out_ref):
    out_ref[...] = dot_nn(x_ref[...], flat(w_ref)).astype(bf16)


def project(value, gathered, begin, rows, heads_wide, member):
    length, width = value.shape
    tile = min(8 * ROW_TILE, length)
    return pl.pallas_call(
        project_kernel,
        grid_spec=pltpu.PrefetchScalarGridSpec(
            num_scalar_prefetch=1,
            grid=(3, length // tile),
            in_specs=[
                pl.BlockSpec((tile, width), lambda t, i, r: (i, 0)),
                pl.BlockSpec((width // rows, rows, heads_wide), lambda t, i, r: (0, begin // rows + t, r[0])),
            ],
            out_specs=pl.BlockSpec((tile, heads_wide), lambda t, i, r: (i, t)),
        ),
        out_shape=jax.ShapeDtypeStruct((length, 3 * heads_wide), bf16),
        compiler_params=params("arbitrary", "arbitrary"),
        cost_estimate=cost(1, 1),
    )(member.reshape(1), value, gathered)


def pull_project_kernel(place_ref, dq_ref, dk_ref, dv_ref, q_ref, k_ref, v_ref, out_ref):
    total = dot_nt(dq_ref[...], flat(q_ref))
    total += dot_nt(dk_ref[...], flat(k_ref))
    total += dot_nt(dv_ref[...], flat(v_ref))
    out_ref[...] = total.astype(out_ref.dtype)


def pull_project(grad_proj, gathered, rows, heads_wide, member, frames, half, kind):
    width = gathered.shape[2]
    tile = min(2 * ROW_TILE, frames)
    steps = frames // tile
    grads = [
        pl.BlockSpec((tile, heads_wide), functools.partial(lambda t, i, r: (r[1] * steps + i, t), t)) for t in range(3)
    ]
    weights = [
        pl.BlockSpec((width // rows, rows, heads_wide), functools.partial(lambda t, i, r: (0, t, r[0]), t))
        for t in range(3)
    ]
    return pl.pallas_call(
        pull_project_kernel,
        grid_spec=pltpu.PrefetchScalarGridSpec(
            num_scalar_prefetch=1,
            grid=(steps,),
            in_specs=grads + weights,
            out_specs=pl.BlockSpec((tile, width), lambda i, r: (i, 0)),
        ),
        out_shape=jax.ShapeDtypeStruct((frames, width), kind),
        compiler_params=params("arbitrary"),
        cost_estimate=cost(6 * frames * width * heads_wide, 8 * frames * width),
    )(jnp.stack([member, half]).astype(jnp.int32), *[grad_proj] * 3, *[gathered] * 3)


def rowwise(kernel, frames, blocked, outs, sums=0, flops=0, light=False):
    tile = min(ROW_TILE, frames)
    in_specs, args, moved = [], [], 0
    for kind, value in blocked:
        if kind == "row":
            in_specs.append(pl.BlockSpec((1, tile), lambda i: (0, i)))
        elif kind == "weight":
            value, block, index = value
            in_specs.append(pl.BlockSpec(block, functools.partial(lambda index, i: index, index)))
        elif kind == "whole":
            in_specs.append(pl.BlockSpec(value.shape, lambda i: (0, 0)))
        else:
            in_specs.append(pl.BlockSpec((tile, value.shape[1]), lambda i: (i, 0)))
        args.append(value)
        moved += value.size * value.dtype.itemsize
    out_specs, shapes = [], []
    for width, kind in outs:
        out_specs.append(pl.BlockSpec((tile, width), lambda i: (i, 0)))
        shapes.append(jax.ShapeDtypeStruct((frames, width), kind))
        moved += frames * width * jnp.dtype(kind).itemsize
    for _ in range(sums):
        out_specs.append(pl.BlockSpec((8, outs[0][0]), lambda i: (0, 0)))
        shapes.append(jax.ShapeDtypeStruct((8, outs[0][0]), f32))
    return pl.pallas_call(
        kernel,
        grid=(frames // tile,),
        in_specs=in_specs,
        out_specs=out_specs,
        out_shape=shapes,
        compiler_params=params("arbitrary"),
        cost_estimate=cost(1, 1) if light else cost(flops, moved),
    )(*args)


def swap_halves(values, lanes):
    half = HEAD_DIM // 2
    ahead = pltpu.roll(values, values.shape[1] - half, 1)
    behind = pltpu.roll(values, half, 1)
    return jnp.where(lanes % HEAD_DIM < half, ahead, behind)


def widen(table, width):
    return jnp.concatenate([table] * (width // table.shape[1]), axis=1)


def span(i):
    return pl.ds(pl.multiple_of(i * BLOCK, BLOCK), BLOCK)


def own_lanes(parts, lanes):
    picked = parts[0]
    for h in range(1, len(parts)):
        picked = jnp.where(lanes // HEAD_DIM == h, parts[h], picked)
    return picked


def by_count(count, most, run):
    for each in range(1, most + 1):
        pl.when(count == each)(functools.partial(run, each))


def attend_forward_kernel(
    range_ref, q_ref, k_ref, v_ref, cos_ref, sin_ref, segc_ref, segr_ref,
    out_ref, qrot_ref, krot_ref, lse_ref, seg_wide,
):
    length, width = q_ref.shape
    heads = width // HEAD_DIM
    blocks = length // BLOCK
    lanes = lax.broadcasted_iota(jnp.int32, (BLOCK, width), 1)

    def turn(i, carry):
        rows = span(i)
        cosine, sine = widen(cos_ref[rows, :], width), widen(sin_ref[rows, :], width)
        for source, target, factor in ((q_ref, qrot_ref, HEAD_DIM**-0.5), (k_ref, krot_ref, None)):
            values = source[rows, :].astype(f32)
            turned = (values * cosine + swap_halves(values, lanes) * sine).astype(bf16)
            if factor is not None:
                turned = turned * jnp.asarray(factor, bf16)
            target[rows, :] = turned
        seg_wide[rows, :] = jnp.broadcast_to(segc_ref[rows, :], (BLOCK, TILE))
        return carry

    lax.fori_loop(0, blocks, turn, 0)

    def one_query(i, carry):
        rows = span(i)

        def work(count):
            keys = pl.ds(pl.multiple_of(range_ref[0, i] * BLOCK, BLOCK), count * BLOCK)
            allowed = widen(seg_wide[rows, :], count * BLOCK) == segr_ref[:, keys]
            query = qrot_ref[rows, :]
            zero = jnp.zeros_like(query)
            mixed = []
            for h in range(heads):
                scores = dot_nt(jnp.where(lanes // HEAD_DIM == h, query, zero), krot_ref[keys, :])
                scores = jnp.where(allowed, scores, -1e30)
                highest = jnp.max(scores, axis=1, keepdims=True)
                powers = jnp.exp(scores - highest)
                totals = jnp.sum(powers, axis=1, keepdims=True)
                mixed.append(dot_nn(powers.astype(bf16), v_ref[keys, :]) * (1.0 / totals))
                logsum = jnp.broadcast_to(highest + jnp.log(totals), (BLOCK, TILE))
                lse_ref[0, h : h + 1, rows] = logsum.T[0:1]
            out_ref[rows, :] = own_lanes(mixed, lanes).astype(bf16)

        by_count(range_ref[1, i] - range_ref[0, i], blocks, work)
        return carry

    lax.fori_loop(0, blocks, one_query, 0)


def attend_forward(ranges, projected, cosine, sine, seg_column, seg_row):
    length, width = projected.shape
    width //= 3
    panels, heads = width // TILE, TILE // HEAD_DIM
    panel = lambda shift: pl.BlockSpec((length, TILE), lambda p, r: (0, shift * panels + p))
    whole = lambda shape: pl.BlockSpec(shape, lambda p, r: (0,) * len(shape))
    return pl.pallas_call(
        attend_forward_kernel,
        grid_spec=pltpu.PrefetchScalarGridSpec(
            num_scalar_prefetch=1,
            grid=(panels,),
            in_specs=[panel(0), panel(1), panel(2), whole(cosine.shape), whole(sine.shape),
                      whole(seg_column.shape), whole(seg_row.shape)],
            out_specs=[panel(0), panel(0), panel(0), pl.BlockSpec((1, heads, length), lambda p, r: (p, 0, 0))],
            scratch_shapes=[pltpu.VMEM((length, TILE), jnp.int32)],
        ),
        out_shape=[jax.ShapeDtypeStruct((length, width), bf16)] * 3
        + [jax.ShapeDtypeStruct((panels, heads, length), f32)],
        compiler_params=params("arbitrary"),
        cost_estimate=cost(8 * length * length * width, 14 * length * width, length * length * width // HEAD_DIM),
    )(ranges, projected, projected, projected, cosine, sine, seg_column, seg_row)


def attend_backward_kernel(
    range_ref, q_ref, k_ref, v_ref, out_ref, do_ref, lse_ref, cos_ref, sin_ref, segc_ref, segr_ref,
    grad_ref, dq, dk_low, dv_low, delta, seg_wide,
):
    length, width = q_ref.shape
    heads = width // HEAD_DIM
    blocks = length // BLOCK
    step = pl.program_id(1)

    @pl.when(step == 0)
    def _():
        lanes = lax.broadcasted_iota(jnp.int32, (BLOCK, width), 1)
        picker = (
            lax.broadcasted_iota(jnp.int32, (8, width), 0)
            == lax.broadcasted_iota(jnp.int32, (8, width), 1) // HEAD_DIM
        ).astype(f32)

        def prepare(i, carry):
            rows = span(i)
            product = do_ref[rows, :].astype(f32) * out_ref[rows, :].astype(f32)
            delta[:, rows] = lax.dot_general(
                picker, product, (((1,), (1,)), ((), ())),
                precision=lax.Precision.HIGHEST, preferred_element_type=f32,
            )
            dq[:, rows] = jnp.zeros((width, BLOCK), f32)
            seg_wide[rows, :] = jnp.broadcast_to(segc_ref[rows, :], (BLOCK, TILE))
            return carry

        lax.fori_loop(0, blocks, prepare, 0)

        def unturn(values, rows):
            return values * widen(cos_ref[rows, :], width) - swap_halves(values, lanes) * widen(sin_ref[rows, :], width)

        def one_key(j, carry):
            rows = span(j)

            def work(count):
                there = pl.ds(pl.multiple_of(range_ref[0, j] * BLOCK, BLOCK), count * BLOCK)
                allowed = widen(seg_wide[rows, :], count * BLOCK) == segr_ref[:, there]
                zero = jnp.zeros((BLOCK, width), bf16)
                key, value = (
                    jnp.concatenate([jnp.where(lanes // HEAD_DIM == h, ref[rows, :], zero) for h in range(heads)], axis=0)
                    for ref in (k_ref, v_ref)
                )
                query, grad_out = q_ref[there, :], do_ref[there, :]
                found, grad_prob = dot_nt(key, query), dot_nt(value, grad_out)
                parts, lows = [], []
                for h in range(heads):
                    half = slice(h * BLOCK, (h + 1) * BLOCK)
                    scores = found[half] - lse_ref[0, h : h + 1, there]
                    part = jnp.exp(jnp.where(allowed, scores, -1e30))
                    parts.append(part.astype(bf16))
                    lows.append((part * (grad_prob[half] - delta[h : h + 1, there])).astype(bf16))
                grad_scores = jnp.concatenate(lows, axis=0)
                grad_v = dot_nn(jnp.concatenate(parts, axis=0), grad_out)
                grad_k = dot_nn(grad_scores, query)
                grad_v, grad_k = ([v[h * BLOCK : (h + 1) * BLOCK] for h in range(heads)] for v in (grad_v, grad_k))
                dq[:, there] += dot_tn(key, grad_scores)
                dk_low[rows, :] = unturn(own_lanes(grad_k, lanes), rows).astype(bf16)
                dv_low[rows, :] = own_lanes(grad_v, lanes).astype(bf16)

            by_count(range_ref[1, j] - range_ref[0, j], blocks, work)
            return carry

        lax.fori_loop(0, blocks, one_key, 0)

        def finish(i, carry):
            rows = span(i)
            grad_ref[rows, :] = unturn(dq[:, rows].T * HEAD_DIM**-0.5, rows).astype(bf16)
            return carry

        lax.fori_loop(0, blocks, finish, 0)

    @pl.when(step == 1)
    def _():
        grad_ref[...] = dk_low[...]

    @pl.when(step == 2)
    def _():
        grad_ref[...] = dv_low[...]


def attend_backward(ranges, queries, keys, projected, mixed, grad_mixed, logsum, cosine, sine, seg_column, seg_row):
    length, width = queries.shape
    panels, heads = width // TILE, TILE // HEAD_DIM
    panel = lambda shift: pl.BlockSpec((length, TILE), lambda p, t, r: (0, shift * panels + p))
    whole = lambda shape: pl.BlockSpec(shape, lambda p, t, r: (0,) * len(shape))
    return pl.pallas_call(
        attend_backward_kernel,
        grid_spec=pltpu.PrefetchScalarGridSpec(
            num_scalar_prefetch=1,
            grid=(panels, 3),
            in_specs=[panel(0), panel(0), panel(2), panel(0), panel(0),
                      pl.BlockSpec((1, heads, length), lambda p, t, r: (p, 0, 0)),
                      whole(cosine.shape), whole(sine.shape), whole(seg_column.shape), whole(seg_row.shape)],
            out_specs=pl.BlockSpec((length, TILE), lambda p, t, r: (0, t * panels + p)),
            scratch_shapes=[
                pltpu.VMEM((TILE, length), f32),
                pltpu.VMEM((length, TILE), bf16),
                pltpu.VMEM((length, TILE), bf16),
                pltpu.VMEM((8, length), f32),
                pltpu.VMEM((length, TILE), jnp.int32),
            ],
        ),
        out_shape=jax.ShapeDtypeStruct((length, 3 * width), bf16),
        compiler_params=params("arbitrary", "arbitrary"),
        cost_estimate=cost(20 * length * length * width, 16 * length * width, length * length * width // HEAD_DIM),
    )(ranges, queries, keys, projected, mixed, grad_mixed, logsum, cosine, sine, seg_column, seg_row)


def gelu_and_slope(x):
    root = math.sqrt(2.0 / math.pi)
    square = x * x
    bend = jnp.tanh(x * (root + root * 0.044715 * square))
    half = 0.5 * x
    half_up = 0.5 + 0.5 * bend
    slope = half_up + half * (1.0 - bend * bend) * (root + 3.0 * root * 0.044715 * square)
    return half + half * bend, slope


def feed_kernel(
    n_ref, cot_ref, resid_ref, up_ref, down_ref, out_ref, back_ref, gup_ref, gdown_ref,
    total, n_turned, act_turned, pre,
):
    step, last = pl.program_id(0), pl.num_programs(0) - 1
    frames, width = n_ref.shape
    tile = min(FEED_TILE, frames)

    def rows_of(i):
        return pl.ds(pl.multiple_of(i * tile, tile), tile)

    @pl.when(step == 0)
    def _():
        def turn(i, carry):
            rows = rows_of(i)
            n_turned[:, rows] = n_ref[rows, :].T
            total[rows, :] = resid_ref[rows, :]
            back_ref[rows, :] = jnp.zeros((tile, width), f32)
            return carry

        lax.fori_loop(0, frames // tile, turn, 0)

    def chunk(i, carry):
        rows = rows_of(i)
        up, down = flat(up_ref), flat(down_ref)
        hidden = dot_nn(n_ref[rows, :], up)
        grad_act = dot_nt(cot_ref[rows, :], down)
        activated, slope = gelu_and_slope(hidden)
        activated = activated.astype(bf16)
        grad_pre = (grad_act * slope).astype(bf16)
        act_turned[:, rows] = activated.T
        pre[rows, :] = grad_pre
        total[rows, :] += dot_nn(activated, down)
        back_ref[rows, :] += dot_nt(grad_pre, up)
        return carry

    lax.fori_loop(0, frames // tile, chunk, 0)

    for begin in range(0, width, FEED_PART):
        rows = slice(begin, begin + FEED_PART)
        gup_ref[rows, :] = dot_nn(n_turned[rows, :], pre[...]).astype(bf16)
    piece = act_turned.shape[0]
    for begin in range(0, piece, FEED_PART):
        rows = slice(begin, begin + FEED_PART)
        gdown_ref[rows, :] = dot_nn(act_turned[rows, :], cot_ref[...]).astype(bf16)

    @pl.when(step == last)
    def _():
        out_ref[...] = total[...].astype(bf16)


def feed_forward_and_back(normed, cot, resid, hidden, piece, w_up, w_down):
    frames, width = normed.shape
    whole = lambda: pl.BlockSpec((frames, width), lambda j: (0, 0), pipeline_mode=pl.Buffered(1))
    return pl.pallas_call(
        feed_kernel,
        grid=(hidden // piece,),
        in_specs=[whole(), whole(), whole(), pl.BlockSpec(*w_up[1:]), pl.BlockSpec(*w_down[1:])],
        out_specs=[pl.BlockSpec((frames, width), lambda j: (0, 0))] * 2
        + [pl.BlockSpec((width, piece), lambda j: (0, j)), pl.BlockSpec((piece, width), lambda j: (j, 0))],
        out_shape=[
            jax.ShapeDtypeStruct((frames, width), bf16),
            jax.ShapeDtypeStruct((frames, width), f32),
            jax.ShapeDtypeStruct((width, hidden), bf16),
            jax.ShapeDtypeStruct((hidden, width), bf16),
        ],
        scratch_shapes=[
            pltpu.VMEM((frames, width), f32),
            pltpu.VMEM((width, frames), bf16),
            pltpu.VMEM((piece, frames), bf16),
            pltpu.VMEM((frames, piece), bf16),
        ],
        compiler_params=params("arbitrary"),
        cost_estimate=cost(12 * frames * width * hidden, 8 * width * hidden + 16 * frames * width, frames * hidden),
    )(normed, cot, resid, w_up[0], w_down[0])


def body(inputs, skips, cotangent, segment_ids, time_steps, w_skip, w_qkv, w_out, w_up, w_down, w_mod):
    micro, _, piece, width = inputs.shape
    length = segment_ids.shape[-1]
    labels = time_steps.shape[-1]
    planes, lows, highs = lax.axis_size("plane"), lax.axis_size("lo"), lax.axis_size("hi")
    line = highs * lows
    group = 2 * lows
    devices = planes * 2 * line
    core, high, low = lax.axis_index("core"), lax.axis_index("hi"), lax.axis_index("lo")
    place = high * lows + low
    member = core * lows + low
    frames = 2 * piece
    heads_wide = width // group
    first_core = core == 0
    swap = [(0, 1), (1, 0)]

    def route(parity):
        pairs = []
        for c in range(2):
            for z in range(line):
                row = c * micro + ((z % 2) ^ parity)
                to_core, to_low = divmod(z // 2, lows)
                pairs.append((c * line + z, (to_core * highs + row) * lows + to_low))
        return pairs

    there = (route(0), route(1))
    back = tuple([(b, a) for a, b in pairs] for pairs in there)
    odd_place = place % 2
    even_row = high % 2 == 0

    def to_rows(value):
        value = value[:, 0]
        near = lax.ppermute(lax.dynamic_index_in_dim(value, odd_place, 0, False), LINE_AXES, there[0])
        far = lax.ppermute(lax.dynamic_index_in_dim(value, 1 - odd_place, 0, False), LINE_AXES, there[1])
        return jnp.concatenate([jnp.where(even_row, near, far), jnp.where(even_row, far, near)], axis=0)

    def from_rows(value):
        value = value.reshape(2, piece, width)
        near = lax.ppermute(lax.dynamic_index_in_dim(value, high % 2, 0, False), LINE_AXES, back[0])
        far = lax.ppermute(lax.dynamic_index_in_dim(value, 1 - high % 2, 0, False), LINE_AXES, back[1])
        even = odd_place == 0
        return jnp.stack([jnp.where(even, near, far), jnp.where(even, far, near)])[:, None]

    def frames_to_row(value):
        if group > 2:
            return lax.all_gather(value, ROW_AXES, axis=0, tiled=True)
        other = lax.ppermute(value, "core", swap)
        return jnp.concatenate([jnp.where(first_core, value, other), jnp.where(first_core, other, value)], axis=0)

    def heads_to_frames(value):
        if group > 2:
            return lax.all_to_all(value, ROW_AXES, split_axis=0, concat_axis=1, tiled=True)
        other = lax.ppermute(lax.dynamic_slice_in_dim(value, (1 - core) * frames, frames, 0), "core", swap)
        own = lax.dynamic_slice_in_dim(value, core * frames, frames, 0)
        return jnp.concatenate([jnp.where(first_core, own, other), jnp.where(first_core, other, own)], axis=1)

    def frames_to_heads(value):
        if group > 2:
            return lax.all_to_all(value, ROW_AXES, split_axis=1, concat_axis=0, tiled=True)
        other = lax.ppermute(lax.dynamic_slice_in_dim(value, (1 - core) * heads_wide, heads_wide, 1), "core", swap)
        own = lax.dynamic_slice_in_dim(value, core * heads_wide, heads_wide, 1)
        return jnp.concatenate([jnp.where(first_core, own, other), jnp.where(first_core, other, own)], axis=0)

    def share_on_line(value):
        pieces = [value]
        for flip in range(1, line):
            pieces.append(lax.ppermute(value, ("hi", "lo"), [(i, i ^ flip) for i in range(line)]))
        pieces = jnp.stack(pieces)
        return jnp.stack([lax.dynamic_index_in_dim(pieces, place ^ i, 0, False) for i in range(line)])

    def gather_planes(value):
        return lax.all_gather(value, ("plane", "core"), axis=0, tiled=True).reshape(devices, -1, width)

    up_rows, down_rows, out_rows = w_up.shape[0], w_down.shape[0], w_out.shape[0]
    skip_rows = w_skip.shape[0]
    columns = w_up.shape[1] // width
    middle = jnp.concatenate([w_qkv[:, i * width : (i + 1) * width] for i in range(3)] + [w_out], axis=0)
    late = jnp.concatenate([w_down] + [w_up[:, i * width : (i + 1) * width] for i in range(columns)], axis=0)
    early = share_on_line(w_skip)
    early, middle, late = lax.optimization_barrier((early, middle, late))
    early = gather_planes(early)
    middle, late = share_on_line(middle), share_on_line(late)
    middle = gather_planes(middle)

    in_place = out_rows % 16 == 0
    hidden = w_up.shape[1]
    chunk = hidden // (2 * planes)

    def weight(gathered, begin, rows, first, count):
        block = (count // rows, rows, width)
        if in_place:
            return gathered, block, (first // count, begin // rows, 0)
        taken = gathered[first // rows : (first + count) // rows, begin : begin + rows]
        return taken.reshape(1, count, width), (1, count, width), (0, 0, 0)

    skip_top, skip_bottom = (weight(early, 0, skip_rows, i * width, width) for i in range(2))
    out_weight = weight(middle, 3 * out_rows, out_rows, 0, width)
    x, s = (v.reshape(frames, width) for v in (inputs, skips))
    (resid_in,) = rowwise(
        merge_kernel, frames, [("", x), ("", s), ("weight", skip_top), ("weight", skip_bottom)], [(width, bf16)], light=True
    )

    labels_own = segment_ids[:, 0]
    labels_other = lax.ppermute(labels_own, "core", swap)
    labels_pick = jnp.where(core == high // micro, labels_own, labels_other)
    seg = lax.dynamic_index_in_dim(labels_pick, high % micro, 0, False)
    names = jnp.arange(labels, dtype=jnp.int32)
    starts = jnp.sum((seg[:, None] < names[None, :]).astype(jnp.int32), axis=0)
    ends = jnp.sum((seg[:, None] <= names[None, :]).astype(jnp.int32), axis=0)
    offset = jnp.sum(jnp.where(seg[:, None] == names[None, :], starts[None, :], 0), axis=1)
    where_at = jnp.arange(length, dtype=jnp.int32) - offset
    by_block = seg.reshape(-1, BLOCK)
    begin = jnp.sum(jnp.where(by_block[:, :1] == names[None, :], starts[None, :], 0), axis=1)
    finish = jnp.sum(jnp.where(by_block[:, -1:] == names[None, :], ends[None, :], 0), axis=1)
    ranges = jnp.stack([begin // BLOCK, (finish + BLOCK - 1) // BLOCK]).astype(jnp.int32)
    half = HEAD_DIM // 2
    rates = jnp.exp(-math.log(10000.0) * jnp.arange(half, dtype=f32) / half)
    angles = where_at.astype(f32)[:, None] * rates
    cosine = jnp.tile(jnp.cos(angles), (1, 4))
    sine = jnp.sin(angles)
    sine = jnp.concatenate([-sine, sine, -sine, sine], axis=1)
    seg_column, seg_row = seg[:, None], seg[None, :]
    mine = lax.dynamic_slice_in_dim(seg, member * frames, frames, 0)

    steps = lax.all_gather(time_steps[:, 0], ("plane", "core"), axis=0, tiled=True).reshape(-1)
    quarter = w_mod.shape[0] // 2
    pace = jnp.exp(-math.log(10000.0) * jnp.arange(quarter, dtype=f32) / quarter)
    turns = steps.astype(f32)[:, None] * pace
    embedded = jnp.concatenate([jnp.sin(turns), jnp.cos(turns)], axis=1).astype(bf16)
    block_mod = jnp.dot(embedded, w_mod, preferred_element_type=f32)
    own_columns = block_mod.shape[1]
    block_mod = block_mod.reshape(planes, 1, highs, 1, labels, own_columns)
    block_mod = jnp.broadcast_to(block_mod, (planes, 2, highs, lows, labels, own_columns))
    block_mod = lax.all_to_all(
        block_mod.reshape(devices, labels, own_columns), ALL_AXES, split_axis=0, concat_axis=0, tiled=True
    )
    modulation = jnp.moveaxis(block_mod, 0, 1).reshape(labels, 4, width)

    def own_qkv(gathered):
        parts = []
        for i in range(3):
            whole = gathered[:, i * out_rows : (i + 1) * out_rows].reshape(width, width)
            parts.append(lax.dynamic_slice_in_dim(whole, member * heads_wide, heads_wide, 1))
        return jnp.concatenate(parts, axis=1)

    mine_column, mine_row = mine[:, None], mine[None, :]
    shift_one, scale_one, shift_two, scale_two = (modulation[:, i] for i in range(4))

    resid_in = to_rows(resid_in.reshape(inputs.shape))
    resid_in, late, cotangent, modulation, cosine, sine, ranges = lax.optimization_barrier(
        (resid_in, late, cotangent, modulation, cosine, sine, ranges)
    )
    (normed_one,) = rowwise(
        norm_kernel,
        frames,
        [("", resid_in), ("", mine_column), ("whole", shift_one), ("whole", scale_one)],
        [(width, bf16)],
        light=True,
    )
    normed_row = frames_to_row(normed_one)
    normed_row, x, s = lax.optimization_barrier((normed_row, x, s))
    stacked = jnp.concatenate([x, s], axis=1)
    if in_place:
        projected = project(normed_row, middle, 0, out_rows, heads_wide, member)
    else:
        projected = jnp.dot(normed_row, own_qkv(middle), preferred_element_type=f32).astype(bf16)
    late = gather_planes(late)
    cot = to_rows(cotangent)
    if in_place:
        per = width // chunk
        up_weight = (late, (devices, up_rows, chunk), lambda j: (0, down_rows // up_rows + j // per, j % per))
        down_weight = (late, (chunk // down_rows, down_rows, width), lambda j: (j, 0, 0))
    else:
        pieces = [late[:, down_rows + i * up_rows : down_rows + (i + 1) * up_rows] for i in range(columns)]
        up_full = jnp.concatenate([v.reshape(width, width) for v in pieces], axis=1)
        up_weight = (up_full[None], (1, width, chunk), lambda j: (0, 0, j))
        down_weight = (late[:, :down_rows].reshape(1, -1, width), (1, chunk, width), lambda j: (0, j, 0))
    mixed_heads, queries, keys, logsum = attend_forward(ranges, projected, cosine, sine, seg_column, seg_row)
    mixed = heads_to_frames(mixed_heads)
    resid_mid, normed_two = rowwise(
        out_norm_kernel,
        frames,
        [("", mixed), ("weight", out_weight), ("", resid_in), ("", mine_column), ("whole", shift_two), ("whole", scale_two)],
        [(width, f32), (width, bf16)],
        flops=2 * frames * width * width,
    )
    normed_two, stacked = lax.optimization_barrier((normed_two, stacked))
    result, grad_normed_two, grad_up, grad_down = feed_forward_and_back(
        normed_two, cot, resid_mid, hidden, chunk, up_weight, down_weight
    )

    def over_cores(kept, axis):
        other = lax.ppermute(lax.dynamic_index_in_dim(kept, 1 - core, axis, False), "core", swap)
        own = lax.dynamic_index_in_dim(kept, core, axis, False)
        return (own.astype(f32) + other.astype(f32)).astype(bf16)

    plane = lax.axis_index("plane")

    def exchange(value, axes, here, count):
        total = lax.dynamic_index_in_dim(value, here, 0, False).astype(f32)
        for flip in range(1, count):
            sent = lax.dynamic_index_in_dim(value, here ^ flip, 0, False)
            total += lax.ppermute(sent, axes, [(i, i ^ flip) for i in range(count)]).astype(f32)
        return total

    def exchange_planes(value):
        return exchange(value, "plane", plane, planes).astype(bf16)

    def exchange_line(value):
        return exchange(value.reshape(line, -1, value.shape[-1]), ("hi", "lo"), place, line)

    grad_up, grad_down = (
        lax.psum_scatter(v, ("plane", "core"), scatter_dimension=0, tiled=True) for v in (grad_up, grad_down)
    )

    grad_mid, grad_mid_low, grad_frames, grad_shift_two, grad_scale_two = rowwise(
        norm_two_back_kernel,
        frames,
        [("", grad_normed_two), ("", resid_mid), ("", cot), ("", mine_column), ("row", mine_row),
         ("whole", scale_two), ("weight", out_weight)],
        [(width, f32), (width, bf16), (width, bf16)],
        sums=2,
        light=True,
    )
    grad_heads = frames_to_heads(grad_frames)
    grad_out = lax.dot_general(mixed, grad_mid_low, (((0,), (0,)), ((), ())), preferred_element_type=f32)
    grad_out = over_cores(grad_out.astype(bf16).reshape(planes, 2, -1, width), 1)
    grad_heads, grad_out, result = lax.optimization_barrier((grad_heads, grad_out, result))
    block_out = from_rows(result)
    grad_proj = attend_backward(
        ranges, queries, keys, projected, mixed_heads, grad_heads, logsum, cosine, sine, seg_column, seg_row
    )
    grad_proj, block_out, grad_up = lax.optimization_barrier((grad_proj, block_out, grad_up))
    grad_up = lax.psum_scatter(grad_up, ("hi", "lo"), scatter_dimension=0, tiled=True)
    if group > 2:
        partial = dot_nt(grad_proj, own_qkv(middle)).astype(bf16)
        grad_one = lax.psum_scatter(partial, ROW_AXES, scatter_dimension=0, tiled=True).astype(f32)
        grad_one_other = jnp.zeros((frames, width), bf16)
    else:
        if in_place:
            pull = functools.partial(pull_project, grad_proj, middle, out_rows, heads_wide, member, frames)
            away, home = pull(1 - core, bf16), pull(core, f32)
        else:
            qkv_own = own_qkv(middle)
            away = lax.dynamic_slice_in_dim(grad_proj, (1 - core) * frames, frames, 0)
            home = lax.dynamic_slice_in_dim(grad_proj, core * frames, frames, 0)
            away, home = dot_nt(away, qkv_own).astype(bf16), dot_nt(home, qkv_own)
        grad_one_other = lax.ppermute(away, "core", swap)
        grad_one = home
    grad_in, grad_shift_one, grad_scale_one = rowwise(
        norm_one_back_kernel,
        frames,
        [("", grad_one), ("", grad_one_other), ("", resid_in), ("", grad_mid), ("", mine_column), ("row", mine_row),
         ("whole", scale_one)],
        [(width, bf16)],
        sums=2,
    )
    grad_in_home = from_rows(grad_in)
    grad_proj, grad_in = lax.optimization_barrier((grad_proj, grad_in))
    grad_qkv = lax.dot_general(normed_row, grad_proj, (((0,), (0,)), ((), ())), preferred_element_type=f32)
    grad_qkv = grad_qkv.astype(bf16)
    if group > 2:
        grad_qkv = grad_qkv.reshape(planes, 2, highs, lows, -1, 3, 1, heads_wide)
        grad_qkv = jnp.moveaxis(grad_qkv, (1, 3), (0, 1)).reshape(group, -1, 3, 1, heads_wide)
        grad_qkv = lax.all_to_all(grad_qkv, ROW_AXES, split_axis=0, concat_axis=3, tiled=True)
        grad_qkv = grad_qkv.reshape(-1, 3 * width)
        grad_qkv = lax.psum_scatter(grad_qkv, ("plane", "hi"), scatter_dimension=0, tiled=True).astype(f32)
    else:
        split = grad_qkv.reshape(planes, 2, -1, 3 * heads_wide)
        other = lax.ppermute(lax.dynamic_index_in_dim(split, 1 - core, 1, False), "core", swap)
        own = lax.dynamic_index_in_dim(split, core, 1, False)
        own, other = (v.reshape(-1, 3 * heads_wide) for v in (own, other))
        left, right = jnp.where(first_core, own, other), jnp.where(first_core, other, own)
        grad_qkv = jnp.concatenate(
            [v[:, i * heads_wide : (i + 1) * heads_wide] for i in range(3) for v in (left, right)], axis=1
        )
        grad_qkv = jnp.concatenate([grad_qkv.reshape(planes, -1, 3 * width), grad_out], axis=2)
        grad_qkv = exchange_planes(grad_qkv)
    grad_mod = jnp.stack([v[:labels] for v in (grad_shift_one, grad_scale_one, grad_shift_two, grad_scale_two)], axis=1)
    grad_mod = jnp.moveaxis(grad_mod.reshape(labels, devices, own_columns), 1, 0)
    grad_mod = lax.all_to_all(grad_mod, ALL_AXES, split_axis=0, concat_axis=0, tiled=True)
    grad_in_home, grad_qkv, grad_down, grad_mod = lax.optimization_barrier((grad_in_home, grad_qkv, grad_down, grad_mod))
    grad_down = lax.psum_scatter(grad_down, ("hi", "lo"), scatter_dimension=0, tiled=True)
    grad_up, grad_down = grad_up.astype(f32), grad_down.astype(f32)
    if group == 2:
        grad_qkv = grad_qkv.reshape(line, -1, 4 * width)
        grad_qkv = lax.all_to_all(grad_qkv, ("hi", "lo"), split_axis=0, concat_axis=0, tiled=True)
        grad_qkv = jnp.sum(grad_qkv.astype(f32), axis=0)
        grad_qkv, grad_out = grad_qkv[:, : 3 * width], grad_qkv[:, 3 * width :]
    else:
        grad_out = exchange_line(exchange_planes(grad_out))
    home = grad_in_home.reshape(frames, width)
    grad_skip_w = lax.dot_general(stacked, home, (((0,), (0,)), ((), ())), preferred_element_type=f32).astype(bf16)
    grad_skip_w = exchange_planes(over_cores(grad_skip_w.reshape(planes, 2, -1, width), 1))
    grad_inputs, grad_skips = rowwise(
        unmerge_kernel,
        frames,
        [("", home), ("weight", skip_top), ("weight", skip_bottom)],
        [(width, bf16), (width, bf16)],
        flops=4 * frames * width * width,
    )
    grad_inputs, grad_skips = (v.reshape(grad_in_home.shape) for v in (grad_inputs, grad_skips))

    grad_skip_w = exchange_line(grad_skip_w)
    grad_mod = jnp.sum(grad_mod.reshape(planes, 2, highs, lows, labels, own_columns), axis=(1, 3))
    grad_mod = lax.dot_general(
        embedded.astype(f32),
        grad_mod.reshape(-1, own_columns),
        (((0,), (0,)), ((), ())),
        precision=lax.Precision.HIGHEST,
        preferred_element_type=f32,
    )
    return (
        block_out,
        grad_inputs,
        grad_skips,
        grad_skip_w,
        grad_qkv,
        grad_out,
        grad_up,
        grad_down,
        grad_mod,
    )


def solution(mesh):
    batch, wide = mesh.devices.shape

    def run(inputs, *rest):
        rows = 2 * inputs.shape[0]
        assert inputs.shape[0] == 2 and inputs.shape[1] == batch and wide % rows == 0
        fine = Mesh(mesh.devices.reshape(batch // 2, 2, rows, wide // rows), ALL_AXES)
        by_batch, by_wide = ("plane", "core"), ("hi", "lo")
        frames = P(None, by_batch, by_wide, None)
        rowed = P(None, by_batch, None)
        weight, columns = P(ALL_AXES, None), P(None, ALL_AXES)
        mapped = jax.shard_map(
            body,
            mesh=fine,
            in_specs=(frames, frames, frames, rowed, rowed) + (weight,) * 5 + (columns,),
            out_specs=(frames, frames, frames) + (weight,) * 5 + (columns,),
            check_vma=False,
        )
        return mapped(inputs, *rest)

    return run
```
